32 devices in a mesh: dp: 4 (over y, x), ctx: 8 (over z, core).
Axes of the slice: x: 2, y: 2, z: 4, core: 2. Of those that a mesh axis runs over, the one named last changes fastest.
Arguments:
- inputs: bfloat16 [8, 2048, 768], P('dp', 'ctx'), may hold values from -6 to 6
- segments: int32 [8, 2048], P('dp', 'ctx'), may hold values from 0 to 7, never falling along the last dimension, each value on 1 to 1024 neighbouring positions
- w_qkv: bfloat16 [768, 2304], P(('dp', 'ctx')), may hold values from -0.21875 to 0.21875
- b_query: bfloat16 [768], P(('dp', 'ctx')), may hold values from -3 to 3
- b_value: bfloat16 [768], P(('dp', 'ctx')), may hold values from -1.75 to 1.75
- w_out: bfloat16 [768, 768], P(('dp', 'ctx')), may hold values from -2.5 to 2.5
- b_attn: bfloat16 [768], P(('dp', 'ctx')), may hold values from -1.75 to 1.75
- gain_one: bfloat16 [768], P(('dp', 'ctx')), may hold values from 0.5 to 1.5
- shift_one: bfloat16 [768], P(('dp', 'ctx')), may hold values from -1.75 to 1.75
- w_in: bfloat16 [768, 3072], P(('dp', 'ctx')), may hold values from -0.21875 to 0.21875
- b_in: bfloat16 [3072], P(('dp', 'ctx')), may hold values from -1.75 to 1.75
- w_back: bfloat16 [3072, 768], P(('dp', 'ctx')), may hold values from -0.109375 to 0.109375
- b_back: bfloat16 [768], P(('dp', 'ctx')), may hold values from -1.75 to 1.75
- gain_two: bfloat16 [768], P(('dp', 'ctx')), may hold values from 0.5 to 1.5
- shift_two: bfloat16 [768], P(('dp', 'ctx')), may hold values from -1.75 to 1.75
- cotangent: bfloat16 [8, 2048, 768], P('dp', 'ctx'), may hold values from -6 to 6
Outputs:
- output: bfloat16 [8, 2048, 768], P('dp', 'ctx')
- input_grad: float32 [8, 2048, 768], P('dp', 'ctx')
- grad_w_qkv: float32 [768, 2304], P(('dp', 'ctx'))
- grad_b_query: float32 [768], P(('dp', 'ctx'))
- grad_b_value: float32 [768], P(('dp', 'ctx'))
- grad_w_out: float32 [768, 768], P(('dp', 'ctx'))
- grad_b_attn: float32 [768], P(('dp', 'ctx'))
- grad_gain_one: float32 [768], P(('dp', 'ctx'))
- grad_shift_one: float32 [768], P(('dp', 'ctx'))
- grad_w_in: float32 [768, 3072], P(('dp', 'ctx'))
- grad_b_in: float32 [3072], P(('dp', 'ctx'))
- grad_w_back: float32 [3072, 768], P(('dp', 'ctx'))
- grad_b_back: float32 [768], P(('dp', 'ctx'))
- grad_gain_two: float32 [768], P(('dp', 'ctx'))
- grad_shift_two: float32 [768], P(('dp', 'ctx'))
The draws below stay inside these ranges and needn't reach their ends.
Inputs may be any that keep to these rules, and one draw needn't show every extreme that they name: `segments`: within each sequence segment numbers never fall; every document has 1 to 1024 tokens, and one of them has exactly that many.
All inputs are finite; a program needn't handle non-finite values.
Results may differ from the reference program's by a relative error of at most 0.015.
Values may be sent and summed in bfloat16 or wider, within the bound.
A program may use at most 192 MiB of HBM per device.

```python
import math
import jax
import jax.numpy as jnp
import numpy as np
from jax import lax

D = 768
HEADS = 12
HEAD_DIM = 64
FF = 3072
SEQ_LEN = 2048
DOCS = 8
NSEQ = 8


def levels(stream_key, shape, split, least, top_value):
    level, own = 1.0, jax.random.fold_in(stream_key, 6)
    for axis_at, parts in split:
        draws = jnp.exp(jax.random.uniform(jax.random.fold_in(own, axis_at), (parts,), jnp.float32, least / len(split), top_value / len(split)))
        level = level * jnp.repeat(draws, shape[axis_at] // parts).reshape([-1 if axis == axis_at else 1 for axis in range(len(shape))])
    return level


def profile(number_of, total, limit, lean):
    weights = [(1 << 20) // math.isqrt(grade ** lean) + 1 for grade in range(2, number_of + 1)]
    rest, given = total - limit - (number_of - 1), [1] * (number_of - 1)
    while rest > 0:
        movable = [i for i in range(number_of - 1) if given[i] < limit]
        pool, left = sum([weights[i] for i in movable]), rest
        for i in movable:
            addition = min(limit - given[i], max(1, left * weights[i] // pool), rest)
            given[i] = given[i] + addition
            rest = rest - addition
    return np.array([limit] + given)


def ragged(key, count, total, most, lean):
    if count == 2:
        one = jax.random.randint(key, (), max(1, total - most), min(most, total - 1) + 1)
        return jnp.stack([one, total - one])
    lengths = jnp.asarray(profile(count, total, most, lean), jnp.int32)
    pairs = (count - 1) // 2
    donor, sink = lengths[1:1 + 2 * pairs:2], lengths[2:2 + 2 * pairs:2]
    room = jnp.minimum(donor - 1, most - sink)
    passed = jax.random.randint(jax.random.fold_in(key, 1), (pairs,), 0, 1 << 20) % (room + 1)
    lengths = lengths.at[1:1 + 2 * pairs:2].set(donor - passed).at[2:2 + 2 * pairs:2].set(sink + passed)
    return lengths[jax.random.permutation(jax.random.fold_in(key, 2), count)]


def noise(stream_key, dims, width, limit, shards=(), kind=jnp.bfloat16):
    array = width * jax.random.normal(stream_key, dims, jnp.float32)
    if shards:
        array = array * levels(stream_key, dims, shards, -0.22, 0.18)
    return jnp.clip(array, -limit, limit).astype(kind)


def setup_inputs(seed: int = 0) -> dict:
    keys = jax.random.split(jax.random.key(seed), 17)
    inputs = noise(keys[0], (NSEQ, SEQ_LEN, D), 1.0, 6.0, ((0, 4), (1, 8)))
    segments = jax.vmap(lambda own: jnp.searchsorted(jnp.cumsum(ragged(own, DOCS, SEQ_LEN, SEQ_LEN // 2, 2)), jnp.arange(SEQ_LEN), side="right"))(jax.random.split(keys[1], NSEQ)).reshape((NSEQ, SEQ_LEN)).astype(jnp.int32)
    w_qkv = noise(keys[2], (D, 3 * D), D ** -0.5, 0.21875, ((0, 32),))
    b_query = noise(keys[3], (D,), 0.5, 3.0, ((0, 32),))
    b_value = noise(keys[4], (D,), 0.3, 1.75, ((0, 32),))
    w_out = noise(keys[5], (D, D), (D // 128) ** -0.5, 2.5, ((0, 32),))
    b_attn = noise(keys[6], (D,), 0.3, 1.75, ((0, 32),))
    gain_one = jnp.clip(1.0 + 0.1 * jax.random.normal(keys[7], (D,), jnp.float32), 0.5, 1.5).astype(jnp.bfloat16)
    shift_one = noise(keys[8], (D,), 0.3, 1.75, ((0, 32),))
    w_in = noise(keys[9], (D, FF), D ** -0.5, 0.21875, ((0, 32),))
    b_in = noise(keys[10], (FF,), 0.3, 1.75, ((0, 32),))
    w_back = noise(keys[11], (FF, D), FF ** -0.5, 0.109375, ((0, 32),))
    b_back = noise(keys[12], (D,), 0.3, 1.75, ((0, 32),))
    gain_two = jnp.clip(1.0 + 0.1 * jax.random.normal(keys[13], (D,), jnp.float32), 0.5, 1.5).astype(jnp.bfloat16)
    shift_two = noise(keys[14], (D,), 0.3, 1.75, ((0, 32),))
    cotangent = noise(keys[15], (NSEQ, SEQ_LEN, D), 1.0, 6.0, ((0, 4), (1, 8)))
    return {"inputs": inputs, "segments": segments, "w_qkv": w_qkv, "b_query": b_query, "b_value": b_value, "w_out": w_out, "b_attn": b_attn, "gain_one": gain_one, "shift_one": shift_one, "w_in": w_in, "b_in": b_in, "w_back": w_back, "b_back": b_back, "gain_two": gain_two, "shift_two": shift_two, "cotangent": cotangent}


negative_fill = -1e+30
layer_eps = 1e-12

@jax.custom_vjp
def low(v):
    return lax.optimization_barrier(v.astype(jnp.bfloat16)).astype(jnp.float32)

@jax.custom_vjp
def low_back(v):
    return v

def low_keep(v):
    return (low(v), None)

def low_pass(kept, grad):
    return (grad,)

def back_keep(v):
    return (v, None)

def back_low(kept, grad):
    return (low(grad),)
low.defvjp(low_keep, low_pass)
low_back.defvjp(back_keep, back_low)

def layer_norm(resid, gain, shift):
    center = resid - lax.optimization_barrier(jnp.mean(resid, axis=-1, keepdims=True))
    spread = lax.optimization_barrier(jnp.mean(center * center, axis=-1, keepdims=True))
    return center * lax.rsqrt(spread + layer_eps) * gain + shift

def exact_dot(left, right):
    return jnp.dot(left, right, precision=lax.Precision.HIGHEST)

def round_both(value):
    return low(low_back(value))

def attend_block(query_block, query_ids, key_rows, value_rows, key_ids):
    scores = jnp.einsum('qhd,khd->hqk', query_block, key_rows, precision=lax.Precision.HIGHEST) * HEAD_DIM ** (-0.5)
    scores = low_back(scores)
    allowed = (query_ids[:, None] == key_ids[None, :])[None]
    scores = jnp.where(allowed, scores, negative_fill)
    weights = low(jax.nn.softmax(scores, axis=-1))
    return jnp.einsum('hqk,khd->qhd', weights, value_rows, precision=lax.Precision.HIGHEST)

def forward(seq_in, seq_ids, params):
    w_qkv, b_query, b_value, w_out, b_attn, gain_one, shift_one, w_in, b_in, w_back, b_back, gain_two, shift_two = params
    length = seq_in.shape[0]
    model_width = seq_in.shape[1]
    projected = exact_dot(seq_in, w_qkv)
    queries = round_both(projected[:, :model_width] + b_query).reshape(length, HEADS, HEAD_DIM)
    key_rows = round_both(projected[:, model_width:2 * model_width]).reshape(length, HEADS, HEAD_DIM)
    value_rows = round_both(projected[:, 2 * model_width:] + b_value).reshape(length, HEADS, HEAD_DIM)
    block_rows = min(512, length)
    block_count = length // block_rows
    attend_saved = jax.checkpoint(attend_block)
    context = lax.map(lambda pieces: attend_saved(pieces[0], pieces[1], key_rows, value_rows, seq_ids), (queries.reshape(block_count, block_rows, HEADS, HEAD_DIM), seq_ids.reshape(block_count, block_rows)))
    attended = round_both(context.reshape(length, model_width))
    attn_out = low_back(exact_dot(attended, w_out) + b_attn)
    normed = layer_norm(seq_in + attn_out, gain_one, shift_one)
    pre_act = low_back(exact_dot(low(normed), w_in) + b_in)
    activ = low(jax.nn.gelu(pre_act, approximate=False))
    branch = low_back(exact_dot(activ, w_back) + b_back)
    return layer_norm(normed + branch, gain_two, shift_two)

def reference(inputs, segments, w_qkv, b_query, b_value, w_out, b_attn, gain_one, shift_one, w_in, b_in, w_back, b_back, gain_two, shift_two, cotangent):
    params = tuple((arr.astype(jnp.float32) for arr in (w_qkv, b_query, b_value, w_out, b_attn, gain_one, shift_one, w_in, b_in, w_back, b_back, gain_two, shift_two)))
    zeroed = tuple((jnp.zeros_like(arr) for arr in params))

    def one_sequence(carry, entries):
        seq_in, seq_ids, seq_cot = entries
        result, backward = jax.vjp(lambda xin, prm: forward(xin, seq_ids, prm), seq_in.astype(jnp.float32), params)
        d_input, d_params = backward(seq_cot.astype(jnp.float32))
        carry = tuple((acc + grad for acc, grad in zip(carry, d_params)))
        return (carry, (result.astype(jnp.bfloat16), d_input))
    totals, (results, d_inputs) = lax.scan(one_sequence, zeroed, (inputs, segments, cotangent))
    return (results, d_inputs, totals[0], totals[1], totals[2], totals[3], totals[4], totals[5], totals[6], totals[7], totals[8], totals[9], totals[10], totals[11], totals[12])
```

```python
import functools
import jax
import jax.numpy as jnp
from jax import lax
from jax.experimental import pallas as pl
from jax.experimental.pallas import tpu as pltpu
from jax.sharding import PartitionSpec as P

HEADS = 12
HEAD_DIM = 64
layer_eps = 1e-12
MESH_ID = pl.DeviceIdType.MESH
BF = jnp.bfloat16
F32 = jnp.float32
VMEM_LIMIT = 64 * 1024 * 1024 - 65536
SCORE_SCALE = 0.125 * 1.4426950408889634
EXCLUDE = -1e30


def place():
    d = lax.axis_index("dp")
    t = lax.axis_index("ctx")
    z = t // 2
    c = t % 2
    dx = d + 1 - 2 * (d % 2)
    dy = (d + 2) % 4
    return d, t, z, c, dx, dy


def remote(src, dst, ss, rs, dev):
    return pltpu.make_async_remote_copy(
        src_ref=src, dst_ref=dst, send_sem=ss, recv_sem=rs, device_id=dev, device_id_type=MESH_ID
    )


def greet(devices):
    bar = pltpu.get_barrier_semaphore()
    for dev in devices:
        pl.semaphore_signal(bar, inc=1, device_id=dev, device_id_type=MESH_ID)
    pl.semaphore_wait(bar, len(devices))


N_ARR = 5
FIRST_X = (0, 1, 2)
FIRST_Y = (3, 4)


def gather_kernel(x, wi, wo, sm, wb, wq, xs, gi, go, gs, gb, gq,
                  loc, s_x, r_x, s_xf, s_xd, r_xd, s_z, r_z, s_px, r_px, s_py, r_py, s_f, r_f, s_c, r_c):
    d, t, z, c, dx, dy = place()
    h = z // 2
    zp = z + 1 - 2 * (z % 2)
    inner = (z + h) % 2 == 1
    dxy = (dx + 2) % 4
    me = lambda zz: (d, zz * 2 + c)
    core = (d, z * 2 + 1 - c)
    nx, ny = (dx, t), (dy, t)
    others = [(z + k) % 4 for k in (1, 2, 3)]
    greet([me(zz) for zz in others] + [core, nx, ny])
    sends = []

    def go_(cp):
        cp.start()
        sends.append(cp)

    own = [wi, wo, sm, wb]
    dst = [gi, go, gs, gb, gq]
    half = 128
    for k in range(2):
        rows = pl.ds(k * half, half)
        go_(remote(x.at[1 - h, rows], xs.at[t, rows], s_x.at[0, k], r_x.at[z, k], me(2 - h)))
        go_(remote(x.at[h, rows], xs.at[t, rows], s_x.at[1, k], r_x.at[z, k], me(zp)))
    locals_ = [pltpu.make_async_copy(x.at[h], xs.at[t], loc.at[0])]
    for a in range(4):
        locals_.append(pltpu.make_async_copy(own[a], dst[a].at[d, z, c], loc.at[1 + a]))
    locals_.append(pltpu.make_async_copy(wq.at[z % 2], gq.at[d, z, c], loc.at[5]))
    for cp in locals_:
        cp.start()

    def mine(a, zz):
        return wq.at[zz % 2] if a == 4 else own[a]

    for a in (4, 3, 0, 1, 2):
        for k in (1, 2, 3):
            zz = others[k - 1]
            go_(remote(mine(a, zz), dst[a].at[d, z, c], s_z.at[a, k - 1], r_z.at[a, z], me(zz)))

    def plane(zz, first):
        for a in (4, 3, 0, 1, 2):
            src = mine(a, z) if first else dst[a].at[d, zz, c]
            go_(remote(src, dst[a].at[d, zz, c], s_px.at[a, zz], r_px.at[a, zz], nx))
            go_(remote(src, dst[a].at[d, zz, c], s_py.at[a, zz], r_py.at[a, zz], ny))

    def got(ref, ss, rs, dev):
        remote(ref, ref, ss, rs, dev).wait_recv()

    def forward(zz):
        for a in FIRST_Y:
            got(dst[a].at[dy, zz, c], s_py.at[a, zz], r_py.at[a, zz], ny)
            go_(remote(dst[a].at[dy, zz, c], dst[a].at[dy, zz, c], s_f.at[a, zz], r_f.at[a, zz], nx))
        for a in FIRST_X:
            got(dst[a].at[dx, zz, c], s_px.at[a, zz], r_px.at[a, zz], nx)
            go_(remote(dst[a].at[dx, zz, c], dst[a].at[dx, zz, c], s_f.at[a, zz], r_f.at[a, zz], ny))

    def across(zz):
        for a in FIRST_Y:
            got(dst[a].at[dx, zz, c], s_px.at[a, zz], r_px.at[a, zz], nx)
            got(dst[a].at[dxy, zz, c], s_f.at[a, zz], r_f.at[a, zz], nx)
        for a in FIRST_X:
            got(dst[a].at[dy, zz, c], s_py.at[a, zz], r_py.at[a, zz], ny)
            got(dst[a].at[dxy, zz, c], s_f.at[a, zz], r_f.at[a, zz], ny)
        for a in range(N_ARR):
            go_(remote(dst[a].at[:, zz, c], dst[a].at[:, zz, c], s_c.at[a, zz], r_c.at[a, zz], core))

    plane(z, True)
    far = [(2 * (1 - h) + j) for j in (0, 1)]
    for k in range(2):
        rows = pl.ds(k * half, half)
        for j in (0, 1):
            got(xs.at[far[j] * 2 + c, rows], s_x.at[0, k], r_x.at[far[j], k], me(2 - h))

            @pl.when(inner)
            def _(j=j, k=k, rows=rows):
                remote(xs.at[far[j] * 2 + c, rows], xs.at[far[j] * 2 + c, rows],
                       s_xf.at[j, k], r_x.at[far[j], k], me(zp)).start()

    for cp in locals_:
        cp.wait()
    order = [z] + others
    forward(z)
    for zz in others[:1]:
        for a in (4, 3, 0, 1, 2):
            got(dst[a].at[d, zz, c], s_z.at[a, 0], r_z.at[a, zz], me(zz))
        plane(zz, False)
    across(z)
    forward(others[0])
    for zz in others[1:]:
        for a in (4, 3, 0, 1, 2):
            got(dst[a].at[d, zz, c], s_z.at[a, 0], r_z.at[a, zz], me(zz))
        plane(zz, False)
    for k in range(2):
        rows = pl.ds(k * half, half)
        got(xs.at[zp * 2 + c, rows], s_x.at[1, k], r_x.at[zp, k], me(zp))
    for zz in (z, zp, far[0], far[1]):
        go_(remote(xs.at[zz * 2 + c], xs.at[zz * 2 + c], s_xd.at[zz], r_xd.at[zz], core))
    across(others[0])
    forward(others[1])
    forward(others[2])
    across(others[1])
    across(others[2])
    for zz in order:
        got(xs.at[zz * 2 + 1 - c], s_xd.at[zz], r_xd.at[zz], core)
        for a in range(N_ARR):
            ref = dst[a].at[:, zz, 1 - c]
            got(ref, s_c.at[a, zz], r_c.at[a, zz], core)
    for cp in sends:
        cp.wait_send()

    @pl.when(inner)
    def _():
        for k in range(2):
            rows = pl.ds(k * half, half)
            for j in (0, 1):
                remote(xs.at[far[j] * 2 + c, rows], xs.at[far[j] * 2 + c, rows],
                       s_xf.at[j, k], r_x.at[far[j], k], me(zp)).wait_send()


def any_spec():
    return pl.BlockSpec(memory_space=pl.ANY)


def vmem_spec():
    return pl.BlockSpec(memory_space=pltpu.VMEM)


def dma(*shape):
    return pltpu.SemaphoreType.DMA(shape)


def gather_all(x, wi, wo, sm, wb, wq):
    grid_of = lambda a: jax.ShapeDtypeStruct((4, 4, 2) + a.shape, a.dtype)
    return pl.pallas_call(
        gather_kernel,
        out_shape=[
            jax.ShapeDtypeStruct((8,) + x.shape[1:], x.dtype),
            grid_of(wi), grid_of(wo), grid_of(sm), grid_of(wb), grid_of(wq[0]),
        ],
        in_specs=[any_spec()] * 6,
        out_specs=[any_spec()] * 6,
        scratch_shapes=[
            dma(6), dma(2, 2), dma(4, 2), dma(2, 2), dma(4), dma(4), dma(N_ARR, 3), dma(N_ARR, 4),
            dma(N_ARR, 4), dma(N_ARR, 4), dma(N_ARR, 4), dma(N_ARR, 4), dma(N_ARR, 4), dma(N_ARR, 4),
            dma(N_ARR, 4), dma(N_ARR, 4),
        ],
        compiler_params=pltpu.CompilerParams(collective_id=1, has_side_effects=True),
        name="gather_all",
    )(x, wi, wo, sm, wb, wq)


def exchange_kernel(a, b, loc, ss, rs):
    d, t, z, c, dx, dy = place()
    others = [(t + k) % 8 for k in range(1, 8)]
    greet([(d, o) for o in others])
    lc = pltpu.make_async_copy(a.at[t], b.at[t], loc)
    lc.start()
    cps = []
    for k in (4, 3, 5, 2, 6, 1, 7):
        cp = remote(a.at[others[k - 1]], b.at[t], ss.at[k - 1], rs.at[k - 1], (d, others[k - 1]))
        cp.start()
        cps.append(cp)
    for k in range(1, 8):
        src = (t + 8 - k) % 8
        remote(b.at[src], b.at[src], ss.at[k - 1], rs.at[k - 1], (d, src)).wait_recv()
    for cp in cps:
        cp.wait_send()
    lc.wait()


def exchange(a, cid):
    return pl.pallas_call(
        exchange_kernel,
        out_shape=jax.ShapeDtypeStruct(a.shape, a.dtype),
        in_specs=[any_spec()],
        out_specs=any_spec(),
        scratch_shapes=[pltpu.SemaphoreType.DMA, dma(7), dma(7)],
        compiler_params=pltpu.CompilerParams(collective_id=cid, has_side_effects=True),
        name="exchange",
    )(a)


QB = 256
KB = 256
NH = 3


def marks_of(ids_row):
    kinds = lax.broadcasted_iota(jnp.int32, (16, ids_row.shape[1]), 0).astype(F32)
    return kinds == ids_row


def fill_keys_queries(qkv, ids, ka, qa):
    hit = marks_of(ids[...])
    ones = jnp.where(hit, 1.0, 0.0)
    away = jnp.where(hit, 0.0, EXCLUDE).astype(BF)
    for g in range(NH):
        rows = slice(g * 64, (g + 1) * 64)
        ka[g] = jnp.concatenate([qkv[1, rows].astype(F32), ones], axis=0).T.astype(BF)
        qa[g, :64] = qkv[0, rows]
        qa[g, 64:] = away


def attn_fwd_kernel(lo, hi, qkv, ids, att, o32, lse, ka, va, qa):
    n = qkv.shape[2]
    fill_keys_queries(qkv, ids, ka, qa)
    for g in range(NH):
        va[g, :64] = qkv[2, g * 64:(g + 1) * 64]
        va[g, 64:] = jnp.ones((16, n), BF)

    def queries(i, _):
        cols = pl.ds(pl.multiple_of(i * QB, QB), QB)

        def block(j, carry):
            at = pl.ds(pl.multiple_of(j * KB, KB), KB)
            out = []
            s = [jnp.dot(ka[g, at, :], qa[g, :, cols], preferred_element_type=F32) for g in range(NH)]
            for g in range(NH):
                m, acc = carry[g]
                m2 = jnp.maximum(m, jnp.max(s[g], axis=0, keepdims=True))
                p = jnp.exp2((s[g] - m2) * SCORE_SCALE).astype(BF)
                acc = acc * jnp.exp2((m - m2) * SCORE_SCALE) + jnp.dot(
                    va[g, :, at], p, preferred_element_type=F32)
                out.append((m2, acc))
            return tuple(out)

        first = tuple((jnp.full((1, QB), -3e38, F32), jnp.zeros((80, QB), F32)) for _ in range(NH))
        res = lax.fori_loop(lo[i], hi[i], block, first)
        for g in range(NH):
            m, acc = res[g]
            total = acc[64:65]
            o = acc[:64] / total
            o32[i, g * 64:(g + 1) * 64] = o
            att[i, g * 64:(g + 1) * 64] = o.astype(BF)
            lse[g, pl.ds(i, 1)] = m * SCORE_SCALE + jnp.log2(total)
        return 0

    lax.fori_loop(0, n // QB, queries, 0)


def smem_spec():
    return pl.BlockSpec(memory_space=pltpu.SMEM)


def attn_fwd(lo, hi, qkv, ids):
    n = qkv.shape[2]
    nq = n // QB
    return pl.pallas_call(
        attn_fwd_kernel,
        in_specs=[smem_spec(), smem_spec(), vmem_spec(), vmem_spec()],
        out_specs=[vmem_spec()] * 3,
        scratch_shapes=[pltpu.VMEM((NH, n, 80), BF), pltpu.VMEM((NH, 80, n), BF), pltpu.VMEM((NH, 80, n), BF)],
        out_shape=[
            jax.ShapeDtypeStruct((nq, 192, QB), BF),
            jax.ShapeDtypeStruct((nq, 192, QB), F32),
            jax.ShapeDtypeStruct((NH, nq, QB), F32),
        ],
        compiler_params=pltpu.CompilerParams(vmem_limit_bytes=VMEM_LIMIT),
        name="attn_fwd",
    )(lo, hi, qkv, ids)


def attn_bwd_kernel(lo, hi, qkv, ids, da, o32, lse, out, ka, qa, vk, dkv):
    n = qkv.shape[2]
    fill_keys_queries(qkv, ids, ka, qa)
    for g in range(NH):
        vk[g] = qkv[2, g * 64:(g + 1) * 64].astype(F32).T.astype(BF)
    dkv[...] = jnp.zeros_like(dkv)

    def queries(i, _):
        cols = pl.ds(pl.multiple_of(i * QB, QB), QB)
        fixed = []
        for g in range(NH):
            rows = slice(g * 64, (g + 1) * 64)
            do = da[i, rows]
            inner = jnp.sum(do.astype(F32) * o32[i, rows], axis=0, keepdims=True)
            zero = jnp.zeros((64, QB), F32)
            ra = jnp.concatenate([do.astype(F32), zero], axis=0).T.astype(BF)
            rb = jnp.concatenate([zero, qkv[0, rows, cols].astype(F32)], axis=0).T.astype(BF)
            fixed.append((inner, lse[g, pl.ds(i, 1)], ra, rb))

        def block(j, carry):
            at = pl.ds(pl.multiple_of(j * KB, KB), KB)
            out = []
            s = [jnp.dot(ka[g, at, :], qa[g, :, cols], preferred_element_type=F32) for g in range(NH)]
            dp = [jnp.dot(vk[g, at, :], da[i, g * 64:(g + 1) * 64], preferred_element_type=F32) for g in range(NH)]
            for g in range(NH):
                inner, lse_i, ra, rb = fixed[g]
                p = jnp.exp2(s[g] * SCORE_SCALE - lse_i)
                ds = (p * (dp[g] - inner)).astype(BF)
                dkv[g, at, :] += jnp.dot(p.astype(BF), ra, preferred_element_type=F32) + jnp.dot(
                    ds, rb, preferred_element_type=F32)
                out.append(carry[g] + jnp.dot(qkv[1, g * 64:(g + 1) * 64, at], ds, preferred_element_type=F32))
            return tuple(out)

        dq = lax.fori_loop(lo[i], hi[i], block, tuple(jnp.zeros((64, QB), F32) for _ in range(NH)))
        for g in range(NH):
            out[0, g * 64:(g + 1) * 64, cols] = (dq[g] * 0.125).astype(BF)
        return 0

    lax.fori_loop(0, n // QB, queries, 0)
    for g in range(NH):
        rows = slice(g * 64, (g + 1) * 64)
        dkv_t = dkv[g].T
        out[1, rows] = (dkv_t[64:] * 0.125).astype(BF)
        out[2, rows] = dkv_t[:64].astype(BF)


def attn_bwd(lo, hi, qkv, ids, da, o32, lse):
    n = qkv.shape[2]
    return pl.pallas_call(
        attn_bwd_kernel,
        in_specs=[smem_spec(), smem_spec()] + [vmem_spec()] * 5,
        out_specs=vmem_spec(),
        scratch_shapes=[
            pltpu.VMEM((NH, n, 80), BF), pltpu.VMEM((NH, 80, n), BF), pltpu.VMEM((NH, n, 64), BF),
            pltpu.VMEM((NH, n, 128), F32),
        ],
        out_shape=jax.ShapeDtypeStruct((3, 192, n), BF),
        compiler_params=pltpu.CompilerParams(vmem_limit_bytes=VMEM_LIMIT),
        name="attn_bwd",
    )(lo, hi, qkv, ids, da, o32, lse)


def scatter_kernel(dxp, di, do_, ds_, db, dq, ox, oi, oo, os_, ob, oq, *rest):
    k_arr = 4
    rd = rest[0:4]
    r1 = rest[4:8]
    r2 = rest[8:12]
    r3 = rest[12:16]
    r4 = rest[16:20]
    r5 = rest[20:24]
    (xd, x3, x4, x5, q0, q1, q2, qr,
     s_d, r_d, s_1, r_1, s_2, r_2, s_3, r_3, s_4, r_4, s_5, r_5,
     s_q1, r_q1, s_q2, r_q2, s_qe, r_qe) = rest[24:]
    d, t, z, c, dx, dy = place()
    x, y = d % 2, d // 2
    h = z // 2
    zp = z + 1 - 2 * (z % 2)
    inner = (z + h) % 2 == 1
    me = lambda zz: (d, zz * 2 + c)
    core = (d, z * 2 + 1 - c)
    nx, ny = (dx, t), (dy, t)
    line = [(t + k) % 8 for k in range(1, 8)]
    greet([(d, o) for o in line] + [nx, ny])
    part = [di, do_, ds_, db]
    outs = [oi, oo, os_, ob]
    by_x = [True, True, True, False]
    far = [2 * (1 - h), 2 * (1 - h) + 1]
    order = [far[0], far[1], zp, z]
    sends = []

    def go_(cp):
        cp.start()
        sends.append(cp)

    def got(ref, ss, rs, dev):
        remote(ref, ref, ss, rs, dev).wait_recv()

    for n_, zz in enumerate(order):
        go_(remote(dxp.at[zz * 2 + 1 - c], xd.at[zz], s_d.at[4, n_], r_d.at[4, n_], core))
    for n_, zz in enumerate(order):
        for a in range(k_arr):
            for yy in range(2):
                go_(remote(part[a].at[yy, :, zz, 1 - c], rd[a].at[yy, :, zz], s_d.at[5 + 2 * a + yy, n_],
                           r_d.at[5 + 2 * a + yy, n_], core))
    go_(remote(dq.at[:, 1 - x], q1, s_q1, r_q1, nx))

    def add_rows(dst, src):
        n0 = dst.shape[0]

        def step(i, _):
            dst[i] = dst[i] + src[i]
            return 0

        lax.fori_loop(0, n0, step, 0)

    def add_tok(dst, src):
        def step(i, _):
            at = pl.ds(pl.multiple_of(i * 32, 32), 32)
            dst[at, :] = dst[at, :] + src[at, :]
            return 0

        lax.fori_loop(0, dst.shape[0] // 32, step, 0)

    for n_, zz in enumerate(order):
        got(xd.at[zz], s_d.at[4, n_], r_d.at[4, n_], core)
        add_tok(xd.at[zz], dxp.at[zz * 2 + c])
        if n_ == 2:
            go_(remote(xd.at[zz], x5, s_5.at[4], r_5.at[4], me(zz)))

        if n_ < 2:
            @pl.when(jnp.logical_not(inner))
            def _(n_=n_, zz=zz):
                remote(xd.at[zz], x3.at[n_], s_3.at[4, n_], r_3.at[4, n_], me(zp)).start()

    for n_, zz in enumerate(order):
        for a in range(k_arr):
            for yy in range(2):
                got(rd[a].at[yy, :, zz], s_d.at[5 + 2 * a + yy, n_], r_d.at[5 + 2 * a + yy, n_], core)
                for xx in range(2):
                    add_rows(rd[a].at[yy, xx, zz], part[a].at[yy, xx, zz, c])
            if by_x[a]:
                go_(remote(rd[a].at[:, 1 - x, zz], r1[a].at[n_], s_1.at[a, n_], r_1.at[a, n_], nx))
            else:
                go_(remote(rd[a].at[1 - y, :, zz], r1[a].at[n_], s_1.at[a, n_], r_1.at[a, n_], ny))
        if n_ == 0:
            got(q1, s_q1, r_q1, nx)
            for yy in range(2):
                for zc in range(8):
                    q0[yy, zc // 2, zc % 2] = q1[yy, zc // 2, zc % 2] + dq[yy, x, zc // 2, zc % 2]
            go_(remote(q0.at[1 - y], q2, s_q2, r_q2, ny))
        if n_ == 1:
            for j in range(2):
                @pl.when(inner)
                def _(j=j):
                    got(x3.at[j], s_3.at[4, j], r_3.at[4, j], me(zp))
                    add_tok(xd.at[far[j]], x3.at[j])
                    remote(xd.at[far[j]], x4, s_4.at[4, j], r_4.at[4], me(far[j])).start()
        if n_ == 2:
            got(q2, s_q2, r_q2, ny)
            for zc in range(8):
                q0[y, zc // 2, zc % 2] = q0[y, zc // 2, zc % 2] + q2[zc // 2, zc % 2]
            for k in range(1, 8):
                to = line[k - 1]
                go_(remote(q0.at[y, to // 2, to % 2], qr.at[t], s_qe.at[k - 1], r_qe.at[k - 1], (d, to)))

    for n_, zz in enumerate(order):
        for a in range(k_arr):
            if by_x[a]:
                got(r1[a].at[n_], s_1.at[a, n_], r_1.at[a, n_], nx)
                for yy in range(2):
                    add_rows(rd[a].at[yy, x, zz], r1[a].at[n_, yy])
                go_(remote(rd[a].at[1 - y, x, zz], r2[a].at[n_], s_2.at[a, n_], r_2.at[a, n_], ny))
            else:
                got(r1[a].at[n_], s_1.at[a, n_], r_1.at[a, n_], ny)
                for xx in range(2):
                    add_rows(rd[a].at[y, xx, zz], r1[a].at[n_, xx])
                go_(remote(rd[a].at[y, 1 - x, zz], r2[a].at[n_], s_2.at[a, n_], r_2.at[a, n_], nx))

    for n_, zz in enumerate(order):
        for a in range(k_arr):
            got(r2[a].at[n_], s_2.at[a, n_], r_2.at[a, n_], ny if by_x[a] else nx)
            add_rows(rd[a].at[y, x, zz], r2[a].at[n_])
            mine_ = rd[a].at[y, x]
            if n_ < 2:
                @pl.when(jnp.logical_not(inner))
                def _(a=a, n_=n_, zz=zz, mine_=mine_):
                    remote(mine_.at[zz], r3[a].at[n_], s_3.at[a, n_], r_3.at[a, n_], me(zp)).start()
            elif n_ == 2:
                go_(remote(mine_.at[zz], r5[a], s_5.at[a], r_5.at[a], me(zz)))
    for n_ in range(2):
        for a in range(k_arr):
            @pl.when(inner)
            def _(a=a, n_=n_):
                mine_ = rd[a].at[y, x, far[n_]]
                got(r3[a].at[n_], s_3.at[a, n_], r_3.at[a, n_], me(zp))
                add_rows(mine_, r3[a].at[n_])
                remote(mine_, r4[a], s_4.at[a, n_], r_4.at[a], me(far[n_])).start()
    src_in = 2 - h
    got(x5, s_5.at[4], r_5.at[4], me(zp))
    got(x4, s_4.at[4, 0], r_4.at[4], me(src_in))

    def tok(i, _):
        at = pl.ds(pl.multiple_of(i * 32, 32), 32)
        ox[h, at, :] = xd[z, at, :] + x5[at, :]
        ox[1 - h, at, :] = x4[at, :]
        return 0

    lax.fori_loop(0, 8, tok, 0)
    for k in range(1, 8):
        src = (t + 8 - k) % 8
        got(qr.at[src], s_qe.at[k - 1], r_qe.at[k - 1], (d, src))
    qr[t] = q0[y, z, c]
    for g in range(4):
        oq[g] = qr[g].astype(F32) + qr[4 + g].astype(F32)
    for a in range(k_arr):
        got(r5[a], s_5.at[a], r_5.at[a], me(zp))
        got(r4[a], s_4.at[a, 0], r_4.at[a], me(src_in))
        acc = rd[a].at[y, x, z]
        for i in range(acc.shape[0]):
            outs[a][i] = acc[i].astype(F32) + r5[a][i].astype(F32) + r4[a][i].astype(F32)
    for cp in sends:
        cp.wait_send()
    for n_ in range(2):
        zz = far[n_]

        @pl.when(jnp.logical_not(inner))
        def _(n_=n_, zz=zz):
            remote(xd.at[zz], x3.at[n_], s_3.at[4, n_], r_3.at[4, n_], me(zp)).wait_send()
            for a in range(k_arr):
                remote(rd[a].at[y, x, zz], r3[a].at[n_], s_3.at[a, n_], r_3.at[a, n_], me(zp)).wait_send()

        @pl.when(inner)
        def _(n_=n_, zz=zz):
            remote(xd.at[zz], x4, s_4.at[4, n_], r_4.at[4], me(zz)).wait_send()
            for a in range(k_arr):
                remote(rd[a].at[y, x, zz], r4[a], s_4.at[a, n_], r_4.at[a], me(zz)).wait_send()


def scatter_all(dxp, di, do_, ds_, db, dq):
    arrs = [di, do_, ds_, db]
    tails = [a.shape[4:] for a in arrs]
    scratch = []
    for lead in ((2, 2, 4), (4, 2), (4,), (2,), (), ()):
        for a, tail in zip(arrs, tails):
            scratch.append(pltpu.VMEM(lead + tail, a.dtype))
    tok = dxp.shape[1:]
    qt = dq.shape[4:]
    scratch += [
        pltpu.VMEM((4,) + tok, BF), pltpu.VMEM((2,) + tok, BF), pltpu.VMEM(tok, BF), pltpu.VMEM(tok, BF),
        pltpu.VMEM((2, 4, 2) + qt, BF), pltpu.VMEM((2, 4, 2) + qt, BF), pltpu.VMEM((4, 2) + qt, BF),
        pltpu.VMEM((8,) + qt, BF),
        dma(13, 4), dma(13, 4), dma(4, 4), dma(4, 4), dma(4, 4), dma(4, 4), dma(5, 2), dma(5, 2),
        dma(5, 2), dma(5), dma(5), dma(5),
        pltpu.SemaphoreType.DMA, pltpu.SemaphoreType.DMA, pltpu.SemaphoreType.DMA, pltpu.SemaphoreType.DMA,
        dma(7), dma(7),
    ]
    return pl.pallas_call(
        scatter_kernel,
        out_shape=[jax.ShapeDtypeStruct((2,) + tok, BF)]
        + [jax.ShapeDtypeStruct(tail, F32) for tail in tails]
        + [jax.ShapeDtypeStruct((4,) + qt, F32)],
        in_specs=[vmem_spec()] * 6,
        out_specs=[vmem_spec()] * 6,
        scratch_shapes=scratch,
        compiler_params=pltpu.CompilerParams(
            collective_id=4, has_side_effects=True, vmem_limit_bytes=VMEM_LIMIT),
        name="scatter_all",
    )(dxp, di, do_, ds_, db, dq)


def erf_parts(u):
    phi_c = 0.5 * (1.0 + lax.erf(u * 0.7071067811865476))
    return phi_c, phi_c + u * jnp.exp(-0.5 * u * u) * 0.3989422804014327


def norm_forward(r):
    center = r - jnp.mean(r, axis=-1, keepdims=True)
    inv = lax.rsqrt(jnp.mean(center * center, axis=-1, keepdims=True) + layer_eps)
    return center * inv, inv


def norm_backward(n, inv, gain, dy):
    gd = gain * dy
    return (gd - jnp.mean(gd, axis=-1, keepdims=True) - n * jnp.mean(gd * n, axis=-1, keepdims=True)) * inv


def on_device_fast(
    inputs, segments, w_qkv, b_query, b_value, w_out, b_attn, gain_one, shift_one,
    w_in, b_in, w_back, b_back, gain_two, shift_two, cotangent,
):
    nseq, span, width = inputs.shape
    tokens = nseq * span
    ff = w_in.shape[1]
    depth = w_in.shape[0]
    d, t, z, c, _, _ = place()
    h = z // 2
    group = (z % 2) * 2 + c
    per = width // 4
    vecs = (b_query, b_value, b_attn, gain_one, shift_one, b_back, gain_two, shift_two)
    ffd = b_in.shape[0]
    small = jnp.concatenate(
        [v.astype(F32) for v in vecs] + [b_in.astype(F32), segments.astype(F32).reshape(-1)])
    small = jnp.pad(small, (0, 1024 - small.shape[0])).reshape(8, 128)
    wq = w_qkv.reshape(depth, 3, 2, 2 * per).transpose(2, 0, 1, 3).reshape(2, depth // 8, 8, 6 * per)
    xs, gi, go, gs, gb, gq = gather_all(
        inputs, w_in.reshape(depth // 8, 8, ff), w_out.reshape(depth // 8, 8, width), small,
        w_back.reshape(ffd // 8, 8, width), wq)
    wide_in = gi.reshape(width, ff)
    wide_out = go.reshape(width, width)
    wide_back = gb.reshape(ff, width)
    flat = gs.reshape(32, 1024)
    nv = len(vecs)
    fv = flat[:, :nv * depth].reshape(32, nv, depth).transpose(1, 0, 2).reshape(nv, width)
    full_b_in = flat[:, nv * depth:nv * depth + ffd].reshape(ff)
    at = nv * depth + ffd
    ids = lax.dynamic_index_in_dim(gs, d, 0, keepdims=False).reshape(8, 1024)[:, at:at + nseq * span]
    ids = lax.dynamic_index_in_dim(ids.reshape(8, nseq, span), h, 1, keepdims=False)
    n = 8 * span
    ids_row = ids.reshape(1, n)
    blocks = ids_row.reshape(n // QB, QB)
    lo = (jnp.sum(ids_row < blocks[:, :1], axis=1) // KB).astype(jnp.int32)
    hi = ((jnp.sum(ids_row <= blocks[:, -1:], axis=1) + KB - 1) // KB).astype(jnp.int32)
    w_own = lax.dynamic_index_in_dim(gq.reshape(width, 3, 2, per), c, 2, keepdims=False).reshape(width, 3 * per)
    bias_q = lax.dynamic_slice_in_dim(fv[0], group * per, per)
    bias_v = lax.dynamic_slice_in_dim(fv[1], group * per, per)
    bias = jnp.concatenate([bias_q, jnp.zeros_like(bias_q), bias_v])
    xseq = xs.reshape(n, width)
    qkv = jnp.einsum("kf,tk->ft", w_own, xseq, preferred_element_type=F32) + bias[:, None]
    qkv = qkv.astype(BF).reshape(3, per, n)
    att, o32, lse = attn_fwd(lo, hi, qkv, ids_row)
    att = exchange(att, 2).reshape(nseq, width, span)

    x32 = inputs.reshape(tokens, width).astype(F32)
    attn_out = jnp.einsum("sit,id->std", att, wide_out, preferred_element_type=F32).reshape(tokens, width)
    resid_one = x32 + attn_out + fv[2]
    n1, inv1 = norm_forward(resid_one)
    normed = n1 * fv[3] + fv[4]
    normed_low = normed.astype(BF)
    pre_act = jnp.dot(normed_low, wide_in, preferred_element_type=F32) + full_b_in
    phi_c, slope = erf_parts(pre_act)
    activ = (pre_act * phi_c).astype(BF)
    branch = jnp.dot(activ, wide_back, preferred_element_type=F32) + fv[5]
    n2, inv2 = norm_forward(normed + branch)
    output = (n2 * fv[6] + fv[7]).astype(BF).reshape(nseq, span, width)
    dy = cotangent.reshape(tokens, width).astype(F32)
    d_two = norm_backward(n2, inv2, fv[6], dy)
    d_branch = d_two.astype(BF)
    grad_w_back = jnp.einsum("tf,td->fd", activ, d_branch, preferred_element_type=F32).astype(BF)
    d_activ = jnp.einsum("td,fd->tf", d_branch, wide_back, preferred_element_type=F32)
    d_pre = (d_activ * slope).astype(BF)
    grad_w_in = jnp.einsum("td,tf->df", normed_low, d_pre, preferred_element_type=F32).astype(BF)
    d_normed = d_two + jnp.einsum("tf,df->td", d_pre, wide_in, preferred_element_type=F32)
    d_one = norm_backward(n1, inv1, fv[3], d_normed)
    d_attn = d_one.astype(BF)
    d_attn3 = d_attn.reshape(nseq, span, width)
    grad_w_out = jnp.einsum("sit,std->id", att, d_attn3, preferred_element_type=F32).astype(BF)
    d_att = jnp.einsum("std,id->sit", d_attn3, wide_out, preferred_element_type=F32).astype(BF)
    d_att = exchange(d_att.reshape(8, per, span), 3)
    d_proj = attn_bwd(lo, hi, qkv, ids_row, d_att, o32, lse)
    proj = d_proj.reshape(3 * per, n)
    dx_part = jnp.einsum("ft,kf->tk", proj, w_own, preferred_element_type=F32).astype(BF)
    grad_w_qkv = jnp.einsum("tk,ft->kf", xseq, proj, preferred_element_type=F32).astype(BF)
    g_bias = jnp.sum(d_proj.astype(F32), axis=2)
    spread = jnp.zeros((2, width), F32)
    spread = lax.dynamic_update_slice(spread, g_bias[::2], (0, group * per))
    sums = [
        spread[0], spread[1],
        jnp.sum(d_attn.astype(F32), axis=0),
        jnp.sum(d_normed * n1, axis=0),
        jnp.sum(d_normed, axis=0),
        jnp.sum(d_branch.astype(F32), axis=0),
        jnp.sum(dy * n2, axis=0),
        jnp.sum(dy, axis=0),
    ]
    g_in = jnp.sum(d_pre.astype(F32), axis=0)
    g_small = jnp.concatenate(
        [jnp.stack(sums).reshape(nv, 32, depth).transpose(1, 0, 2).reshape(32, nv * depth), g_in.reshape(32, ffd)],
        axis=1)
    g_small = jnp.pad(g_small, ((0, 0), (0, 1024 - g_small.shape[1])))
    owner = (2, 2, 4, 2)
    ox, oi, oo, os_, ob, oq = scatter_all(
        dx_part.reshape(8, span, width),
        grad_w_in.reshape(owner + (depth // 8, 8, ff)),
        grad_w_out.reshape(owner + (depth // 8, 8, width)),
        g_small.reshape(owner + (8, 128)),
        grad_w_back.reshape(owner + (ffd // 8, 8, width)),
        grad_w_qkv.reshape(owner + (depth // 8, 8, 3 * per)),
    )
    input_grad = d_one.reshape(nseq, span, width) + ox.astype(F32)
    g_qkv = oq.reshape(4, depth, 3, per).transpose(1, 2, 0, 3).reshape(depth, 3 * width)
    sv = os_.reshape(1024)
    vec = lambda k: sv[k * depth:(k + 1) * depth]
    return (
        output, input_grad, g_qkv, vec(0), vec(1), oo.reshape(depth, width), vec(2), vec(3), vec(4),
        oi.reshape(depth, ff), sv[nv * depth:nv * depth + ffd], ob.reshape(ffd, width), vec(5), vec(6), vec(7),
    )


negative_fill = -1e30


def layer_norm(resid, gain, shift):
    center = resid - jnp.mean(resid, axis=-1, keepdims=True)
    spread = jnp.mean(center * center, axis=-1, keepdims=True)
    return center * lax.rsqrt(spread + layer_eps) * gain + shift


def gelu_exact(values):
    return jax.nn.gelu(values, approximate=False)


def attend_forward(entries):
    query_rows, key_rows, value_rows, query_ids, key_ids = entries
    scores = jnp.einsum(
        "qhd,khd->hqk", query_rows, key_rows, preferred_element_type=jnp.float32
    ) * HEAD_DIM ** (-0.5)
    allowed = (query_ids[:, None] == key_ids[None, :])[None]
    scores = jnp.where(allowed, scores, negative_fill)
    peak = jnp.max(scores, axis=-1, keepdims=True)
    raised = jnp.exp(scores - peak)
    total = jnp.sum(raised, axis=-1, keepdims=True)
    probs_low = (raised / total).astype(jnp.bfloat16)
    context = jnp.einsum("hqk,khd->qhd", probs_low, value_rows, preferred_element_type=jnp.float32)
    return (context, (peak + jnp.log(total))[..., 0])


def score_terms(query_rows, key_rows, value_rows, grad_context, log_total, query_ids, key_ids):
    scale = HEAD_DIM ** (-0.5)
    scores = (
        jnp.einsum("qhd,khd->hqk", query_rows, key_rows, preferred_element_type=jnp.float32) * scale
    )
    allowed = (query_ids[:, None] == key_ids[None, :])[None]
    probs = jnp.where(allowed, jnp.exp(scores - log_total[..., None]), 0.0)
    d_probs = jnp.einsum(
        "qhd,khd->hqk", grad_context, value_rows, preferred_element_type=jnp.float32
    )
    return (probs, d_probs)


def attend_backward(entries):
    query_rows, key_rows, value_rows, grad_context, log_total, query_ids, key_ids = entries
    scale = HEAD_DIM ** (-0.5)
    probs, d_probs = score_terms(
        query_rows, key_rows, value_rows, grad_context, log_total, query_ids, key_ids
    )
    inner = jnp.sum(probs * d_probs, axis=-1, keepdims=True)
    d_scores = (probs * (d_probs - inner)).astype(jnp.bfloat16)
    d_queries = (
        jnp.einsum("hqk,khd->qhd", d_scores, key_rows, preferred_element_type=jnp.float32) * scale
    )
    d_keys = (
        jnp.einsum("hqk,qhd->khd", d_scores, query_rows, preferred_element_type=jnp.float32) * scale
    )
    d_values = jnp.einsum(
        "hqk,qhd->khd", probs.astype(jnp.bfloat16), grad_context, preferred_element_type=jnp.float32
    )
    length = key_rows.shape[0]
    return (
        d_queries,
        d_keys.reshape(length, HEADS * HEAD_DIM),
        d_values.reshape(length, HEADS * HEAD_DIM),
    )


def on_device_general(
    inputs,
    segments,
    w_qkv,
    b_query,
    b_value,
    w_out,
    b_attn,
    gain_one,
    shift_one,
    w_in,
    b_in,
    w_back,
    b_back,
    gain_two,
    shift_two,
    cotangent,
):
    seq_count, group_len, model_width = inputs.shape
    tok_count = seq_count * group_len
    gathered = (
        lax.all_gather(w_qkv, ("dp", "ctx"), axis=0, tiled=True),
        lax.all_gather(b_query, ("dp", "ctx"), axis=0, tiled=True),
        lax.all_gather(b_value, ("dp", "ctx"), axis=0, tiled=True),
        lax.all_gather(w_out, ("dp", "ctx"), axis=0, tiled=True),
        lax.all_gather(b_attn, ("dp", "ctx"), axis=0, tiled=True),
        lax.all_gather(gain_one, ("dp", "ctx"), axis=0, tiled=True),
        lax.all_gather(shift_one, ("dp", "ctx"), axis=0, tiled=True),
        lax.all_gather(w_in, ("dp", "ctx"), axis=0, tiled=True),
        lax.all_gather(b_in, ("dp", "ctx"), axis=0, tiled=True),
        lax.all_gather(w_back, ("dp", "ctx"), axis=0, tiled=True),
        lax.all_gather(b_back, ("dp", "ctx"), axis=0, tiled=True),
        lax.all_gather(gain_two, ("dp", "ctx"), axis=0, tiled=True),
        lax.all_gather(shift_two, ("dp", "ctx"), axis=0, tiled=True),
    )
    (
        wide_qkv,
        full_b_query,
        full_b_value,
        wide_out,
        full_b_attn,
        full_gain_one,
        full_shift_one,
        wide_in,
        full_b_in,
        wide_back,
        full_b_back,
        full_gain_two,
        full_shift_two,
    ) = gathered
    tokens = inputs.reshape(tok_count, model_width)
    projected = jnp.dot(tokens, wide_qkv, preferred_element_type=jnp.float32)
    query_low = (projected[:, :model_width] + full_b_query.astype(jnp.float32)).astype(jnp.bfloat16)
    key_low = projected[:, model_width : 2 * model_width].astype(jnp.bfloat16)
    value_low = (projected[:, 2 * model_width :] + full_b_value.astype(jnp.float32)).astype(
        jnp.bfloat16
    )
    key_ids = lax.all_gather(segments, "ctx", axis=1, tiled=True)
    key_local = key_low.reshape(seq_count, group_len, model_width)
    value_local = value_low.reshape(seq_count, group_len, model_width)
    key_whole, value_whole = (
        lax.all_gather(key_local, "ctx", axis=1, tiled=True),
        lax.all_gather(value_local, "ctx", axis=1, tiled=True),
    )
    seq_len = key_whole.shape[1]
    query_heads = query_low.reshape(seq_count, group_len, HEADS, HEAD_DIM)
    context, log_total = lax.map(
        attend_forward,
        (
            query_heads,
            key_whole.reshape(seq_count, seq_len, HEADS, HEAD_DIM),
            value_whole.reshape(seq_count, seq_len, HEADS, HEAD_DIM),
            segments,
            key_ids,
        ),
    )
    attended = context.reshape(tok_count, model_width).astype(jnp.bfloat16)
    attn_out = jnp.dot(attended, wide_out, preferred_element_type=jnp.float32) + full_b_attn.astype(
        jnp.float32
    )
    resid_one = tokens.astype(jnp.float32) + attn_out
    normed, norm_one_back = jax.vjp(
        layer_norm, resid_one, full_gain_one.astype(jnp.float32), full_shift_one.astype(jnp.float32)
    )
    normed_low = normed.astype(jnp.bfloat16)
    pre_act = jnp.dot(normed_low, wide_in, preferred_element_type=jnp.float32) + full_b_in.astype(
        jnp.float32
    )
    activ_f, gelu_back = jax.vjp(gelu_exact, pre_act)
    activ = activ_f.astype(jnp.bfloat16)
    branch = jnp.dot(activ, wide_back, preferred_element_type=jnp.float32) + full_b_back.astype(
        jnp.float32
    )
    resid_two = normed + branch
    final_norm, norm_two_back = jax.vjp(
        layer_norm, resid_two, full_gain_two.astype(jnp.float32), full_shift_two.astype(jnp.float32)
    )
    output = final_norm.astype(jnp.bfloat16).reshape(seq_count, group_len, model_width)
    back_qkv, back_out, back_in, back_back = (
        lax.all_gather(w_qkv, ("dp", "ctx"), axis=0, tiled=True),
        lax.all_gather(w_out, ("dp", "ctx"), axis=0, tiled=True),
        lax.all_gather(w_in, ("dp", "ctx"), axis=0, tiled=True),
        lax.all_gather(w_back, ("dp", "ctx"), axis=0, tiled=True),
    )
    d_final = cotangent.reshape(tok_count, model_width).astype(jnp.float32)
    d_two, grad_gain_two, grad_shift_two = norm_two_back(d_final)
    d_branch = d_two.astype(jnp.bfloat16)
    grad_b_back = jnp.sum(d_branch.astype(jnp.float32), axis=0)
    grad_w_back = jnp.einsum("tf,td->fd", activ, d_branch, preferred_element_type=jnp.float32)
    d_activ = jnp.einsum("td,fd->tf", d_branch, back_back, preferred_element_type=jnp.float32)
    d_pre = gelu_back(d_activ)[0].astype(jnp.bfloat16)
    grad_b_in = jnp.sum(d_pre.astype(jnp.float32), axis=0)
    grad_w_in = jnp.einsum("td,tf->df", normed_low, d_pre, preferred_element_type=jnp.float32)
    d_normed = d_two + jnp.einsum("tf,df->td", d_pre, back_in, preferred_element_type=jnp.float32)
    d_one, grad_gain_one, grad_shift_one = norm_one_back(d_normed)
    d_attn = d_one.astype(jnp.bfloat16)
    grad_b_attn = jnp.sum(d_attn.astype(jnp.float32), axis=0)
    grad_w_out = jnp.einsum("ti,td->id", attended, d_attn, preferred_element_type=jnp.float32)
    d_attended = jnp.einsum(
        "td,id->ti", d_attn, back_out, preferred_element_type=jnp.float32
    ).astype(jnp.bfloat16)
    key_back, value_back = (
        lax.all_gather(key_local, "ctx", axis=1, tiled=True),
        lax.all_gather(value_local, "ctx", axis=1, tiled=True),
    )
    grad_heads = d_attended.reshape(seq_count, group_len, HEADS, HEAD_DIM)
    d_query_part, d_key_part, d_value_part = lax.map(
        attend_backward,
        (
            query_heads,
            key_back.reshape(seq_count, seq_len, HEADS, HEAD_DIM),
            value_back.reshape(seq_count, seq_len, HEADS, HEAD_DIM),
            grad_heads,
            log_total,
            segments,
            key_ids,
        ),
    )
    d_key_sum, d_value_sum = (
        lax.psum_scatter(
            d_key_part.astype(jnp.bfloat16), "ctx", scatter_dimension=1, tiled=True
        ).astype(jnp.float32),
        lax.psum_scatter(
            d_value_part.astype(jnp.bfloat16), "ctx", scatter_dimension=1, tiled=True
        ).astype(jnp.float32),
    )
    d_queries = d_query_part.reshape(tok_count, model_width).astype(jnp.bfloat16)
    d_keys = d_key_sum.reshape(tok_count, model_width).astype(jnp.bfloat16)
    d_values = d_value_sum.reshape(tok_count, model_width).astype(jnp.bfloat16)
    d_proj = jnp.concatenate([d_queries, d_keys, d_values], axis=1)
    grad_w_qkv = jnp.einsum("td,te->de", tokens, d_proj, preferred_element_type=jnp.float32)
    grad_b_query = jnp.sum(d_queries.astype(jnp.float32), axis=0)
    grad_b_value = jnp.sum(d_values.astype(jnp.float32), axis=0)
    input_grad = d_one + jnp.einsum(
        "te,de->td", d_proj, back_qkv, preferred_element_type=jnp.float32
    )
    summed = (
        lax.psum_scatter(grad_w_qkv, ("dp", "ctx"), scatter_dimension=0, tiled=True),
        lax.psum_scatter(grad_b_query, ("dp", "ctx"), scatter_dimension=0, tiled=True),
        lax.psum_scatter(grad_b_value, ("dp", "ctx"), scatter_dimension=0, tiled=True),
        lax.psum_scatter(grad_w_out, ("dp", "ctx"), scatter_dimension=0, tiled=True),
        lax.psum_scatter(grad_b_attn, ("dp", "ctx"), scatter_dimension=0, tiled=True),
        lax.psum_scatter(grad_gain_one, ("dp", "ctx"), scatter_dimension=0, tiled=True),
        lax.psum_scatter(grad_shift_one, ("dp", "ctx"), scatter_dimension=0, tiled=True),
        lax.psum_scatter(grad_w_in, ("dp", "ctx"), scatter_dimension=0, tiled=True),
        lax.psum_scatter(grad_b_in, ("dp", "ctx"), scatter_dimension=0, tiled=True),
        lax.psum_scatter(grad_w_back, ("dp", "ctx"), scatter_dimension=0, tiled=True),
        lax.psum_scatter(grad_b_back, ("dp", "ctx"), scatter_dimension=0, tiled=True),
        lax.psum_scatter(grad_gain_two, ("dp", "ctx"), scatter_dimension=0, tiled=True),
        lax.psum_scatter(grad_shift_two, ("dp", "ctx"), scatter_dimension=0, tiled=True),
    )
    return (
        output,
        input_grad.reshape(seq_count, group_len, model_width),
        summed[0],
        summed[1],
        summed[2],
        summed[3],
        summed[4],
        summed[5],
        summed[6],
        summed[7],
        summed[8],
        summed[9],
        summed[10],
        summed[11],
        summed[12],
    )


def solution(mesh):
    placed = (
        P("dp", "ctx", None),
        P("dp", "ctx"),
        P(("dp", "ctx"), None),
        P(("dp", "ctx")),
        P(("dp", "ctx")),
        P(("dp", "ctx"), None),
        P(("dp", "ctx")),
        P(("dp", "ctx")),
        P(("dp", "ctx")),
        P(("dp", "ctx"), None),
        P(("dp", "ctx")),
        P(("dp", "ctx"), None),
        P(("dp", "ctx")),
        P(("dp", "ctx")),
        P(("dp", "ctx")),
        P("dp", "ctx", None),
    )
    fits = mesh.shape["dp"] == 4 and mesh.shape["ctx"] == 8
    return jax.shard_map(
        on_device_fast if fits else on_device_general,
        mesh=mesh,
        in_specs=placed,
        out_specs=(
            P("dp", "ctx", None),
            P("dp", "ctx", None),
            P(("dp", "ctx"), None),
            P(("dp", "ctx")),
            P(("dp", "ctx")),
            P(("dp", "ctx"), None),
            P(("dp", "ctx")),
            P(("dp", "ctx")),
            P(("dp", "ctx")),
            P(("dp", "ctx"), None),
            P(("dp", "ctx")),
            P(("dp", "ctx"), None),
            P(("dp", "ctx")),
            P(("dp", "ctx")),
            P(("dp", "ctx")),
        ),
        check_vma=False,
    )
```

```python
import functools
import jax
import jax.numpy as jnp
from jax import lax
from jax.experimental import pallas as pl
from jax.experimental.pallas import tpu as pltpu
from jax.sharding import PartitionSpec as P

HEADS = 12
HEAD_DIM = 64
layer_eps = 1e-12
MESH_ID = pl.DeviceIdType.MESH
BF = jnp.bfloat16
F32 = jnp.float32
VMEM_LIMIT = 64 * 1024 * 1024 - 65536
SCORE_SCALE = 0.125 * 1.4426950408889634
EXCLUDE = -1e30


def place():
    d = lax.axis_index("dp")
    t = lax.axis_index("ctx")
    z = t // 2
    c = t % 2
    dx = d + 1 - 2 * (d % 2)
    dy = (d + 2) % 4
    return d, t, z, c, dx, dy


def remote(src, dst, ss, rs, dev):
    return pltpu.make_async_remote_copy(
        src_ref=src, dst_ref=dst, send_sem=ss, recv_sem=rs, device_id=dev, device_id_type=MESH_ID
    )


def greet(devices):
    bar = pltpu.get_barrier_semaphore()
    for dev in devices:
        pl.semaphore_signal(bar, inc=1, device_id=dev, device_id_type=MESH_ID)
    pl.semaphore_wait(bar, len(devices))


def exchange_kernel(a, b, loc, ss, rs):
    d, t, z, c, dx, dy = place()
    others = [(t + k) % 8 for k in range(1, 8)]
    greet([(d, o) for o in others])
    lc = pltpu.make_async_copy(a.at[t], b.at[t], loc)
    lc.start()
    cps = []
    for k in (4, 3, 5, 2, 6, 1, 7):
        cp = remote(a.at[others[k - 1]], b.at[t], ss.at[k - 1], rs.at[k - 1], (d, others[k - 1]))
        cp.start()
        cps.append(cp)
    for k in range(1, 8):
        src = (t + 8 - k) % 8
        remote(b.at[src], b.at[src], ss.at[k - 1], rs.at[k - 1], (d, src)).wait_recv()
    for cp in cps:
        cp.wait_send()
    lc.wait()


def exchange(a, cid):
    return pl.pallas_call(
        exchange_kernel,
        out_shape=jax.ShapeDtypeStruct(a.shape, a.dtype),
        in_specs=[any_spec()],
        out_specs=any_spec(),
        scratch_shapes=[pltpu.SemaphoreType.DMA, dma(7), dma(7)],
        compiler_params=pltpu.CompilerParams(collective_id=cid, has_side_effects=True),
        name="exchange",
    )(a)


QB = 256
KB = 256
NH = 3


def marks_of(ids_row):
    kinds = lax.broadcasted_iota(jnp.int32, (16, ids_row.shape[1]), 0).astype(F32)
    return kinds == ids_row


def fill_keys_queries(qkv, ids, ka, qa):
    hit = marks_of(ids[...])
    ones = jnp.where(hit, 1.0, 0.0)
    away = jnp.where(hit, 0.0, EXCLUDE).astype(BF)
    for g in range(NH):
        rows = slice(g * 64, (g + 1) * 64)
        ka[g] = jnp.concatenate([qkv[1, rows].astype(F32), ones], axis=0).T.astype(BF)
        qa[g, :64] = qkv[0, rows]
        qa[g, 64:] = away


def attn_fwd_kernel(lo, hi, qkv, ids, att, o32, lse, ka, va, qa):
    n = qkv.shape[2]
    fill_keys_queries(qkv, ids, ka, qa)
    for g in range(NH):
        va[g, :64] = qkv[2, g * 64:(g + 1) * 64]
        va[g, 64:] = jnp.ones((16, n), BF)

    def queries(i, _):
        cols = pl.ds(pl.multiple_of(i * QB, QB), QB)

        def block(j, carry):
            at = pl.ds(pl.multiple_of(j * KB, KB), KB)
            out = []
            s = [jnp.dot(ka[g, at, :], qa[g, :, cols], preferred_element_type=F32) for g in range(NH)]
            for g in range(NH):
                m, acc = carry[g]
                m2 = jnp.maximum(m, jnp.max(s[g], axis=0, keepdims=True))
                p = jnp.exp2((s[g] - m2) * SCORE_SCALE).astype(BF)
                acc = acc * jnp.exp2((m - m2) * SCORE_SCALE) + jnp.dot(
                    va[g, :, at], p, preferred_element_type=F32)
                out.append((m2, acc))
            return tuple(out)

        first = tuple((jnp.full((1, QB), -3e38, F32), jnp.zeros((80, QB), F32)) for _ in range(NH))
        res = lax.fori_loop(lo[i], hi[i], block, first)
        for g in range(NH):
            m, acc = res[g]
            total = acc[64:65]
            o = acc[:64] / total
            o32[i, g * 64:(g + 1) * 64] = o
            att[i, g * 64:(g + 1) * 64] = o.astype(BF)
            lse[g, pl.ds(i, 1)] = m * SCORE_SCALE + jnp.log2(total)
        return 0

    lax.fori_loop(0, n // QB, queries, 0)


def smem_spec():
    return pl.BlockSpec(memory_space=pltpu.SMEM)


def attn_fwd(lo, hi, qkv, ids):
    n = qkv.shape[2]
    nq = n // QB
    return pl.pallas_call(
        attn_fwd_kernel,
        in_specs=[smem_spec(), smem_spec(), vmem_spec(), vmem_spec()],
        out_specs=[vmem_spec()] * 3,
        scratch_shapes=[pltpu.VMEM((NH, n, 80), BF), pltpu.VMEM((NH, 80, n), BF), pltpu.VMEM((NH, 80, n), BF)],
        out_shape=[
            jax.ShapeDtypeStruct((nq, 192, QB), BF),
            jax.ShapeDtypeStruct((nq, 192, QB), F32),
            jax.ShapeDtypeStruct((NH, nq, QB), F32),
        ],
        compiler_params=pltpu.CompilerParams(vmem_limit_bytes=VMEM_LIMIT),
        name="attn_fwd",
    )(lo, hi, qkv, ids)


def attn_bwd_kernel(lo, hi, qkv, ids, da, o32, lse, out, ka, qa, vk, dkv):
    n = qkv.shape[2]
    fill_keys_queries(qkv, ids, ka, qa)
    for g in range(NH):
        vk[g] = qkv[2, g * 64:(g + 1) * 64].astype(F32).T.astype(BF)
    dkv[...] = jnp.zeros_like(dkv)

    def queries(i, _):
        cols = pl.ds(pl.multiple_of(i * QB, QB), QB)
        fixed = []
        for g in range(NH):
            rows = slice(g * 64, (g + 1) * 64)
            do = da[i, rows]
            inner = jnp.sum(do.astype(F32) * o32[i, rows], axis=0, keepdims=True)
            zero = jnp.zeros((64, QB), F32)
            ra = jnp.concatenate([do.astype(F32), zero], axis=0).T.astype(BF)
            rb = jnp.concatenate([zero, qkv[0, rows, cols].astype(F32)], axis=0).T.astype(BF)
            fixed.append((inner, lse[g, pl.ds(i, 1)], ra, rb))

        def block(j, carry):
            at = pl.ds(pl.multiple_of(j * KB, KB), KB)
            out = []
            s = [jnp.dot(ka[g, at, :], qa[g, :, cols], preferred_element_type=F32) for g in range(NH)]
            dp = [jnp.dot(vk[g, at, :], da[i, g * 64:(g + 1) * 64], preferred_element_type=F32) for g in range(NH)]
            for g in range(NH):
                inner, lse_i, ra, rb = fixed[g]
                p = jnp.exp2(s[g] * SCORE_SCALE - lse_i)
                ds = (p * (dp[g] - inner)).astype(BF)
                dkv[g, at, :] += jnp.dot(p.astype(BF), ra, preferred_element_type=F32) + jnp.dot(
                    ds, rb, preferred_element_type=F32)
                out.append(carry[g] + jnp.dot(qkv[1, g * 64:(g + 1) * 64, at], ds, preferred_element_type=F32))
            return tuple(out)

        dq = lax.fori_loop(lo[i], hi[i], block, tuple(jnp.zeros((64, QB), F32) for _ in range(NH)))
        for g in range(NH):
            out[0, g * 64:(g + 1) * 64, cols] = (dq[g] * 0.125).astype(BF)
        return 0

    lax.fori_loop(0, n // QB, queries, 0)
    for g in range(NH):
        rows = slice(g * 64, (g + 1) * 64)
        dkv_t = dkv[g].T
        out[1, rows] = (dkv_t[64:] * 0.125).astype(BF)
        out[2, rows] = dkv_t[:64].astype(BF)


def attn_bwd(lo, hi, qkv, ids, da, o32, lse):
    n = qkv.shape[2]
    return pl.pallas_call(
        attn_bwd_kernel,
        in_specs=[smem_spec(), smem_spec()] + [vmem_spec()] * 5,
        out_specs=vmem_spec(),
        scratch_shapes=[
            pltpu.VMEM((NH, n, 80), BF), pltpu.VMEM((NH, 80, n), BF), pltpu.VMEM((NH, n, 64), BF),
            pltpu.VMEM((NH, n, 128), F32),
        ],
        out_shape=jax.ShapeDtypeStruct((3, 192, n), BF),
        compiler_params=pltpu.CompilerParams(vmem_limit_bytes=VMEM_LIMIT),
        name="attn_bwd",
    )(lo, hi, qkv, ids, da, o32, lse)


N_ARR = 7
WIDE = (0, 1, 2)
EARLY = (3, 4, 5, 6)
FIRST_X = (0, 1, 3)
FIRST_Y = (2, 4, 5, 6)


def window(i):
    return (i // 4) * (i % 4), 8 - (1 - i // 4) * (3 - i % 4)


def front_kernel(x, idb, wi, wo, wb, sm, wq,
                 xs, ids, gi, go, gb, gs, att, qkv, o32, lse, wt,
                 gq, ka, va, qa, sb,
                 loc, s_x, r_x, s_xf, s_xd, r_xd, s_z, r_z, s_up, s_dn, s_px, r_px, s_py, r_py, s_f, r_f,
                 s_c, r_c, s_e, r_e):
    d, t, z, c, dx, dy = place()
    h = z // 2
    zp = z + 1 - 2 * (z % 2)
    inner = (z + h) % 2 == 1
    dxy = (dx + 2) % 4
    z1, z2 = 2 - h, 3 * (1 - h)
    others = [zp, z1, z2]
    far = [z1, z2]
    me = lambda zz: (d, zz * 2 + c)
    core = (d, z * 2 + 1 - c)
    nx, ny = (dx, t), (dy, t)
    greet([(d, (t + k) % 8) for k in range(1, 8)] + [nx, ny])
    sends = []

    def go_(cp):
        cp.start()
        sends.append(cp)

    def got(ref, ss, rs, dev):
        remote(ref, ref, ss, rs, dev).wait_recv()

    per = wq.shape[2] // 6
    dst = [gi, go, gb, gs, gq.at[0], gq.at[1], gq.at[2]]

    def mine(a, zz):
        if a < 4:
            return (wi, wo, wb, sm)[a]
        return wq.at[:, :, pl.ds(pl.multiple_of((a - 4) * 2 * per + (zz % 2) * per, per), per)]

    half = x.shape[1] // 2

    def piece(k, hh, tt):
        if k == 2:
            return idb.at[hh], ids.at[tt]
        rows = pl.ds(k * half, half)
        return x.at[hh, rows], xs.at[tt, rows]

    for a in EARLY:
        for k in range(3):
            zz = others[k]
            go_(remote(mine(a, zz), dst[a].at[d, z, c], s_z.at[a - 3, k], r_z.at[a, z], me(zz)))

    def plane(arrs, zz, first):
        for a in arrs:
            src = mine(a, z) if first else dst[a].at[d, zz, c]
            go_(remote(src, dst[a].at[d, zz, c], s_px.at[a, zz], r_px.at[a, zz], nx))
            go_(remote(src, dst[a].at[d, zz, c], s_py.at[a, zz], r_py.at[a, zz], ny))

    plane(EARLY, z, True)
    for k in (2, 0, 1):
        src, to = piece(k, 1 - h, t)
        go_(remote(src, to, s_x.at[0, k], r_x.at[z, k], me(z1)))
        src, to = piece(k, h, t)
        go_(remote(src, to, s_x.at[1, k], r_x.at[z, k], me(zp)))

    def chain(zz, first, wait):
        for a in WIDE:
            src = mine(a, z) if first else dst[a].at[d, zz, c]
            up = remote(src, dst[a].at[d, zz, c], s_up.at[a, zz], r_z.at[a, zz], me((z + 1) % 4))
            dn = remote(src, dst[a].at[d, zz, c], s_dn.at[a, zz], r_z.at[a, zz], me((z + 3) % 4))

            @pl.when(jnp.logical_and(zz <= z, z < 3))
            def _(up=up):
                if wait:
                    up.wait_send()
                else:
                    up.start()

            @pl.when(jnp.logical_and(zz >= z, z > 0))
            def _(dn=dn):
                if wait:
                    dn.wait_send()
                else:
                    dn.start()

    chain(z, True, False)
    plane(WIDE, z, True)
    locals_ = [pltpu.make_async_copy(piece(k, h, t)[0], piece(k, h, t)[1], loc.at[N_ARR + k]) for k in range(3)]
    for a in (4, 5, 6, 3, 0, 1, 2):
        locals_.append(pltpu.make_async_copy(mine(a, z), dst[a].at[d, z, c], loc.at[a]))
    for cp in locals_:
        cp.start()

    def forward(arrs, zz):
        for a in arrs:
            if a in FIRST_Y:
                got(dst[a].at[dy, zz, c], s_py.at[a, zz], r_py.at[a, zz], ny)
                go_(remote(dst[a].at[dy, zz, c], dst[a].at[dy, zz, c], s_f.at[a, zz], r_f.at[a, zz], nx))
            else:
                got(dst[a].at[dx, zz, c], s_px.at[a, zz], r_px.at[a, zz], nx)
                go_(remote(dst[a].at[dx, zz, c], dst[a].at[dx, zz, c], s_f.at[a, zz], r_f.at[a, zz], ny))

    def across(arrs, zz):
        for a in arrs:
            if a in FIRST_Y:
                got(dst[a].at[dx, zz, c], s_px.at[a, zz], r_px.at[a, zz], nx)
                got(dst[a].at[dxy, zz, c], s_f.at[a, zz], r_f.at[a, zz], nx)
            else:
                got(dst[a].at[dy, zz, c], s_py.at[a, zz], r_py.at[a, zz], ny)
                got(dst[a].at[dxy, zz, c], s_f.at[a, zz], r_f.at[a, zz], ny)
            go_(remote(dst[a].at[:, zz, c], dst[a].at[:, zz, c], s_c.at[a, zz], r_c.at[a, zz], core))

    def crossed(arrs, zz):
        for a in arrs:
            ref = dst[a].at[:, zz, 1 - c]
            got(ref, s_c.at[a, zz], r_c.at[a, zz], core)

    def arrive(arrs, k):
        for a in arrs:
            got(dst[a].at[d, others[k], c], s_z.at[0, 0], r_z.at[a, others[k]], me(others[k]))

    for k in range(3):
        arrive(EARLY, k)
        plane(EARLY, others[k], False)
    for cp in locals_:
        cp.wait()
    for zz in [z] + others:
        forward(EARLY, zz)

    def relay(k, wait):
        for j in range(2):
            ref = piece(k, h, far[j] * 2 + c)[1]
            cp = remote(ref, ref, s_xf.at[j, k], r_x.at[far[j], k], me(zp))

            @pl.when(inner)
            def _(cp=cp):
                if wait:
                    cp.wait_send()
                else:
                    cp.wait_recv()
                    cp.start()

    def relayed(k):
        for j in range(2):
            ref = piece(k, h, far[j] * 2 + c)[1]

            @pl.when(jnp.logical_not(inner))
            def _(ref=ref, j=j):
                got(ref, s_x.at[0, k], r_x.at[far[j], k], me(zp))

    def to_core(zz):
        for k in range(3):
            ref = piece(k, h, zz * 2 + c)[1]
            go_(remote(ref, ref, s_xd.at[zz, k], r_xd.at[zz, k], core))

    def from_core(zz):
        for k in range(3):
            got(piece(k, h, zz * 2 + 1 - c)[1], s_xd.at[zz, k], r_xd.at[zz, k], core)

    to_core(z)
    for k in (2, 0):
        relay(k, False)
    for zz in [z] + others:
        across(EARLY, zz)
    relay(1, False)
    for k in range(3):
        got(piece(k, h, zp * 2 + c)[1], s_x.at[1, k], r_x.at[zp, k], me(zp))
    to_core(zp)
    for zz in [z] + others:
        crossed(EARLY, zz)
    width = wt.shape[3]
    for j in range(3):
        for q in range(2):
            w = gq[j, 2 * q:2 * q + 2].astype(F32).reshape(width // 2, per)
            w = w.T.astype(BF)
            for cc in range(2):
                wt[j, cc, :, q * (width // 2):(q + 1) * (width // 2)] = w[cc * (per // 2):(cc + 1) * (per // 2)]
    group = (z % 2) * 2 + c
    span = x.shape[1]

    def column(row):
        v = gs[group, :, :, row].reshape(8, 128).T
        return jnp.concatenate([v[:24, r:r + 1] for r in range(8)], axis=0)

    bias = [column(0), None, column(1)]
    for g in range(NH):
        va[g, 64:] = jnp.ones((16, va.shape[2]), BF)

    def project(zz):
        def one(j, _):
            tb = zz * 2 + j
            cols = pl.ds(pl.multiple_of(tb * span, span), span)
            xb = xs[tb]
            hit = marks_of(ids[tb, 0:1])
            ones = jnp.where(hit, 1.0, 0.0)
            away = jnp.where(hit, 0.0, EXCLUDE).astype(BF)
            for s in range(3):
                r = lax.dot_general(wt[s, c], xb, (((1,), (1,)), ((), ())), preferred_element_type=F32)
                if bias[s] is not None:
                    r = r + bias[s]
                low = r.astype(BF)
                qkv[s, :, cols] = low
                for g in range(NH):
                    part = low[g * 64:(g + 1) * 64]
                    if s == 0:
                        qa[g, :64, cols] = part
                        qa[g, 64:, cols] = away
                    elif s == 1:
                        ka[g, cols, :] = jnp.concatenate([part.astype(F32), ones], axis=0).T.astype(BF)
                    else:
                        va[g, :64, cols] = part
            return 0

        lax.fori_loop(0, 2, one, 0)

    forward(WIDE, z)
    for zz in (z, zp):
        from_core(zz)
        project(zz)
    for k in (2, 0, 1):
        relayed(k)
    for zz in far:
        to_core(zz)
    for zz in far:
        from_core(zz)
        project(zz)

    def attend(k):
        i = (t + k) % 8
        cols = pl.ds(pl.multiple_of(i * QB, QB), QB)
        lo, hi = window(i)

        def block(j, carry):
            at = pl.ds(pl.multiple_of(j * KB, KB), KB)
            out = []
            s = [jnp.dot(ka[g, at, :], qa[g, :, cols], preferred_element_type=F32) for g in range(NH)]
            for g in range(NH):
                m, acc = carry[g]
                m2 = jnp.maximum(m, jnp.max(s[g], axis=0, keepdims=True))
                p = jnp.exp2((s[g] - m2) * SCORE_SCALE).astype(BF)
                acc = acc * jnp.exp2((m - m2) * SCORE_SCALE) + jnp.dot(
                    va[g, :, at], p, preferred_element_type=F32)
                out.append((m2, acc))
            return tuple(out)

        first = tuple((jnp.full((1, QB), -3e38, F32), jnp.zeros((80, QB), F32)) for _ in range(NH))
        res = lax.fori_loop(lo, hi, block, first)
        for g in range(NH):
            m, acc = res[g]
            total = acc[64:65]
            o = acc[:64] / total
            o32[i, g * 64:(g + 1) * 64] = o
            if k:
                sb[i, g * 64:(g + 1) * 64] = o.astype(BF)
            else:
                att[t, g * 64:(g + 1) * 64] = o.astype(BF)
            lse[g, pl.ds(i, 1)] = m * SCORE_SCALE + jnp.log2(total)
        if k:
            go_(remote(sb.at[i], att.at[t], s_e.at[k - 1], r_e.at[k - 1], (d, i)))

    def onward(k):
        arrive(WIDE, k)
        chain(others[k], False, False)
        plane(WIDE, others[k], False)

    order = ORDER_K
    attend(order[0])
    onward(0)
    attend(order[1])
    across(WIDE, z)
    attend(order[2])
    onward(1)
    attend(order[3])
    forward(WIDE, zp)
    attend(order[4])
    onward(2)
    attend(order[5])
    forward(WIDE, z1)
    across(WIDE, zp)
    attend(order[6])
    attend(order[7])
    forward(WIDE, z2)
    across(WIDE, z1)
    across(WIDE, z2)
    for zz in [z] + others:
        crossed(WIDE, zz)
    for k in range(1, 8):
        src = (t + 8 - k) % 8
        got(att.at[src], s_e.at[k - 1], r_e.at[k - 1], (d, src))
    for cp in sends:
        cp.wait_send()
    chain(z, True, True)
    for zz in others:
        chain(zz, False, True)
    for k in range(3):
        relay(k, True)


ORDER_K = (4, 3, 5, 2, 6, 1, 7, 0)


def any_spec():
    return pl.BlockSpec(memory_space=pl.ANY)


def vmem_spec():
    return pl.BlockSpec(memory_space=pltpu.VMEM)


def dma(*shape):
    return pltpu.SemaphoreType.DMA(shape)


def front(x, idb, wi, wo, wb, sm, wq):
    span, width = x.shape[1:]
    n = 8 * span
    per = width // 4
    grid_of = lambda a: jax.ShapeDtypeStruct((4, 4, 2) + a.shape, a.dtype)
    return pl.pallas_call(
        front_kernel,
        out_shape=[
            jax.ShapeDtypeStruct((8, span, width), x.dtype),
            jax.ShapeDtypeStruct((8, 8, span), F32),
            grid_of(wi), grid_of(wo), grid_of(wb), grid_of(sm),
            jax.ShapeDtypeStruct((8, per, span), BF),
            jax.ShapeDtypeStruct((3, per, n), BF),
            jax.ShapeDtypeStruct((8, per, span), F32),
            jax.ShapeDtypeStruct((NH, 8, span), F32),
            jax.ShapeDtypeStruct((3, 2, per, width), BF),
        ],
        in_specs=[any_spec()] * 7,
        out_specs=[vmem_spec()] * 2 + [any_spec()] * 3 + [vmem_spec()] * 6,
        scratch_shapes=[
            pltpu.VMEM((3, 4, 4, 2) + wq.shape[:2] + (2 * per,), BF),
            pltpu.VMEM((NH, n, 80), BF), pltpu.VMEM((NH, 80, n), BF), pltpu.VMEM((NH, 80, n), BF),
            pltpu.VMEM((8, per, span), BF),
            dma(N_ARR + 3), dma(2, 3), dma(4, 3), dma(2, 3), dma(4, 3), dma(4, 3), dma(4, 3), dma(N_ARR, 4),
            dma(3, 4), dma(3, 4),
            dma(N_ARR, 4), dma(N_ARR, 4), dma(N_ARR, 4), dma(N_ARR, 4), dma(N_ARR, 4), dma(N_ARR, 4),
            dma(N_ARR, 4), dma(N_ARR, 4), dma(7), dma(7),
        ],
        compiler_params=pltpu.CompilerParams(
            collective_id=1, has_side_effects=True, vmem_limit_bytes=VMEM_LIMIT),
        name="front",
    )(x, idb, wi, wo, wb, sm, wq)


def scatter_kernel(dxp, di, do_, ds_, db, dq, ox, oi, oo, os_, ob, oq, *rest):
    k_arr = 4
    rd = rest[0:4]
    r1 = rest[4:8]
    r2 = rest[8:12]
    r3 = rest[12:16]
    r4 = rest[16:20]
    r5 = rest[20:24]
    (xd, x3, x4, x5, q0, q1, q2, qr,
     s_d, r_d, s_1, r_1, s_2, r_2, s_3, r_3, s_4, r_4, s_5, r_5,
     s_q1, r_q1, s_q2, r_q2, s_qe, r_qe) = rest[24:]
    d, t, z, c, dx, dy = place()
    x, y = d % 2, d // 2
    h = z // 2
    zp = z + 1 - 2 * (z % 2)
    inner = (z + h) % 2 == 1
    me = lambda zz: (d, zz * 2 + c)
    core = (d, z * 2 + 1 - c)
    nx, ny = (dx, t), (dy, t)
    line = [(t + k) % 8 for k in range(1, 8)]
    greet([(d, o) for o in line] + [nx, ny])
    part = [di, do_, ds_, db]
    outs = [oi, oo, os_, ob]
    by_x = [True, True, True, False]
    far = [2 * (1 - h), 2 * (1 - h) + 1]
    order = [far[0], far[1], zp, z]
    sends = []

    def go_(cp):
        cp.start()
        sends.append(cp)

    def got(ref, ss, rs, dev):
        remote(ref, ref, ss, rs, dev).wait_recv()

    for n_, zz in enumerate(order):
        go_(remote(dxp.at[zz * 2 + 1 - c], xd.at[zz], s_d.at[4, n_], r_d.at[4, n_], core))
    for n_, zz in enumerate(order):
        for a in range(k_arr):
            for yy in range(2):
                go_(remote(part[a].at[yy, :, zz, 1 - c], rd[a].at[yy, :, zz], s_d.at[5 + 2 * a + yy, n_],
                           r_d.at[5 + 2 * a + yy, n_], core))
    go_(remote(dq.at[:, 1 - x], q1, s_q1, r_q1, nx))

    def add_rows(dst, src):
        n0 = dst.shape[0]

        def step(i, _):
            dst[i] = dst[i] + src[i]
            return 0

        lax.fori_loop(0, n0, step, 0)

    def add_tok(dst, src):
        def step(i, _):
            at = pl.ds(pl.multiple_of(i * 32, 32), 32)
            dst[at, :] = dst[at, :] + src[at, :]
            return 0

        lax.fori_loop(0, dst.shape[0] // 32, step, 0)

    for n_, zz in enumerate(order):
        got(xd.at[zz], s_d.at[4, n_], r_d.at[4, n_], core)
        add_tok(xd.at[zz], dxp.at[zz * 2 + c])
        if n_ == 2:
            go_(remote(xd.at[zz], x5, s_5.at[4], r_5.at[4], me(zz)))

        if n_ < 2:
            @pl.when(jnp.logical_not(inner))
            def _(n_=n_, zz=zz):
                remote(xd.at[zz], x3.at[n_], s_3.at[4, n_], r_3.at[4, n_], me(zp)).start()

    for n_, zz in enumerate(order):
        for a in range(k_arr):
            for yy in range(2):
                got(rd[a].at[yy, :, zz], s_d.at[5 + 2 * a + yy, n_], r_d.at[5 + 2 * a + yy, n_], core)
                for xx in range(2):
                    add_rows(rd[a].at[yy, xx, zz], part[a].at[yy, xx, zz, c])
            if by_x[a]:
                go_(remote(rd[a].at[:, 1 - x, zz], r1[a].at[n_], s_1.at[a, n_], r_1.at[a, n_], nx))
            else:
                go_(remote(rd[a].at[1 - y, :, zz], r1[a].at[n_], s_1.at[a, n_], r_1.at[a, n_], ny))
        if n_ == 0:
            got(q1, s_q1, r_q1, nx)
            for yy in range(2):
                for zc in range(8):
                    q0[yy, zc // 2, zc % 2] = q1[yy, zc // 2, zc % 2] + dq[yy, x, zc // 2, zc % 2]
            go_(remote(q0.at[1 - y], q2, s_q2, r_q2, ny))
        if n_ == 1:
            for j in range(2):
                @pl.when(inner)
                def _(j=j):
                    got(x3.at[j], s_3.at[4, j], r_3.at[4, j], me(zp))
                    add_tok(xd.at[far[j]], x3.at[j])
                    remote(xd.at[far[j]], x4, s_4.at[4, j], r_4.at[4], me(far[j])).start()
        if n_ == 2:
            got(q2, s_q2, r_q2, ny)
            for zc in range(8):
                q0[y, zc // 2, zc % 2] = q0[y, zc // 2, zc % 2] + q2[zc // 2, zc % 2]
            for k in range(1, 8):
                to = line[k - 1]
                go_(remote(q0.at[y, to // 2, to % 2], qr.at[t], s_qe.at[k - 1], r_qe.at[k - 1], (d, to)))

    for n_, zz in enumerate(order):
        for a in range(k_arr):
            if by_x[a]:
                got(r1[a].at[n_], s_1.at[a, n_], r_1.at[a, n_], nx)
                for yy in range(2):
                    add_rows(rd[a].at[yy, x, zz], r1[a].at[n_, yy])
                go_(remote(rd[a].at[1 - y, x, zz], r2[a].at[n_], s_2.at[a, n_], r_2.at[a, n_], ny))
            else:
                got(r1[a].at[n_], s_1.at[a, n_], r_1.at[a, n_], ny)
                for xx in range(2):
                    add_rows(rd[a].at[y, xx, zz], r1[a].at[n_, xx])
                go_(remote(rd[a].at[y, 1 - x, zz], r2[a].at[n_], s_2.at[a, n_], r_2.at[a, n_], nx))

    for n_, zz in enumerate(order):
        for a in range(k_arr):
            got(r2[a].at[n_], s_2.at[a, n_], r_2.at[a, n_], ny if by_x[a] else nx)
            add_rows(rd[a].at[y, x, zz], r2[a].at[n_])
            mine_ = rd[a].at[y, x]
            if n_ < 2:
                @pl.when(jnp.logical_not(inner))
                def _(a=a, n_=n_, zz=zz, mine_=mine_):
                    remote(mine_.at[zz], r3[a].at[n_], s_3.at[a, n_], r_3.at[a, n_], me(zp)).start()
            elif n_ == 2:
                go_(remote(mine_.at[zz], r5[a], s_5.at[a], r_5.at[a], me(zz)))
    for n_ in range(2):
        for a in range(k_arr):
            @pl.when(inner)
            def _(a=a, n_=n_):
                mine_ = rd[a].at[y, x, far[n_]]
                got(r3[a].at[n_], s_3.at[a, n_], r_3.at[a, n_], me(zp))
                add_rows(mine_, r3[a].at[n_])
                remote(mine_, r4[a], s_4.at[a, n_], r_4.at[a], me(far[n_])).start()
    src_in = 2 - h
    got(x5, s_5.at[4], r_5.at[4], me(zp))
    got(x4, s_4.at[4, 0], r_4.at[4], me(src_in))

    def tok(i, _):
        at = pl.ds(pl.multiple_of(i * 32, 32), 32)
        ox[h, at, :] = xd[z, at, :] + x5[at, :]
        ox[1 - h, at, :] = x4[at, :]
        return 0

    lax.fori_loop(0, 8, tok, 0)
    for k in range(1, 8):
        src = (t + 8 - k) % 8
        got(qr.at[src], s_qe.at[k - 1], r_qe.at[k - 1], (d, src))
    qr[t] = q0[y, z, c]
    for g in range(4):
        oq[g] = qr[g].astype(F32) + qr[4 + g].astype(F32)
    for a in range(k_arr):
        got(r5[a], s_5.at[a], r_5.at[a], me(zp))
        got(r4[a], s_4.at[a, 0], r_4.at[a], me(src_in))
        acc = rd[a].at[y, x, z]
        for i in range(acc.shape[0]):
            outs[a][i] = acc[i].astype(F32) + r5[a][i].astype(F32) + r4[a][i].astype(F32)
    for cp in sends:
        cp.wait_send()
    for n_ in range(2):
        zz = far[n_]

        @pl.when(jnp.logical_not(inner))
        def _(n_=n_, zz=zz):
            remote(xd.at[zz], x3.at[n_], s_3.at[4, n_], r_3.at[4, n_], me(zp)).wait_send()
            for a in range(k_arr):
                remote(rd[a].at[y, x, zz], r3[a].at[n_], s_3.at[a, n_], r_3.at[a, n_], me(zp)).wait_send()

        @pl.when(inner)
        def _(n_=n_, zz=zz):
            remote(xd.at[zz], x4, s_4.at[4, n_], r_4.at[4], me(zz)).wait_send()
            for a in range(k_arr):
                remote(rd[a].at[y, x, zz], r4[a], s_4.at[a, n_], r_4.at[a], me(zz)).wait_send()


def scatter_all(dxp, di, do_, ds_, db, dq):
    arrs = [di, do_, ds_, db]
    tails = [a.shape[4:] for a in arrs]
    scratch = []
    for lead in ((2, 2, 4), (4, 2), (4,), (2,), (), ()):
        for a, tail in zip(arrs, tails):
            scratch.append(pltpu.VMEM(lead + tail, a.dtype))
    tok = dxp.shape[1:]
    qt = dq.shape[4:]
    scratch += [
        pltpu.VMEM((4,) + tok, BF), pltpu.VMEM((2,) + tok, BF), pltpu.VMEM(tok, BF), pltpu.VMEM(tok, BF),
        pltpu.VMEM((2, 4, 2) + qt, BF), pltpu.VMEM((2, 4, 2) + qt, BF), pltpu.VMEM((4, 2) + qt, BF),
        pltpu.VMEM((8,) + qt, BF),
        dma(13, 4), dma(13, 4), dma(4, 4), dma(4, 4), dma(4, 4), dma(4, 4), dma(5, 2), dma(5, 2),
        dma(5, 2), dma(5), dma(5), dma(5),
        pltpu.SemaphoreType.DMA, pltpu.SemaphoreType.DMA, pltpu.SemaphoreType.DMA, pltpu.SemaphoreType.DMA,
        dma(7), dma(7),
    ]
    return pl.pallas_call(
        scatter_kernel,
        out_shape=[jax.ShapeDtypeStruct((2,) + tok, BF)]
        + [jax.ShapeDtypeStruct(tail, F32) for tail in tails]
        + [jax.ShapeDtypeStruct((4,) + qt, F32)],
        in_specs=[vmem_spec()] * 6,
        out_specs=[vmem_spec()] * 6,
        scratch_shapes=scratch,
        compiler_params=pltpu.CompilerParams(
            collective_id=4, has_side_effects=True, vmem_limit_bytes=VMEM_LIMIT),
        name="scatter_all",
    )(dxp, di, do_, ds_, db, dq)


def erf_parts(u):
    phi_c = 0.5 * (1.0 + lax.erf(u * 0.7071067811865476))
    return phi_c, phi_c + u * jnp.exp(-0.5 * u * u) * 0.3989422804014327


def norm_forward(r):
    center = r - jnp.mean(r, axis=-1, keepdims=True)
    inv = lax.rsqrt(jnp.mean(center * center, axis=-1, keepdims=True) + layer_eps)
    return center * inv, inv


def norm_backward(n, inv, gain, dy):
    gd = gain * dy
    return (gd - jnp.mean(gd, axis=-1, keepdims=True) - n * jnp.mean(gd * n, axis=-1, keepdims=True)) * inv


def on_device_fast(
    inputs, segments, w_qkv, b_query, b_value, w_out, b_attn, gain_one, shift_one,
    w_in, b_in, w_back, b_back, gain_two, shift_two, cotangent,
):
    nseq, span, width = inputs.shape
    tokens = nseq * span
    ff = w_in.shape[1]
    depth = w_in.shape[0]
    d, t, z, c, _, _ = place()
    h = z // 2
    group = (z % 2) * 2 + c
    per = width // 4
    vecs = (b_query, b_value, b_attn, gain_one, shift_one, b_back, gain_two, shift_two)
    ffd = b_in.shape[0]
    nv = len(vecs)
    small = jnp.pad(jnp.stack(vecs).astype(F32), ((0, 8), (0, 128 - depth)))
    small = lax.dynamic_update_slice(small, b_in.astype(F32)[None], (nv, 0))
    idb = jnp.broadcast_to(segments.astype(F32)[:, None], (nseq, 8, span))
    xs, ids, gi, go, gb, gs, att, qkv, o32, lse, wt = front(
        inputs, idb, w_in.reshape(depth // 8, 8, ff), w_out.reshape(depth // 8, 8, width),
        w_back.reshape(ffd // 8, 8, width), small, w_qkv.reshape(depth // 8, 8, 3 * width))
    wide_in = gi.reshape(width, ff)
    wide_out = go.reshape(width, width)
    wide_back = gb.reshape(ff, width)
    flat = gs.reshape(32, 16, 128)
    fv = flat[:, :nv, :depth].transpose(1, 0, 2).reshape(nv, width)
    full_b_in = flat[:, nv, :ffd].reshape(ff)
    n = 8 * span
    ids_row = ids[:, 0].reshape(1, n)
    blocks = ids_row.reshape(n // QB, QB)
    lo = (jnp.sum(ids_row < blocks[:, :1], axis=1) // KB).astype(jnp.int32)
    hi = ((jnp.sum(ids_row <= blocks[:, -1:], axis=1) + KB - 1) // KB).astype(jnp.int32)
    w_own = lax.dynamic_index_in_dim(wt, c, 1, keepdims=False).reshape(3 * per, width)
    xseq = xs.reshape(n, width)
    att = att.reshape(nseq, width, span)

    x32 = inputs.reshape(tokens, width).astype(F32)
    attn_out = jnp.einsum("sit,id->std", att, wide_out, preferred_element_type=F32).reshape(tokens, width)
    resid_one = x32 + attn_out + fv[2]
    n1, inv1 = norm_forward(resid_one)
    normed = n1 * fv[3] + fv[4]
    normed_low = normed.astype(BF)
    pre_act = jnp.dot(normed_low, wide_in, preferred_element_type=F32) + full_b_in
    phi_c, slope = erf_parts(pre_act)
    activ = (pre_act * phi_c).astype(BF)
    branch = jnp.dot(activ, wide_back, preferred_element_type=F32) + fv[5]
    n2, inv2 = norm_forward(normed + branch)
    output = (n2 * fv[6] + fv[7]).astype(BF).reshape(nseq, span, width)
    dy = cotangent.reshape(tokens, width).astype(F32)
    d_two = norm_backward(n2, inv2, fv[6], dy)
    d_branch = d_two.astype(BF)
    grad_w_back = jnp.einsum("tf,td->fd", activ, d_branch, preferred_element_type=F32).astype(BF)
    d_activ = jnp.einsum("td,fd->tf", d_branch, wide_back, preferred_element_type=F32)
    d_pre = (d_activ * slope).astype(BF)
    grad_w_in = jnp.einsum("td,tf->df", normed_low, d_pre, preferred_element_type=F32).astype(BF)
    d_normed = d_two + jnp.einsum("tf,df->td", d_pre, wide_in, preferred_element_type=F32)
    d_one = norm_backward(n1, inv1, fv[3], d_normed)
    d_attn = d_one.astype(BF)
    d_attn3 = d_attn.reshape(nseq, span, width)
    grad_w_out = jnp.einsum("sit,std->id", att, d_attn3, preferred_element_type=F32).astype(BF)
    d_att = jnp.einsum("std,id->sit", d_attn3, wide_out, preferred_element_type=F32).astype(BF)
    d_att = exchange(d_att.reshape(8, per, span), 3)
    d_proj = attn_bwd(lo, hi, qkv, ids_row, d_att, o32, lse)
    proj = d_proj.reshape(3 * per, n)
    dx_part = jnp.einsum("ft,fk->tk", proj, w_own, preferred_element_type=F32).astype(BF)
    grad_w_qkv = jnp.einsum("tk,ft->kf", xseq, proj, preferred_element_type=F32).astype(BF)
    g_bias = jnp.sum(d_proj.astype(F32), axis=2)
    spread = jnp.zeros((2, width), F32)
    spread = lax.dynamic_update_slice(spread, g_bias[::2], (0, group * per))
    sums = [
        spread[0], spread[1],
        jnp.sum(d_attn.astype(F32), axis=0),
        jnp.sum(d_normed * n1, axis=0),
        jnp.sum(d_normed, axis=0),
        jnp.sum(d_branch.astype(F32), axis=0),
        jnp.sum(dy * n2, axis=0),
        jnp.sum(dy, axis=0),
    ]
    g_in = jnp.sum(d_pre.astype(F32), axis=0)
    g_small = jnp.concatenate(
        [jnp.stack(sums).reshape(nv, 32, depth).transpose(1, 0, 2).reshape(32, nv * depth), g_in.reshape(32, ffd)],
        axis=1)
    g_small = jnp.pad(g_small, ((0, 0), (0, 1024 - g_small.shape[1])))
    owner = (2, 2, 4, 2)
    ox, oi, oo, os_, ob, oq = scatter_all(
        dx_part.reshape(8, span, width),
        grad_w_in.reshape(owner + (depth // 8, 8, ff)),
        grad_w_out.reshape(owner + (depth // 8, 8, width)),
        g_small.reshape(owner + (8, 128)),
        grad_w_back.reshape(owner + (ffd // 8, 8, width)),
        grad_w_qkv.reshape(owner + (depth // 8, 8, 3 * per)),
    )
    input_grad = d_one.reshape(nseq, span, width) + ox.astype(F32)
    g_qkv = oq.reshape(4, depth, 3, per).transpose(1, 2, 0, 3).reshape(depth, 3 * width)
    sv = os_.reshape(1024)
    vec = lambda k: sv[k * depth:(k + 1) * depth]
    return (
        output, input_grad, g_qkv, vec(0), vec(1), oo.reshape(depth, width), vec(2), vec(3), vec(4),
        oi.reshape(depth, ff), sv[nv * depth:nv * depth + ffd], ob.reshape(ffd, width), vec(5), vec(6), vec(7),
    )


negative_fill = -1e30


def layer_norm(resid, gain, shift):
    center = resid - jnp.mean(resid, axis=-1, keepdims=True)
    spread = jnp.mean(center * center, axis=-1, keepdims=True)
    return center * lax.rsqrt(spread + layer_eps) * gain + shift


def gelu_exact(values):
    return jax.nn.gelu(values, approximate=False)


def attend_forward(entries):
    query_rows, key_rows, value_rows, query_ids, key_ids = entries
    scores = jnp.einsum(
        "qhd,khd->hqk", query_rows, key_rows, preferred_element_type=jnp.float32
    ) * HEAD_DIM ** (-0.5)
    allowed = (query_ids[:, None] == key_ids[None, :])[None]
    scores = jnp.where(allowed, scores, negative_fill)
    peak = jnp.max(scores, axis=-1, keepdims=True)
    raised = jnp.exp(scores - peak)
    total = jnp.sum(raised, axis=-1, keepdims=True)
    probs_low = (raised / total).astype(jnp.bfloat16)
    context = jnp.einsum("hqk,khd->qhd", probs_low, value_rows, preferred_element_type=jnp.float32)
    return (context, (peak + jnp.log(total))[..., 0])


def score_terms(query_rows, key_rows, value_rows, grad_context, log_total, query_ids, key_ids):
    scale = HEAD_DIM ** (-0.5)
    scores = (
        jnp.einsum("qhd,khd->hqk", query_rows, key_rows, preferred_element_type=jnp.float32) * scale
    )
    allowed = (query_ids[:, None] == key_ids[None, :])[None]
    probs = jnp.where(allowed, jnp.exp(scores - log_total[..., None]), 0.0)
    d_probs = jnp.einsum(
        "qhd,khd->hqk", grad_context, value_rows, preferred_element_type=jnp.float32
    )
    return (probs, d_probs)


def attend_backward(entries):
    query_rows, key_rows, value_rows, grad_context, log_total, query_ids, key_ids = entries
    scale = HEAD_DIM ** (-0.5)
    probs, d_probs = score_terms(
        query_rows, key_rows, value_rows, grad_context, log_total, query_ids, key_ids
    )
    inner = jnp.sum(probs * d_probs, axis=-1, keepdims=True)
    d_scores = (probs * (d_probs - inner)).astype(jnp.bfloat16)
    d_queries = (
        jnp.einsum("hqk,khd->qhd", d_scores, key_rows, preferred_element_type=jnp.float32) * scale
    )
    d_keys = (
        jnp.einsum("hqk,qhd->khd", d_scores, query_rows, preferred_element_type=jnp.float32) * scale
    )
    d_values = jnp.einsum(
        "hqk,qhd->khd", probs.astype(jnp.bfloat16), grad_context, preferred_element_type=jnp.float32
    )
    length = key_rows.shape[0]
    return (
        d_queries,
        d_keys.reshape(length, HEADS * HEAD_DIM),
        d_values.reshape(length, HEADS * HEAD_DIM),
    )


def on_device_general(
    inputs,
    segments,
    w_qkv,
    b_query,
    b_value,
    w_out,
    b_attn,
    gain_one,
    shift_one,
    w_in,
    b_in,
    w_back,
    b_back,
    gain_two,
    shift_two,
    cotangent,
):
    seq_count, group_len, model_width = inputs.shape
    tok_count = seq_count * group_len
    gathered = (
        lax.all_gather(w_qkv, ("dp", "ctx"), axis=0, tiled=True),
        lax.all_gather(b_query, ("dp", "ctx"), axis=0, tiled=True),
        lax.all_gather(b_value, ("dp", "ctx"), axis=0, tiled=True),
        lax.all_gather(w_out, ("dp", "ctx"), axis=0, tiled=True),
        lax.all_gather(b_attn, ("dp", "ctx"), axis=0, tiled=True),
        lax.all_gather(gain_one, ("dp", "ctx"), axis=0, tiled=True),
        lax.all_gather(shift_one, ("dp", "ctx"), axis=0, tiled=True),
        lax.all_gather(w_in, ("dp", "ctx"), axis=0, tiled=True),
        lax.all_gather(b_in, ("dp", "ctx"), axis=0, tiled=True),
        lax.all_gather(w_back, ("dp", "ctx"), axis=0, tiled=True),
        lax.all_gather(b_back, ("dp", "ctx"), axis=0, tiled=True),
        lax.all_gather(gain_two, ("dp", "ctx"), axis=0, tiled=True),
        lax.all_gather(shift_two, ("dp", "ctx"), axis=0, tiled=True),
    )
    (
        wide_qkv,
        full_b_query,
        full_b_value,
        wide_out,
        full_b_attn,
        full_gain_one,
        full_shift_one,
        wide_in,
        full_b_in,
        wide_back,
        full_b_back,
        full_gain_two,
        full_shift_two,
    ) = gathered
    tokens = inputs.reshape(tok_count, model_width)
    projected = jnp.dot(tokens, wide_qkv, preferred_element_type=jnp.float32)
    query_low = (projected[:, :model_width] + full_b_query.astype(jnp.float32)).astype(jnp.bfloat16)
    key_low = projected[:, model_width : 2 * model_width].astype(jnp.bfloat16)
    value_low = (projected[:, 2 * model_width :] + full_b_value.astype(jnp.float32)).astype(
        jnp.bfloat16
    )
    key_ids = lax.all_gather(segments, "ctx", axis=1, tiled=True)
    key_local = key_low.reshape(seq_count, group_len, model_width)
    value_local = value_low.reshape(seq_count, group_len, model_width)
    key_whole, value_whole = (
        lax.all_gather(key_local, "ctx", axis=1, tiled=True),
        lax.all_gather(value_local, "ctx", axis=1, tiled=True),
    )
    seq_len = key_whole.shape[1]
    query_heads = query_low.reshape(seq_count, group_len, HEADS, HEAD_DIM)
    context, log_total = lax.map(
        attend_forward,
        (
            query_heads,
            key_whole.reshape(seq_count, seq_len, HEADS, HEAD_DIM),
            value_whole.reshape(seq_count, seq_len, HEADS, HEAD_DIM),
            segments,
            key_ids,
        ),
    )
    attended = context.reshape(tok_count, model_width).astype(jnp.bfloat16)
    attn_out = jnp.dot(attended, wide_out, preferred_element_type=jnp.float32) + full_b_attn.astype(
        jnp.float32
    )
    resid_one = tokens.astype(jnp.float32) + attn_out
    normed, norm_one_back = jax.vjp(
        layer_norm, resid_one, full_gain_one.astype(jnp.float32), full_shift_one.astype(jnp.float32)
    )
    normed_low = normed.astype(jnp.bfloat16)
    pre_act = jnp.dot(normed_low, wide_in, preferred_element_type=jnp.float32) + full_b_in.astype(
        jnp.float32
    )
    activ_f, gelu_back = jax.vjp(gelu_exact, pre_act)
    activ = activ_f.astype(jnp.bfloat16)
    branch = jnp.dot(activ, wide_back, preferred_element_type=jnp.float32) + full_b_back.astype(
        jnp.float32
    )
    resid_two = normed + branch
    final_norm, norm_two_back = jax.vjp(
        layer_norm, resid_two, full_gain_two.astype(jnp.float32), full_shift_two.astype(jnp.float32)
    )
    output = final_norm.astype(jnp.bfloat16).reshape(seq_count, group_len, model_width)
    back_qkv, back_out, back_in, back_back = (
        lax.all_gather(w_qkv, ("dp", "ctx"), axis=0, tiled=True),
        lax.all_gather(w_out, ("dp", "ctx"), axis=0, tiled=True),
        lax.all_gather(w_in, ("dp", "ctx"), axis=0, tiled=True),
        lax.all_gather(w_back, ("dp", "ctx"), axis=0, tiled=True),
    )
    d_final = cotangent.reshape(tok_count, model_width).astype(jnp.float32)
    d_two, grad_gain_two, grad_shift_two = norm_two_back(d_final)
    d_branch = d_two.astype(jnp.bfloat16)
    grad_b_back = jnp.sum(d_branch.astype(jnp.float32), axis=0)
    grad_w_back = jnp.einsum("tf,td->fd", activ, d_branch, preferred_element_type=jnp.float32)
    d_activ = jnp.einsum("td,fd->tf", d_branch, back_back, preferred_element_type=jnp.float32)
    d_pre = gelu_back(d_activ)[0].astype(jnp.bfloat16)
    grad_b_in = jnp.sum(d_pre.astype(jnp.float32), axis=0)
    grad_w_in = jnp.einsum("td,tf->df", normed_low, d_pre, preferred_element_type=jnp.float32)
    d_normed = d_two + jnp.einsum("tf,df->td", d_pre, back_in, preferred_element_type=jnp.float32)
    d_one, grad_gain_one, grad_shift_one = norm_one_back(d_normed)
    d_attn = d_one.astype(jnp.bfloat16)
    grad_b_attn = jnp.sum(d_attn.astype(jnp.float32), axis=0)
    grad_w_out = jnp.einsum("ti,td->id", attended, d_attn, preferred_element_type=jnp.float32)
    d_attended = jnp.einsum(
        "td,id->ti", d_attn, back_out, preferred_element_type=jnp.float32
    ).astype(jnp.bfloat16)
    key_back, value_back = (
        lax.all_gather(key_local, "ctx", axis=1, tiled=True),
        lax.all_gather(value_local, "ctx", axis=1, tiled=True),
    )
    grad_heads = d_attended.reshape(seq_count, group_len, HEADS, HEAD_DIM)
    d_query_part, d_key_part, d_value_part = lax.map(
        attend_backward,
        (
            query_heads,
            key_back.reshape(seq_count, seq_len, HEADS, HEAD_DIM),
            value_back.reshape(seq_count, seq_len, HEADS, HEAD_DIM),
            grad_heads,
            log_total,
            segments,
            key_ids,
        ),
    )
    d_key_sum, d_value_sum = (
        lax.psum_scatter(
            d_key_part.astype(jnp.bfloat16), "ctx", scatter_dimension=1, tiled=True
        ).astype(jnp.float32),
        lax.psum_scatter(
            d_value_part.astype(jnp.bfloat16), "ctx", scatter_dimension=1, tiled=True
        ).astype(jnp.float32),
    )
    d_queries = d_query_part.reshape(tok_count, model_width).astype(jnp.bfloat16)
    d_keys = d_key_sum.reshape(tok_count, model_width).astype(jnp.bfloat16)
    d_values = d_value_sum.reshape(tok_count, model_width).astype(jnp.bfloat16)
    d_proj = jnp.concatenate([d_queries, d_keys, d_values], axis=1)
    grad_w_qkv = jnp.einsum("td,te->de", tokens, d_proj, preferred_element_type=jnp.float32)
    grad_b_query = jnp.sum(d_queries.astype(jnp.float32), axis=0)
    grad_b_value = jnp.sum(d_values.astype(jnp.float32), axis=0)
    input_grad = d_one + jnp.einsum(
        "te,de->td", d_proj, back_qkv, preferred_element_type=jnp.float32
    )
    summed = (
        lax.psum_scatter(grad_w_qkv, ("dp", "ctx"), scatter_dimension=0, tiled=True),
        lax.psum_scatter(grad_b_query, ("dp", "ctx"), scatter_dimension=0, tiled=True),
        lax.psum_scatter(grad_b_value, ("dp", "ctx"), scatter_dimension=0, tiled=True),
        lax.psum_scatter(grad_w_out, ("dp", "ctx"), scatter_dimension=0, tiled=True),
        lax.psum_scatter(grad_b_attn, ("dp", "ctx"), scatter_dimension=0, tiled=True),
        lax.psum_scatter(grad_gain_one, ("dp", "ctx"), scatter_dimension=0, tiled=True),
        lax.psum_scatter(grad_shift_one, ("dp", "ctx"), scatter_dimension=0, tiled=True),
        lax.psum_scatter(grad_w_in, ("dp", "ctx"), scatter_dimension=0, tiled=True),
        lax.psum_scatter(grad_b_in, ("dp", "ctx"), scatter_dimension=0, tiled=True),
        lax.psum_scatter(grad_w_back, ("dp", "ctx"), scatter_dimension=0, tiled=True),
        lax.psum_scatter(grad_b_back, ("dp", "ctx"), scatter_dimension=0, tiled=True),
        lax.psum_scatter(grad_gain_two, ("dp", "ctx"), scatter_dimension=0, tiled=True),
        lax.psum_scatter(grad_shift_two, ("dp", "ctx"), scatter_dimension=0, tiled=True),
    )
    return (
        output,
        input_grad.reshape(seq_count, group_len, model_width),
        summed[0],
        summed[1],
        summed[2],
        summed[3],
        summed[4],
        summed[5],
        summed[6],
        summed[7],
        summed[8],
        summed[9],
        summed[10],
        summed[11],
        summed[12],
    )


def solution(mesh):
    placed = (
        P("dp", "ctx", None),
        P("dp", "ctx"),
        P(("dp", "ctx"), None),
        P(("dp", "ctx")),
        P(("dp", "ctx")),
        P(("dp", "ctx"), None),
        P(("dp", "ctx")),
        P(("dp", "ctx")),
        P(("dp", "ctx")),
        P(("dp", "ctx"), None),
        P(("dp", "ctx")),
        P(("dp", "ctx"), None),
        P(("dp", "ctx")),
        P(("dp", "ctx")),
        P(("dp", "ctx")),
        P("dp", "ctx", None),
    )
    fits = mesh.shape["dp"] == 4 and mesh.shape["ctx"] == 8
    return jax.shard_map(
        on_device_fast if fits else on_device_general,
        mesh=mesh,
        in_specs=placed,
        out_specs=(
            P("dp", "ctx", None),
            P("dp", "ctx", None),
            P(("dp", "ctx"), None),
            P(("dp", "ctx")),
            P(("dp", "ctx")),
            P(("dp", "ctx"), None),
            P(("dp", "ctx")),
            P(("dp", "ctx")),
            P(("dp", "ctx")),
            P(("dp", "ctx"), None),
            P(("dp", "ctx")),
            P(("dp", "ctx"), None),
            P(("dp", "ctx")),
            P(("dp", "ctx")),
            P(("dp", "ctx")),
        ),
        check_vma=False,
    )
```

```python
import functools
import jax
import jax.numpy as jnp
from jax import lax
from jax.experimental import pallas as pl
from jax.experimental.pallas import tpu as pltpu
from jax.sharding import PartitionSpec as P

HEADS = 12
HEAD_DIM = 64
layer_eps = 1e-12
MESH_ID = pl.DeviceIdType.MESH
BF = jnp.bfloat16
F32 = jnp.float32
VMEM_LIMIT = 64 * 1024 * 1024 - 65536
SCORE_SCALE = 0.125 * 1.4426950408889634
EXCLUDE = -1e30


def place():
    d = lax.axis_index("dp")
    t = lax.axis_index("ctx")
    z = t // 2
    c = t % 2
    dx = d + 1 - 2 * (d % 2)
    dy = (d + 2) % 4
    return d, t, z, c, dx, dy


def remote(src, dst, ss, rs, dev):
    return pltpu.make_async_remote_copy(
        src_ref=src, dst_ref=dst, send_sem=ss, recv_sem=rs, device_id=dev, device_id_type=MESH_ID
    )


def greet(devices):
    bar = pltpu.get_barrier_semaphore()
    for dev in devices:
        pl.semaphore_signal(bar, inc=1, device_id=dev, device_id_type=MESH_ID)
    pl.semaphore_wait(bar, len(devices))


QB = 256
KB = 256
NH = 3


def marks_of(ids_row):
    kinds = lax.broadcasted_iota(jnp.int32, (16, ids_row.shape[1]), 0).astype(F32)
    return kinds == ids_row


N_ARR = 7
WIDE = (0, 1, 2)
EARLY = (3, 4, 5, 6)
FIRST_X = (0, 1, 3)
FIRST_Y = (2, 4, 5, 6)


def window(i):
    return (i // 4) * (i % 4), 8 - (1 - i // 4) * (3 - i % 4)


def front_kernel(x, idb, wi, wo, wb, sm, wq,
                 xs, ids, gi, go, gb, gs, att, qkv, o32, lse, wt,
                 gq, ka, va, qa, sb,
                 loc, s_x, r_x, s_xf, s_xd, r_xd, s_z, r_z, s_up, s_dn, s_px, r_px, s_py, r_py, s_f, r_f,
                 s_c, r_c, s_e, r_e):
    d, t, z, c, dx, dy = place()
    h = z // 2
    zp = z + 1 - 2 * (z % 2)
    inner = (z + h) % 2 == 1
    dxy = (dx + 2) % 4
    z1, z2 = 2 - h, 3 * (1 - h)
    others = [zp, z1, z2]
    far = [z1, z2]
    me = lambda zz: (d, zz * 2 + c)
    core = (d, z * 2 + 1 - c)
    nx, ny = (dx, t), (dy, t)
    greet([(d, (t + k) % 8) for k in range(1, 8)] + [nx, ny])
    sends = []

    def go_(cp):
        cp.start()
        sends.append(cp)

    def got(ref, ss, rs, dev):
        remote(ref, ref, ss, rs, dev).wait_recv()

    per = wq.shape[2] // 6
    dst = [gi, go, gb, gs, gq.at[0], gq.at[1], gq.at[2]]

    def mine(a, zz):
        if a < 4:
            return (wi, wo, wb, sm)[a]
        return wq.at[:, :, pl.ds(pl.multiple_of((a - 4) * 2 * per + (zz % 2) * per, per), per)]

    half = x.shape[1] // 2

    def piece(k, hh, tt):
        if k == 2:
            return idb.at[hh], ids.at[tt]
        rows = pl.ds(k * half, half)
        return x.at[hh, rows], xs.at[tt, rows]

    for a in EARLY:
        for k in range(3):
            zz = others[k]
            go_(remote(mine(a, zz), dst[a].at[d, z, c], s_z.at[a - 3, k], r_z.at[a, z], me(zz)))

    def plane(arrs, zz, first):
        for a in arrs:
            src = mine(a, z) if first else dst[a].at[d, zz, c]
            go_(remote(src, dst[a].at[d, zz, c], s_px.at[a, zz], r_px.at[a, zz], nx))
            go_(remote(src, dst[a].at[d, zz, c], s_py.at[a, zz], r_py.at[a, zz], ny))

    plane(EARLY, z, True)
    for k in (2, 0, 1):
        src, to = piece(k, 1 - h, t)
        go_(remote(src, to, s_x.at[0, k], r_x.at[z, k], me(z1)))
        src, to = piece(k, h, t)
        go_(remote(src, to, s_x.at[1, k], r_x.at[z, k], me(zp)))

    def chain(zz, first, wait):
        for a in WIDE:
            src = mine(a, z) if first else dst[a].at[d, zz, c]
            up = remote(src, dst[a].at[d, zz, c], s_up.at[a, zz], r_z.at[a, zz], me((z + 1) % 4))
            dn = remote(src, dst[a].at[d, zz, c], s_dn.at[a, zz], r_z.at[a, zz], me((z + 3) % 4))

            @pl.when(jnp.logical_and(zz <= z, z < 3))
            def _(up=up):
                if wait:
                    up.wait_send()
                else:
                    up.start()

            @pl.when(jnp.logical_and(zz >= z, z > 0))
            def _(dn=dn):
                if wait:
                    dn.wait_send()
                else:
                    dn.start()

    chain(z, True, False)
    plane(WIDE, z, True)
    locals_ = [pltpu.make_async_copy(piece(k, h, t)[0], piece(k, h, t)[1], loc.at[N_ARR + k]) for k in range(3)]
    for a in (4, 5, 6, 3, 0, 1, 2):
        locals_.append(pltpu.make_async_copy(mine(a, z), dst[a].at[d, z, c], loc.at[a]))
    for cp in locals_:
        cp.start()

    def forward(arrs, zz):
        for a in arrs:
            if a in FIRST_Y:
                got(dst[a].at[dy, zz, c], s_py.at[a, zz], r_py.at[a, zz], ny)
                go_(remote(dst[a].at[dy, zz, c], dst[a].at[dy, zz, c], s_f.at[a, zz], r_f.at[a, zz], nx))
            else:
                got(dst[a].at[dx, zz, c], s_px.at[a, zz], r_px.at[a, zz], nx)
                go_(remote(dst[a].at[dx, zz, c], dst[a].at[dx, zz, c], s_f.at[a, zz], r_f.at[a, zz], ny))

    def across(arrs, zz):
        for a in arrs:
            if a in FIRST_Y:
                got(dst[a].at[dx, zz, c], s_px.at[a, zz], r_px.at[a, zz], nx)
                got(dst[a].at[dxy, zz, c], s_f.at[a, zz], r_f.at[a, zz], nx)
            else:
                got(dst[a].at[dy, zz, c], s_py.at[a, zz], r_py.at[a, zz], ny)
                got(dst[a].at[dxy, zz, c], s_f.at[a, zz], r_f.at[a, zz], ny)
            go_(remote(dst[a].at[:, zz, c], dst[a].at[:, zz, c], s_c.at[a, zz], r_c.at[a, zz], core))

    def crossed(arrs, zz):
        for a in arrs:
            ref = dst[a].at[:, zz, 1 - c]
            got(ref, s_c.at[a, zz], r_c.at[a, zz], core)

    def arrive(arrs, k):
        for a in arrs:
            got(dst[a].at[d, others[k], c], s_z.at[0, 0], r_z.at[a, others[k]], me(others[k]))

    for k in range(3):
        arrive(EARLY, k)
        plane(EARLY, others[k], False)
    for cp in locals_:
        cp.wait()
    for zz in [z] + others:
        forward(EARLY, zz)

    def relay(k, wait):
        for j in range(2):
            ref = piece(k, h, far[j] * 2 + c)[1]
            cp = remote(ref, ref, s_xf.at[j, k], r_x.at[far[j], k], me(zp))

            @pl.when(inner)
            def _(cp=cp):
                if wait:
                    cp.wait_send()
                else:
                    cp.wait_recv()
                    cp.start()

    def relayed(k):
        for j in range(2):
            ref = piece(k, h, far[j] * 2 + c)[1]

            @pl.when(jnp.logical_not(inner))
            def _(ref=ref, j=j):
                got(ref, s_x.at[0, k], r_x.at[far[j], k], me(zp))

    def to_core(zz):
        for k in range(3):
            ref = piece(k, h, zz * 2 + c)[1]
            go_(remote(ref, ref, s_xd.at[zz, k], r_xd.at[zz, k], core))

    def from_core(zz):
        for k in range(3):
            got(piece(k, h, zz * 2 + 1 - c)[1], s_xd.at[zz, k], r_xd.at[zz, k], core)

    to_core(z)
    for k in (2, 0):
        relay(k, False)
    for zz in [z] + others:
        across(EARLY, zz)
    relay(1, False)
    for k in range(3):
        got(piece(k, h, zp * 2 + c)[1], s_x.at[1, k], r_x.at[zp, k], me(zp))
    to_core(zp)
    for zz in [z] + others:
        crossed(EARLY, zz)
    width = wt.shape[3]
    for j in range(3):
        for q in range(2):
            w = gq[j, 2 * q:2 * q + 2].astype(F32).reshape(width // 2, per)
            w = w.T.astype(BF)
            for cc in range(2):
                wt[j, cc, :, q * (width // 2):(q + 1) * (width // 2)] = w[cc * (per // 2):(cc + 1) * (per // 2)]
    group = (z % 2) * 2 + c
    span = x.shape[1]

    def column(row):
        v = gs[group, :, :, row].reshape(8, 128).T
        return jnp.concatenate([v[:24, r:r + 1] for r in range(8)], axis=0)

    bias = [column(0), None, column(1)]
    for g in range(NH):
        va[g, 64:] = jnp.ones((16, va.shape[2]), BF)

    def project(zz):
        def one(j, _):
            tb = zz * 2 + j
            cols = pl.ds(pl.multiple_of(tb * span, span), span)
            xb = xs[tb]
            hit = marks_of(ids[tb, 0:1])
            ones = jnp.where(hit, 1.0, 0.0)
            away = jnp.where(hit, 0.0, EXCLUDE).astype(BF)
            for s in range(3):
                r = lax.dot_general(wt[s, c], xb, (((1,), (1,)), ((), ())), preferred_element_type=F32)
                if bias[s] is not None:
                    r = r + bias[s]
                low = r.astype(BF)
                qkv[s, :, cols] = low
                for g in range(NH):
                    part = low[g * 64:(g + 1) * 64]
                    if s == 0:
                        qa[g, :64, cols] = part
                        qa[g, 64:, cols] = away
                    elif s == 1:
                        ka[g, cols, :] = jnp.concatenate([part.astype(F32), ones], axis=0).T.astype(BF)
                    else:
                        va[g, :64, cols] = part
            return 0

        lax.fori_loop(0, 2, one, 0)

    forward(WIDE, z)
    for zz in (z, zp):
        from_core(zz)
        project(zz)
    for k in (2, 0, 1):
        relayed(k)
    for zz in far:
        to_core(zz)
    for zz in far:
        from_core(zz)
        project(zz)

    def attend(k):
        i = (t + k) % 8
        cols = pl.ds(pl.multiple_of(i * QB, QB), QB)
        lo, hi = window(i)

        def block(j, carry):
            at = pl.ds(pl.multiple_of(j * KB, KB), KB)
            out = []
            s = [jnp.dot(ka[g, at, :], qa[g, :, cols], preferred_element_type=F32) for g in range(NH)]
            for g in range(NH):
                m, acc = carry[g]
                m2 = jnp.maximum(m, jnp.max(s[g], axis=0, keepdims=True))
                p = jnp.exp2((s[g] - m2) * SCORE_SCALE).astype(BF)
                acc = acc * jnp.exp2((m - m2) * SCORE_SCALE) + jnp.dot(
                    va[g, :, at], p, preferred_element_type=F32)
                out.append((m2, acc))
            return tuple(out)

        first = tuple((jnp.full((1, QB), -3e38, F32), jnp.zeros((80, QB), F32)) for _ in range(NH))
        res = lax.fori_loop(lo, hi, block, first)
        for g in range(NH):
            m, acc = res[g]
            total = acc[64:65]
            o = acc[:64] / total
            o32[i, g * 64:(g + 1) * 64] = o
            if k:
                sb[i, g * 64:(g + 1) * 64] = o.astype(BF)
            else:
                att[t, g * 64:(g + 1) * 64] = o.astype(BF)
            lse[g, pl.ds(i, 1)] = m * SCORE_SCALE + jnp.log2(total)
        if k:
            go_(remote(sb.at[i], att.at[t], s_e.at[k - 1], r_e.at[k - 1], (d, i)))

    def onward(k):
        arrive(WIDE, k)
        chain(others[k], False, False)
        plane(WIDE, others[k], False)

    order = ORDER_K
    attend(order[0])
    onward(0)
    attend(order[1])
    across(WIDE, z)
    attend(order[2])
    onward(1)
    attend(order[3])
    forward(WIDE, zp)
    attend(order[4])
    onward(2)
    attend(order[5])
    forward(WIDE, z1)
    across(WIDE, zp)
    attend(order[6])
    attend(order[7])
    forward(WIDE, z2)
    across(WIDE, z1)
    across(WIDE, z2)
    for zz in [z] + others:
        crossed(WIDE, zz)
    for k in range(1, 8):
        src = (t + 8 - k) % 8
        got(att.at[src], s_e.at[k - 1], r_e.at[k - 1], (d, src))
    for cp in sends:
        cp.wait_send()
    chain(z, True, True)
    for zz in others:
        chain(zz, False, True)
    for k in range(3):
        relay(k, True)


ORDER_K = (4, 3, 5, 2, 6, 1, 7, 0)


def any_spec():
    return pl.BlockSpec(memory_space=pl.ANY)


def vmem_spec():
    return pl.BlockSpec(memory_space=pltpu.VMEM)


def dma(*shape):
    return pltpu.SemaphoreType.DMA(shape)


def front(x, idb, wi, wo, wb, sm, wq):
    span, width = x.shape[1:]
    n = 8 * span
    per = width // 4
    grid_of = lambda a: jax.ShapeDtypeStruct((4, 4, 2) + a.shape, a.dtype)
    return pl.pallas_call(
        front_kernel,
        out_shape=[
            jax.ShapeDtypeStruct((8, span, width), x.dtype),
            jax.ShapeDtypeStruct((8, 8, span), F32),
            grid_of(wi), grid_of(wo), grid_of(wb), grid_of(sm),
            jax.ShapeDtypeStruct((8, per, span), BF),
            jax.ShapeDtypeStruct((3, per, n), BF),
            jax.ShapeDtypeStruct((8, per, span), F32),
            jax.ShapeDtypeStruct((NH, 8, span), F32),
            jax.ShapeDtypeStruct((3, 2, per, width), BF),
        ],
        in_specs=[any_spec()] * 7,
        out_specs=[vmem_spec()] * 2 + [any_spec()] * 3 + [vmem_spec()] * 6,
        scratch_shapes=[
            pltpu.VMEM((3, 4, 4, 2) + wq.shape[:2] + (2 * per,), BF),
            pltpu.VMEM((NH, n, 80), BF), pltpu.VMEM((NH, 80, n), BF), pltpu.VMEM((NH, 80, n), BF),
            pltpu.VMEM((8, per, span), BF),
            dma(N_ARR + 3), dma(2, 3), dma(4, 3), dma(2, 3), dma(4, 3), dma(4, 3), dma(4, 3), dma(N_ARR, 4),
            dma(3, 4), dma(3, 4),
            dma(N_ARR, 4), dma(N_ARR, 4), dma(N_ARR, 4), dma(N_ARR, 4), dma(N_ARR, 4), dma(N_ARR, 4),
            dma(N_ARR, 4), dma(N_ARR, 4), dma(7), dma(7),
        ],
        compiler_params=pltpu.CompilerParams(
            collective_id=1, has_side_effects=True, vmem_limit_bytes=VMEM_LIMIT),
        name="front",
    )(x, idb, wi, wo, wb, sm, wq)


def back_kernel(dat, di, do_, db, ds_, qkv, ids, o32, lse, wt, xs, d_one,
                ox, oi, oo, ob, os_, oq, ov, *rest):
    rd, own, r1, r2, r3, r4, r5 = [rest[4 * i:4 * i + 4] for i in range(7)]
    (da, ka, qa, vk, dkv, pr, xv, dxp, dw, lq, lv,
     xd, x3, x4, x5, q0, q1, q2, qr, v0, v1, v2, vr,
     loc, s_e, r_e, s_d, r_d, s_1, r_1, s_2, r_2, s_3, r_3, s_4, r_4, s_5, r_5,
     s_q1, r_q1, s_q2, r_q2, s_qe, r_qe) = rest[28:]
    d, t, z, c, dx, dy = place()
    x, y = d % 2, d // 2
    h = z // 2
    zp = z + 1 - 2 * (z % 2)
    inner = (z + h) % 2 == 1
    me = lambda zz: (d, zz * 2 + c)
    core = (d, z * 2 + 1 - c)
    nx, ny = (dx, t), (dy, t)
    line = [(t + k) % 8 for k in range(1, 8)]
    far = [2 * (1 - h), 2 * (1 - h) + 1]
    order = [far[0], far[1], zp, z]
    group = (z % 2) * 2 + c
    part = [di, do_, db, ds_]
    outs = [oi, oo, ob, os_]
    by_x = [True, True, False, True]
    sends = []
    greet([(d, o) for o in line] + [nx, ny])

    def go_(cp):
        cp.start()
        sends.append(cp)

    def got(ref, ss, rs, dev):
        remote(ref, ref, ss, rs, dev).wait_recv()

    for k in NEAR[1:]:
        i = line[k - 1]
        go_(remote(dat.at[i], da.at[t], s_e.at[k - 1], r_e.at[k - 1], (d, i)))
    for n_, zz in enumerate(order):
        for a in range(4):
            for yy in range(2):
                go_(remote(part[a].at[yy, :, zz, 1 - c], rd[a].at[yy, :, zz], s_d.at[1 + 2 * a + yy, n_],
                           r_d.at[1 + 2 * a + yy, n_], core))
    local = []

    def here(src, to):
        cp = pltpu.make_async_copy(src, to, loc.at[len(local)])
        cp.start()
        local.append(cp)

    here(dat.at[t], da.at[t])
    for a in range(4):
        for yy in range(2):
            here(part[a].at[yy, :, :, c], own[a].at[yy])
    here(xs, xv)

    n = qkv.shape[2]
    span = da.shape[2]

    def fill(tb, _):
        cols = pl.ds(pl.multiple_of(tb * span, span), span)
        hit = marks_of(ids[tb, 0:1])
        ones = jnp.where(hit, 1.0, 0.0)
        away = jnp.where(hit, 0.0, EXCLUDE).astype(BF)
        for g in range(NH):
            rows = slice(g * 64, (g + 1) * 64)
            ka[g, cols, :] = jnp.concatenate([qkv[1, rows, cols].astype(F32), ones], axis=0).T.astype(BF)
            vk[g, cols, :] = qkv[2, rows, cols].astype(F32).T.astype(BF)
            qa[g, :64, cols] = qkv[0, rows, cols]
            qa[g, 64:, cols] = away
            dkv[g, cols, :] = jnp.zeros((span, 128), F32)
        return 0

    lax.fori_loop(0, 8, fill, 0)

    def attend(k):
        i = (t + 8 - k) % 8
        if k:
            got(da.at[i], s_e.at[k - 1], r_e.at[k - 1], (d, i))
        cols = pl.ds(pl.multiple_of(i * QB, QB), QB)
        lo, hi = window(i)
        fixed = []
        for g in range(NH):
            rows = slice(g * 64, (g + 1) * 64)
            do = da[i, rows].astype(F32)
            inside = jnp.sum(do * o32[i, rows], axis=0, keepdims=True)
            zero = jnp.zeros((64, QB), F32)
            ra = jnp.concatenate([do, zero], axis=0).T.astype(BF)
            rb = jnp.concatenate([zero, qkv[0, rows, cols].astype(F32)], axis=0).T.astype(BF)
            fixed.append((inside, lse[g, pl.ds(i, 1)], ra, rb))

        def block(j, carry):
            at = pl.ds(pl.multiple_of(j * KB, KB), KB)
            out = []
            s = [jnp.dot(ka[g, at, :], qa[g, :, cols], preferred_element_type=F32) for g in range(NH)]
            dp = [jnp.dot(vk[g, at, :], da[i, g * 64:(g + 1) * 64], preferred_element_type=F32)
                  for g in range(NH)]
            for g in range(NH):
                inside, lse_i, ra, rb = fixed[g]
                p = jnp.exp2(s[g] * SCORE_SCALE - lse_i)
                ds = (p * (dp[g] - inside)).astype(BF)
                dkv[g, at, :] += jnp.dot(p.astype(BF), ra, preferred_element_type=F32) + jnp.dot(
                    ds, rb, preferred_element_type=F32)
                out.append(carry[g] + jnp.dot(qkv[1, g * 64:(g + 1) * 64, at], ds, preferred_element_type=F32))
            return tuple(out)

        dq = lax.fori_loop(lo, hi, block, tuple(jnp.zeros((64, QB), F32) for _ in range(NH)))
        for g in range(NH):
            pr[0, g * 64:(g + 1) * 64, cols] = (dq[g] * 0.125).astype(BF)

    def add_rows(dst, src):
        def step(i, _):
            dst[i] = dst[i] + src[i]
            return 0

        lax.fori_loop(0, dst.shape[0], step, 0)

    def add_tok(dst, src):
        def step(i, _):
            at = pl.ds(pl.multiple_of(i * 32, 32), 32)
            dst[at, :] = dst[at, :] + src[at, :]
            return 0

        lax.fori_loop(0, dst.shape[0] // 32, step, 0)

    def first(n_):
        zz = order[n_]
        for a in range(4):
            for yy in range(2):
                got(rd[a].at[yy, :, zz], s_d.at[1 + 2 * a + yy, n_], r_d.at[1 + 2 * a + yy, n_], core)
                for xx in range(2):
                    add_rows(rd[a].at[yy, xx, zz], own[a].at[yy, xx, zz])
            if by_x[a]:
                go_(remote(rd[a].at[:, 1 - x, zz], r1[a].at[n_], s_1.at[a, n_], r_1.at[a, n_], nx))
            else:
                go_(remote(rd[a].at[1 - y, :, zz], r1[a].at[n_], s_1.at[a, n_], r_1.at[a, n_], ny))

    def second(n_):
        zz = order[n_]
        for a in range(4):
            got(r1[a].at[n_], s_1.at[a, n_], r_1.at[a, n_], nx if by_x[a] else ny)
            for w in range(2):
                add_rows(rd[a].at[w, x, zz] if by_x[a] else rd[a].at[y, w, zz], r1[a].at[n_, w])
            if by_x[a]:
                go_(remote(rd[a].at[1 - y, x, zz], r2[a].at[n_], s_2.at[a, n_], r_2.at[a, n_], ny))
            else:
                go_(remote(rd[a].at[y, 1 - x, zz], r2[a].at[n_], s_2.at[a, n_], r_2.at[a, n_], nx))

    def to_inner(a, n_):
        ref = xd.at[far[n_]] if a == 4 else rd[a].at[y, x, far[n_]]
        land = x3 if a == 4 else r3[a]
        return remote(ref, land.at[n_], s_3.at[a, n_], r_3.at[a, n_], me(zp))

    def to_far(a, n_):
        ref = xd.at[far[n_]] if a == 4 else rd[a].at[y, x, far[n_]]
        return remote(ref, x4 if a == 4 else r4[a], s_4.at[a, n_], r_4.at[a], me(far[n_]))

    def third(n_):
        zz = order[n_]
        for a in range(4):
            got(r2[a].at[n_], s_2.at[a, n_], r_2.at[a, n_], ny if by_x[a] else nx)
            add_rows(rd[a].at[y, x, zz], r2[a].at[n_])
            if n_ < 2:
                @pl.when(jnp.logical_not(inner))
                def _(a=a):
                    to_inner(a, n_).start()
            elif n_ == 2:
                go_(remote(rd[a].at[y, x, zz], r5[a], s_5.at[a], r_5.at[a], me(zz)))

    def fourth(n_, arrs):
        @pl.when(inner)
        def _():
            for a in arrs:
                to_inner(a, n_).wait_recv()
                if a == 4:
                    add_tok(xd.at[far[n_]], x3.at[n_])
                else:
                    add_rows(rd[a].at[y, x, far[n_]], r3[a].at[n_])
                to_far(a, n_).start()

    for cp in local:
        cp.wait()
    first(0)
    first(1)
    attend(NEAR[0])
    attend(NEAR[1])
    second(0)
    first(2)
    attend(NEAR[2])
    attend(NEAR[3])
    second(1)
    first(3)
    attend(NEAR[4])
    third(0)
    attend(NEAR[5])
    second(2)
    attend(NEAR[6])
    third(1)
    fourth(0, range(4))
    attend(NEAR[7])
    second(3)
    for g in range(NH):
        rows = slice(g * 64, (g + 1) * 64)
        flip = dkv[g].T
        pr[1, rows] = (flip[64:] * 0.125).astype(BF)
        pr[2, rows] = flip[:64].astype(BF)

    def token_grad(tb):
        cols = pl.ds(pl.multiple_of(tb * span, span), span)
        acc = None
        for s in range(3):
            term = jnp.dot(pr[s, :, cols].astype(F32).T.astype(BF), wt[s, c], preferred_element_type=F32)
            acc = term if acc is None else acc + term
        dxp[tb] = acc.astype(BF)

    def token_pair(j, _):
        token_grad(j * 2 + 1 - c)
        return 0

    lax.fori_loop(0, 4, token_pair, 0)
    for n_, zz in enumerate(order):
        go_(remote(dxp.at[zz * 2 + 1 - c], xd.at[zz], s_d.at[0, n_], r_d.at[0, n_], core))
    third(2)
    fourth(1, range(4))

    def token_mine(j, _):
        token_grad(j * 2 + c)
        return 0

    lax.fori_loop(0, 4, token_mine, 0)
    for n_, zz in enumerate(order):
        got(xd.at[zz], s_d.at[0, n_], r_d.at[0, n_], core)
        add_tok(xd.at[zz], dxp.at[zz * 2 + c])
        if n_ < 2:
            @pl.when(jnp.logical_not(inner))
            def _(n_=n_):
                to_inner(4, n_).start()
        elif n_ == 2:
            go_(remote(xd.at[zz], x5, s_5.at[4], r_5.at[4], me(zz)))
    per = pr.shape[1]
    width = wt.shape[3]
    xall = xv[...].reshape(n, width)
    for s in range(3):
        dw[s * per:(s + 1) * per] = jnp.dot(pr[s], xall, preferred_element_type=F32)
    for q in range(2):
        w = dw[:, q * (width // 2):(q + 1) * (width // 2)].T
        lq[q] = w.reshape(lq.shape[1:]).astype(BF)
    lv[...] = jnp.zeros_like(lv)
    for row, s in ((0, 0), (1, 2)):
        col = jnp.sum(pr[s].astype(F32), axis=1, keepdims=True)
        for r in range(8):
            piece = jnp.broadcast_to(col[24 * r:24 * r + 24], (24, 128)).T
            lv[group // 2, group % 2, r // 2, r % 2, row:row + 1, :24] = piece[0:1]
    lq_x = lq
    go_(remote(lq_x.at[:, 1 - x], q1, s_q1.at[0], r_q1.at[0], nx))
    go_(remote(lv.at[:, 1 - x], v1, s_q1.at[1], r_q1.at[1], nx))
    third(3)
    fourth(0, (4,))
    fourth(1, (4,))
    got(q1, s_q1.at[0], r_q1.at[0], nx)
    got(v1, s_q1.at[1], r_q1.at[1], nx)
    for yy in range(2):
        for zc in range(8):
            at = (zc // 2, zc % 2)
            q0[(yy,) + at] = q1[(yy,) + at] + lq[(yy, x) + at]
            v0[(yy,) + at] = v1[(yy,) + at] + lv[(yy, x) + at]
    go_(remote(q0.at[1 - y], q2, s_q2.at[0], r_q2.at[0], ny))
    go_(remote(v0.at[1 - y], v2, s_q2.at[1], r_q2.at[1], ny))
    src_in = 2 - h
    for a in range(4):
        got(r5[a], s_5.at[a], r_5.at[a], me(zp))
        got(r4[a], s_4.at[a, 0], r_4.at[a], me(src_in))
        acc = rd[a].at[y, x, z]
        for i in range(acc.shape[0]):
            outs[a][i] = acc[i].astype(F32) + r5[a][i].astype(F32) + r4[a][i].astype(F32)
    got(q2, s_q2.at[0], r_q2.at[0], ny)
    got(v2, s_q2.at[1], r_q2.at[1], ny)
    for zc in range(8):
        at = (zc // 2, zc % 2)
        q0[(y,) + at] = q0[(y,) + at] + q2[at]
        v0[(y,) + at] = v0[(y,) + at] + v2[at]
    for k in range(1, 8):
        to = line[k - 1]
        go_(remote(q0.at[y, to // 2, to % 2], qr.at[t], s_qe.at[0, k - 1], r_qe.at[0, k - 1], (d, to)))
        go_(remote(v0.at[y, to // 2, to % 2], vr.at[t], s_qe.at[1, k - 1], r_qe.at[1, k - 1], (d, to)))
    qr[t] = q0[y, z, c]
    vr[t] = v0[y, z, c]
    got(x5, s_5.at[4], r_5.at[4], me(zp))
    got(x4, s_4.at[4, 0], r_4.at[4], me(src_in))

    def tok(i, _):
        at = pl.ds(pl.multiple_of(i * 32, 32), 32)
        ox[h, at, :] = d_one[h, at, :] + (xd[z, at, :].astype(F32) + x5[at, :].astype(F32))
        ox[1 - h, at, :] = d_one[1 - h, at, :] + x4[at, :].astype(F32)
        return 0

    lax.fori_loop(0, span // 32, tok, 0)
    for k in range(1, 8):
        src = (t + 8 - k) % 8
        got(qr.at[src], s_qe.at[0, k - 1], r_qe.at[0, k - 1], (d, src))
        got(vr.at[src], s_qe.at[1, k - 1], r_qe.at[1, k - 1], (d, src))
    for g in range(4):
        oq[g] = qr[g].astype(F32) + qr[4 + g].astype(F32)
    total = vr[0]
    for k in range(1, 8):
        total = total + vr[k]
    ov[...] = total
    for cp in sends:
        cp.wait_send()
    for n_ in range(2):
        @pl.when(jnp.logical_not(inner))
        def _(n_=n_):
            for a in range(5):
                to_inner(a, n_).wait_send()

        @pl.when(inner)
        def _(n_=n_):
            for a in range(5):
                to_far(a, n_).wait_send()


NEAR = (0, 1, 7, 2, 6, 3, 5, 4)


def back(dat, di, do_, db, ds_, qkv, ids, o32, lse, wt, xs, d_one):
    arrs = [di, do_, db, ds_]
    tails = [a.shape[4:] for a in arrs]
    per, width = wt.shape[2:]
    n = qkv.shape[2]
    tok = xs.shape[1:]
    qt = di.shape[4:6] + (3 * per,)
    vt = (8, 128)
    scratch = []
    for lead in ((2, 2, 4), (2, 2, 4), (4, 2), (4,), (2,), (), ()):
        for a, tail in zip(arrs, tails):
            scratch.append(pltpu.VMEM(lead + tail, a.dtype))
    grid = (2, 2, 4, 2)
    scratch += [
        pltpu.VMEM(dat.shape, BF),
        pltpu.VMEM((NH, n, 80), BF), pltpu.VMEM((NH, 80, n), BF), pltpu.VMEM((NH, n, 64), BF),
        pltpu.VMEM((NH, n, 128), F32), pltpu.VMEM((3, per, n), BF),
        pltpu.VMEM(xs.shape, BF), pltpu.VMEM(xs.shape, BF), pltpu.VMEM((3 * per, width), F32),
        pltpu.VMEM(grid + qt, BF), pltpu.VMEM(grid + vt, F32),
        pltpu.VMEM((4,) + tok, BF), pltpu.VMEM((2,) + tok, BF), pltpu.VMEM(tok, BF), pltpu.VMEM(tok, BF),
        pltpu.VMEM((2, 4, 2) + qt, BF), pltpu.VMEM((2, 4, 2) + qt, BF), pltpu.VMEM((4, 2) + qt, BF),
        pltpu.VMEM((8,) + qt, BF),
        pltpu.VMEM((2, 4, 2) + vt, F32), pltpu.VMEM((2, 4, 2) + vt, F32), pltpu.VMEM((4, 2) + vt, F32),
        pltpu.VMEM((8,) + vt, F32),
        dma(10), dma(7), dma(7), dma(9, 4), dma(9, 4), dma(4, 4), dma(4, 4), dma(4, 4), dma(4, 4),
        dma(5, 2), dma(5, 2), dma(5, 2), dma(5), dma(5), dma(5),
        dma(2), dma(2), dma(2), dma(2), dma(2, 7), dma(2, 7),
    ]
    return pl.pallas_call(
        back_kernel,
        out_shape=[jax.ShapeDtypeStruct((2,) + tok, F32)]
        + [jax.ShapeDtypeStruct(tail, F32) for tail in tails]
        + [jax.ShapeDtypeStruct((4,) + qt, F32), jax.ShapeDtypeStruct(vt, F32)],
        in_specs=[any_spec()] * 5 + [vmem_spec()] * 5 + [any_spec(), vmem_spec()],
        out_specs=[vmem_spec()] * 7,
        scratch_shapes=scratch,
        compiler_params=pltpu.CompilerParams(
            collective_id=4, has_side_effects=True, vmem_limit_bytes=VMEM_LIMIT),
        name="back",
    )(dat, di, do_, db, ds_, qkv, ids, o32, lse, wt, xs, d_one)


def erf_parts(u):
    phi_c = 0.5 * (1.0 + lax.erf(u * 0.7071067811865476))
    return phi_c, phi_c + u * jnp.exp(-0.5 * u * u) * 0.3989422804014327


def norm_forward(r):
    center = r - jnp.mean(r, axis=-1, keepdims=True)
    inv = lax.rsqrt(jnp.mean(center * center, axis=-1, keepdims=True) + layer_eps)
    return center * inv, inv


def norm_backward(n, inv, gain, dy):
    gd = gain * dy
    return (gd - jnp.mean(gd, axis=-1, keepdims=True) - n * jnp.mean(gd * n, axis=-1, keepdims=True)) * inv


def on_device_fast(
    inputs, segments, w_qkv, b_query, b_value, w_out, b_attn, gain_one, shift_one,
    w_in, b_in, w_back, b_back, gain_two, shift_two, cotangent,
):
    nseq, span, width = inputs.shape
    tokens = nseq * span
    ff = w_in.shape[1]
    depth = w_in.shape[0]
    d, t, z, c, _, _ = place()
    per = width // 4
    vecs = (b_query, b_value, b_attn, gain_one, shift_one, b_back, gain_two, shift_two)
    ffd = b_in.shape[0]
    nv = len(vecs)
    small = jnp.pad(jnp.stack(vecs).astype(F32), ((0, 8), (0, 128 - depth)))
    small = lax.dynamic_update_slice(small, b_in.astype(F32)[None], (nv, 0))
    idb = jnp.broadcast_to(segments.astype(F32)[:, None], (nseq, 8, span))
    xs, ids, gi, go, gb, gs, att, qkv, o32, lse, wt = front(
        inputs, idb, w_in.reshape(depth // 8, 8, ff), w_out.reshape(depth // 8, 8, width),
        w_back.reshape(ffd // 8, 8, width), small, w_qkv.reshape(depth // 8, 8, 3 * width))
    wide_in = gi.reshape(width, ff)
    wide_out = go.reshape(width, width)
    wide_back = gb.reshape(ff, width)
    flat = gs.reshape(32, 16, 128)
    fv = flat[:, :nv, :depth].transpose(1, 0, 2).reshape(nv, width)
    full_b_in = flat[:, nv, :ffd].reshape(ff)
    att = att.reshape(nseq, width, span)

    x32 = inputs.reshape(tokens, width).astype(F32)
    attn_out = jnp.einsum("sit,id->std", att, wide_out, preferred_element_type=F32).reshape(tokens, width)
    resid_one = x32 + attn_out + fv[2]
    n1, inv1 = norm_forward(resid_one)
    normed = n1 * fv[3] + fv[4]
    normed_low = normed.astype(BF)
    pre_act = jnp.dot(normed_low, wide_in, preferred_element_type=F32) + full_b_in
    phi_c, slope = erf_parts(pre_act)
    activ = (pre_act * phi_c).astype(BF)
    branch = jnp.dot(activ, wide_back, preferred_element_type=F32) + fv[5]
    n2, inv2 = norm_forward(normed + branch)
    output = (n2 * fv[6] + fv[7]).astype(BF).reshape(nseq, span, width)
    dy = cotangent.reshape(tokens, width).astype(F32)
    d_two = norm_backward(n2, inv2, fv[6], dy)
    d_branch = d_two.astype(BF)
    grad_w_back = jnp.einsum("tf,td->fd", activ, d_branch, preferred_element_type=F32).astype(BF)
    d_activ = jnp.einsum("td,fd->tf", d_branch, wide_back, preferred_element_type=F32)
    d_pre = (d_activ * slope).astype(BF)
    grad_w_in = jnp.einsum("td,tf->df", normed_low, d_pre, preferred_element_type=F32).astype(BF)
    d_normed = d_two + jnp.einsum("tf,df->td", d_pre, wide_in, preferred_element_type=F32)
    d_one = norm_backward(n1, inv1, fv[3], d_normed)
    d_attn = d_one.astype(BF)
    d_attn3 = d_attn.reshape(nseq, span, width)
    grad_w_out = jnp.einsum("sit,std->id", att, d_attn3, preferred_element_type=F32).astype(BF)
    d_att = jnp.einsum("std,id->sit", d_attn3, wide_out, preferred_element_type=F32).astype(BF)
    sums = [
        jnp.sum(d_attn.astype(F32), axis=0),
        jnp.sum(d_normed * n1, axis=0),
        jnp.sum(d_normed, axis=0),
        jnp.sum(d_branch.astype(F32), axis=0),
        jnp.sum(dy * n2, axis=0),
        jnp.sum(dy, axis=0),
    ]
    g_in = jnp.sum(d_pre.astype(F32), axis=0)
    g_small = jnp.concatenate(
        [jnp.stack(sums).reshape(nv - 2, 32, depth).transpose(1, 0, 2).reshape(32, (nv - 2) * depth), g_in.reshape(32, ffd)],
        axis=1)
    g_small = jnp.pad(g_small, ((0, 0), (0, 1024 - g_small.shape[1])))
    owner = (2, 2, 4, 2)
    input_grad, oi, oo, ob, os_, oq, ov = back(
        d_att.reshape(8, per, span),
        grad_w_in.reshape(owner + (depth // 8, 8, ff)),
        grad_w_out.reshape(owner + (depth // 8, 8, width)),
        grad_w_back.reshape(owner + (ffd // 8, 8, width)),
        g_small.reshape(owner + (8, 128)),
        qkv, ids, o32, lse, wt, xs, d_one.reshape(nseq, span, width),
    )
    g_qkv = oq.reshape(4, depth, 3, per).transpose(1, 2, 0, 3).reshape(depth, 3 * width)
    sv = os_.reshape(1024)
    vec = lambda k: sv[k * depth:(k + 1) * depth]
    return (
        output, input_grad, g_qkv, ov[0, :depth], ov[1, :depth], oo.reshape(depth, width), vec(0), vec(1), vec(2),
        oi.reshape(depth, ff), sv[(nv - 2) * depth:(nv - 2) * depth + ffd], ob.reshape(ffd, width),
        vec(3), vec(4), vec(5),
    )


negative_fill = -1e30


def layer_norm(resid, gain, shift):
    center = resid - jnp.mean(resid, axis=-1, keepdims=True)
    spread = jnp.mean(center * center, axis=-1, keepdims=True)
    return center * lax.rsqrt(spread + layer_eps) * gain + shift


def gelu_exact(values):
    return jax.nn.gelu(values, approximate=False)


def attend_forward(entries):
    query_rows, key_rows, value_rows, query_ids, key_ids = entries
    scores = jnp.einsum(
        "qhd,khd->hqk", query_rows, key_rows, preferred_element_type=jnp.float32
    ) * HEAD_DIM ** (-0.5)
    allowed = (query_ids[:, None] == key_ids[None, :])[None]
    scores = jnp.where(allowed, scores, negative_fill)
    peak = jnp.max(scores, axis=-1, keepdims=True)
    raised = jnp.exp(scores - peak)
    total = jnp.sum(raised, axis=-1, keepdims=True)
    probs_low = (raised / total).astype(jnp.bfloat16)
    context = jnp.einsum("hqk,khd->qhd", probs_low, value_rows, preferred_element_type=jnp.float32)
    return (context, (peak + jnp.log(total))[..., 0])


def score_terms(query_rows, key_rows, value_rows, grad_context, log_total, query_ids, key_ids):
    scale = HEAD_DIM ** (-0.5)
    scores = (
        jnp.einsum("qhd,khd->hqk", query_rows, key_rows, preferred_element_type=jnp.float32) * scale
    )
    allowed = (query_ids[:, None] == key_ids[None, :])[None]
    probs = jnp.where(allowed, jnp.exp(scores - log_total[..., None]), 0.0)
    d_probs = jnp.einsum(
        "qhd,khd->hqk", grad_context, value_rows, preferred_element_type=jnp.float32
    )
    return (probs, d_probs)


def attend_backward(entries):
    query_rows, key_rows, value_rows, grad_context, log_total, query_ids, key_ids = entries
    scale = HEAD_DIM ** (-0.5)
    probs, d_probs = score_terms(
        query_rows, key_rows, value_rows, grad_context, log_total, query_ids, key_ids
    )
    inner = jnp.sum(probs * d_probs, axis=-1, keepdims=True)
    d_scores = (probs * (d_probs - inner)).astype(jnp.bfloat16)
    d_queries = (
        jnp.einsum("hqk,khd->qhd", d_scores, key_rows, preferred_element_type=jnp.float32) * scale
    )
    d_keys = (
        jnp.einsum("hqk,qhd->khd", d_scores, query_rows, preferred_element_type=jnp.float32) * scale
    )
    d_values = jnp.einsum(
        "hqk,qhd->khd", probs.astype(jnp.bfloat16), grad_context, preferred_element_type=jnp.float32
    )
    length = key_rows.shape[0]
    return (
        d_queries,
        d_keys.reshape(length, HEADS * HEAD_DIM),
        d_values.reshape(length, HEADS * HEAD_DIM),
    )


def on_device_general(
    inputs,
    segments,
    w_qkv,
    b_query,
    b_value,
    w_out,
    b_attn,
    gain_one,
    shift_one,
    w_in,
    b_in,
    w_back,
    b_back,
    gain_two,
    shift_two,
    cotangent,
):
    seq_count, group_len, model_width = inputs.shape
    tok_count = seq_count * group_len
    gathered = (
        lax.all_gather(w_qkv, ("dp", "ctx"), axis=0, tiled=True),
        lax.all_gather(b_query, ("dp", "ctx"), axis=0, tiled=True),
        lax.all_gather(b_value, ("dp", "ctx"), axis=0, tiled=True),
        lax.all_gather(w_out, ("dp", "ctx"), axis=0, tiled=True),
        lax.all_gather(b_attn, ("dp", "ctx"), axis=0, tiled=True),
        lax.all_gather(gain_one, ("dp", "ctx"), axis=0, tiled=True),
        lax.all_gather(shift_one, ("dp", "ctx"), axis=0, tiled=True),
        lax.all_gather(w_in, ("dp", "ctx"), axis=0, tiled=True),
        lax.all_gather(b_in, ("dp", "ctx"), axis=0, tiled=True),
        lax.all_gather(w_back, ("dp", "ctx"), axis=0, tiled=True),
        lax.all_gather(b_back, ("dp", "ctx"), axis=0, tiled=True),
        lax.all_gather(gain_two, ("dp", "ctx"), axis=0, tiled=True),
        lax.all_gather(shift_two, ("dp", "ctx"), axis=0, tiled=True),
    )
    (
        wide_qkv,
        full_b_query,
        full_b_value,
        wide_out,
        full_b_attn,
        full_gain_one,
        full_shift_one,
        wide_in,
        full_b_in,
        wide_back,
        full_b_back,
        full_gain_two,
        full_shift_two,
    ) = gathered
    tokens = inputs.reshape(tok_count, model_width)
    projected = jnp.dot(tokens, wide_qkv, preferred_element_type=jnp.float32)
    query_low = (projected[:, :model_width] + full_b_query.astype(jnp.float32)).astype(jnp.bfloat16)
    key_low = projected[:, model_width : 2 * model_width].astype(jnp.bfloat16)
    value_low = (projected[:, 2 * model_width :] + full_b_value.astype(jnp.float32)).astype(
        jnp.bfloat16
    )
    key_ids = lax.all_gather(segments, "ctx", axis=1, tiled=True)
    key_local = key_low.reshape(seq_count, group_len, model_width)
    value_local = value_low.reshape(seq_count, group_len, model_width)
    key_whole, value_whole = (
        lax.all_gather(key_local, "ctx", axis=1, tiled=True),
        lax.all_gather(value_local, "ctx", axis=1, tiled=True),
    )
    seq_len = key_whole.shape[1]
    query_heads = query_low.reshape(seq_count, group_len, HEADS, HEAD_DIM)
    context, log_total = lax.map(
        attend_forward,
        (
            query_heads,
            key_whole.reshape(seq_count, seq_len, HEADS, HEAD_DIM),
            value_whole.reshape(seq_count, seq_len, HEADS, HEAD_DIM),
            segments,
            key_ids,
        ),
    )
    attended = context.reshape(tok_count, model_width).astype(jnp.bfloat16)
    attn_out = jnp.dot(attended, wide_out, preferred_element_type=jnp.float32) + full_b_attn.astype(
        jnp.float32
    )
    resid_one = tokens.astype(jnp.float32) + attn_out
    normed, norm_one_back = jax.vjp(
        layer_norm, resid_one, full_gain_one.astype(jnp.float32), full_shift_one.astype(jnp.float32)
    )
    normed_low = normed.astype(jnp.bfloat16)
    pre_act = jnp.dot(normed_low, wide_in, preferred_element_type=jnp.float32) + full_b_in.astype(
        jnp.float32
    )
    activ_f, gelu_back = jax.vjp(gelu_exact, pre_act)
    activ = activ_f.astype(jnp.bfloat16)
    branch = jnp.dot(activ, wide_back, preferred_element_type=jnp.float32) + full_b_back.astype(
        jnp.float32
    )
    resid_two = normed + branch
    final_norm, norm_two_back = jax.vjp(
        layer_norm, resid_two, full_gain_two.astype(jnp.float32), full_shift_two.astype(jnp.float32)
    )
    output = final_norm.astype(jnp.bfloat16).reshape(seq_count, group_len, model_width)
    back_qkv, back_out, back_in, back_back = (
        lax.all_gather(w_qkv, ("dp", "ctx"), axis=0, tiled=True),
        lax.all_gather(w_out, ("dp", "ctx"), axis=0, tiled=True),
        lax.all_gather(w_in, ("dp", "ctx"), axis=0, tiled=True),
        lax.all_gather(w_back, ("dp", "ctx"), axis=0, tiled=True),
    )
    d_final = cotangent.reshape(tok_count, model_width).astype(jnp.float32)
    d_two, grad_gain_two, grad_shift_two = norm_two_back(d_final)
    d_branch = d_two.astype(jnp.bfloat16)
    grad_b_back = jnp.sum(d_branch.astype(jnp.float32), axis=0)
    grad_w_back = jnp.einsum("tf,td->fd", activ, d_branch, preferred_element_type=jnp.float32)
    d_activ = jnp.einsum("td,fd->tf", d_branch, back_back, preferred_element_type=jnp.float32)
    d_pre = gelu_back(d_activ)[0].astype(jnp.bfloat16)
    grad_b_in = jnp.sum(d_pre.astype(jnp.float32), axis=0)
    grad_w_in = jnp.einsum("td,tf->df", normed_low, d_pre, preferred_element_type=jnp.float32)
    d_normed = d_two + jnp.einsum("tf,df->td", d_pre, back_in, preferred_element_type=jnp.float32)
    d_one, grad_gain_one, grad_shift_one = norm_one_back(d_normed)
    d_attn = d_one.astype(jnp.bfloat16)
    grad_b_attn = jnp.sum(d_attn.astype(jnp.float32), axis=0)
    grad_w_out = jnp.einsum("ti,td->id", attended, d_attn, preferred_element_type=jnp.float32)
    d_attended = jnp.einsum(
        "td,id->ti", d_attn, back_out, preferred_element_type=jnp.float32
    ).astype(jnp.bfloat16)
    key_back, value_back = (
        lax.all_gather(key_local, "ctx", axis=1, tiled=True),
        lax.all_gather(value_local, "ctx", axis=1, tiled=True),
    )
    grad_heads = d_attended.reshape(seq_count, group_len, HEADS, HEAD_DIM)
    d_query_part, d_key_part, d_value_part = lax.map(
        attend_backward,
        (
            query_heads,
            key_back.reshape(seq_count, seq_len, HEADS, HEAD_DIM),
            value_back.reshape(seq_count, seq_len, HEADS, HEAD_DIM),
            grad_heads,
            log_total,
            segments,
            key_ids,
        ),
    )
    d_key_sum, d_value_sum = (
        lax.psum_scatter(
            d_key_part.astype(jnp.bfloat16), "ctx", scatter_dimension=1, tiled=True
        ).astype(jnp.float32),
        lax.psum_scatter(
            d_value_part.astype(jnp.bfloat16), "ctx", scatter_dimension=1, tiled=True
        ).astype(jnp.float32),
    )
    d_queries = d_query_part.reshape(tok_count, model_width).astype(jnp.bfloat16)
    d_keys = d_key_sum.reshape(tok_count, model_width).astype(jnp.bfloat16)
    d_values = d_value_sum.reshape(tok_count, model_width).astype(jnp.bfloat16)
    d_proj = jnp.concatenate([d_queries, d_keys, d_values], axis=1)
    grad_w_qkv = jnp.einsum("td,te->de", tokens, d_proj, preferred_element_type=jnp.float32)
    grad_b_query = jnp.sum(d_queries.astype(jnp.float32), axis=0)
    grad_b_value = jnp.sum(d_values.astype(jnp.float32), axis=0)
    input_grad = d_one + jnp.einsum(
        "te,de->td", d_proj, back_qkv, preferred_element_type=jnp.float32
    )
    summed = (
        lax.psum_scatter(grad_w_qkv, ("dp", "ctx"), scatter_dimension=0, tiled=True),
        lax.psum_scatter(grad_b_query, ("dp", "ctx"), scatter_dimension=0, tiled=True),
        lax.psum_scatter(grad_b_value, ("dp", "ctx"), scatter_dimension=0, tiled=True),
        lax.psum_scatter(grad_w_out, ("dp", "ctx"), scatter_dimension=0, tiled=True),
        lax.psum_scatter(grad_b_attn, ("dp", "ctx"), scatter_dimension=0, tiled=True),
        lax.psum_scatter(grad_gain_one, ("dp", "ctx"), scatter_dimension=0, tiled=True),
        lax.psum_scatter(grad_shift_one, ("dp", "ctx"), scatter_dimension=0, tiled=True),
        lax.psum_scatter(grad_w_in, ("dp", "ctx"), scatter_dimension=0, tiled=True),
        lax.psum_scatter(grad_b_in, ("dp", "ctx"), scatter_dimension=0, tiled=True),
        lax.psum_scatter(grad_w_back, ("dp", "ctx"), scatter_dimension=0, tiled=True),
        lax.psum_scatter(grad_b_back, ("dp", "ctx"), scatter_dimension=0, tiled=True),
        lax.psum_scatter(grad_gain_two, ("dp", "ctx"), scatter_dimension=0, tiled=True),
        lax.psum_scatter(grad_shift_two, ("dp", "ctx"), scatter_dimension=0, tiled=True),
    )
    return (
        output,
        input_grad.reshape(seq_count, group_len, model_width),
        summed[0],
        summed[1],
        summed[2],
        summed[3],
        summed[4],
        summed[5],
        summed[6],
        summed[7],
        summed[8],
        summed[9],
        summed[10],
        summed[11],
        summed[12],
    )


def solution(mesh):
    placed = (
        P("dp", "ctx", None),
        P("dp", "ctx"),
        P(("dp", "ctx"), None),
        P(("dp", "ctx")),
        P(("dp", "ctx")),
        P(("dp", "ctx"), None),
        P(("dp", "ctx")),
        P(("dp", "ctx")),
        P(("dp", "ctx")),
        P(("dp", "ctx"), None),
        P(("dp", "ctx")),
        P(("dp", "ctx"), None),
        P(("dp", "ctx")),
        P(("dp", "ctx")),
        P(("dp", "ctx")),
        P("dp", "ctx", None),
    )
    fits = mesh.shape["dp"] == 4 and mesh.shape["ctx"] == 8
    return jax.shard_map(
        on_device_fast if fits else on_device_general,
        mesh=mesh,
        in_specs=placed,
        out_specs=(
            P("dp", "ctx", None),
            P("dp", "ctx", None),
            P(("dp", "ctx"), None),
            P(("dp", "ctx")),
            P(("dp", "ctx")),
            P(("dp", "ctx"), None),
            P(("dp", "ctx")),
            P(("dp", "ctx")),
            P(("dp", "ctx")),
            P(("dp", "ctx"), None),
            P(("dp", "ctx")),
            P(("dp", "ctx"), None),
            P(("dp", "ctx")),
            P(("dp", "ctx")),
            P(("dp", "ctx")),
        ),
        check_vma=False,
    )
```

```python
import functools
import jax
import jax.numpy as jnp
from jax import lax
from jax.experimental import pallas as pl
from jax.experimental.pallas import tpu as pltpu
from jax.sharding import PartitionSpec as P

HEADS = 12
HEAD_DIM = 64
layer_eps = 1e-12
MESH_ID = pl.DeviceIdType.MESH
BF = jnp.bfloat16
F32 = jnp.float32
VMEM_LIMIT = 64 * 1024 * 1024 - 65536
SCORE_SCALE = 0.125 * 1.4426950408889634
EXCLUDE = -1e30


def place():
    d = lax.axis_index("dp")
    t = lax.axis_index("ctx")
    z = t // 2
    c = t % 2
    dx = d + 1 - 2 * (d % 2)
    dy = (d + 2) % 4
    return d, t, z, c, dx, dy


def remote(src, dst, ss, rs, dev):
    return pltpu.make_async_remote_copy(
        src_ref=src, dst_ref=dst, send_sem=ss, recv_sem=rs, device_id=dev, device_id_type=MESH_ID
    )


def greet(devices):
    bar = pltpu.get_barrier_semaphore()
    for dev in devices:
        pl.semaphore_signal(bar, inc=1, device_id=dev, device_id_type=MESH_ID)
    pl.semaphore_wait(bar, len(devices))


QB = 256
KB = 256
NH = 3


def marks_of(ids_row):
    kinds = lax.broadcasted_iota(jnp.int32, (16, ids_row.shape[1]), 0).astype(F32)
    return kinds == ids_row


N_ARR = 7
WIDE = (0, 1, 2)
EARLY = (3, 4, 5, 6)
FIRST_X = (0, 1, 3)
FIRST_Y = (2, 4, 5, 6)


def window(i):
    return (i // 4) * (i % 4), 8 - (1 - i // 4) * (3 - i % 4)


def front_kernel(x, idb, wi, wo, wb, sm, wq,
                 xs, ids, gi, go, gb, fv, bi, att, qkv, o32, lse, wt,
                 gs, gq, ka, va, qa, sb,
                 loc, s_x, r_x, s_xf, s_xd, r_xd, s_z, r_z, s_up, s_dn, s_px, r_px, s_py, r_py, s_f, r_f,
                 s_c, r_c, s_e, r_e):
    d, t, z, c, dx, dy = place()
    h = z // 2
    zp = z + 1 - 2 * (z % 2)
    inner = (z + h) % 2 == 1
    dxy = (dx + 2) % 4
    z1, z2 = 2 - h, 3 * (1 - h)
    others = [zp, z1, z2]
    far = [z1, z2]
    me = lambda zz: (d, zz * 2 + c)
    core = (d, z * 2 + 1 - c)
    nx, ny = (dx, t), (dy, t)
    greet([(d, (t + k) % 8) for k in range(1, 8)] + [nx, ny])
    sends = []

    def go_(cp):
        cp.start()
        sends.append(cp)

    def got(ref, ss, rs, dev):
        remote(ref, ref, ss, rs, dev).wait_recv()

    per = wq.shape[2] // 6
    dst = [gi, go, gb, gs, gq.at[0], gq.at[1], gq.at[2]]

    def mine(a, zz):
        if a < 4:
            return (wi, wo, wb, sm)[a]
        return wq.at[:, :, pl.ds(pl.multiple_of((a - 4) * 2 * per + (zz % 2) * per, per), per)]

    half = x.shape[1] // 2

    def piece(k, hh, tt):
        if k == 2:
            return idb.at[hh], ids.at[tt]
        rows = pl.ds(k * half, half)
        return x.at[hh, rows], xs.at[tt, rows]

    for a in EARLY:
        for k in range(3):
            zz = others[k]
            go_(remote(mine(a, zz), dst[a].at[d, z, c], s_z.at[a - 3, k], r_z.at[a, z], me(zz)))

    def plane(arrs, zz, first):
        for a in arrs:
            src = mine(a, z) if first else dst[a].at[d, zz, c]
            go_(remote(src, dst[a].at[d, zz, c], s_px.at[a, zz], r_px.at[a, zz], nx))
            go_(remote(src, dst[a].at[d, zz, c], s_py.at[a, zz], r_py.at[a, zz], ny))

    plane(EARLY, z, True)
    for k in (2, 0, 1):
        src, to = piece(k, 1 - h, t)
        go_(remote(src, to, s_x.at[0, k], r_x.at[z, k], me(z1)))
        src, to = piece(k, h, t)
        go_(remote(src, to, s_x.at[1, k], r_x.at[z, k], me(zp)))

    def chain(zz, first, wait):
        for a in WIDE:
            src = mine(a, z) if first else dst[a].at[d, zz, c]
            up = remote(src, dst[a].at[d, zz, c], s_up.at[a, zz], r_z.at[a, zz], me((z + 1) % 4))
            dn = remote(src, dst[a].at[d, zz, c], s_dn.at[a, zz], r_z.at[a, zz], me((z + 3) % 4))

            @pl.when(jnp.logical_and(zz <= z, z < 3))
            def _(up=up):
                if wait:
                    up.wait_send()
                else:
                    up.start()

            @pl.when(jnp.logical_and(zz >= z, z > 0))
            def _(dn=dn):
                if wait:
                    dn.wait_send()
                else:
                    dn.start()

    chain(z, True, False)
    plane(WIDE, z, True)
    locals_ = [pltpu.make_async_copy(piece(k, h, t)[0], piece(k, h, t)[1], loc.at[N_ARR + k]) for k in range(3)]
    for a in (4, 5, 6, 3, 0, 1, 2):
        locals_.append(pltpu.make_async_copy(mine(a, z), dst[a].at[d, z, c], loc.at[a]))
    for cp in locals_:
        cp.start()

    def forward(arrs, zz):
        for a in arrs:
            if a in FIRST_Y:
                got(dst[a].at[dy, zz, c], s_py.at[a, zz], r_py.at[a, zz], ny)
                go_(remote(dst[a].at[dy, zz, c], dst[a].at[dy, zz, c], s_f.at[a, zz], r_f.at[a, zz], nx))
            else:
                got(dst[a].at[dx, zz, c], s_px.at[a, zz], r_px.at[a, zz], nx)
                go_(remote(dst[a].at[dx, zz, c], dst[a].at[dx, zz, c], s_f.at[a, zz], r_f.at[a, zz], ny))

    def across(arrs, zz):
        for a in arrs:
            if a in FIRST_Y:
                got(dst[a].at[dx, zz, c], s_px.at[a, zz], r_px.at[a, zz], nx)
                got(dst[a].at[dxy, zz, c], s_f.at[a, zz], r_f.at[a, zz], nx)
            else:
                got(dst[a].at[dy, zz, c], s_py.at[a, zz], r_py.at[a, zz], ny)
                got(dst[a].at[dxy, zz, c], s_f.at[a, zz], r_f.at[a, zz], ny)
            go_(remote(dst[a].at[:, zz, c], dst[a].at[:, zz, c], s_c.at[a, zz], r_c.at[a, zz], core))

    def crossed(arrs, zz):
        for a in arrs:
            ref = dst[a].at[:, zz, 1 - c]
            got(ref, s_c.at[a, zz], r_c.at[a, zz], core)

    def arrive(arrs, k):
        for a in arrs:
            got(dst[a].at[d, others[k], c], s_z.at[0, 0], r_z.at[a, others[k]], me(others[k]))

    for k in range(3):
        arrive(EARLY, k)
        plane(EARLY, others[k], False)
    for cp in locals_[:7]:
        cp.wait()
    for zz in [z] + others:
        forward(EARLY, zz)

    def relay(k, wait):
        for j in range(2):
            ref = piece(k, h, far[j] * 2 + c)[1]
            cp = remote(ref, ref, s_xf.at[j, k], r_x.at[far[j], k], me(zp))

            @pl.when(inner)
            def _(cp=cp):
                if wait:
                    cp.wait_send()
                else:
                    cp.wait_recv()
                    cp.start()

    def relayed(k):
        for j in range(2):
            ref = piece(k, h, far[j] * 2 + c)[1]

            @pl.when(jnp.logical_not(inner))
            def _(ref=ref, j=j):
                got(ref, s_x.at[0, k], r_x.at[far[j], k], me(zp))

    def to_core(zz):
        for k in range(3):
            ref = piece(k, h, zz * 2 + c)[1]
            go_(remote(ref, ref, s_xd.at[zz, k], r_xd.at[zz, k], core))

    def from_core(zz):
        for k in range(3):
            got(piece(k, h, zz * 2 + 1 - c)[1], s_xd.at[zz, k], r_xd.at[zz, k], core)

    to_core(z)
    for k in (2, 0):
        relay(k, False)
    for zz in [z] + others:
        across(EARLY, zz)
    relay(1, False)
    for k in range(3):
        got(piece(k, h, zp * 2 + c)[1], s_x.at[1, k], r_x.at[zp, k], me(zp))
    to_core(zp)
    for zz in [z] + others:
        crossed(EARLY, zz)
    width = wt.shape[3]
    for j in range(3):
        for q in range(2):
            w = gq[j, 2 * q:2 * q + 2].astype(F32).reshape(width // 2, per)
            w = w.T.astype(BF)
            for cc in range(2):
                wt[j, cc, :, q * (width // 2):(q + 1) * (width // 2)] = w[cc * (per // 2):(cc + 1) * (per // 2)]
    group = (z % 2) * 2 + c
    span = x.shape[1]

    def column(row):
        v = gs[group, :, :, row].reshape(8, 128).T
        return jnp.concatenate([v[:24, r:r + 1] for r in range(8)], axis=0)

    bias = [column(0), None, column(1)]
    for g in range(NH):
        va[g, 64:] = jnp.ones((16, va.shape[2]), BF)

    def project(zz):
        def one(j, _):
            tb = zz * 2 + j
            cols = pl.ds(pl.multiple_of(tb * span, span), span)
            xb = xs[tb]
            hit = marks_of(ids[tb, 0:1])
            ones = jnp.where(hit, 1.0, 0.0)
            away = jnp.where(hit, 0.0, EXCLUDE).astype(BF)
            for s in range(3):
                r = lax.dot_general(wt[s, c], xb, (((1,), (1,)), ((), ())), preferred_element_type=F32)
                if bias[s] is not None:
                    r = r + bias[s]
                low = r.astype(BF)
                qkv[s, :, cols] = low
                for g in range(NH):
                    part = low[g * 64:(g + 1) * 64]
                    if s == 0:
                        qa[g, :64, cols] = part
                        qa[g, 64:, cols] = away
                    elif s == 1:
                        ka[g, cols, :] = jnp.concatenate([part.astype(F32), ones], axis=0).T.astype(BF)
                    else:
                        va[g, :64, cols] = part
            return 0

        lax.fori_loop(0, 2, one, 0)

    forward(WIDE, z)
    for zz in (z, zp):
        from_core(zz)
        project(zz)
    for k in (2, 0, 1):
        relayed(k)
    for zz in far:
        to_core(zz)
    for zz in far:
        from_core(zz)
        project(zz)

    def attend(k):
        i = (t + k) % 8
        cols = pl.ds(pl.multiple_of(i * QB, QB), QB)
        lo, hi = window(i)

        def block(j, carry):
            at = pl.ds(pl.multiple_of(j * KB, KB), KB)
            out = []
            s = [jnp.dot(ka[g, at, :], qa[g, :, cols], preferred_element_type=F32) for g in range(NH)]
            for g in range(NH):
                m, acc = carry[g]
                m2 = jnp.maximum(m, jnp.max(s[g], axis=0, keepdims=True))
                p = jnp.exp2((s[g] - m2) * SCORE_SCALE).astype(BF)
                acc = acc * jnp.exp2((m - m2) * SCORE_SCALE) + jnp.dot(
                    va[g, :, at], p, preferred_element_type=F32)
                out.append((m2, acc))
            return tuple(out)

        first = tuple((jnp.full((1, QB), -3e38, F32), jnp.zeros((80, QB), F32)) for _ in range(NH))
        res = lax.fori_loop(lo, hi, block, first)
        for g in range(NH):
            m, acc = res[g]
            total = acc[64:65]
            o = acc[:64] / total
            o32[i, g * 64:(g + 1) * 64] = o
            if k:
                sb[i, g * 64:(g + 1) * 64] = o.astype(BF)
            else:
                att[t, g * 64:(g + 1) * 64] = o.astype(BF)
            lse[g, pl.ds(i, 1)] = m * SCORE_SCALE + jnp.log2(total)
        if k:
            go_(remote(sb.at[i], att.at[t], s_e.at[k - 1], r_e.at[k - 1], (d, i)))

    def onward(k):
        arrive(WIDE, k)
        chain(others[k], False, False)
        plane(WIDE, others[k], False)

    order = ORDER_K
    attend(order[0])
    onward(0)
    attend(order[1])
    for cp in locals_[7:]:
        cp.wait()
    across(WIDE, z)
    attend(order[2])
    onward(1)
    attend(order[3])
    forward(WIDE, zp)
    attend(order[4])
    onward(2)
    attend(order[5])
    forward(WIDE, z1)
    across(WIDE, zp)
    attend(order[6])
    attend(order[7])
    forward(WIDE, z2)
    across(WIDE, z1)
    across(WIDE, z2)
    for r in range(32):
        v = gs.at[r // 8, (r // 2) % 4, r % 2]
        fv[:, 24 * r:24 * r + 24] = v[0:8, 0:24]
        bi[:, 96 * r:96 * r + 96] = v[8:9, 0:96]
    for zz in [z] + others:
        crossed(WIDE, zz)
    for k in range(1, 8):
        src = (t + 8 - k) % 8
        got(att.at[src], s_e.at[k - 1], r_e.at[k - 1], (d, src))
    for cp in sends:
        cp.wait_send()
    chain(z, True, True)
    for zz in others:
        chain(zz, False, True)
    for k in range(3):
        relay(k, True)


ORDER_K = (4, 3, 5, 2, 6, 1, 7, 0)


def any_spec():
    return pl.BlockSpec(memory_space=pl.ANY)


def vmem_spec():
    return pl.BlockSpec(memory_space=pltpu.VMEM)


def dma(*shape):
    return pltpu.SemaphoreType.DMA(shape)


def front(x, idb, wi, wo, wb, sm, wq):
    span, width = x.shape[1:]
    n = 8 * span
    per = width // 4
    grid_of = lambda a: jax.ShapeDtypeStruct((4, 4, 2) + a.shape, a.dtype)
    return pl.pallas_call(
        front_kernel,
        out_shape=[
            jax.ShapeDtypeStruct((8, span, width), x.dtype),
            jax.ShapeDtypeStruct((8, 8, span), F32),
            grid_of(wi), grid_of(wo), grid_of(wb),
            jax.ShapeDtypeStruct((8, width), F32), jax.ShapeDtypeStruct((1, wi.shape[2]), F32),
            jax.ShapeDtypeStruct((8, per, span), BF),
            jax.ShapeDtypeStruct((3, per, n), BF),
            jax.ShapeDtypeStruct((8, per, span), F32),
            jax.ShapeDtypeStruct((NH, 8, span), F32),
            jax.ShapeDtypeStruct((3, 2, per, width), BF),
        ],
        in_specs=[any_spec()] * 7,
        out_specs=[vmem_spec()] * 2 + [any_spec()] * 3 + [vmem_spec()] * 7,
        scratch_shapes=[
            pltpu.VMEM((4, 4, 2) + sm.shape, F32),
            pltpu.VMEM((3, 4, 4, 2) + wq.shape[:2] + (2 * per,), BF),
            pltpu.VMEM((NH, n, 80), BF), pltpu.VMEM((NH, 80, n), BF), pltpu.VMEM((NH, 80, n), BF),
            pltpu.VMEM((8, per, span), BF),
            dma(N_ARR + 3), dma(2, 3), dma(4, 3), dma(2, 3), dma(4, 3), dma(4, 3), dma(4, 3), dma(N_ARR, 4),
            dma(3, 4), dma(3, 4),
            dma(N_ARR, 4), dma(N_ARR, 4), dma(N_ARR, 4), dma(N_ARR, 4), dma(N_ARR, 4), dma(N_ARR, 4),
            dma(N_ARR, 4), dma(N_ARR, 4), dma(7), dma(7),
        ],
        compiler_params=pltpu.CompilerParams(
            collective_id=1, has_side_effects=True, vmem_limit_bytes=VMEM_LIMIT),
        name="front",
    )(x, idb, wi, wo, wb, sm, wq)


def back_kernel(dat, di, do_, db, ds_, qkv, ids, o32, lse, wt, xs, d_one,
                ox, oi, oo, ob, os_, oq, ov, *rest):
    rd, own, r1, r2, r3, r4, r5 = [rest[4 * i:4 * i + 4] for i in range(7)]
    (da, ka, qa, vk, dkv, pr, xv, dxp, dw, lq, lv,
     xd, x3, x4, x5, q0, q1, q2, qr, v0, v1, v2, vr,
     loc, s_e, r_e, s_d, r_d, s_1, r_1, s_2, r_2, s_3, r_3, s_4, r_4, s_5, r_5,
     s_q1, r_q1, s_q2, r_q2, s_qe, r_qe) = rest[28:]
    d, t, z, c, dx, dy = place()
    x, y = d % 2, d // 2
    h = z // 2
    zp = z + 1 - 2 * (z % 2)
    inner = (z + h) % 2 == 1
    me = lambda zz: (d, zz * 2 + c)
    core = (d, z * 2 + 1 - c)
    nx, ny = (dx, t), (dy, t)
    line = [(t + k) % 8 for k in range(1, 8)]
    far = [2 * (1 - h), 2 * (1 - h) + 1]
    order = [far[0], far[1], zp, z]
    group = (z % 2) * 2 + c
    part = [di, do_, db, ds_]
    outs = [oi, oo, ob, os_]
    by_x = [True, True, False, True]
    sends = []
    greet([(d, o) for o in line] + [nx, ny])

    def go_(cp):
        cp.start()
        sends.append(cp)

    def got(ref, ss, rs, dev):
        remote(ref, ref, ss, rs, dev).wait_recv()

    for k in NEAR[1:]:
        i = line[k - 1]
        go_(remote(dat.at[i], da.at[t], s_e.at[k - 1], r_e.at[k - 1], (d, i)))
    for n_, zz in enumerate(order):
        for a in range(4):
            for yy in range(2):
                go_(remote(part[a].at[yy, :, zz, 1 - c], rd[a].at[yy, :, zz], s_d.at[1 + 2 * a + yy, n_],
                           r_d.at[1 + 2 * a + yy, n_], core))
    local = []

    def here(src, to):
        cp = pltpu.make_async_copy(src, to, loc.at[len(local)])
        cp.start()
        local.append(cp)

    here(dat.at[t], da.at[t])
    for a in range(4):
        for yy in range(2):
            here(part[a].at[yy, :, :, c], own[a].at[yy])
    here(xs, xv)

    n = qkv.shape[2]
    span = da.shape[2]

    def fill(tb, _):
        cols = pl.ds(pl.multiple_of(tb * span, span), span)
        hit = marks_of(ids[tb, 0:1])
        ones = jnp.where(hit, 1.0, 0.0)
        away = jnp.where(hit, 0.0, EXCLUDE).astype(BF)
        for g in range(NH):
            rows = slice(g * 64, (g + 1) * 64)
            ka[g, cols, :] = jnp.concatenate([qkv[1, rows, cols].astype(F32), ones], axis=0).T.astype(BF)
            vk[g, cols, :] = qkv[2, rows, cols].astype(F32).T.astype(BF)
            qa[g, :64, cols] = qkv[0, rows, cols]
            qa[g, 64:, cols] = away
            dkv[g, cols, :] = jnp.zeros((span, 128), F32)
        return 0

    lax.fori_loop(0, 8, fill, 0)

    def attend(k):
        i = (t + 8 - k) % 8
        if k:
            got(da.at[i], s_e.at[k - 1], r_e.at[k - 1], (d, i))
        cols = pl.ds(pl.multiple_of(i * QB, QB), QB)
        lo, hi = window(i)
        fixed = []
        for g in range(NH):
            rows = slice(g * 64, (g + 1) * 64)
            do = da[i, rows].astype(F32)
            inside = jnp.sum(do * o32[i, rows], axis=0, keepdims=True)
            zero = jnp.zeros((64, QB), F32)
            ra = jnp.concatenate([do, zero], axis=0).T.astype(BF)
            rb = jnp.concatenate([zero, qkv[0, rows, cols].astype(F32)], axis=0).T.astype(BF)
            fixed.append((inside, lse[g, pl.ds(i, 1)], ra, rb))

        def block(j, carry):
            at = pl.ds(pl.multiple_of(j * KB, KB), KB)
            out = []
            s = [jnp.dot(ka[g, at, :], qa[g, :, cols], preferred_element_type=F32) for g in range(NH)]
            dp = [jnp.dot(vk[g, at, :], da[i, g * 64:(g + 1) * 64], preferred_element_type=F32)
                  for g in range(NH)]
            for g in range(NH):
                inside, lse_i, ra, rb = fixed[g]
                p = jnp.exp2(s[g] * SCORE_SCALE - lse_i)
                ds = (p * (dp[g] - inside)).astype(BF)
                dkv[g, at, :] += jnp.dot(p.astype(BF), ra, preferred_element_type=F32) + jnp.dot(
                    ds, rb, preferred_element_type=F32)
                out.append(carry[g] + jnp.dot(qkv[1, g * 64:(g + 1) * 64, at], ds, preferred_element_type=F32))
            return tuple(out)

        dq = lax.fori_loop(lo, hi, block, tuple(jnp.zeros((64, QB), F32) for _ in range(NH)))
        for g in range(NH):
            pr[0, g * 64:(g + 1) * 64, cols] = (dq[g] * 0.125).astype(BF)

    def add_rows(dst, src):
        def step(i, _):
            dst[i] = dst[i] + src[i]
            return 0

        lax.fori_loop(0, dst.shape[0], step, 0)

    def add_tok(dst, src):
        def step(i, _):
            at = pl.ds(pl.multiple_of(i * 32, 32), 32)
            dst[at, :] = dst[at, :] + src[at, :]
            return 0

        lax.fori_loop(0, dst.shape[0] // 32, step, 0)

    def first(n_):
        zz = order[n_]
        for a in range(4):
            for yy in range(2):
                got(rd[a].at[yy, :, zz], s_d.at[1 + 2 * a + yy, n_], r_d.at[1 + 2 * a + yy, n_], core)
                for xx in range(2):
                    add_rows(rd[a].at[yy, xx, zz], own[a].at[yy, xx, zz])
            if by_x[a]:
                go_(remote(rd[a].at[:, 1 - x, zz], r1[a].at[n_], s_1.at[a, n_], r_1.at[a, n_], nx))
            else:
                go_(remote(rd[a].at[1 - y, :, zz], r1[a].at[n_], s_1.at[a, n_], r_1.at[a, n_], ny))

    def second(n_):
        zz = order[n_]
        for a in range(4):
            got(r1[a].at[n_], s_1.at[a, n_], r_1.at[a, n_], nx if by_x[a] else ny)
            for w in range(2):
                add_rows(rd[a].at[w, x, zz] if by_x[a] else rd[a].at[y, w, zz], r1[a].at[n_, w])
            if by_x[a]:
                go_(remote(rd[a].at[1 - y, x, zz], r2[a].at[n_], s_2.at[a, n_], r_2.at[a, n_], ny))
            else:
                go_(remote(rd[a].at[y, 1 - x, zz], r2[a].at[n_], s_2.at[a, n_], r_2.at[a, n_], nx))

    def to_inner(a, n_):
        ref = xd.at[far[n_]] if a == 4 else rd[a].at[y, x, far[n_]]
        land = x3 if a == 4 else r3[a]
        return remote(ref, land.at[n_], s_3.at[a, n_], r_3.at[a, n_], me(zp))

    def to_far(a, n_):
        ref = xd.at[far[n_]] if a == 4 else rd[a].at[y, x, far[n_]]
        return remote(ref, x4 if a == 4 else r4[a], s_4.at[a, n_], r_4.at[a], me(far[n_]))

    def third(n_):
        zz = order[n_]
        for a in range(4):
            got(r2[a].at[n_], s_2.at[a, n_], r_2.at[a, n_], ny if by_x[a] else nx)
            add_rows(rd[a].at[y, x, zz], r2[a].at[n_])
            if n_ < 2:
                @pl.when(jnp.logical_not(inner))
                def _(a=a):
                    to_inner(a, n_).start()
            elif n_ == 2:
                go_(remote(rd[a].at[y, x, zz], r5[a], s_5.at[a], r_5.at[a], me(zz)))

    def fourth(n_, arrs):
        @pl.when(inner)
        def _():
            for a in arrs:
                to_inner(a, n_).wait_recv()
                if a == 4:
                    add_tok(xd.at[far[n_]], x3.at[n_])
                else:
                    add_rows(rd[a].at[y, x, far[n_]], r3[a].at[n_])
                to_far(a, n_).start()

    for cp in local:
        cp.wait()
    first(0)
    first(1)
    attend(NEAR[0])
    attend(NEAR[1])
    second(0)
    first(2)
    attend(NEAR[2])
    attend(NEAR[3])
    second(1)
    first(3)
    attend(NEAR[4])
    third(0)
    attend(NEAR[5])
    second(2)
    attend(NEAR[6])
    third(1)
    fourth(0, range(4))
    attend(NEAR[7])
    second(3)
    for g in range(NH):
        rows = slice(g * 64, (g + 1) * 64)
        flip = dkv[g].T
        pr[1, rows] = (flip[64:] * 0.125).astype(BF)
        pr[2, rows] = flip[:64].astype(BF)

    def token_grad(tb):
        cols = pl.ds(pl.multiple_of(tb * span, span), span)
        acc = None
        for s in range(3):
            term = jnp.dot(pr[s, :, cols].astype(F32).T.astype(BF), wt[s, c], preferred_element_type=F32)
            acc = term if acc is None else acc + term
        dxp[tb] = acc.astype(BF)

    def token_pair(j, _):
        token_grad(j * 2 + 1 - c)
        return 0

    lax.fori_loop(0, 4, token_pair, 0)
    for n_, zz in enumerate(order):
        go_(remote(dxp.at[zz * 2 + 1 - c], xd.at[zz], s_d.at[0, n_], r_d.at[0, n_], core))
    third(2)
    fourth(1, range(4))

    def token_mine(j, _):
        token_grad(j * 2 + c)
        return 0

    lax.fori_loop(0, 4, token_mine, 0)
    for n_, zz in enumerate(order):
        got(xd.at[zz], s_d.at[0, n_], r_d.at[0, n_], core)
        add_tok(xd.at[zz], dxp.at[zz * 2 + c])
        if n_ < 2:
            @pl.when(jnp.logical_not(inner))
            def _(n_=n_):
                to_inner(4, n_).start()
        elif n_ == 2:
            go_(remote(xd.at[zz], x5, s_5.at[4], r_5.at[4], me(zz)))
    per = pr.shape[1]
    width = wt.shape[3]
    xall = xv[...].reshape(n, width)
    for s in range(3):
        dw[s * per:(s + 1) * per] = jnp.dot(pr[s], xall, preferred_element_type=F32)
    for q in range(2):
        w = dw[:, q * (width // 2):(q + 1) * (width // 2)].T
        lq[q] = w.reshape(lq.shape[1:]).astype(BF)
    lv[...] = jnp.zeros_like(lv)
    for row, s in ((0, 0), (1, 2)):
        col = jnp.sum(pr[s].astype(F32), axis=1, keepdims=True)
        for r in range(8):
            piece = jnp.broadcast_to(col[24 * r:24 * r + 24], (24, 128)).T
            lv[group // 2, group % 2, r // 2, r % 2, row:row + 1, :24] = piece[0:1]
    lq_x = lq
    go_(remote(lq_x.at[:, 1 - x], q1, s_q1.at[0], r_q1.at[0], nx))
    go_(remote(lv.at[:, 1 - x], v1, s_q1.at[1], r_q1.at[1], nx))
    third(3)
    fourth(0, (4,))
    fourth(1, (4,))
    got(q1, s_q1.at[0], r_q1.at[0], nx)
    got(v1, s_q1.at[1], r_q1.at[1], nx)
    for yy in range(2):
        for zc in range(8):
            at = (zc // 2, zc % 2)
            q0[(yy,) + at] = q1[(yy,) + at] + lq[(yy, x) + at]
            v0[(yy,) + at] = v1[(yy,) + at] + lv[(yy, x) + at]
    go_(remote(q0.at[1 - y], q2, s_q2.at[0], r_q2.at[0], ny))
    go_(remote(v0.at[1 - y], v2, s_q2.at[1], r_q2.at[1], ny))
    src_in = 2 - h
    for a in range(4):
        got(r5[a], s_5.at[a], r_5.at[a], me(zp))
        got(r4[a], s_4.at[a, 0], r_4.at[a], me(src_in))
        acc = rd[a].at[y, x, z]
        for i in range(acc.shape[0]):
            outs[a][i] = acc[i].astype(F32) + r5[a][i].astype(F32) + r4[a][i].astype(F32)
    got(q2, s_q2.at[0], r_q2.at[0], ny)
    got(v2, s_q2.at[1], r_q2.at[1], ny)
    for zc in range(8):
        at = (zc // 2, zc % 2)
        q0[(y,) + at] = q0[(y,) + at] + q2[at]
        v0[(y,) + at] = v0[(y,) + at] + v2[at]
    for k in range(1, 8):
        to = line[k - 1]
        go_(remote(q0.at[y, to // 2, to % 2], qr.at[t], s_qe.at[0, k - 1], r_qe.at[0, k - 1], (d, to)))
        go_(remote(v0.at[y, to // 2, to % 2], vr.at[t], s_qe.at[1, k - 1], r_qe.at[1, k - 1], (d, to)))
    qr[t] = q0[y, z, c]
    vr[t] = v0[y, z, c]
    got(x5, s_5.at[4], r_5.at[4], me(zp))
    got(x4, s_4.at[4, 0], r_4.at[4], me(src_in))

    def tok(i, _):
        at = pl.ds(pl.multiple_of(i * 32, 32), 32)
        ox[h, at, :] = d_one[h, at, :] + (xd[z, at, :].astype(F32) + x5[at, :].astype(F32))
        ox[1 - h, at, :] = d_one[1 - h, at, :] + x4[at, :].astype(F32)
        return 0

    lax.fori_loop(0, span // 32, tok, 0)
    for k in range(1, 8):
        src = (t + 8 - k) % 8
        got(qr.at[src], s_qe.at[0, k - 1], r_qe.at[0, k - 1], (d, src))
        got(vr.at[src], s_qe.at[1, k - 1], r_qe.at[1, k - 1], (d, src))
    for g in range(4):
        oq[g] = qr[g].astype(F32) + qr[4 + g].astype(F32)
    total = vr[0]
    for k in range(1, 8):
        total = total + vr[k]
    ov[...] = total
    for cp in sends:
        cp.wait_send()
    for n_ in range(2):
        @pl.when(jnp.logical_not(inner))
        def _(n_=n_):
            for a in range(5):
                to_inner(a, n_).wait_send()

        @pl.when(inner)
        def _(n_=n_):
            for a in range(5):
                to_far(a, n_).wait_send()


NEAR = (0, 1, 7, 2, 6, 3, 5, 4)


def back(dat, di, do_, db, ds_, qkv, ids, o32, lse, wt, xs, d_one):
    arrs = [di, do_, db, ds_]
    tails = [a.shape[4:] for a in arrs]
    per, width = wt.shape[2:]
    n = qkv.shape[2]
    tok = xs.shape[1:]
    qt = di.shape[4:6] + (3 * per,)
    vt = (8, 128)
    scratch = []
    for lead in ((2, 2, 4), (2, 2, 4), (4, 2), (4,), (2,), (), ()):
        for a, tail in zip(arrs, tails):
            scratch.append(pltpu.VMEM(lead + tail, a.dtype))
    grid = (2, 2, 4, 2)
    scratch += [
        pltpu.VMEM(dat.shape, BF),
        pltpu.VMEM((NH, n, 80), BF), pltpu.VMEM((NH, 80, n), BF), pltpu.VMEM((NH, n, 64), BF),
        pltpu.VMEM((NH, n, 128), F32), pltpu.VMEM((3, per, n), BF),
        pltpu.VMEM(xs.shape, BF), pltpu.VMEM(xs.shape, BF), pltpu.VMEM((3 * per, width), F32),
        pltpu.VMEM(grid + qt, BF), pltpu.VMEM(grid + vt, F32),
        pltpu.VMEM((4,) + tok, BF), pltpu.VMEM((2,) + tok, BF), pltpu.VMEM(tok, BF), pltpu.VMEM(tok, BF),
        pltpu.VMEM((2, 4, 2) + qt, BF), pltpu.VMEM((2, 4, 2) + qt, BF), pltpu.VMEM((4, 2) + qt, BF),
        pltpu.VMEM((8,) + qt, BF),
        pltpu.VMEM((2, 4, 2) + vt, F32), pltpu.VMEM((2, 4, 2) + vt, F32), pltpu.VMEM((4, 2) + vt, F32),
        pltpu.VMEM((8,) + vt, F32),
        dma(10), dma(7), dma(7), dma(9, 4), dma(9, 4), dma(4, 4), dma(4, 4), dma(4, 4), dma(4, 4),
        dma(5, 2), dma(5, 2), dma(5, 2), dma(5), dma(5), dma(5),
        dma(2), dma(2), dma(2), dma(2), dma(2, 7), dma(2, 7),
    ]
    return pl.pallas_call(
        back_kernel,
        out_shape=[jax.ShapeDtypeStruct((2,) + tok, F32)]
        + [jax.ShapeDtypeStruct(tail, F32) for tail in tails]
        + [jax.ShapeDtypeStruct((4,) + qt, F32), jax.ShapeDtypeStruct(vt, F32)],
        in_specs=[any_spec()] * 5 + [vmem_spec()] * 5 + [any_spec(), vmem_spec()],
        out_specs=[vmem_spec()] * 7,
        scratch_shapes=scratch,
        compiler_params=pltpu.CompilerParams(
            collective_id=4, has_side_effects=True, vmem_limit_bytes=VMEM_LIMIT),
        name="back",
    )(dat, di, do_, db, ds_, qkv, ids, o32, lse, wt, xs, d_one)


def erf_parts(u):
    phi_c = 0.5 * (1.0 + lax.erf(u * 0.7071067811865476))
    return phi_c, phi_c + u * jnp.exp(-0.5 * u * u) * 0.3989422804014327


def norm_forward(r):
    center = r - jnp.mean(r, axis=-1, keepdims=True)
    inv = lax.rsqrt(jnp.mean(center * center, axis=-1, keepdims=True) + layer_eps)
    return center * inv, inv


def norm_backward(n, inv, gain, dy):
    gd = gain * dy
    return (gd - jnp.mean(gd, axis=-1, keepdims=True) - n * jnp.mean(gd * n, axis=-1, keepdims=True)) * inv


def mid_kernel(x, att, wo, wi, wb, fv, bi, cot,
               out, d_one, dat, g_in, g_out, g_back, g_small,
               vo, vi, vb, att_t, acc, n1, inv1, low, low_t, slope, act, act_t, d_pre, d_two, d_br, d_attn,
               yi, yo, yb, yx, yd, ys, part, sums, sum_in, sem_w, sem_o):
    tokens, width = x.shape
    span = tokens // 2
    ff = vi.shape[1]
    loads = [pltpu.make_async_copy(a, b, sem_w.at[k]) for k, (a, b) in enumerate(((wo, vo), (wi, vi), (wb, vb)))]
    for cp in loads:
        cp.start()
    outs = []

    def put(src, to):
        cp = pltpu.make_async_copy(src, to, sem_o.at[len(outs)])
        cp.start()
        outs.append(cp)

    def loop(count, size, fn):
        def one(j, _):
            fn(pl.ds(pl.multiple_of(j * size, size), size))
            return 0

        lax.fori_loop(0, count, one, 0)

    halves = (slice(0, span), slice(span, tokens))
    rb = tokens // 4
    nt = (((1,), (1,)), ((), ()))
    part[...] = jnp.zeros_like(part)

    def count_in(k, v):
        part[k] += jnp.sum(v.reshape(v.shape[0] // 8, 8, width), axis=0)

    for s in range(2):
        att_t[halves[s]] = att[s].astype(F32).T.astype(BF)
    loads[0].wait()
    for s in range(2):
        acc[halves[s]] = jnp.dot(att_t[halves[s]], vo[...], preferred_element_type=F32)

    def norm_one(r):
        n, inv = norm_forward(x[r].astype(F32) + acc[r] + fv[2:3])
        n1[r] = n
        inv1[r] = inv
        low[r] = (n * fv[3:4] + fv[4:5]).astype(BF)

    loop(4, rb, norm_one)
    loads[1].wait()

    def widen(f):
        pre = [jnp.dot(low[r], vi[:, f], preferred_element_type=F32) + bi[:, f] for r in halves]
        for r, u in zip(halves, pre):
            phi_c, sl = erf_parts(u)
            slope[r, f] = sl
            a = u * phi_c
            act[r, f] = a.astype(BF)
            act_t[f, r] = a.T.astype(BF)

    loop(ff // 256, 256, widen)
    loads[2].wait()

    def narrow(f):
        for r in halves:
            acc[r, f] = jnp.dot(act[r], vb[:, f], preferred_element_type=F32)

    loop(width // 256, 256, narrow)

    def norm_two(r):
        normed = n1[r] * fv[3:4] + fv[4:5]
        n2, inv2 = norm_forward(normed + acc[r] + fv[5:6])
        yx[r] = (n2 * fv[6:7] + fv[7:8]).astype(BF)
        dy = cot[r].astype(F32)
        d2 = norm_backward(n2, inv2, fv[6:7], dy)
        d_two[r] = d2
        d2 = d2.astype(BF)
        d_br[r] = d2
        count_in(3, d2.astype(F32))
        count_in(4, dy * n2)
        count_in(5, dy)

    loop(4, rb, norm_two)
    put(yx, out)

    def back_widen(f):
        da = [lax.dot_general(d_br[r], vb[f, :], nt, preferred_element_type=F32) for r in halves]
        total = None
        for r, v in zip(halves, da):
            dp = (v * slope[r, f]).astype(BF)
            d_pre[r, f] = dp
            col = jnp.sum(dp.astype(F32), axis=0, keepdims=True)
            total = col if total is None else total + col
        sum_in[:, f] = total

    loop(ff // 256, 256, back_widen)

    def back_narrow(k):
        for r in halves:
            acc[r, k] = lax.dot_general(d_pre[r], vi[k, :], nt, preferred_element_type=F32)

    loop(width // 256, 256, back_narrow)

    def back_one(r):
        dn = d_two[r] + acc[r]
        n = n1[r]
        d1 = norm_backward(n, inv1[r], fv[3:4], dn)
        d_one[r] = d1
        d1 = d1.astype(BF)
        d_attn[r] = d1
        count_in(0, d1.astype(F32))
        count_in(1, dn * n)
        count_in(2, dn)

    loop(4, rb, back_one)
    for s in range(2):
        yd[s] = lax.dot_general(vo[...], d_attn[halves[s]], nt, preferred_element_type=F32).astype(BF)
    put(yd, dat)

    def grad_back(f):
        yb[f, :] = jnp.dot(act_t[f, :], d_br[...], preferred_element_type=F32).astype(BF)

    loop(ff // 256, 256, grad_back)
    put(yb, g_back)
    for k in range(3):
        low_t[k * 256:(k + 1) * 256] = low[:, k * 256:(k + 1) * 256].astype(F32).T.astype(BF)
    for k in range(3):
        rows = slice(k * 256, (k + 1) * 256)

        def grad_in(f, rows=rows):
            yi[rows, f] = jnp.dot(low_t[rows], d_pre[:, f], preferred_element_type=F32).astype(BF)

        loop(ff // 768, 768, grad_in)
        put(yi.at[rows], g_in.at[rows])

    def grad_out(k):
        yo[k] = (jnp.dot(att[0, k], d_attn[halves[0]], preferred_element_type=F32)
                 + jnp.dot(att[1, k], d_attn[halves[1]], preferred_element_type=F32)).astype(BF)

    loop(3, 256, grad_out)
    put(yo, g_out)
    ys[...] = jnp.zeros_like(ys)
    for k in range(6):
        sums[k:k + 1] = jnp.sum(part[k], axis=0, keepdims=True)
    for r in range(32):
        at = (r // 16, (r // 8) % 2, (r // 2) % 4, r % 2)
        ys[at + (slice(0, 6), slice(0, 24))] = sums[0:6, 24 * r:24 * r + 24]
        ys[at + (slice(6, 7), slice(0, 96))] = sum_in[:, 96 * r:96 * r + 96]
    put(ys, g_small)
    for cp in outs:
        cp.wait()


def mid(x, att, wo, wi, wb, fv, bi, cot):
    tokens, width = x.shape
    ff = wi.shape[1]
    tok = lambda dt: pltpu.VMEM((tokens, width), dt)
    wide = lambda dt: pltpu.VMEM((tokens, ff), dt)
    owner = (2, 2, 4, 2, 8, 128)
    shape = jax.ShapeDtypeStruct
    return pl.pallas_call(
        mid_kernel,
        out_shape=[
            shape((tokens, width), BF), shape((tokens, width), F32), shape(att.shape, BF), shape(wi.shape, BF),
            shape(wo.shape, BF), shape(wb.shape, BF), shape(owner, F32),
        ],
        in_specs=[vmem_spec()] * 2 + [any_spec()] * 3 + [vmem_spec()] * 3,
        out_specs=[any_spec(), vmem_spec()] + [any_spec()] * 5,
        scratch_shapes=[
            pltpu.VMEM(wo.shape, BF), pltpu.VMEM(wi.shape, BF), pltpu.VMEM(wb.shape, BF),
            tok(BF), tok(F32), tok(F32), pltpu.VMEM((tokens, 1), F32), tok(BF), pltpu.VMEM((width, tokens), BF),
            wide(F32), wide(BF), pltpu.VMEM((ff, tokens), BF), wide(BF), tok(F32), tok(BF), tok(BF),
            pltpu.VMEM(wi.shape, BF), pltpu.VMEM(wo.shape, BF), pltpu.VMEM(wb.shape, BF),
            tok(BF), pltpu.VMEM(att.shape, BF), pltpu.VMEM(owner, F32),
            pltpu.VMEM((6, 8, width), F32), pltpu.VMEM((8, width), F32), pltpu.VMEM((1, ff), F32),
            dma(3), dma(8),
        ],
        compiler_params=pltpu.CompilerParams(vmem_limit_bytes=VMEM_LIMIT),
        name="mid",
    )(x, att, wo, wi, wb, fv, bi, cot)


def on_device_fast(
    inputs, segments, w_qkv, b_query, b_value, w_out, b_attn, gain_one, shift_one,
    w_in, b_in, w_back, b_back, gain_two, shift_two, cotangent,
):
    nseq, span, width = inputs.shape
    tokens = nseq * span
    ff = w_in.shape[1]
    depth = w_in.shape[0]
    d, t, z, c, _, _ = place()
    per = width // 4
    vecs = (b_query, b_value, b_attn, gain_one, shift_one, b_back, gain_two, shift_two)
    ffd = b_in.shape[0]
    nv = len(vecs)
    small = jnp.pad(jnp.stack(vecs).astype(F32), ((0, 8), (0, 128 - depth)))
    small = lax.dynamic_update_slice(small, b_in.astype(F32)[None], (nv, 0))
    idb = jnp.broadcast_to(segments.astype(F32)[:, None], (nseq, 8, span))
    xs, ids, gi, go, gb, fv, bi, att, qkv, o32, lse, wt = front(
        inputs, idb, w_in.reshape(depth // 8, 8, ff), w_out.reshape(depth // 8, 8, width),
        w_back.reshape(ffd // 8, 8, width), small, w_qkv.reshape(depth // 8, 8, 3 * width))
    output, d_one, d_att, grad_w_in, grad_w_out, grad_w_back, g_small = mid(
        inputs.reshape(tokens, width), att.reshape(nseq, width, span), go.reshape(width, width),
        gi.reshape(width, ff), gb.reshape(ff, width), fv, bi, cotangent.reshape(tokens, width))
    output = output.reshape(nseq, span, width)
    owner = (2, 2, 4, 2)
    input_grad, oi, oo, ob, os_, oq, ov = back(
        d_att.reshape(8, per, span),
        grad_w_in.reshape(owner + (depth // 8, 8, ff)),
        grad_w_out.reshape(owner + (depth // 8, 8, width)),
        grad_w_back.reshape(owner + (ffd // 8, 8, width)),
        g_small, qkv, ids, o32, lse, wt, xs, d_one.reshape(nseq, span, width),
    )
    g_qkv = oq.reshape(4, depth, 3, per).transpose(1, 2, 0, 3).reshape(depth, 3 * width)
    vec = lambda k: os_[k, :depth]
    return (
        output, input_grad, g_qkv, ov[0, :depth], ov[1, :depth], oo.reshape(depth, width), vec(0), vec(1), vec(2),
        oi.reshape(depth, ff), os_[6, :ffd], ob.reshape(ffd, width),
        vec(3), vec(4), vec(5),
    )


negative_fill = -1e30


def layer_norm(resid, gain, shift):
    center = resid - jnp.mean(resid, axis=-1, keepdims=True)
    spread = jnp.mean(center * center, axis=-1, keepdims=True)
    return center * lax.rsqrt(spread + layer_eps) * gain + shift


def gelu_exact(values):
    return jax.nn.gelu(values, approximate=False)


def attend_forward(entries):
    query_rows, key_rows, value_rows, query_ids, key_ids = entries
    scores = jnp.einsum(
        "qhd,khd->hqk", query_rows, key_rows, preferred_element_type=jnp.float32
    ) * HEAD_DIM ** (-0.5)
    allowed = (query_ids[:, None] == key_ids[None, :])[None]
    scores = jnp.where(allowed, scores, negative_fill)
    peak = jnp.max(scores, axis=-1, keepdims=True)
    raised = jnp.exp(scores - peak)
    total = jnp.sum(raised, axis=-1, keepdims=True)
    probs_low = (raised / total).astype(jnp.bfloat16)
    context = jnp.einsum("hqk,khd->qhd", probs_low, value_rows, preferred_element_type=jnp.float32)
    return (context, (peak + jnp.log(total))[..., 0])


def score_terms(query_rows, key_rows, value_rows, grad_context, log_total, query_ids, key_ids):
    scale = HEAD_DIM ** (-0.5)
    scores = (
        jnp.einsum("qhd,khd->hqk", query_rows, key_rows, preferred_element_type=jnp.float32) * scale
    )
    allowed = (query_ids[:, None] == key_ids[None, :])[None]
    probs = jnp.where(allowed, jnp.exp(scores - log_total[..., None]), 0.0)
    d_probs = jnp.einsum(
        "qhd,khd->hqk", grad_context, value_rows, preferred_element_type=jnp.float32
    )
    return (probs, d_probs)


def attend_backward(entries):
    query_rows, key_rows, value_rows, grad_context, log_total, query_ids, key_ids = entries
    scale = HEAD_DIM ** (-0.5)
    probs, d_probs = score_terms(
        query_rows, key_rows, value_rows, grad_context, log_total, query_ids, key_ids
    )
    inner = jnp.sum(probs * d_probs, axis=-1, keepdims=True)
    d_scores = (probs * (d_probs - inner)).astype(jnp.bfloat16)
    d_queries = (
        jnp.einsum("hqk,khd->qhd", d_scores, key_rows, preferred_element_type=jnp.float32) * scale
    )
    d_keys = (
        jnp.einsum("hqk,qhd->khd", d_scores, query_rows, preferred_element_type=jnp.float32) * scale
    )
    d_values = jnp.einsum(
        "hqk,qhd->khd", probs.astype(jnp.bfloat16), grad_context, preferred_element_type=jnp.float32
    )
    length = key_rows.shape[0]
    return (
        d_queries,
        d_keys.reshape(length, HEADS * HEAD_DIM),
        d_values.reshape(length, HEADS * HEAD_DIM),
    )


def on_device_general(
    inputs,
    segments,
    w_qkv,
    b_query,
    b_value,
    w_out,
    b_attn,
    gain_one,
    shift_one,
    w_in,
    b_in,
    w_back,
    b_back,
    gain_two,
    shift_two,
    cotangent,
):
    seq_count, group_len, model_width = inputs.shape
    tok_count = seq_count * group_len
    gathered = (
        lax.all_gather(w_qkv, ("dp", "ctx"), axis=0, tiled=True),
        lax.all_gather(b_query, ("dp", "ctx"), axis=0, tiled=True),
        lax.all_gather(b_value, ("dp", "ctx"), axis=0, tiled=True),
        lax.all_gather(w_out, ("dp", "ctx"), axis=0, tiled=True),
        lax.all_gather(b_attn, ("dp", "ctx"), axis=0, tiled=True),
        lax.all_gather(gain_one, ("dp", "ctx"), axis=0, tiled=True),
        lax.all_gather(shift_one, ("dp", "ctx"), axis=0, tiled=True),
        lax.all_gather(w_in, ("dp", "ctx"), axis=0, tiled=True),
        lax.all_gather(b_in, ("dp", "ctx"), axis=0, tiled=True),
        lax.all_gather(w_back, ("dp", "ctx"), axis=0, tiled=True),
        lax.all_gather(b_back, ("dp", "ctx"), axis=0, tiled=True),
        lax.all_gather(gain_two, ("dp", "ctx"), axis=0, tiled=True),
        lax.all_gather(shift_two, ("dp", "ctx"), axis=0, tiled=True),
    )
    (
        wide_qkv,
        full_b_query,
        full_b_value,
        wide_out,
        full_b_attn,
        full_gain_one,
        full_shift_one,
        wide_in,
        full_b_in,
        wide_back,
        full_b_back,
        full_gain_two,
        full_shift_two,
    ) = gathered
    tokens = inputs.reshape(tok_count, model_width)
    projected = jnp.dot(tokens, wide_qkv, preferred_element_type=jnp.float32)
    query_low = (projected[:, :model_width] + full_b_query.astype(jnp.float32)).astype(jnp.bfloat16)
    key_low = projected[:, model_width : 2 * model_width].astype(jnp.bfloat16)
    value_low = (projected[:, 2 * model_width :] + full_b_value.astype(jnp.float32)).astype(
        jnp.bfloat16
    )
    key_ids = lax.all_gather(segments, "ctx", axis=1, tiled=True)
    key_local = key_low.reshape(seq_count, group_len, model_width)
    value_local = value_low.reshape(seq_count, group_len, model_width)
    key_whole, value_whole = (
        lax.all_gather(key_local, "ctx", axis=1, tiled=True),
        lax.all_gather(value_local, "ctx", axis=1, tiled=True),
    )
    seq_len = key_whole.shape[1]
    query_heads = query_low.reshape(seq_count, group_len, HEADS, HEAD_DIM)
    context, log_total = lax.map(
        attend_forward,
        (
            query_heads,
            key_whole.reshape(seq_count, seq_len, HEADS, HEAD_DIM),
            value_whole.reshape(seq_count, seq_len, HEADS, HEAD_DIM),
            segments,
            key_ids,
        ),
    )
    attended = context.reshape(tok_count, model_width).astype(jnp.bfloat16)
    attn_out = jnp.dot(attended, wide_out, preferred_element_type=jnp.float32) + full_b_attn.astype(
        jnp.float32
    )
    resid_one = tokens.astype(jnp.float32) + attn_out
    normed, norm_one_back = jax.vjp(
        layer_norm, resid_one, full_gain_one.astype(jnp.float32), full_shift_one.astype(jnp.float32)
    )
    normed_low = normed.astype(jnp.bfloat16)
    pre_act = jnp.dot(normed_low, wide_in, preferred_element_type=jnp.float32) + full_b_in.astype(
        jnp.float32
    )
    activ_f, gelu_back = jax.vjp(gelu_exact, pre_act)
    activ = activ_f.astype(jnp.bfloat16)
    branch = jnp.dot(activ, wide_back, preferred_element_type=jnp.float32) + full_b_back.astype(
        jnp.float32
    )
    resid_two = normed + branch
    final_norm, norm_two_back = jax.vjp(
        layer_norm, resid_two, full_gain_two.astype(jnp.float32), full_shift_two.astype(jnp.float32)
    )
    output = final_norm.astype(jnp.bfloat16).reshape(seq_count, group_len, model_width)
    back_qkv, back_out, back_in, back_back = (
        lax.all_gather(w_qkv, ("dp", "ctx"), axis=0, tiled=True),
        lax.all_gather(w_out, ("dp", "ctx"), axis=0, tiled=True),
        lax.all_gather(w_in, ("dp", "ctx"), axis=0, tiled=True),
        lax.all_gather(w_back, ("dp", "ctx"), axis=0, tiled=True),
    )
    d_final = cotangent.reshape(tok_count, model_width).astype(jnp.float32)
    d_two, grad_gain_two, grad_shift_two = norm_two_back(d_final)
    d_branch = d_two.astype(jnp.bfloat16)
    grad_b_back = jnp.sum(d_branch.astype(jnp.float32), axis=0)
    grad_w_back = jnp.einsum("tf,td->fd", activ, d_branch, preferred_element_type=jnp.float32)
    d_activ = jnp.einsum("td,fd->tf", d_branch, back_back, preferred_element_type=jnp.float32)
    d_pre = gelu_back(d_activ)[0].astype(jnp.bfloat16)
    grad_b_in = jnp.sum(d_pre.astype(jnp.float32), axis=0)
    grad_w_in = jnp.einsum("td,tf->df", normed_low, d_pre, preferred_element_type=jnp.float32)
    d_normed = d_two + jnp.einsum("tf,df->td", d_pre, back_in, preferred_element_type=jnp.float32)
    d_one, grad_gain_one, grad_shift_one = norm_one_back(d_normed)
    d_attn = d_one.astype(jnp.bfloat16)
    grad_b_attn = jnp.sum(d_attn.astype(jnp.float32), axis=0)
    grad_w_out = jnp.einsum("ti,td->id", attended, d_attn, preferred_element_type=jnp.float32)
    d_attended = jnp.einsum(
        "td,id->ti", d_attn, back_out, preferred_element_type=jnp.float32
    ).astype(jnp.bfloat16)
    key_back, value_back = (
        lax.all_gather(key_local, "ctx", axis=1, tiled=True),
        lax.all_gather(value_local, "ctx", axis=1, tiled=True),
    )
    grad_heads = d_attended.reshape(seq_count, group_len, HEADS, HEAD_DIM)
    d_query_part, d_key_part, d_value_part = lax.map(
        attend_backward,
        (
            query_heads,
            key_back.reshape(seq_count, seq_len, HEADS, HEAD_DIM),
            value_back.reshape(seq_count, seq_len, HEADS, HEAD_DIM),
            grad_heads,
            log_total,
            segments,
            key_ids,
        ),
    )
    d_key_sum, d_value_sum = (
        lax.psum_scatter(
            d_key_part.astype(jnp.bfloat16), "ctx", scatter_dimension=1, tiled=True
        ).astype(jnp.float32),
        lax.psum_scatter(
            d_value_part.astype(jnp.bfloat16), "ctx", scatter_dimension=1, tiled=True
        ).astype(jnp.float32),
    )
    d_queries = d_query_part.reshape(tok_count, model_width).astype(jnp.bfloat16)
    d_keys = d_key_sum.reshape(tok_count, model_width).astype(jnp.bfloat16)
    d_values = d_value_sum.reshape(tok_count, model_width).astype(jnp.bfloat16)
    d_proj = jnp.concatenate([d_queries, d_keys, d_values], axis=1)
    grad_w_qkv = jnp.einsum("td,te->de", tokens, d_proj, preferred_element_type=jnp.float32)
    grad_b_query = jnp.sum(d_queries.astype(jnp.float32), axis=0)
    grad_b_value = jnp.sum(d_values.astype(jnp.float32), axis=0)
    input_grad = d_one + jnp.einsum(
        "te,de->td", d_proj, back_qkv, preferred_element_type=jnp.float32
    )
    summed = (
        lax.psum_scatter(grad_w_qkv, ("dp", "ctx"), scatter_dimension=0, tiled=True),
        lax.psum_scatter(grad_b_query, ("dp", "ctx"), scatter_dimension=0, tiled=True),
        lax.psum_scatter(grad_b_value, ("dp", "ctx"), scatter_dimension=0, tiled=True),
        lax.psum_scatter(grad_w_out, ("dp", "ctx"), scatter_dimension=0, tiled=True),
        lax.psum_scatter(grad_b_attn, ("dp", "ctx"), scatter_dimension=0, tiled=True),
        lax.psum_scatter(grad_gain_one, ("dp", "ctx"), scatter_dimension=0, tiled=True),
        lax.psum_scatter(grad_shift_one, ("dp", "ctx"), scatter_dimension=0, tiled=True),
        lax.psum_scatter(grad_w_in, ("dp", "ctx"), scatter_dimension=0, tiled=True),
        lax.psum_scatter(grad_b_in, ("dp", "ctx"), scatter_dimension=0, tiled=True),
        lax.psum_scatter(grad_w_back, ("dp", "ctx"), scatter_dimension=0, tiled=True),
        lax.psum_scatter(grad_b_back, ("dp", "ctx"), scatter_dimension=0, tiled=True),
        lax.psum_scatter(grad_gain_two, ("dp", "ctx"), scatter_dimension=0, tiled=True),
        lax.psum_scatter(grad_shift_two, ("dp", "ctx"), scatter_dimension=0, tiled=True),
    )
    return (
        output,
        input_grad.reshape(seq_count, group_len, model_width),
        summed[0],
        summed[1],
        summed[2],
        summed[3],
        summed[4],
        summed[5],
        summed[6],
        summed[7],
        summed[8],
        summed[9],
        summed[10],
        summed[11],
        summed[12],
    )


def solution(mesh):
    placed = (
        P("dp", "ctx", None),
        P("dp", "ctx"),
        P(("dp", "ctx"), None),
        P(("dp", "ctx")),
        P(("dp", "ctx")),
        P(("dp", "ctx"), None),
        P(("dp", "ctx")),
        P(("dp", "ctx")),
        P(("dp", "ctx")),
        P(("dp", "ctx"), None),
        P(("dp", "ctx")),
        P(("dp", "ctx"), None),
        P(("dp", "ctx")),
        P(("dp", "ctx")),
        P(("dp", "ctx")),
        P("dp", "ctx", None),
    )
    fits = mesh.shape["dp"] == 4 and mesh.shape["ctx"] == 8
    return jax.shard_map(
        on_device_fast if fits else on_device_general,
        mesh=mesh,
        in_specs=placed,
        out_specs=(
            P("dp", "ctx", None),
            P("dp", "ctx", None),
            P(("dp", "ctx"), None),
            P(("dp", "ctx")),
            P(("dp", "ctx")),
            P(("dp", "ctx"), None),
            P(("dp", "ctx")),
            P(("dp", "ctx")),
            P(("dp", "ctx")),
            P(("dp", "ctx"), None),
            P(("dp", "ctx")),
            P(("dp", "ctx"), None),
            P(("dp", "ctx")),
            P(("dp", "ctx")),
            P(("dp", "ctx")),
        ),
        check_vma=False,
    )
```

```python
import functools
import jax
import jax.numpy as jnp
from jax import lax
from jax.experimental import pallas as pl
from jax.experimental.pallas import tpu as pltpu
from jax.sharding import PartitionSpec as P

HEADS = 12
HEAD_DIM = 64
layer_eps = 1e-12
MESH_ID = pl.DeviceIdType.MESH
BF = jnp.bfloat16
F32 = jnp.float32
VMEM_LIMIT = 64 * 1024 * 1024 - 65536
SCORE_SCALE = 0.125 * 1.4426950408889634
EXCLUDE = -1e30


def place():
    d = lax.axis_index("dp")
    t = lax.axis_index("ctx")
    z = t // 2
    c = t % 2
    dx = d + 1 - 2 * (d % 2)
    dy = (d + 2) % 4
    return d, t, z, c, dx, dy


def remote(src, dst, ss, rs, dev):
    return pltpu.make_async_remote_copy(
        src_ref=src, dst_ref=dst, send_sem=ss, recv_sem=rs, device_id=dev, device_id_type=MESH_ID
    )


def greet(devices):
    bar = pltpu.get_barrier_semaphore()
    for dev in devices:
        pl.semaphore_signal(bar, inc=1, device_id=dev, device_id_type=MESH_ID)
    pl.semaphore_wait(bar, len(devices))


QB = 256
KB = 256
NH = 3


def marks_of(ids_row):
    kinds = lax.broadcasted_iota(jnp.int32, (16, ids_row.shape[1]), 0).astype(F32)
    return kinds == ids_row


N_ARR = 7
WIDE = (0, 1, 2)
EARLY = (3, 4, 5, 6)
FIRST_X = (0, 1, 3)
FIRST_Y = (2, 4, 5, 6)


def window(i):
    return (i // 4) * (i % 4), 8 - (1 - i // 4) * (3 - i % 4)


def front_kernel(x, seg, wi, wo, wb, vs, bv, wq,
                 xs, ids, gi, go, gb, fv, bi, att, qkv, o32, lse, wt,
                 idb, sm, gs, gq, ka, va, qa, sb,
                 loc, s_x, r_x, s_xf, s_xd, r_xd, s_z, r_z, s_up, s_dn, s_px, r_px, s_py, r_py, s_f, r_f,
                 s_c, r_c, s_e, r_e):
    d, t, z, c, dx, dy = place()
    h = z // 2
    zp = z + 1 - 2 * (z % 2)
    inner = (z + h) % 2 == 1
    dxy = (dx + 2) % 4
    z1, z2 = 2 - h, 3 * (1 - h)
    others = [zp, z1, z2]
    far = [z1, z2]
    me = lambda zz: (d, zz * 2 + c)
    core = (d, z * 2 + 1 - c)
    nx, ny = (dx, t), (dy, t)
    for hh in range(2):
        idb[hh] = jnp.broadcast_to(seg[hh:hh + 1].astype(F32), idb.shape[1:])
    sm[...] = jnp.zeros_like(sm)
    sm[0:8, 0:24] = vs[...].astype(F32)
    sm[8:9, 0:96] = bv[...].astype(F32)
    greet([(d, (t + k) % 8) for k in range(1, 8)] + [nx, ny])
    sends = []

    def go_(cp):
        cp.start()
        sends.append(cp)

    def got(ref, ss, rs, dev):
        remote(ref, ref, ss, rs, dev).wait_recv()

    per = wq.shape[2] // 6
    dst = [gi, go, gb, gs, gq.at[0], gq.at[1], gq.at[2]]

    def mine(a, zz):
        if a < 4:
            return (wi, wo, wb, sm)[a]
        return wq.at[:, :, pl.ds(pl.multiple_of((a - 4) * 2 * per + (zz % 2) * per, per), per)]

    half = x.shape[1] // 2

    def piece(k, hh, tt):
        if k == 2:
            return idb.at[hh], ids.at[tt]
        rows = pl.ds(k * half, half)
        return x.at[hh, rows], xs.at[tt, rows]

    for a in EARLY:
        for k in range(3):
            zz = others[k]
            go_(remote(mine(a, zz), dst[a].at[d, z, c], s_z.at[a - 3, k], r_z.at[a, z], me(zz)))

    def plane(arrs, zz, first):
        for a in arrs:
            src = mine(a, z) if first else dst[a].at[d, zz, c]
            go_(remote(src, dst[a].at[d, zz, c], s_px.at[a, zz], r_px.at[a, zz], nx))
            go_(remote(src, dst[a].at[d, zz, c], s_py.at[a, zz], r_py.at[a, zz], ny))

    plane(EARLY, z, True)
    for k in (2, 0, 1):
        src, to = piece(k, 1 - h, t)
        go_(remote(src, to, s_x.at[0, k], r_x.at[z, k], me(z1)))
        src, to = piece(k, h, t)
        go_(remote(src, to, s_x.at[1, k], r_x.at[z, k], me(zp)))

    def chain(zz, first, wait):
        for a in WIDE:
            src = mine(a, z) if first else dst[a].at[d, zz, c]
            up = remote(src, dst[a].at[d, zz, c], s_up.at[a, zz], r_z.at[a, zz], me((z + 1) % 4))
            dn = remote(src, dst[a].at[d, zz, c], s_dn.at[a, zz], r_z.at[a, zz], me((z + 3) % 4))

            @pl.when(jnp.logical_and(zz <= z, z < 3))
            def _(up=up):
                if wait:
                    up.wait_send()
                else:
                    up.start()

            @pl.when(jnp.logical_and(zz >= z, z > 0))
            def _(dn=dn):
                if wait:
                    dn.wait_send()
                else:
                    dn.start()

    chain(z, True, False)
    plane(WIDE, z, True)
    locals_ = [pltpu.make_async_copy(piece(k, h, t)[0], piece(k, h, t)[1], loc.at[N_ARR + k]) for k in range(3)]
    for a in (4, 5, 6, 3, 0, 1, 2):
        locals_.append(pltpu.make_async_copy(mine(a, z), dst[a].at[d, z, c], loc.at[a]))
    for cp in locals_:
        cp.start()

    def forward(arrs, zz):
        for a in arrs:
            if a in FIRST_Y:
                got(dst[a].at[dy, zz, c], s_py.at[a, zz], r_py.at[a, zz], ny)
                go_(remote(dst[a].at[dy, zz, c], dst[a].at[dy, zz, c], s_f.at[a, zz], r_f.at[a, zz], nx))
            else:
                got(dst[a].at[dx, zz, c], s_px.at[a, zz], r_px.at[a, zz], nx)
                go_(remote(dst[a].at[dx, zz, c], dst[a].at[dx, zz, c], s_f.at[a, zz], r_f.at[a, zz], ny))

    def across(arrs, zz):
        for a in arrs:
            if a in FIRST_Y:
                got(dst[a].at[dx, zz, c], s_px.at[a, zz], r_px.at[a, zz], nx)
                got(dst[a].at[dxy, zz, c], s_f.at[a, zz], r_f.at[a, zz], nx)
            else:
                got(dst[a].at[dy, zz, c], s_py.at[a, zz], r_py.at[a, zz], ny)
                got(dst[a].at[dxy, zz, c], s_f.at[a, zz], r_f.at[a, zz], ny)
            go_(remote(dst[a].at[:, zz, c], dst[a].at[:, zz, c], s_c.at[a, zz], r_c.at[a, zz], core))

    def crossed(arrs, zz):
        for a in arrs:
            ref = dst[a].at[:, zz, 1 - c]
            got(ref, s_c.at[a, zz], r_c.at[a, zz], core)

    def arrive(arrs, k):
        for a in arrs:
            got(dst[a].at[d, others[k], c], s_z.at[0, 0], r_z.at[a, others[k]], me(others[k]))

    for k in range(3):
        arrive(EARLY, k)
        plane(EARLY, others[k], False)
    for cp in locals_[:7]:
        cp.wait()
    for zz in [z] + others:
        forward(EARLY, zz)

    def relay(k, wait):
        for j in range(2):
            ref = piece(k, h, far[j] * 2 + c)[1]
            cp = remote(ref, ref, s_xf.at[j, k], r_x.at[far[j], k], me(zp))

            @pl.when(inner)
            def _(cp=cp):
                if wait:
                    cp.wait_send()
                else:
                    cp.wait_recv()
                    cp.start()

    def relayed(k):
        for j in range(2):
            ref = piece(k, h, far[j] * 2 + c)[1]

            @pl.when(jnp.logical_not(inner))
            def _(ref=ref, j=j):
                got(ref, s_x.at[0, k], r_x.at[far[j], k], me(zp))

    def to_core(zz):
        for k in range(3):
            ref = piece(k, h, zz * 2 + c)[1]
            go_(remote(ref, ref, s_xd.at[zz, k], r_xd.at[zz, k], core))

    def from_core(zz):
        for k in range(3):
            got(piece(k, h, zz * 2 + 1 - c)[1], s_xd.at[zz, k], r_xd.at[zz, k], core)

    to_core(z)
    for k in (2, 0):
        relay(k, False)
    for zz in [z] + others:
        across(EARLY, zz)
    relay(1, False)
    for k in range(3):
        got(piece(k, h, zp * 2 + c)[1], s_x.at[1, k], r_x.at[zp, k], me(zp))
    to_core(zp)
    for zz in [z] + others:
        crossed(EARLY, zz)
    width = wt.shape[3]
    for j in range(3):
        for q in range(2):
            w = gq[j, 2 * q:2 * q + 2].astype(F32).reshape(width // 2, per)
            w = w.T.astype(BF)
            for cc in range(2):
                wt[j, cc, :, q * (width // 2):(q + 1) * (width // 2)] = w[cc * (per // 2):(cc + 1) * (per // 2)]
    group = (z % 2) * 2 + c
    span = x.shape[1]

    def column(row):
        v = gs[group, :, :, row].reshape(8, 128).T
        return jnp.concatenate([v[:24, r:r + 1] for r in range(8)], axis=0)

    bias = [column(0), None, column(1)]
    for g in range(NH):
        va[g, 64:] = jnp.ones((16, va.shape[2]), BF)

    def project(zz):
        def one(j, _):
            tb = zz * 2 + j
            cols = pl.ds(pl.multiple_of(tb * span, span), span)
            xb = xs[tb]
            hit = marks_of(ids[tb, 0:1])
            ones = jnp.where(hit, 1.0, 0.0)
            away = jnp.where(hit, 0.0, EXCLUDE).astype(BF)
            for s in range(3):
                r = lax.dot_general(wt[s, c], xb, (((1,), (1,)), ((), ())), preferred_element_type=F32)
                if bias[s] is not None:
                    r = r + bias[s]
                low = r.astype(BF)
                qkv[s, :, cols] = low
                for g in range(NH):
                    part = low[g * 64:(g + 1) * 64]
                    if s == 0:
                        qa[g, :64, cols] = part
                        qa[g, 64:, cols] = away
                    elif s == 1:
                        ka[g, cols, :] = jnp.concatenate([part.astype(F32), ones], axis=0).T.astype(BF)
                    else:
                        va[g, :64, cols] = part
            return 0

        lax.fori_loop(0, 2, one, 0)

    forward(WIDE, z)
    for zz in (z, zp):
        from_core(zz)
        project(zz)
    for k in (2, 0, 1):
        relayed(k)
    for zz in far:
        to_core(zz)
    for zz in far:
        from_core(zz)
        project(zz)

    def attend(k):
        i = (t + k) % 8
        cols = pl.ds(pl.multiple_of(i * QB, QB), QB)
        lo, hi = window(i)

        def block(j, carry):
            at = pl.ds(pl.multiple_of(j * KB, KB), KB)
            out = []
            s = [jnp.dot(ka[g, at, :], qa[g, :, cols], preferred_element_type=F32) for g in range(NH)]
            for g in range(NH):
                m, acc = carry[g]
                m2 = jnp.maximum(m, jnp.max(s[g], axis=0, keepdims=True))
                p = jnp.exp2((s[g] - m2) * SCORE_SCALE).astype(BF)
                acc = acc * jnp.exp2((m - m2) * SCORE_SCALE) + jnp.dot(
                    va[g, :, at], p, preferred_element_type=F32)
                out.append((m2, acc))
            return tuple(out)

        first = tuple((jnp.full((1, QB), -3e38, F32), jnp.zeros((80, QB), F32)) for _ in range(NH))
        res = lax.fori_loop(lo, hi, block, first)
        for g in range(NH):
            m, acc = res[g]
            total = acc[64:65]
            o = acc[:64] / total
            o32[i, g * 64:(g + 1) * 64] = o
            if k:
                sb[i, g * 64:(g + 1) * 64] = o.astype(BF)
            else:
                att[t, g * 64:(g + 1) * 64] = o.astype(BF)
            lse[g, pl.ds(i, 1)] = m * SCORE_SCALE + jnp.log2(total)
        if k:
            go_(remote(sb.at[i], att.at[t], s_e.at[k - 1], r_e.at[k - 1], (d, i)))

    def onward(k):
        arrive(WIDE, k)
        chain(others[k], False, False)
        plane(WIDE, others[k], False)

    order = ORDER_K
    attend(order[0])
    onward(0)
    attend(order[1])
    for cp in locals_[7:]:
        cp.wait()
    across(WIDE, z)
    attend(order[2])
    onward(1)
    attend(order[3])
    forward(WIDE, zp)
    attend(order[4])
    onward(2)
    attend(order[5])
    forward(WIDE, z1)
    across(WIDE, zp)
    attend(order[6])
    attend(order[7])
    forward(WIDE, z2)
    across(WIDE, z1)
    across(WIDE, z2)
    for r in range(32):
        v = gs.at[r // 8, (r // 2) % 4, r % 2]
        fv[:, 24 * r:24 * r + 24] = v[0:8, 0:24]
        bi[:, 96 * r:96 * r + 96] = v[8:9, 0:96]
    for zz in [z] + others:
        crossed(WIDE, zz)
    for k in range(1, 8):
        src = (t + 8 - k) % 8
        got(att.at[src], s_e.at[k - 1], r_e.at[k - 1], (d, src))
    for cp in sends:
        cp.wait_send()
    chain(z, True, True)
    for zz in others:
        chain(zz, False, True)
    for k in range(3):
        relay(k, True)


ORDER_K = (4, 3, 5, 2, 6, 1, 7, 0)


def any_spec():
    return pl.BlockSpec(memory_space=pl.ANY)


def vmem_spec():
    return pl.BlockSpec(memory_space=pltpu.VMEM)


def dma(*shape):
    return pltpu.SemaphoreType.DMA(shape)


def front(x, seg, wi, wo, wb, vs, bv, wq):
    span, width = x.shape[1:]
    n = 8 * span
    per = width // 4
    grid_of = lambda a: jax.ShapeDtypeStruct((4, 4, 2) + a.shape, a.dtype)
    return pl.pallas_call(
        front_kernel,
        out_shape=[
            jax.ShapeDtypeStruct((8, span, width), x.dtype),
            jax.ShapeDtypeStruct((8, 8, span), F32),
            grid_of(wi), grid_of(wo), grid_of(wb),
            jax.ShapeDtypeStruct((8, width), F32), jax.ShapeDtypeStruct((1, wi.shape[2]), F32),
            jax.ShapeDtypeStruct((8, per, span), BF),
            jax.ShapeDtypeStruct((3, per, n), BF),
            jax.ShapeDtypeStruct((8, per, span), F32),
            jax.ShapeDtypeStruct((NH, 8, span), F32),
            jax.ShapeDtypeStruct((3, 2, per, width), BF),
        ],
        in_specs=[any_spec(), vmem_spec()] + [any_spec()] * 3 + [vmem_spec()] * 2 + [any_spec()],
        out_specs=[vmem_spec()] * 2 + [any_spec()] * 3 + [vmem_spec()] * 7,
        scratch_shapes=[
            pltpu.VMEM((2, 8, span), F32), pltpu.VMEM((16, 128), F32), pltpu.VMEM((4, 4, 2, 16, 128), F32),
            pltpu.VMEM((3, 4, 4, 2) + wq.shape[:2] + (2 * per,), BF),
            pltpu.VMEM((NH, n, 80), BF), pltpu.VMEM((NH, 80, n), BF), pltpu.VMEM((NH, 80, n), BF),
            pltpu.VMEM((8, per, span), BF),
            dma(N_ARR + 3), dma(2, 3), dma(4, 3), dma(2, 3), dma(4, 3), dma(4, 3), dma(4, 3), dma(N_ARR, 4),
            dma(3, 4), dma(3, 4),
            dma(N_ARR, 4), dma(N_ARR, 4), dma(N_ARR, 4), dma(N_ARR, 4), dma(N_ARR, 4), dma(N_ARR, 4),
            dma(N_ARR, 4), dma(N_ARR, 4), dma(7), dma(7),
        ],
        compiler_params=pltpu.CompilerParams(
            collective_id=1, has_side_effects=True, vmem_limit_bytes=VMEM_LIMIT),
        name="front",
    )(x, seg, wi, wo, wb, vs, bv, wq)


def back_kernel(dat, di, do_, db, ds_, qkv, ids, o32, lse, wt, xs, d_one,
                ox, oi, oo, ob, os_, oq, *rest):
    rd, own, r1, r2, r3, r4, r5 = [rest[4 * i:4 * i + 4] for i in range(7)]
    (da, ka, qa, vk, dkv, pr, xv, dxp, dw, lq, lv,
     xd, x3, x4, x5, q0, q1, q2, qr, v0, v1, v2, vr,
     loc, s_e, r_e, s_d, r_d, s_1, r_1, s_2, r_2, s_3, r_3, s_4, r_4, s_5, r_5,
     s_q1, r_q1, s_q2, r_q2, s_qe, r_qe) = rest[28:]
    d, t, z, c, dx, dy = place()
    x, y = d % 2, d // 2
    h = z // 2
    zp = z + 1 - 2 * (z % 2)
    inner = (z + h) % 2 == 1
    me = lambda zz: (d, zz * 2 + c)
    core = (d, z * 2 + 1 - c)
    nx, ny = (dx, t), (dy, t)
    line = [(t + k) % 8 for k in range(1, 8)]
    far = [2 * (1 - h), 2 * (1 - h) + 1]
    order = [far[0], far[1], zp, z]
    group = (z % 2) * 2 + c
    part = [di, do_, db, ds_]
    outs = [oi, oo, ob, os_.at[pl.ds(0, 8)]]
    by_x = [True, True, False, True]
    sends = []
    greet([(d, o) for o in line] + [nx, ny])

    def go_(cp):
        cp.start()
        sends.append(cp)

    def got(ref, ss, rs, dev):
        remote(ref, ref, ss, rs, dev).wait_recv()

    for k in NEAR[1:]:
        i = line[k - 1]
        go_(remote(dat.at[i], da.at[t], s_e.at[k - 1], r_e.at[k - 1], (d, i)))
    for n_, zz in enumerate(order):
        for a in range(4):
            for yy in range(2):
                go_(remote(part[a].at[yy, :, zz, 1 - c], rd[a].at[yy, :, zz], s_d.at[1 + 2 * a + yy, n_],
                           r_d.at[1 + 2 * a + yy, n_], core))
    local = []

    def here(src, to):
        cp = pltpu.make_async_copy(src, to, loc.at[len(local)])
        cp.start()
        local.append(cp)

    here(dat.at[t], da.at[t])
    for a in range(4):
        for yy in range(2):
            here(part[a].at[yy, :, :, c], own[a].at[yy])
    here(xs, xv)

    n = qkv.shape[2]
    span = da.shape[2]

    def fill(tb, _):
        cols = pl.ds(pl.multiple_of(tb * span, span), span)
        hit = marks_of(ids[tb, 0:1])
        ones = jnp.where(hit, 1.0, 0.0)
        away = jnp.where(hit, 0.0, EXCLUDE).astype(BF)
        for g in range(NH):
            rows = slice(g * 64, (g + 1) * 64)
            ka[g, cols, :] = jnp.concatenate([qkv[1, rows, cols].astype(F32), ones], axis=0).T.astype(BF)
            vk[g, cols, :] = qkv[2, rows, cols].astype(F32).T.astype(BF)
            qa[g, :64, cols] = qkv[0, rows, cols]
            qa[g, 64:, cols] = away
            dkv[g, cols, :] = jnp.zeros((span, 128), F32)
        return 0

    lax.fori_loop(0, 8, fill, 0)

    def attend(k):
        i = (t + 8 - k) % 8
        if k:
            got(da.at[i], s_e.at[k - 1], r_e.at[k - 1], (d, i))
        cols = pl.ds(pl.multiple_of(i * QB, QB), QB)
        lo, hi = window(i)
        fixed = []
        for g in range(NH):
            rows = slice(g * 64, (g + 1) * 64)
            do = da[i, rows].astype(F32)
            inside = jnp.sum(do * o32[i, rows], axis=0, keepdims=True)
            zero = jnp.zeros((64, QB), F32)
            ra = jnp.concatenate([do, zero], axis=0).T.astype(BF)
            rb = jnp.concatenate([zero, qkv[0, rows, cols].astype(F32)], axis=0).T.astype(BF)
            fixed.append((inside, lse[g, pl.ds(i, 1)], ra, rb))

        def block(j, carry):
            at = pl.ds(pl.multiple_of(j * KB, KB), KB)
            out = []
            s = [jnp.dot(ka[g, at, :], qa[g, :, cols], preferred_element_type=F32) for g in range(NH)]
            dp = [jnp.dot(vk[g, at, :], da[i, g * 64:(g + 1) * 64], preferred_element_type=F32)
                  for g in range(NH)]
            for g in range(NH):
                inside, lse_i, ra, rb = fixed[g]
                p = jnp.exp2(s[g] * SCORE_SCALE - lse_i)
                ds = (p * (dp[g] - inside)).astype(BF)
                dkv[g, at, :] += jnp.dot(p.astype(BF), ra, preferred_element_type=F32) + jnp.dot(
                    ds, rb, preferred_element_type=F32)
                out.append(carry[g] + jnp.dot(qkv[1, g * 64:(g + 1) * 64, at], ds, preferred_element_type=F32))
            return tuple(out)

        dq = lax.fori_loop(lo, hi, block, tuple(jnp.zeros((64, QB), F32) for _ in range(NH)))
        for g in range(NH):
            pr[0, g * 64:(g + 1) * 64, cols] = (dq[g] * 0.125).astype(BF)

    def add_rows(dst, src):
        def step(i, _):
            dst[i] = dst[i] + src[i]
            return 0

        lax.fori_loop(0, dst.shape[0], step, 0)

    def add_tok(dst, src):
        def step(i, _):
            at = pl.ds(pl.multiple_of(i * 32, 32), 32)
            dst[at, :] = dst[at, :] + src[at, :]
            return 0

        lax.fori_loop(0, dst.shape[0] // 32, step, 0)

    def first(n_):
        zz = order[n_]
        for a in range(4):
            for yy in range(2):
                got(rd[a].at[yy, :, zz], s_d.at[1 + 2 * a + yy, n_], r_d.at[1 + 2 * a + yy, n_], core)
                for xx in range(2):
                    add_rows(rd[a].at[yy, xx, zz], own[a].at[yy, xx, zz])
            if by_x[a]:
                go_(remote(rd[a].at[:, 1 - x, zz], r1[a].at[n_], s_1.at[a, n_], r_1.at[a, n_], nx))
            else:
                go_(remote(rd[a].at[1 - y, :, zz], r1[a].at[n_], s_1.at[a, n_], r_1.at[a, n_], ny))

    def second(n_):
        zz = order[n_]
        for a in range(4):
            got(r1[a].at[n_], s_1.at[a, n_], r_1.at[a, n_], nx if by_x[a] else ny)
            for w in range(2):
                add_rows(rd[a].at[w, x, zz] if by_x[a] else rd[a].at[y, w, zz], r1[a].at[n_, w])
            if by_x[a]:
                go_(remote(rd[a].at[1 - y, x, zz], r2[a].at[n_], s_2.at[a, n_], r_2.at[a, n_], ny))
            else:
                go_(remote(rd[a].at[y, 1 - x, zz], r2[a].at[n_], s_2.at[a, n_], r_2.at[a, n_], nx))

    def to_inner(a, n_):
        ref = xd.at[far[n_]] if a == 4 else rd[a].at[y, x, far[n_]]
        land = x3 if a == 4 else r3[a]
        return remote(ref, land.at[n_], s_3.at[a, n_], r_3.at[a, n_], me(zp))

    def to_far(a, n_):
        ref = xd.at[far[n_]] if a == 4 else rd[a].at[y, x, far[n_]]
        return remote(ref, x4 if a == 4 else r4[a], s_4.at[a, n_], r_4.at[a], me(far[n_]))

    def third(n_):
        zz = order[n_]
        for a in range(4):
            got(r2[a].at[n_], s_2.at[a, n_], r_2.at[a, n_], ny if by_x[a] else nx)
            add_rows(rd[a].at[y, x, zz], r2[a].at[n_])
            if n_ < 2:
                @pl.when(jnp.logical_not(inner))
                def _(a=a):
                    to_inner(a, n_).start()
            elif n_ == 2:
                go_(remote(rd[a].at[y, x, zz], r5[a], s_5.at[a], r_5.at[a], me(zz)))

    def fourth(n_, arrs):
        @pl.when(inner)
        def _():
            for a in arrs:
                to_inner(a, n_).wait_recv()
                if a == 4:
                    add_tok(xd.at[far[n_]], x3.at[n_])
                else:
                    add_rows(rd[a].at[y, x, far[n_]], r3[a].at[n_])
                to_far(a, n_).start()

    for cp in local:
        cp.wait()
    first(0)
    first(1)
    attend(NEAR[0])
    attend(NEAR[1])
    second(0)
    first(2)
    attend(NEAR[2])
    attend(NEAR[3])
    second(1)
    first(3)
    attend(NEAR[4])
    third(0)
    attend(NEAR[5])
    second(2)
    attend(NEAR[6])
    third(1)
    fourth(0, range(4))
    attend(NEAR[7])
    second(3)
    for g in range(NH):
        rows = slice(g * 64, (g + 1) * 64)
        flip = dkv[g].T
        pr[1, rows] = (flip[64:] * 0.125).astype(BF)
        pr[2, rows] = flip[:64].astype(BF)

    def token_grad(tb):
        cols = pl.ds(pl.multiple_of(tb * span, span), span)
        acc = None
        for s in range(3):
            term = jnp.dot(pr[s, :, cols].astype(F32).T.astype(BF), wt[s, c], preferred_element_type=F32)
            acc = term if acc is None else acc + term
        dxp[tb] = acc.astype(BF)

    def token_pair(j, _):
        token_grad(j * 2 + 1 - c)
        return 0

    lax.fori_loop(0, 4, token_pair, 0)
    for n_, zz in enumerate(order):
        go_(remote(dxp.at[zz * 2 + 1 - c], xd.at[zz], s_d.at[0, n_], r_d.at[0, n_], core))
    third(2)
    fourth(1, range(4))

    def token_mine(j, _):
        token_grad(j * 2 + c)
        return 0

    lax.fori_loop(0, 4, token_mine, 0)
    for n_, zz in enumerate(order):
        got(xd.at[zz], s_d.at[0, n_], r_d.at[0, n_], core)
        add_tok(xd.at[zz], dxp.at[zz * 2 + c])
        if n_ < 2:
            @pl.when(jnp.logical_not(inner))
            def _(n_=n_):
                to_inner(4, n_).start()
        elif n_ == 2:
            go_(remote(xd.at[zz], x5, s_5.at[4], r_5.at[4], me(zz)))
    per = pr.shape[1]
    width = wt.shape[3]
    xall = xv[...].reshape(n, width)
    for s in range(3):
        dw[s * per:(s + 1) * per] = jnp.dot(pr[s], xall, preferred_element_type=F32)
    for q in range(2):
        w = dw[:, q * (width // 2):(q + 1) * (width // 2)].T
        lq[q] = w.reshape(lq.shape[1:]).astype(BF)
    lv[...] = jnp.zeros_like(lv)
    for row, s in ((0, 0), (1, 2)):
        col = jnp.sum(pr[s].astype(F32), axis=1, keepdims=True)
        for r in range(8):
            piece = jnp.broadcast_to(col[24 * r:24 * r + 24], (24, 128)).T
            lv[group // 2, group % 2, r // 2, r % 2, row:row + 1, :24] = piece[0:1]
    lq_x = lq
    go_(remote(lq_x.at[:, 1 - x], q1, s_q1.at[0], r_q1.at[0], nx))
    go_(remote(lv.at[:, 1 - x], v1, s_q1.at[1], r_q1.at[1], nx))
    third(3)
    fourth(0, (4,))
    fourth(1, (4,))
    got(q1, s_q1.at[0], r_q1.at[0], nx)
    got(v1, s_q1.at[1], r_q1.at[1], nx)
    for yy in range(2):
        for zc in range(8):
            at = (zc // 2, zc % 2)
            q0[(yy,) + at] = q1[(yy,) + at] + lq[(yy, x) + at]
            v0[(yy,) + at] = v1[(yy,) + at] + lv[(yy, x) + at]
    go_(remote(q0.at[1 - y], q2, s_q2.at[0], r_q2.at[0], ny))
    go_(remote(v0.at[1 - y], v2, s_q2.at[1], r_q2.at[1], ny))
    src_in = 2 - h
    for a in range(4):
        got(r5[a], s_5.at[a], r_5.at[a], me(zp))
        got(r4[a], s_4.at[a, 0], r_4.at[a], me(src_in))
        acc = rd[a].at[y, x, z]
        for i in range(acc.shape[0]):
            outs[a][i] = acc[i].astype(F32) + r5[a][i].astype(F32) + r4[a][i].astype(F32)
    got(q2, s_q2.at[0], r_q2.at[0], ny)
    got(v2, s_q2.at[1], r_q2.at[1], ny)
    for zc in range(8):
        at = (zc // 2, zc % 2)
        q0[(y,) + at] = q0[(y,) + at] + q2[at]
        v0[(y,) + at] = v0[(y,) + at] + v2[at]
    for k in range(1, 8):
        to = line[k - 1]
        go_(remote(q0.at[y, to // 2, to % 2], qr.at[t], s_qe.at[0, k - 1], r_qe.at[0, k - 1], (d, to)))
        go_(remote(v0.at[y, to // 2, to % 2], vr.at[t], s_qe.at[1, k - 1], r_qe.at[1, k - 1], (d, to)))
    qr[t] = q0[y, z, c]
    vr[t] = v0[y, z, c]
    got(x5, s_5.at[4], r_5.at[4], me(zp))
    got(x4, s_4.at[4, 0], r_4.at[4], me(src_in))

    def tok(i, _):
        at = pl.ds(pl.multiple_of(i * 32, 32), 32)
        ox[h, at, :] = d_one[h, at, :] + (xd[z, at, :].astype(F32) + x5[at, :].astype(F32))
        ox[1 - h, at, :] = d_one[1 - h, at, :] + x4[at, :].astype(F32)
        return 0

    lax.fori_loop(0, span // 32, tok, 0)
    for k in range(1, 8):
        src = (t + 8 - k) % 8
        got(qr.at[src], s_qe.at[0, k - 1], r_qe.at[0, k - 1], (d, src))
        got(vr.at[src], s_qe.at[1, k - 1], r_qe.at[1, k - 1], (d, src))
    for g in range(4):
        oq[g] = qr[g].astype(F32) + qr[4 + g].astype(F32)
    total = vr[0]
    for k in range(1, 8):
        total = total + vr[k]
    os_[8:16] = total
    for cp in sends:
        cp.wait_send()
    for n_ in range(2):
        @pl.when(jnp.logical_not(inner))
        def _(n_=n_):
            for a in range(5):
                to_inner(a, n_).wait_send()

        @pl.when(inner)
        def _(n_=n_):
            for a in range(5):
                to_far(a, n_).wait_send()


NEAR = (0, 1, 7, 2, 6, 3, 5, 4)


def back(dat, di, do_, db, ds_, qkv, ids, o32, lse, wt, xs, d_one):
    arrs = [di, do_, db, ds_]
    tails = [a.shape[4:] for a in arrs]
    per, width = wt.shape[2:]
    n = qkv.shape[2]
    tok = xs.shape[1:]
    qt = di.shape[4:6] + (3 * per,)
    vt = (8, 128)
    scratch = []
    for lead in ((2, 2, 4), (2, 2, 4), (4, 2), (4,), (2,), (), ()):
        for a, tail in zip(arrs, tails):
            scratch.append(pltpu.VMEM(lead + tail, a.dtype))
    grid = (2, 2, 4, 2)
    scratch += [
        pltpu.VMEM(dat.shape, BF),
        pltpu.VMEM((NH, n, 80), BF), pltpu.VMEM((NH, 80, n), BF), pltpu.VMEM((NH, n, 64), BF),
        pltpu.VMEM((NH, n, 128), F32), pltpu.VMEM((3, per, n), BF),
        pltpu.VMEM(xs.shape, BF), pltpu.VMEM(xs.shape, BF), pltpu.VMEM((3 * per, width), F32),
        pltpu.VMEM(grid + qt, BF), pltpu.VMEM(grid + vt, F32),
        pltpu.VMEM((4,) + tok, BF), pltpu.VMEM((2,) + tok, BF), pltpu.VMEM(tok, BF), pltpu.VMEM(tok, BF),
        pltpu.VMEM((2, 4, 2) + qt, BF), pltpu.VMEM((2, 4, 2) + qt, BF), pltpu.VMEM((4, 2) + qt, BF),
        pltpu.VMEM((8,) + qt, BF),
        pltpu.VMEM((2, 4, 2) + vt, F32), pltpu.VMEM((2, 4, 2) + vt, F32), pltpu.VMEM((4, 2) + vt, F32),
        pltpu.VMEM((8,) + vt, F32),
        dma(10), dma(7), dma(7), dma(9, 4), dma(9, 4), dma(4, 4), dma(4, 4), dma(4, 4), dma(4, 4),
        dma(5, 2), dma(5, 2), dma(5, 2), dma(5), dma(5), dma(5),
        dma(2), dma(2), dma(2), dma(2), dma(2, 7), dma(2, 7),
    ]
    return pl.pallas_call(
        back_kernel,
        out_shape=[jax.ShapeDtypeStruct((2,) + tok, F32)]
        + [jax.ShapeDtypeStruct(tail, F32) for tail in tails[:3] + [(16, 128)]]
        + [jax.ShapeDtypeStruct((4,) + qt, F32)],
        in_specs=[any_spec()] * 5 + [vmem_spec()] * 5 + [any_spec(), vmem_spec()],
        out_specs=[vmem_spec()] * 6,
        scratch_shapes=scratch,
        compiler_params=pltpu.CompilerParams(
            collective_id=4, has_side_effects=True, vmem_limit_bytes=VMEM_LIMIT),
        name="back",
    )(dat, di, do_, db, ds_, qkv, ids, o32, lse, wt, xs, d_one)


def erf_parts(u):
    phi_c = 0.5 * (1.0 + lax.erf(u * 0.7071067811865476))
    return phi_c, phi_c + u * jnp.exp(-0.5 * u * u) * 0.3989422804014327


def norm_forward(r):
    center = r - jnp.mean(r, axis=-1, keepdims=True)
    inv = lax.rsqrt(jnp.mean(center * center, axis=-1, keepdims=True) + layer_eps)
    return center * inv, inv


def norm_backward(n, inv, gain, dy):
    gd = gain * dy
    return (gd - jnp.mean(gd, axis=-1, keepdims=True) - n * jnp.mean(gd * n, axis=-1, keepdims=True)) * inv


def mid_kernel(x, att, wo, wi, wb, fv, bi, cot,
               out, d_one, dat, g_in, g_out, g_back, g_small,
               vo, vi, vb, att_t, acc, n1, inv1, low, low_t, slope, act, act_t, d_pre, d_two, d_br, d_attn,
               yi, yo, yb, yx, yd, ys, part, sums, sum_in, sem_w, sem_o):
    tokens, width = x.shape
    span = tokens // 2
    ff = vi.shape[1]
    loads = [pltpu.make_async_copy(a, b, sem_w.at[k]) for k, (a, b) in enumerate(((wo, vo), (wi, vi), (wb, vb)))]
    for cp in loads:
        cp.start()
    outs = []

    def put(src, to):
        cp = pltpu.make_async_copy(src, to, sem_o.at[len(outs)])
        cp.start()
        outs.append(cp)

    def loop(count, size, fn):
        def one(j, _):
            fn(pl.ds(pl.multiple_of(j * size, size), size))
            return 0

        lax.fori_loop(0, count, one, 0)

    halves = (slice(0, span), slice(span, tokens))
    rb = tokens // 4
    nt = (((1,), (1,)), ((), ()))
    part[...] = jnp.zeros_like(part)

    def count_in(k, v):
        part[k] += jnp.sum(v.reshape(v.shape[0] // 8, 8, width), axis=0)

    for s in range(2):
        att_t[halves[s]] = att[s].astype(F32).T.astype(BF)
    loads[0].wait()
    for s in range(2):
        acc[halves[s]] = jnp.dot(att_t[halves[s]], vo[...], preferred_element_type=F32)

    def norm_one(r):
        n, inv = norm_forward(x[r].astype(F32) + acc[r] + fv[2:3])
        n1[r] = n
        inv1[r] = inv
        low[r] = (n * fv[3:4] + fv[4:5]).astype(BF)

    loop(4, rb, norm_one)
    loads[1].wait()

    def widen(f):
        pre = [jnp.dot(low[r], vi[:, f], preferred_element_type=F32) + bi[:, f] for r in halves]
        for r, u in zip(halves, pre):
            phi_c, sl = erf_parts(u)
            slope[r, f] = sl
            a = u * phi_c
            act[r, f] = a.astype(BF)
            act_t[f, r] = a.T.astype(BF)

    loop(ff // 256, 256, widen)
    loads[2].wait()

    def narrow(f):
        for r in halves:
            acc[r, f] = jnp.dot(act[r], vb[:, f], preferred_element_type=F32)

    loop(width // 256, 256, narrow)

    def norm_two(r):
        normed = n1[r] * fv[3:4] + fv[4:5]
        n2, inv2 = norm_forward(normed + acc[r] + fv[5:6])
        yx[r] = (n2 * fv[6:7] + fv[7:8]).astype(BF)
        dy = cot[r].astype(F32)
        d2 = norm_backward(n2, inv2, fv[6:7], dy)
        d_two[r] = d2
        d2 = d2.astype(BF)
        d_br[r] = d2
        count_in(3, d2.astype(F32))
        count_in(4, dy * n2)
        count_in(5, dy)

    loop(4, rb, norm_two)
    put(yx, out)

    def back_widen(f):
        da = [lax.dot_general(d_br[r], vb[f, :], nt, preferred_element_type=F32) for r in halves]
        total = None
        for r, v in zip(halves, da):
            dp = (v * slope[r, f]).astype(BF)
            d_pre[r, f] = dp
            col = jnp.sum(dp.astype(F32), axis=0, keepdims=True)
            total = col if total is None else total + col
        sum_in[:, f] = total

    loop(ff // 256, 256, back_widen)

    def back_narrow(k):
        for r in halves:
            acc[r, k] = lax.dot_general(d_pre[r], vi[k, :], nt, preferred_element_type=F32)

    loop(width // 256, 256, back_narrow)

    def back_one(r):
        dn = d_two[r] + acc[r]
        n = n1[r]
        d1 = norm_backward(n, inv1[r], fv[3:4], dn)
        d_one[r] = d1
        d1 = d1.astype(BF)
        d_attn[r] = d1
        count_in(0, d1.astype(F32))
        count_in(1, dn * n)
        count_in(2, dn)

    loop(4, rb, back_one)
    for s in range(2):
        yd[s] = lax.dot_general(vo[...], d_attn[halves[s]], nt, preferred_element_type=F32).astype(BF)
    put(yd, dat)

    def grad_back(f):
        yb[f, :] = jnp.dot(act_t[f, :], d_br[...], preferred_element_type=F32).astype(BF)

    loop(ff // 256, 256, grad_back)
    put(yb, g_back)
    for k in range(3):
        low_t[k * 256:(k + 1) * 256] = low[:, k * 256:(k + 1) * 256].astype(F32).T.astype(BF)
    for k in range(3):
        rows = slice(k * 256, (k + 1) * 256)

        def grad_in(f, rows=rows):
            yi[rows, f] = jnp.dot(low_t[rows], d_pre[:, f], preferred_element_type=F32).astype(BF)

        loop(ff // 768, 768, grad_in)
        put(yi.at[rows], g_in.at[rows])

    def grad_out(k):
        yo[k] = (jnp.dot(att[0, k], d_attn[halves[0]], preferred_element_type=F32)
                 + jnp.dot(att[1, k], d_attn[halves[1]], preferred_element_type=F32)).astype(BF)

    loop(3, 256, grad_out)
    put(yo, g_out)
    ys[...] = jnp.zeros_like(ys)
    for k in range(6):
        sums[k:k + 1] = jnp.sum(part[k], axis=0, keepdims=True)
    for r in range(32):
        at = (r // 16, (r // 8) % 2, (r // 2) % 4, r % 2)
        ys[at + (slice(0, 6), slice(0, 24))] = sums[0:6, 24 * r:24 * r + 24]
        ys[at + (slice(6, 7), slice(0, 96))] = sum_in[:, 96 * r:96 * r + 96]
    put(ys, g_small)
    for cp in outs:
        cp.wait()


def mid(x, att, wo, wi, wb, fv, bi, cot):
    tokens, width = x.shape
    ff = wi.shape[1]
    tok = lambda dt: pltpu.VMEM((tokens, width), dt)
    wide = lambda dt: pltpu.VMEM((tokens, ff), dt)
    owner = (2, 2, 4, 2, 8, 128)
    shape = jax.ShapeDtypeStruct
    return pl.pallas_call(
        mid_kernel,
        out_shape=[
            shape((tokens, width), BF), shape((tokens, width), F32), shape(att.shape, BF), shape(wi.shape, BF),
            shape(wo.shape, BF), shape(wb.shape, BF), shape(owner, F32),
        ],
        in_specs=[vmem_spec()] * 2 + [any_spec()] * 3 + [vmem_spec()] * 3,
        out_specs=[any_spec(), vmem_spec()] + [any_spec()] * 5,
        scratch_shapes=[
            pltpu.VMEM(wo.shape, BF), pltpu.VMEM(wi.shape, BF), pltpu.VMEM(wb.shape, BF),
            tok(BF), tok(F32), tok(F32), pltpu.VMEM((tokens, 1), F32), tok(BF), pltpu.VMEM((width, tokens), BF),
            wide(F32), wide(BF), pltpu.VMEM((ff, tokens), BF), wide(BF), tok(F32), tok(BF), tok(BF),
            pltpu.VMEM(wi.shape, BF), pltpu.VMEM(wo.shape, BF), pltpu.VMEM(wb.shape, BF),
            tok(BF), pltpu.VMEM(att.shape, BF), pltpu.VMEM(owner, F32),
            pltpu.VMEM((6, 8, width), F32), pltpu.VMEM((8, width), F32), pltpu.VMEM((1, ff), F32),
            dma(3), dma(8),
        ],
        compiler_params=pltpu.CompilerParams(vmem_limit_bytes=VMEM_LIMIT),
        name="mid",
    )(x, att, wo, wi, wb, fv, bi, cot)


def finish_kernel(ix, oi, oo, ob, oq, px, pi, po, pb, pq, wide, sem):
    copies = [pltpu.make_async_copy(a, b, sem.at[k]) for k, (a, b) in enumerate(((ix, px), (oi, pi), (ob, pb), (oo, po)))]
    for cp in copies:
        cp.start()
    per = oq.shape[3] // 3
    for g in range(4):
        v = oq[g].reshape(wide.shape[0], 3 * per)
        for k in range(3):
            wide[:, (k * 4 + g) * per:(k * 4 + g + 1) * per] = v[:, k * per:(k + 1) * per]
    copies.append(pltpu.make_async_copy(wide, pq, sem.at[4]))
    copies[4].start()
    for cp in copies:
        cp.wait()


def finish(ix, oi, oo, ob, oq):
    shape = jax.ShapeDtypeStruct
    wide = (oq.shape[1] * oq.shape[2], oq.shape[3] * 4)
    return pl.pallas_call(
        finish_kernel,
        out_shape=[shape(a.shape, F32) for a in (ix, oi, oo, ob)] + [shape(wide, F32)],
        in_specs=[vmem_spec()] * 5,
        out_specs=[any_spec()] * 5,
        scratch_shapes=[pltpu.VMEM(wide, F32), dma(5)],
        name="finish",
    )(ix, oi, oo, ob, oq)


def on_device_fast(
    inputs, segments, w_qkv, b_query, b_value, w_out, b_attn, gain_one, shift_one,
    w_in, b_in, w_back, b_back, gain_two, shift_two, cotangent,
):
    nseq, span, width = inputs.shape
    tokens = nseq * span
    ff = w_in.shape[1]
    depth = w_in.shape[0]
    d, t, z, c, _, _ = place()
    per = width // 4
    vecs = (b_query, b_value, b_attn, gain_one, shift_one, b_back, gain_two, shift_two)
    ffd = b_in.shape[0]
    xs, ids, gi, go, gb, fv, bi, att, qkv, o32, lse, wt = front(
        inputs, segments, w_in.reshape(depth // 8, 8, ff), w_out.reshape(depth // 8, 8, width),
        w_back.reshape(ffd // 8, 8, width),
        jnp.stack(vecs), b_in.reshape(1, ffd), w_qkv.reshape(depth // 8, 8, 3 * width))
    output, d_one, d_att, grad_w_in, grad_w_out, grad_w_back, g_small = mid(
        inputs.reshape(tokens, width), att.reshape(nseq, width, span), go.reshape(width, width),
        gi.reshape(width, ff), gb.reshape(ff, width), fv, bi, cotangent.reshape(tokens, width))
    output = output.reshape(nseq, span, width)
    owner = (2, 2, 4, 2)
    input_grad, oi, oo, ob, os_, oq = back(
        d_att.reshape(8, per, span),
        grad_w_in.reshape(owner + (depth // 8, 8, ff)),
        grad_w_out.reshape(owner + (depth // 8, 8, width)),
        grad_w_back.reshape(owner + (ffd // 8, 8, width)),
        g_small, qkv, ids, o32, lse, wt, xs, d_one.reshape(nseq, span, width),
    )
    input_grad, oi, oo, ob, g_qkv = finish(input_grad, oi, oo, ob, oq)
    vec = lambda k: os_[k, :depth]
    return (
        output, input_grad, g_qkv, vec(8), vec(9), oo.reshape(depth, width), vec(0), vec(1), vec(2),
        oi.reshape(depth, ff), os_[6, :ffd], ob.reshape(ffd, width),
        vec(3), vec(4), vec(5),
    )


negative_fill = -1e30


def layer_norm(resid, gain, shift):
    center = resid - jnp.mean(resid, axis=-1, keepdims=True)
    spread = jnp.mean(center * center, axis=-1, keepdims=True)
    return center * lax.rsqrt(spread + layer_eps) * gain + shift


def gelu_exact(values):
    return jax.nn.gelu(values, approximate=False)


def attend_forward(entries):
    query_rows, key_rows, value_rows, query_ids, key_ids = entries
    scores = jnp.einsum(
        "qhd,khd->hqk", query_rows, key_rows, preferred_element_type=jnp.float32
    ) * HEAD_DIM ** (-0.5)
    allowed = (query_ids[:, None] == key_ids[None, :])[None]
    scores = jnp.where(allowed, scores, negative_fill)
    peak = jnp.max(scores, axis=-1, keepdims=True)
    raised = jnp.exp(scores - peak)
    total = jnp.sum(raised, axis=-1, keepdims=True)
    probs_low = (raised / total).astype(jnp.bfloat16)
    context = jnp.einsum("hqk,khd->qhd", probs_low, value_rows, preferred_element_type=jnp.float32)
    return (context, (peak + jnp.log(total))[..., 0])


def score_terms(query_rows, key_rows, value_rows, grad_context, log_total, query_ids, key_ids):
    scale = HEAD_DIM ** (-0.5)
    scores = (
        jnp.einsum("qhd,khd->hqk", query_rows, key_rows, preferred_element_type=jnp.float32) * scale
    )
    allowed = (query_ids[:, None] == key_ids[None, :])[None]
    probs = jnp.where(allowed, jnp.exp(scores - log_total[..., None]), 0.0)
    d_probs = jnp.einsum(
        "qhd,khd->hqk", grad_context, value_rows, preferred_element_type=jnp.float32
    )
    return (probs, d_probs)


def attend_backward(entries):
    query_rows, key_rows, value_rows, grad_context, log_total, query_ids, key_ids = entries
    scale = HEAD_DIM ** (-0.5)
    probs, d_probs = score_terms(
        query_rows, key_rows, value_rows, grad_context, log_total, query_ids, key_ids
    )
    inner = jnp.sum(probs * d_probs, axis=-1, keepdims=True)
    d_scores = (probs * (d_probs - inner)).astype(jnp.bfloat16)
    d_queries = (
        jnp.einsum("hqk,khd->qhd", d_scores, key_rows, preferred_element_type=jnp.float32) * scale
    )
    d_keys = (
        jnp.einsum("hqk,qhd->khd", d_scores, query_rows, preferred_element_type=jnp.float32) * scale
    )
    d_values = jnp.einsum(
        "hqk,qhd->khd", probs.astype(jnp.bfloat16), grad_context, preferred_element_type=jnp.float32
    )
    length = key_rows.shape[0]
    return (
        d_queries,
        d_keys.reshape(length, HEADS * HEAD_DIM),
        d_values.reshape(length, HEADS * HEAD_DIM),
    )


def on_device_general(
    inputs,
    segments,
    w_qkv,
    b_query,
    b_value,
    w_out,
    b_attn,
    gain_one,
    shift_one,
    w_in,
    b_in,
    w_back,
    b_back,
    gain_two,
    shift_two,
    cotangent,
):
    seq_count, group_len, model_width = inputs.shape
    tok_count = seq_count * group_len
    gathered = (
        lax.all_gather(w_qkv, ("dp", "ctx"), axis=0, tiled=True),
        lax.all_gather(b_query, ("dp", "ctx"), axis=0, tiled=True),
        lax.all_gather(b_value, ("dp", "ctx"), axis=0, tiled=True),
        lax.all_gather(w_out, ("dp", "ctx"), axis=0, tiled=True),
        lax.all_gather(b_attn, ("dp", "ctx"), axis=0, tiled=True),
        lax.all_gather(gain_one, ("dp", "ctx"), axis=0, tiled=True),
        lax.all_gather(shift_one, ("dp", "ctx"), axis=0, tiled=True),
        lax.all_gather(w_in, ("dp", "ctx"), axis=0, tiled=True),
        lax.all_gather(b_in, ("dp", "ctx"), axis=0, tiled=True),
        lax.all_gather(w_back, ("dp", "ctx"), axis=0, tiled=True),
        lax.all_gather(b_back, ("dp", "ctx"), axis=0, tiled=True),
        lax.all_gather(gain_two, ("dp", "ctx"), axis=0, tiled=True),
        lax.all_gather(shift_two, ("dp", "ctx"), axis=0, tiled=True),
    )
    (
        wide_qkv,
        full_b_query,
        full_b_value,
        wide_out,
        full_b_attn,
        full_gain_one,
        full_shift_one,
        wide_in,
        full_b_in,
        wide_back,
        full_b_back,
        full_gain_two,
        full_shift_two,
    ) = gathered
    tokens = inputs.reshape(tok_count, model_width)
    projected = jnp.dot(tokens, wide_qkv, preferred_element_type=jnp.float32)
    query_low = (projected[:, :model_width] + full_b_query.astype(jnp.float32)).astype(jnp.bfloat16)
    key_low = projected[:, model_width : 2 * model_width].astype(jnp.bfloat16)
    value_low = (projected[:, 2 * model_width :] + full_b_value.astype(jnp.float32)).astype(
        jnp.bfloat16
    )
    key_ids = lax.all_gather(segments, "ctx", axis=1, tiled=True)
    key_local = key_low.reshape(seq_count, group_len, model_width)
    value_local = value_low.reshape(seq_count, group_len, model_width)
    key_whole, value_whole = (
        lax.all_gather(key_local, "ctx", axis=1, tiled=True),
        lax.all_gather(value_local, "ctx", axis=1, tiled=True),
    )
    seq_len = key_whole.shape[1]
    query_heads = query_low.reshape(seq_count, group_len, HEADS, HEAD_DIM)
    context, log_total = lax.map(
        attend_forward,
        (
            query_heads,
            key_whole.reshape(seq_count, seq_len, HEADS, HEAD_DIM),
            value_whole.reshape(seq_count, seq_len, HEADS, HEAD_DIM),
            segments,
            key_ids,
        ),
    )
    attended = context.reshape(tok_count, model_width).astype(jnp.bfloat16)
    attn_out = jnp.dot(attended, wide_out, preferred_element_type=jnp.float32) + full_b_attn.astype(
        jnp.float32
    )
    resid_one = tokens.astype(jnp.float32) + attn_out
    normed, norm_one_back = jax.vjp(
        layer_norm, resid_one, full_gain_one.astype(jnp.float32), full_shift_one.astype(jnp.float32)
    )
    normed_low = normed.astype(jnp.bfloat16)
    pre_act = jnp.dot(normed_low, wide_in, preferred_element_type=jnp.float32) + full_b_in.astype(
        jnp.float32
    )
    activ_f, gelu_back = jax.vjp(gelu_exact, pre_act)
    activ = activ_f.astype(jnp.bfloat16)
    branch = jnp.dot(activ, wide_back, preferred_element_type=jnp.float32) + full_b_back.astype(
        jnp.float32
    )
    resid_two = normed + branch
    final_norm, norm_two_back = jax.vjp(
        layer_norm, resid_two, full_gain_two.astype(jnp.float32), full_shift_two.astype(jnp.float32)
    )
    output = final_norm.astype(jnp.bfloat16).reshape(seq_count, group_len, model_width)
    back_qkv, back_out, back_in, back_back = (
        lax.all_gather(w_qkv, ("dp", "ctx"), axis=0, tiled=True),
        lax.all_gather(w_out, ("dp", "ctx"), axis=0, tiled=True),
        lax.all_gather(w_in, ("dp", "ctx"), axis=0, tiled=True),
        lax.all_gather(w_back, ("dp", "ctx"), axis=0, tiled=True),
    )
    d_final = cotangent.reshape(tok_count, model_width).astype(jnp.float32)
    d_two, grad_gain_two, grad_shift_two = norm_two_back(d_final)
    d_branch = d_two.astype(jnp.bfloat16)
    grad_b_back = jnp.sum(d_branch.astype(jnp.float32), axis=0)
    grad_w_back = jnp.einsum("tf,td->fd", activ, d_branch, preferred_element_type=jnp.float32)
    d_activ = jnp.einsum("td,fd->tf", d_branch, back_back, preferred_element_type=jnp.float32)
    d_pre = gelu_back(d_activ)[0].astype(jnp.bfloat16)
    grad_b_in = jnp.sum(d_pre.astype(jnp.float32), axis=0)
    grad_w_in = jnp.einsum("td,tf->df", normed_low, d_pre, preferred_element_type=jnp.float32)
    d_normed = d_two + jnp.einsum("tf,df->td", d_pre, back_in, preferred_element_type=jnp.float32)
    d_one, grad_gain_one, grad_shift_one = norm_one_back(d_normed)
    d_attn = d_one.astype(jnp.bfloat16)
    grad_b_attn = jnp.sum(d_attn.astype(jnp.float32), axis=0)
    grad_w_out = jnp.einsum("ti,td->id", attended, d_attn, preferred_element_type=jnp.float32)
    d_attended = jnp.einsum(
        "td,id->ti", d_attn, back_out, preferred_element_type=jnp.float32
    ).astype(jnp.bfloat16)
    key_back, value_back = (
        lax.all_gather(key_local, "ctx", axis=1, tiled=True),
        lax.all_gather(value_local, "ctx", axis=1, tiled=True),
    )
    grad_heads = d_attended.reshape(seq_count, group_len, HEADS, HEAD_DIM)
    d_query_part, d_key_part, d_value_part = lax.map(
        attend_backward,
        (
            query_heads,
            key_back.reshape(seq_count, seq_len, HEADS, HEAD_DIM),
            value_back.reshape(seq_count, seq_len, HEADS, HEAD_DIM),
            grad_heads,
            log_total,
            segments,
            key_ids,
        ),
    )
    d_key_sum, d_value_sum = (
        lax.psum_scatter(
            d_key_part.astype(jnp.bfloat16), "ctx", scatter_dimension=1, tiled=True
        ).astype(jnp.float32),
        lax.psum_scatter(
            d_value_part.astype(jnp.bfloat16), "ctx", scatter_dimension=1, tiled=True
        ).astype(jnp.float32),
    )
    d_queries = d_query_part.reshape(tok_count, model_width).astype(jnp.bfloat16)
    d_keys = d_key_sum.reshape(tok_count, model_width).astype(jnp.bfloat16)
    d_values = d_value_sum.reshape(tok_count, model_width).astype(jnp.bfloat16)
    d_proj = jnp.concatenate([d_queries, d_keys, d_values], axis=1)
    grad_w_qkv = jnp.einsum("td,te->de", tokens, d_proj, preferred_element_type=jnp.float32)
    grad_b_query = jnp.sum(d_queries.astype(jnp.float32), axis=0)
    grad_b_value = jnp.sum(d_values.astype(jnp.float32), axis=0)
    input_grad = d_one + jnp.einsum(
        "te,de->td", d_proj, back_qkv, preferred_element_type=jnp.float32
    )
    summed = (
        lax.psum_scatter(grad_w_qkv, ("dp", "ctx"), scatter_dimension=0, tiled=True),
        lax.psum_scatter(grad_b_query, ("dp", "ctx"), scatter_dimension=0, tiled=True),
        lax.psum_scatter(grad_b_value, ("dp", "ctx"), scatter_dimension=0, tiled=True),
        lax.psum_scatter(grad_w_out, ("dp", "ctx"), scatter_dimension=0, tiled=True),
        lax.psum_scatter(grad_b_attn, ("dp", "ctx"), scatter_dimension=0, tiled=True),
        lax.psum_scatter(grad_gain_one, ("dp", "ctx"), scatter_dimension=0, tiled=True),
        lax.psum_scatter(grad_shift_one, ("dp", "ctx"), scatter_dimension=0, tiled=True),
        lax.psum_scatter(grad_w_in, ("dp", "ctx"), scatter_dimension=0, tiled=True),
        lax.psum_scatter(grad_b_in, ("dp", "ctx"), scatter_dimension=0, tiled=True),
        lax.psum_scatter(grad_w_back, ("dp", "ctx"), scatter_dimension=0, tiled=True),
        lax.psum_scatter(grad_b_back, ("dp", "ctx"), scatter_dimension=0, tiled=True),
        lax.psum_scatter(grad_gain_two, ("dp", "ctx"), scatter_dimension=0, tiled=True),
        lax.psum_scatter(grad_shift_two, ("dp", "ctx"), scatter_dimension=0, tiled=True),
    )
    return (
        output,
        input_grad.reshape(seq_count, group_len, model_width),
        summed[0],
        summed[1],
        summed[2],
        summed[3],
        summed[4],
        summed[5],
        summed[6],
        summed[7],
        summed[8],
        summed[9],
        summed[10],
        summed[11],
        summed[12],
    )


def solution(mesh):
    placed = (
        P("dp", "ctx", None),
        P("dp", "ctx"),
        P(("dp", "ctx"), None),
        P(("dp", "ctx")),
        P(("dp", "ctx")),
        P(("dp", "ctx"), None),
        P(("dp", "ctx")),
        P(("dp", "ctx")),
        P(("dp", "ctx")),
        P(("dp", "ctx"), None),
        P(("dp", "ctx")),
        P(("dp", "ctx"), None),
        P(("dp", "ctx")),
        P(("dp", "ctx")),
        P(("dp", "ctx")),
        P("dp", "ctx", None),
    )
    fits = mesh.shape["dp"] == 4 and mesh.shape["ctx"] == 8
    return jax.shard_map(
        on_device_fast if fits else on_device_general,
        mesh=mesh,
        in_specs=placed,
        out_specs=(
            P("dp", "ctx", None),
            P("dp", "ctx", None),
            P(("dp", "ctx"), None),
            P(("dp", "ctx")),
            P(("dp", "ctx")),
            P(("dp", "ctx"), None),
            P(("dp", "ctx")),
            P(("dp", "ctx")),
            P(("dp", "ctx")),
            P(("dp", "ctx"), None),
            P(("dp", "ctx")),
            P(("dp", "ctx"), None),
            P(("dp", "ctx")),
            P(("dp", "ctx")),
            P(("dp", "ctx")),
        ),
        check_vma=False,
    )
```

```python
import functools
import jax
import jax.numpy as jnp
from jax import lax
from jax.experimental import pallas as pl
from jax.experimental.pallas import tpu as pltpu
from jax.sharding import PartitionSpec as P

HEADS = 12
HEAD_DIM = 64
layer_eps = 1e-12
MESH_ID = pl.DeviceIdType.MESH
BF = jnp.bfloat16
F32 = jnp.float32
VMEM_LIMIT = 64 * 1024 * 1024 - 65536
SCORE_SCALE = 0.125 * 1.4426950408889634
EXCLUDE = -1e30


def place():
    d = lax.axis_index("dp")
    t = lax.axis_index("ctx")
    z = t // 2
    c = t % 2
    dx = d + 1 - 2 * (d % 2)
    dy = (d + 2) % 4
    return d, t, z, c, dx, dy


def remote(src, dst, ss, rs, dev):
    return pltpu.make_async_remote_copy(
        src_ref=src, dst_ref=dst, send_sem=ss, recv_sem=rs, device_id=dev, device_id_type=MESH_ID
    )


def greet(devices):
    bar = pltpu.get_barrier_semaphore()
    for dev in devices:
        pl.semaphore_signal(bar, inc=1, device_id=dev, device_id_type=MESH_ID)
    pl.semaphore_wait(bar, len(devices))


QB = 256
KB = 256
NH = 3


def marks_of(ids_row):
    kinds = lax.broadcasted_iota(jnp.int32, (16, ids_row.shape[1]), 0).astype(F32)
    return kinds == ids_row


N_ARR = 7
WIDE = (0, 1, 2)
EARLY = (3, 4, 5, 6)
FIRST_X = (0, 1, 3)
FIRST_Y = (2, 4, 5, 6)


def window(i):
    return (i // 4) * (i % 4), 8 - (1 - i // 4) * (3 - i % 4)


def front_kernel(x, seg, wi, wo, wb, vs, bv, wq,
                 xs, ids, gi, go, gb, fv, bi, att, qkv, o32, lse, wt,
                 idb, sm, gs, gq, ka, va, qa, sb,
                 loc, s_x, r_x, s_xf, s_xd, r_xd, s_z, r_z, s_up, s_dn, s_px, r_px, s_py, r_py, s_f, r_f,
                 s_c, r_c, s_e, r_e):
    d, t, z, c, dx, dy = place()
    h = z // 2
    zp = z + 1 - 2 * (z % 2)
    inner = (z + h) % 2 == 1
    dxy = (dx + 2) % 4
    z1, z2 = 2 - h, 3 * (1 - h)
    others = [zp, z1, z2]
    far = [z1, z2]
    me = lambda zz: (d, zz * 2 + c)
    core = (d, z * 2 + 1 - c)
    nx, ny = (dx, t), (dy, t)
    for hh in range(2):
        idb[hh] = jnp.broadcast_to(seg[hh:hh + 1].astype(F32), idb.shape[1:])
    sm[...] = jnp.zeros_like(sm)
    sm[0:8, 0:24] = vs[...].astype(F32)
    sm[8:9, 0:96] = bv[...].astype(F32)
    greet([(d, (t + k) % 8) for k in range(1, 8)] + [nx, ny])
    sends = []

    def go_(cp):
        cp.start()
        sends.append(cp)

    def got(ref, ss, rs, dev):
        remote(ref, ref, ss, rs, dev).wait_recv()

    per = wq.shape[2] // 6
    dst = [gi, go, gb, gs, gq.at[0], gq.at[1], gq.at[2]]

    def mine(a, zz):
        if a < 4:
            return (wi, wo, wb, sm)[a]
        return wq.at[:, :, pl.ds(pl.multiple_of((a - 4) * 2 * per + (zz % 2) * per, per), per)]

    half = x.shape[1] // 2

    def piece(k, hh, tt):
        if k == 2:
            return idb.at[hh], ids.at[tt]
        rows = pl.ds(k * half, half)
        return x.at[hh, rows], xs.at[tt, rows]

    for a in EARLY:
        for k in range(3):
            zz = others[k]
            go_(remote(mine(a, zz), dst[a].at[d, z, c], s_z.at[a - 3, k], r_z.at[a, z], me(zz)))

    def plane(arrs, zz, first):
        for a in arrs:
            src = mine(a, z) if first else dst[a].at[d, zz, c]
            go_(remote(src, dst[a].at[d, zz, c], s_px.at[a, zz], r_px.at[a, zz], nx))
            go_(remote(src, dst[a].at[d, zz, c], s_py.at[a, zz], r_py.at[a, zz], ny))

    plane(EARLY, z, True)
    for k in (2, 0, 1):
        src, to = piece(k, 1 - h, t)
        go_(remote(src, to, s_x.at[0, k], r_x.at[z, k], me(z1)))
        src, to = piece(k, h, t)
        go_(remote(src, to, s_x.at[1, k], r_x.at[z, k], me(zp)))

    def chain(zz, first, wait):
        for a in WIDE:
            src = mine(a, z) if first else dst[a].at[d, zz, c]
            up = remote(src, dst[a].at[d, zz, c], s_up.at[a, zz], r_z.at[a, zz], me((z + 1) % 4))
            dn = remote(src, dst[a].at[d, zz, c], s_dn.at[a, zz], r_z.at[a, zz], me((z + 3) % 4))

            @pl.when(jnp.logical_and(zz <= z, z < 3))
            def _(up=up):
                if wait:
                    up.wait_send()
                else:
                    up.start()

            @pl.when(jnp.logical_and(zz >= z, z > 0))
            def _(dn=dn):
                if wait:
                    dn.wait_send()
                else:
                    dn.start()

    chain(z, True, False)
    plane(WIDE, z, True)
    locals_ = [pltpu.make_async_copy(piece(k, h, t)[0], piece(k, h, t)[1], loc.at[N_ARR + k]) for k in range(3)]
    for a in (4, 5, 6, 3, 0, 1, 2):
        locals_.append(pltpu.make_async_copy(mine(a, z), dst[a].at[d, z, c], loc.at[a]))
    for cp in locals_:
        cp.start()

    def forward(arrs, zz):
        for a in arrs:
            if a in FIRST_Y:
                got(dst[a].at[dy, zz, c], s_py.at[a, zz], r_py.at[a, zz], ny)
                go_(remote(dst[a].at[dy, zz, c], dst[a].at[dy, zz, c], s_f.at[a, zz], r_f.at[a, zz], nx))
            else:
                got(dst[a].at[dx, zz, c], s_px.at[a, zz], r_px.at[a, zz], nx)
                go_(remote(dst[a].at[dx, zz, c], dst[a].at[dx, zz, c], s_f.at[a, zz], r_f.at[a, zz], ny))

    def across(arrs, zz):
        for a in arrs:
            if a in FIRST_Y:
                got(dst[a].at[dx, zz, c], s_px.at[a, zz], r_px.at[a, zz], nx)
                got(dst[a].at[dxy, zz, c], s_f.at[a, zz], r_f.at[a, zz], nx)
            else:
                got(dst[a].at[dy, zz, c], s_py.at[a, zz], r_py.at[a, zz], ny)
                got(dst[a].at[dxy, zz, c], s_f.at[a, zz], r_f.at[a, zz], ny)
            go_(remote(dst[a].at[:, zz, c], dst[a].at[:, zz, c], s_c.at[a, zz], r_c.at[a, zz], core))

    def crossed(arrs, zz):
        for a in arrs:
            ref = dst[a].at[:, zz, 1 - c]
            got(ref, s_c.at[a, zz], r_c.at[a, zz], core)

    def arrive(arrs, k):
        for a in arrs:
            got(dst[a].at[d, others[k], c], s_z.at[0, 0], r_z.at[a, others[k]], me(others[k]))

    for k in range(3):
        arrive(EARLY, k)
        plane(EARLY, others[k], False)
    for cp in locals_[:7]:
        cp.wait()
    for zz in [z] + others:
        forward(EARLY, zz)

    def relay(k, wait):
        for j in range(2):
            ref = piece(k, h, far[j] * 2 + c)[1]
            cp = remote(ref, ref, s_xf.at[j, k], r_x.at[far[j], k], me(zp))

            @pl.when(inner)
            def _(cp=cp):
                if wait:
                    cp.wait_send()
                else:
                    cp.wait_recv()
                    cp.start()

    def relayed(k):
        for j in range(2):
            ref = piece(k, h, far[j] * 2 + c)[1]

            @pl.when(jnp.logical_not(inner))
            def _(ref=ref, j=j):
                got(ref, s_x.at[0, k], r_x.at[far[j], k], me(zp))

    def to_core(zz):
        for k in range(3):
            ref = piece(k, h, zz * 2 + c)[1]
            go_(remote(ref, ref, s_xd.at[zz, k], r_xd.at[zz, k], core))

    def from_core(zz):
        for k in range(3):
            got(piece(k, h, zz * 2 + 1 - c)[1], s_xd.at[zz, k], r_xd.at[zz, k], core)

    to_core(z)
    for k in (2, 0):
        relay(k, False)
    for zz in [z] + others:
        across(EARLY, zz)
    relay(1, False)
    for k in range(3):
        got(piece(k, h, zp * 2 + c)[1], s_x.at[1, k], r_x.at[zp, k], me(zp))
    to_core(zp)
    for zz in [z] + others:
        crossed(EARLY, zz)
    width = wt.shape[3]
    for j in range(3):
        for q in range(2):
            w = gq[j, 2 * q:2 * q + 2].astype(F32).reshape(width // 2, per)
            w = w.T.astype(BF)
            for cc in range(2):
                wt[j, cc, :, q * (width // 2):(q + 1) * (width // 2)] = w[cc * (per // 2):(cc + 1) * (per // 2)]
    group = (z % 2) * 2 + c
    span = x.shape[1]

    def column(row):
        v = gs[group, :, :, row].reshape(8, 128).T
        return jnp.concatenate([v[:24, r:r + 1] for r in range(8)], axis=0)

    bias = [column(0), None, column(1)]
    for g in range(NH):
        va[g, 64:] = jnp.ones((16, va.shape[2]), BF)

    def project(zz):
        def one(j, _):
            tb = zz * 2 + j
            cols = pl.ds(pl.multiple_of(tb * span, span), span)
            xb = xs[tb]
            hit = marks_of(ids[tb, 0:1])
            ones = jnp.where(hit, 1.0, 0.0)
            away = jnp.where(hit, 0.0, EXCLUDE).astype(BF)
            for s in range(3):
                r = lax.dot_general(wt[s, c], xb, (((1,), (1,)), ((), ())), preferred_element_type=F32)
                if bias[s] is not None:
                    r = r + bias[s]
                low = r.astype(BF)
                qkv[s, :, cols] = low
                for g in range(NH):
                    part = low[g * 64:(g + 1) * 64]
                    if s == 0:
                        qa[g, :64, cols] = part
                        qa[g, 64:, cols] = away
                    elif s == 1:
                        ka[g, cols, :] = jnp.concatenate([part.astype(F32), ones], axis=0).T.astype(BF)
                    else:
                        va[g, :64, cols] = part
            return 0

        lax.fori_loop(0, 2, one, 0)

    forward(WIDE, z)
    for zz in (z, zp):
        from_core(zz)
        project(zz)
    for k in (2, 0, 1):
        relayed(k)
    for zz in far:
        to_core(zz)
    for zz in far:
        from_core(zz)
        project(zz)

    def attend(k):
        i = (t + k) % 8
        cols = pl.ds(pl.multiple_of(i * QB, QB), QB)
        lo, hi = window(i)

        def block(j, carry):
            at = pl.ds(pl.multiple_of(j * KB, KB), KB)
            out = []
            s = [jnp.dot(ka[g, at, :], qa[g, :, cols], preferred_element_type=F32) for g in range(NH)]
            for g in range(NH):
                m, acc = carry[g]
                m2 = jnp.maximum(m, jnp.max(s[g], axis=0, keepdims=True))
                p = jnp.exp2((s[g] - m2) * SCORE_SCALE).astype(BF)
                acc = acc * jnp.exp2((m - m2) * SCORE_SCALE) + jnp.dot(
                    va[g, :, at], p, preferred_element_type=F32)
                out.append((m2, acc))
            return tuple(out)

        first = tuple((jnp.full((1, QB), -3e38, F32), jnp.zeros((80, QB), F32)) for _ in range(NH))
        res = lax.fori_loop(lo, hi, block, first)
        for g in range(NH):
            m, acc = res[g]
            total = acc[64:65]
            o = acc[:64] / total
            o32[i, g * 64:(g + 1) * 64] = o
            if k:
                sb[i, g * 64:(g + 1) * 64] = o.astype(BF)
            else:
                att[t, g * 64:(g + 1) * 64] = o.astype(BF)
            lse[g, pl.ds(i, 1)] = m * SCORE_SCALE + jnp.log2(total)
        if k:
            go_(remote(sb.at[i], att.at[t], s_e.at[k - 1], r_e.at[k - 1], (d, i)))

    def onward(k):
        arrive(WIDE, k)
        chain(others[k], False, False)
        plane(WIDE, others[k], False)

    order = ORDER_K
    onward(0)
    attend(order[0])
    attend(order[1])
    for cp in locals_[7:]:
        cp.wait()
    across(WIDE, z)
    onward(1)
    attend(order[2])
    attend(order[3])
    forward(WIDE, zp)
    onward(2)
    attend(order[4])
    attend(order[5])
    forward(WIDE, z1)
    across(WIDE, zp)
    attend(order[6])
    attend(order[7])
    forward(WIDE, z2)
    across(WIDE, z1)
    across(WIDE, z2)
    for r in range(32):
        v = gs.at[r // 8, (r // 2) % 4, r % 2]
        fv[:, 24 * r:24 * r + 24] = v[0:8, 0:24]
        bi[:, 96 * r:96 * r + 96] = v[8:9, 0:96]
    for zz in [z] + others:
        crossed(WIDE, zz)
    for k in range(1, 8):
        src = (t + 8 - k) % 8
        got(att.at[src], s_e.at[k - 1], r_e.at[k - 1], (d, src))
    for cp in sends:
        cp.wait_send()
    chain(z, True, True)
    for zz in others:
        chain(zz, False, True)
    for k in range(3):
        relay(k, True)


ORDER_K = (4, 3, 5, 2, 6, 1, 7, 0)


def any_spec():
    return pl.BlockSpec(memory_space=pl.ANY)


def vmem_spec():
    return pl.BlockSpec(memory_space=pltpu.VMEM)


def dma(*shape):
    return pltpu.SemaphoreType.DMA(shape)


def front(x, seg, wi, wo, wb, vs, bv, wq):
    span, width = x.shape[1:]
    n = 8 * span
    per = width // 4
    grid_of = lambda a: jax.ShapeDtypeStruct((4, 4, 2) + a.shape, a.dtype)
    return pl.pallas_call(
        front_kernel,
        out_shape=[
            jax.ShapeDtypeStruct((8, span, width), x.dtype),
            jax.ShapeDtypeStruct((8, 8, span), F32),
            grid_of(wi), grid_of(wo), grid_of(wb),
            jax.ShapeDtypeStruct((8, width), F32), jax.ShapeDtypeStruct((1, wi.shape[2]), F32),
            jax.ShapeDtypeStruct((8, per, span), BF),
            jax.ShapeDtypeStruct((3, per, n), BF),
            jax.ShapeDtypeStruct((8, per, span), F32),
            jax.ShapeDtypeStruct((NH, 8, span), F32),
            jax.ShapeDtypeStruct((3, 2, per, width), BF),
        ],
        in_specs=[any_spec(), vmem_spec()] + [any_spec()] * 3 + [vmem_spec()] * 2 + [any_spec()],
        out_specs=[vmem_spec()] * 2 + [any_spec()] * 3 + [vmem_spec()] * 7,
        scratch_shapes=[
            pltpu.VMEM((2, 8, span), F32), pltpu.VMEM((16, 128), F32), pltpu.VMEM((4, 4, 2, 16, 128), F32),
            pltpu.VMEM((3, 4, 4, 2) + wq.shape[:2] + (2 * per,), BF),
            pltpu.VMEM((NH, n, 80), BF), pltpu.VMEM((NH, 80, n), BF), pltpu.VMEM((NH, 80, n), BF),
            pltpu.VMEM((8, per, span), BF),
            dma(N_ARR + 3), dma(2, 3), dma(4, 3), dma(2, 3), dma(4, 3), dma(4, 3), dma(4, 3), dma(N_ARR, 4),
            dma(3, 4), dma(3, 4),
            dma(N_ARR, 4), dma(N_ARR, 4), dma(N_ARR, 4), dma(N_ARR, 4), dma(N_ARR, 4), dma(N_ARR, 4),
            dma(N_ARR, 4), dma(N_ARR, 4), dma(7), dma(7),
        ],
        compiler_params=pltpu.CompilerParams(
            collective_id=1, has_side_effects=True, vmem_limit_bytes=VMEM_LIMIT),
        name="front",
    )(x, seg, wi, wo, wb, vs, bv, wq)


def back_kernel(dat, di, do_, db, ds_, qkv, ids, o32, lse, wt, xs, d_one,
                ox, oi, oo, ob, os_, oq, *rest):
    rd, own, r1, r2, r3, r4, r5 = [rest[4 * i:4 * i + 4] for i in range(7)]
    (da, ka, qa, vk, dkv, pr, xv, dxp, dw, lq, lv,
     xd, x3, x4, x5, q0, q1, q2, qr, v0, v1, v2, vr,
     loc, s_e, r_e, s_d, r_d, s_1, r_1, s_2, r_2, s_3, r_3, s_4, r_4, s_5, r_5,
     s_q1, r_q1, s_q2, r_q2, s_qe, r_qe) = rest[28:]
    d, t, z, c, dx, dy = place()
    x, y = d % 2, d // 2
    h = z // 2
    zp = z + 1 - 2 * (z % 2)
    inner = (z + h) % 2 == 1
    me = lambda zz: (d, zz * 2 + c)
    core = (d, z * 2 + 1 - c)
    nx, ny = (dx, t), (dy, t)
    line = [(t + k) % 8 for k in range(1, 8)]
    far = [2 * (1 - h), 2 * (1 - h) + 1]
    order = [far[0], far[1], zp, z]
    group = (z % 2) * 2 + c
    part = [di, do_, db, ds_]
    outs = [oi, oo, ob, os_.at[pl.ds(0, 8)]]
    by_x = [True, True, False, True]
    sends = []
    greet([(d, o) for o in line] + [nx, ny])

    def go_(cp):
        cp.start()
        sends.append(cp)

    def got(ref, ss, rs, dev):
        remote(ref, ref, ss, rs, dev).wait_recv()

    for k in NEAR[1:]:
        i = line[k - 1]
        go_(remote(dat.at[i], da.at[t], s_e.at[k - 1], r_e.at[k - 1], (d, i)))
    for n_, zz in enumerate(order):
        for a in range(4):
            for yy in range(2):
                go_(remote(part[a].at[yy, :, zz, 1 - c], rd[a].at[yy, :, zz], s_d.at[1 + 2 * a + yy, n_],
                           r_d.at[1 + 2 * a + yy, n_], core))
    local = []

    def here(src, to):
        cp = pltpu.make_async_copy(src, to, loc.at[len(local)])
        cp.start()
        local.append(cp)

    here(dat.at[t], da.at[t])
    for a in range(4):
        for yy in range(2):
            here(part[a].at[yy, :, :, c], own[a].at[yy])
    here(xs, xv)

    n = qkv.shape[2]
    span = da.shape[2]

    def fill(tb, _):
        cols = pl.ds(pl.multiple_of(tb * span, span), span)
        hit = marks_of(ids[tb, 0:1])
        ones = jnp.where(hit, 1.0, 0.0)
        away = jnp.where(hit, 0.0, EXCLUDE).astype(BF)
        for g in range(NH):
            rows = slice(g * 64, (g + 1) * 64)
            ka[g, cols, :] = jnp.concatenate([qkv[1, rows, cols].astype(F32), ones], axis=0).T.astype(BF)
            vk[g, cols, :] = qkv[2, rows, cols].astype(F32).T.astype(BF)
            qa[g, :64, cols] = qkv[0, rows, cols]
            qa[g, 64:, cols] = away
            dkv[g, cols, :] = jnp.zeros((span, 128), F32)
        return 0

    lax.fori_loop(0, 8, fill, 0)

    def attend(k):
        i = (t + 8 - k) % 8
        if k:
            got(da.at[i], s_e.at[k - 1], r_e.at[k - 1], (d, i))
        cols = pl.ds(pl.multiple_of(i * QB, QB), QB)
        lo, hi = window(i)
        fixed = []
        for g in range(NH):
            rows = slice(g * 64, (g + 1) * 64)
            do = da[i, rows].astype(F32)
            inside = jnp.sum(do * o32[i, rows], axis=0, keepdims=True)
            zero = jnp.zeros((64, QB), F32)
            ra = jnp.concatenate([do, zero], axis=0).T.astype(BF)
            rb = jnp.concatenate([zero, qkv[0, rows, cols].astype(F32)], axis=0).T.astype(BF)
            fixed.append((inside, lse[g, pl.ds(i, 1)], ra, rb))

        def block(j, carry):
            at = pl.ds(pl.multiple_of(j * KB, KB), KB)
            out = []
            s = [jnp.dot(ka[g, at, :], qa[g, :, cols], preferred_element_type=F32) for g in range(NH)]
            dp = [jnp.dot(vk[g, at, :], da[i, g * 64:(g + 1) * 64], preferred_element_type=F32)
                  for g in range(NH)]
            for g in range(NH):
                inside, lse_i, ra, rb = fixed[g]
                p = jnp.exp2(s[g] * SCORE_SCALE - lse_i)
                ds = (p * (dp[g] - inside)).astype(BF)
                dkv[g, at, :] += jnp.dot(p.astype(BF), ra, preferred_element_type=F32) + jnp.dot(
                    ds, rb, preferred_element_type=F32)
                out.append(carry[g] + jnp.dot(qkv[1, g * 64:(g + 1) * 64, at], ds, preferred_element_type=F32))
            return tuple(out)

        dq = lax.fori_loop(lo, hi, block, tuple(jnp.zeros((64, QB), F32) for _ in range(NH)))
        for g in range(NH):
            pr[0, g * 64:(g + 1) * 64, cols] = (dq[g] * 0.125).astype(BF)

    def add_rows(dst, src):
        def step(i, _):
            dst[i] = dst[i] + src[i]
            return 0

        lax.fori_loop(0, dst.shape[0], step, 0)

    def add_tok(dst, src):
        def step(i, _):
            at = pl.ds(pl.multiple_of(i * 32, 32), 32)
            dst[at, :] = dst[at, :] + src[at, :]
            return 0

        lax.fori_loop(0, dst.shape[0] // 32, step, 0)

    def first(n_):
        zz = order[n_]
        for a in range(4):
            for yy in range(2):
                got(rd[a].at[yy, :, zz], s_d.at[1 + 2 * a + yy, n_], r_d.at[1 + 2 * a + yy, n_], core)
                for xx in range(2):
                    add_rows(rd[a].at[yy, xx, zz], own[a].at[yy, xx, zz])
            if by_x[a]:
                go_(remote(rd[a].at[:, 1 - x, zz], r1[a].at[n_], s_1.at[a, n_], r_1.at[a, n_], nx))
            else:
                go_(remote(rd[a].at[1 - y, :, zz], r1[a].at[n_], s_1.at[a, n_], r_1.at[a, n_], ny))

    def second(n_):
        zz = order[n_]
        for a in range(4):
            got(r1[a].at[n_], s_1.at[a, n_], r_1.at[a, n_], nx if by_x[a] else ny)
            for w in range(2):
                add_rows(rd[a].at[w, x, zz] if by_x[a] else rd[a].at[y, w, zz], r1[a].at[n_, w])
            if by_x[a]:
                go_(remote(rd[a].at[1 - y, x, zz], r2[a].at[n_], s_2.at[a, n_], r_2.at[a, n_], ny))
            else:
                go_(remote(rd[a].at[y, 1 - x, zz], r2[a].at[n_], s_2.at[a, n_], r_2.at[a, n_], nx))

    def to_inner(a, n_):
        ref = xd.at[far[n_]] if a == 4 else rd[a].at[y, x, far[n_]]
        land = x3 if a == 4 else r3[a]
        return remote(ref, land.at[n_], s_3.at[a, n_], r_3.at[a, n_], me(zp))

    def to_far(a, n_):
        ref = xd.at[far[n_]] if a == 4 else rd[a].at[y, x, far[n_]]
        return remote(ref, x4 if a == 4 else r4[a], s_4.at[a, n_], r_4.at[a], me(far[n_]))

    def third(n_):
        zz = order[n_]
        for a in range(4):
            got(r2[a].at[n_], s_2.at[a, n_], r_2.at[a, n_], ny if by_x[a] else nx)
            add_rows(rd[a].at[y, x, zz], r2[a].at[n_])
            if n_ < 2:
                @pl.when(jnp.logical_not(inner))
                def _(a=a):
                    to_inner(a, n_).start()
            elif n_ == 2:
                go_(remote(rd[a].at[y, x, zz], r5[a], s_5.at[a], r_5.at[a], me(zz)))

    def fourth(n_, arrs):
        @pl.when(inner)
        def _():
            for a in arrs:
                to_inner(a, n_).wait_recv()
                if a == 4:
                    add_tok(xd.at[far[n_]], x3.at[n_])
                else:
                    add_rows(rd[a].at[y, x, far[n_]], r3[a].at[n_])
                to_far(a, n_).start()

    for cp in local:
        cp.wait()
    first(0)
    first(1)
    attend(NEAR[0])
    attend(NEAR[1])
    second(0)
    first(2)
    attend(NEAR[2])
    attend(NEAR[3])
    second(1)
    first(3)
    attend(NEAR[4])
    third(0)
    attend(NEAR[5])
    second(2)
    attend(NEAR[6])
    third(1)
    fourth(0, range(4))
    attend(NEAR[7])
    second(3)
    for g in range(NH):
        rows = slice(g * 64, (g + 1) * 64)
        flip = dkv[g].T
        pr[1, rows] = (flip[64:] * 0.125).astype(BF)
        pr[2, rows] = flip[:64].astype(BF)

    def token_grad(tb):
        cols = pl.ds(pl.multiple_of(tb * span, span), span)
        acc = None
        for s in range(3):
            term = jnp.dot(pr[s, :, cols].astype(F32).T.astype(BF), wt[s, c], preferred_element_type=F32)
            acc = term if acc is None else acc + term
        dxp[tb] = acc.astype(BF)

    def token_pair(j, _):
        token_grad(j * 2 + 1 - c)
        return 0

    per = pr.shape[1]
    width = wt.shape[3]

    def weight_grad(n_, q):
        xall = xv[:, :, pl.ds(pl.multiple_of(q * (width // 2), 128), width // 2)].reshape(n, width // 2)
        for s in range(3):
            dw[s * per:(s + 1) * per] = jnp.dot(pr[s], xall, preferred_element_type=F32)
        lq[q] = dw[...].T.reshape(lq.shape[1:]).astype(BF)
        go_(remote(lq.at[q, 1 - x], q1.at[q], s_q1.at[n_], r_q1.at[n_], nx))

    def summed(yy):
        for zc in range(8):
            at = (zc // 2, zc % 2)
            q0[(yy,) + at] = q1[(yy,) + at] + lq[(yy, x) + at]

    lax.fori_loop(0, 4, token_pair, 0)
    for n_, zz in enumerate(order):
        go_(remote(dxp.at[zz * 2 + 1 - c], xd.at[zz], s_d.at[0, n_], r_d.at[0, n_], core))
    third(2)
    fourth(1, range(4))
    weight_grad(0, 1 - y)
    def token_mine(j, _):
        token_grad(j * 2 + c)
        return 0

    lax.fori_loop(0, 4, token_mine, 0)
    for n_, zz in enumerate(order):
        got(xd.at[zz], s_d.at[0, n_], r_d.at[0, n_], core)
        add_tok(xd.at[zz], dxp.at[zz * 2 + c])
        if n_ < 2:
            @pl.when(jnp.logical_not(inner))
            def _(n_=n_):
                to_inner(4, n_).start()
        elif n_ == 2:
            go_(remote(xd.at[zz], x5, s_5.at[4], r_5.at[4], me(zz)))
    weight_grad(1, y)
    lv[...] = jnp.zeros_like(lv)
    for row, s in ((0, 0), (1, 2)):
        col = jnp.sum(pr[s].astype(F32), axis=1, keepdims=True)
        for r in range(8):
            piece = jnp.broadcast_to(col[24 * r:24 * r + 24], (24, 128)).T
            lv[group // 2, group % 2, r // 2, r % 2, row:row + 1, :24] = piece[0:1]
    go_(remote(lv.at[:, 1 - x], v1, s_q1.at[2], r_q1.at[2], nx))
    got(q1.at[1 - y], s_q1.at[0], r_q1.at[0], nx)
    summed(1 - y)
    go_(remote(q0.at[1 - y], q2, s_q2.at[0], r_q2.at[0], ny))
    got(v1, s_q1.at[2], r_q1.at[2], nx)
    for yy in range(2):
        for zc in range(8):
            at = (zc // 2, zc % 2)
            v0[(yy,) + at] = v1[(yy,) + at] + lv[(yy, x) + at]
    go_(remote(v0.at[1 - y], v2, s_q2.at[1], r_q2.at[1], ny))
    third(3)
    fourth(0, (4,))
    got(q1.at[y], s_q1.at[1], r_q1.at[1], nx)
    summed(y)
    got(q2, s_q2.at[0], r_q2.at[0], ny)
    got(v2, s_q2.at[1], r_q2.at[1], ny)
    for zc in range(8):
        at = (zc // 2, zc % 2)
        q0[(y,) + at] = q0[(y,) + at] + q2[at]
        v0[(y,) + at] = v0[(y,) + at] + v2[at]
    for k in range(1, 8):
        to = line[k - 1]
        go_(remote(q0.at[y, to // 2, to % 2], qr.at[t], s_qe.at[0, k - 1], r_qe.at[0, k - 1], (d, to)))
        go_(remote(v0.at[y, to // 2, to % 2], vr.at[t], s_qe.at[1, k - 1], r_qe.at[1, k - 1], (d, to)))
    qr[t] = q0[y, z, c]
    vr[t] = v0[y, z, c]
    fourth(1, (4,))
    src_in = 2 - h
    for a in range(4):
        got(r5[a], s_5.at[a], r_5.at[a], me(zp))
        got(r4[a], s_4.at[a, 0], r_4.at[a], me(src_in))
        acc = rd[a].at[y, x, z]
        for i in range(acc.shape[0]):
            outs[a][i] = acc[i].astype(F32) + r5[a][i].astype(F32) + r4[a][i].astype(F32)
    got(x5, s_5.at[4], r_5.at[4], me(zp))
    got(x4, s_4.at[4, 0], r_4.at[4], me(src_in))

    def tok(i, _):
        at = pl.ds(pl.multiple_of(i * 32, 32), 32)
        ox[h, at, :] = d_one[h, at, :] + (xd[z, at, :].astype(F32) + x5[at, :].astype(F32))
        ox[1 - h, at, :] = d_one[1 - h, at, :] + x4[at, :].astype(F32)
        return 0

    lax.fori_loop(0, span // 32, tok, 0)
    for k in range(1, 8):
        src = (t + 8 - k) % 8
        got(qr.at[src], s_qe.at[0, k - 1], r_qe.at[0, k - 1], (d, src))
        got(vr.at[src], s_qe.at[1, k - 1], r_qe.at[1, k - 1], (d, src))
    for g in range(4):
        oq[g] = qr[g].astype(F32) + qr[4 + g].astype(F32)
    total = vr[0]
    for k in range(1, 8):
        total = total + vr[k]
    os_[8:16] = total
    for cp in sends:
        cp.wait_send()
    for n_ in range(2):
        @pl.when(jnp.logical_not(inner))
        def _(n_=n_):
            for a in range(5):
                to_inner(a, n_).wait_send()

        @pl.when(inner)
        def _(n_=n_):
            for a in range(5):
                to_far(a, n_).wait_send()


NEAR = (0, 1, 7, 2, 6, 3, 5, 4)


def back(dat, di, do_, db, ds_, qkv, ids, o32, lse, wt, xs, d_one):
    arrs = [di, do_, db, ds_]
    tails = [a.shape[4:] for a in arrs]
    per, width = wt.shape[2:]
    n = qkv.shape[2]
    tok = xs.shape[1:]
    qt = di.shape[4:6] + (3 * per,)
    vt = (8, 128)
    scratch = []
    for lead in ((2, 2, 4), (2, 2, 4), (4, 2), (4,), (2,), (), ()):
        for a, tail in zip(arrs, tails):
            scratch.append(pltpu.VMEM(lead + tail, a.dtype))
    grid = (2, 2, 4, 2)
    scratch += [
        pltpu.VMEM(dat.shape, BF),
        pltpu.VMEM((NH, n, 80), BF), pltpu.VMEM((NH, 80, n), BF), pltpu.VMEM((NH, n, 64), BF),
        pltpu.VMEM((NH, n, 128), F32), pltpu.VMEM((3, per, n), BF),
        pltpu.VMEM(xs.shape, BF), pltpu.VMEM(xs.shape, BF), pltpu.VMEM((3 * per, width // 2), F32),
        pltpu.VMEM(grid + qt, BF), pltpu.VMEM(grid + vt, F32),
        pltpu.VMEM((4,) + tok, BF), pltpu.VMEM((2,) + tok, BF), pltpu.VMEM(tok, BF), pltpu.VMEM(tok, BF),
        pltpu.VMEM((2, 4, 2) + qt, BF), pltpu.VMEM((2, 4, 2) + qt, BF), pltpu.VMEM((4, 2) + qt, BF),
        pltpu.VMEM((8,) + qt, BF),
        pltpu.VMEM((2, 4, 2) + vt, F32), pltpu.VMEM((2, 4, 2) + vt, F32), pltpu.VMEM((4, 2) + vt, F32),
        pltpu.VMEM((8,) + vt, F32),
        dma(10), dma(7), dma(7), dma(9, 4), dma(9, 4), dma(4, 4), dma(4, 4), dma(4, 4), dma(4, 4),
        dma(5, 2), dma(5, 2), dma(5, 2), dma(5), dma(5), dma(5),
        dma(3), dma(3), dma(2), dma(2), dma(2, 7), dma(2, 7),
    ]
    return pl.pallas_call(
        back_kernel,
        out_shape=[jax.ShapeDtypeStruct((2,) + tok, F32)]
        + [jax.ShapeDtypeStruct(tail, F32) for tail in tails[:3] + [(16, 128)]]
        + [jax.ShapeDtypeStruct((4,) + qt, F32)],
        in_specs=[any_spec()] * 5 + [vmem_spec()] * 5 + [any_spec(), vmem_spec()],
        out_specs=[vmem_spec()] * 6,
        scratch_shapes=scratch,
        compiler_params=pltpu.CompilerParams(
            collective_id=4, has_side_effects=True, vmem_limit_bytes=VMEM_LIMIT),
        name="back",
    )(dat, di, do_, db, ds_, qkv, ids, o32, lse, wt, xs, d_one)


def erf_parts(u):
    phi_c = 0.5 * (1.0 + lax.erf(u * 0.7071067811865476))
    return phi_c, phi_c + u * jnp.exp(-0.5 * u * u) * 0.3989422804014327


def norm_forward(r):
    center = r - jnp.mean(r, axis=-1, keepdims=True)
    inv = lax.rsqrt(jnp.mean(center * center, axis=-1, keepdims=True) + layer_eps)
    return center * inv, inv


def norm_backward(n, inv, gain, dy):
    gd = gain * dy
    return (gd - jnp.mean(gd, axis=-1, keepdims=True) - n * jnp.mean(gd * n, axis=-1, keepdims=True)) * inv


def mid_kernel(x, att, wo, wi, wb, fv, bi, cot,
               out, d_one, dat, g_in, g_out, g_back, g_small,
               vo, vi, vb, att_t, acc, n1, inv1, low, low_t, slope, act, act_t, d_pre, d_two, d_br, d_attn,
               yi, yo, yb, yx, yd, ys, part, sums, sum_in, sem_w, sem_o):
    tokens, width = x.shape
    span = tokens // 2
    ff = vi.shape[1]
    loads = [pltpu.make_async_copy(a, b, sem_w.at[k]) for k, (a, b) in enumerate(((wo, vo), (wi, vi), (wb, vb)))]
    for cp in loads:
        cp.start()
    outs = []

    def put(src, to):
        cp = pltpu.make_async_copy(src, to, sem_o.at[len(outs)])
        cp.start()
        outs.append(cp)

    def loop(count, size, fn):
        def one(j, _):
            fn(pl.ds(pl.multiple_of(j * size, size), size))
            return 0

        lax.fori_loop(0, count, one, 0)

    halves = (slice(0, span), slice(span, tokens))
    rb = tokens // 4
    nt = (((1,), (1,)), ((), ()))
    part[...] = jnp.zeros_like(part)

    def count_in(k, v):
        part[k] += jnp.sum(v.reshape(v.shape[0] // 8, 8, width), axis=0)

    for s in range(2):
        att_t[halves[s]] = att[s].astype(F32).T.astype(BF)
    loads[0].wait()
    for s in range(2):
        acc[halves[s]] = jnp.dot(att_t[halves[s]], vo[...], preferred_element_type=F32)

    def norm_one(r):
        n, inv = norm_forward(x[r].astype(F32) + acc[r] + fv[2:3])
        n1[r] = n
        inv1[r] = inv
        low[r] = (n * fv[3:4] + fv[4:5]).astype(BF)

    loop(4, rb, norm_one)
    loads[1].wait()

    def widen(f):
        pre = [jnp.dot(low[r], vi[:, f], preferred_element_type=F32) + bi[:, f] for r in halves]
        for r, u in zip(halves, pre):
            phi_c, sl = erf_parts(u)
            slope[r, f] = sl
            a = u * phi_c
            act[r, f] = a.astype(BF)
            act_t[f, r] = a.T.astype(BF)

    loop(ff // 256, 256, widen)
    loads[2].wait()

    def narrow(f):
        for r in halves:
            acc[r, f] = jnp.dot(act[r], vb[:, f], preferred_element_type=F32)

    loop(width // 256, 256, narrow)

    def norm_two(r):
        normed = n1[r] * fv[3:4] + fv[4:5]
        n2, inv2 = norm_forward(normed + acc[r] + fv[5:6])
        yx[r] = (n2 * fv[6:7] + fv[7:8]).astype(BF)
        dy = cot[r].astype(F32)
        d2 = norm_backward(n2, inv2, fv[6:7], dy)
        d_two[r] = d2
        d2 = d2.astype(BF)
        d_br[r] = d2
        count_in(3, d2.astype(F32))
        count_in(4, dy * n2)
        count_in(5, dy)

    loop(4, rb, norm_two)
    put(yx, out)

    def back_widen(f):
        da = [lax.dot_general(d_br[r], vb[f, :], nt, preferred_element_type=F32) for r in halves]
        total = None
        for r, v in zip(halves, da):
            dp = (v * slope[r, f]).astype(BF)
            d_pre[r, f] = dp
            col = jnp.sum(dp.astype(F32), axis=0, keepdims=True)
            total = col if total is None else total + col
        sum_in[:, f] = total

    loop(ff // 256, 256, back_widen)

    def back_narrow(k):
        for r in halves:
            acc[r, k] = lax.dot_general(d_pre[r], vi[k, :], nt, preferred_element_type=F32)

    loop(width // 256, 256, back_narrow)

    def back_one(r):
        dn = d_two[r] + acc[r]
        n = n1[r]
        d1 = norm_backward(n, inv1[r], fv[3:4], dn)
        d_one[r] = d1
        d1 = d1.astype(BF)
        d_attn[r] = d1
        count_in(0, d1.astype(F32))
        count_in(1, dn * n)
        count_in(2, dn)

    loop(4, rb, back_one)
    for s in range(2):
        yd[s] = lax.dot_general(vo[...], d_attn[halves[s]], nt, preferred_element_type=F32).astype(BF)
    put(yd, dat)

    def grad_back(f):
        yb[f, :] = jnp.dot(act_t[f, :], d_br[...], preferred_element_type=F32).astype(BF)

    loop(ff // 256, 256, grad_back)
    put(yb, g_back)
    for k in range(3):
        low_t[k * 256:(k + 1) * 256] = low[:, k * 256:(k + 1) * 256].astype(F32).T.astype(BF)
    for k in range(3):
        rows = slice(k * 256, (k + 1) * 256)

        def grad_in(f, rows=rows):
            yi[rows, f] = jnp.dot(low_t[rows], d_pre[:, f], preferred_element_type=F32).astype(BF)

        loop(ff // 768, 768, grad_in)
        put(yi.at[rows], g_in.at[rows])

    def grad_out(k):
        yo[k] = (jnp.dot(att[0, k], d_attn[halves[0]], preferred_element_type=F32)
                 + jnp.dot(att[1, k], d_attn[halves[1]], preferred_element_type=F32)).astype(BF)

    loop(3, 256, grad_out)
    put(yo, g_out)
    ys[...] = jnp.zeros_like(ys)
    for k in range(6):
        sums[k:k + 1] = jnp.sum(part[k], axis=0, keepdims=True)
    for r in range(32):
        at = (r // 16, (r // 8) % 2, (r // 2) % 4, r % 2)
        ys[at + (slice(0, 6), slice(0, 24))] = sums[0:6, 24 * r:24 * r + 24]
        ys[at + (slice(6, 7), slice(0, 96))] = sum_in[:, 96 * r:96 * r + 96]
    put(ys, g_small)
    for cp in outs:
        cp.wait()


def mid(x, att, wo, wi, wb, fv, bi, cot):
    tokens, width = x.shape
    ff = wi.shape[1]
    tok = lambda dt: pltpu.VMEM((tokens, width), dt)
    wide = lambda dt: pltpu.VMEM((tokens, ff), dt)
    owner = (2, 2, 4, 2, 8, 128)
    shape = jax.ShapeDtypeStruct
    return pl.pallas_call(
        mid_kernel,
        out_shape=[
            shape((tokens, width), BF), shape((tokens, width), F32), shape(att.shape, BF), shape(wi.shape, BF),
            shape(wo.shape, BF), shape(wb.shape, BF), shape(owner, F32),
        ],
        in_specs=[vmem_spec()] * 2 + [any_spec()] * 3 + [vmem_spec()] * 3,
        out_specs=[any_spec(), vmem_spec()] + [any_spec()] * 5,
        scratch_shapes=[
            pltpu.VMEM(wo.shape, BF), pltpu.VMEM(wi.shape, BF), pltpu.VMEM(wb.shape, BF),
            tok(BF), tok(F32), tok(F32), pltpu.VMEM((tokens, 1), F32), tok(BF), pltpu.VMEM((width, tokens), BF),
            wide(F32), wide(BF), pltpu.VMEM((ff, tokens), BF), wide(BF), tok(F32), tok(BF), tok(BF),
            pltpu.VMEM(wi.shape, BF), pltpu.VMEM(wo.shape, BF), pltpu.VMEM(wb.shape, BF),
            tok(BF), pltpu.VMEM(att.shape, BF), pltpu.VMEM(owner, F32),
            pltpu.VMEM((6, 8, width), F32), pltpu.VMEM((8, width), F32), pltpu.VMEM((1, ff), F32),
            dma(3), dma(8),
        ],
        compiler_params=pltpu.CompilerParams(vmem_limit_bytes=VMEM_LIMIT),
        name="mid",
    )(x, att, wo, wi, wb, fv, bi, cot)


def finish_kernel(ix, oi, oo, ob, oq, px, pi, po, pb, pq, wide, sem):
    copies = [pltpu.make_async_copy(a, b, sem.at[k]) for k, (a, b) in enumerate(((ix, px), (oi, pi), (ob, pb), (oo, po)))]
    for cp in copies:
        cp.start()
    per = oq.shape[3] // 3
    for g in range(4):
        v = oq[g].reshape(wide.shape[0], 3 * per)
        for k in range(3):
            wide[:, (k * 4 + g) * per:(k * 4 + g + 1) * per] = v[:, k * per:(k + 1) * per]
    copies.append(pltpu.make_async_copy(wide, pq, sem.at[4]))
    copies[4].start()
    for cp in copies:
        cp.wait()


def finish(ix, oi, oo, ob, oq):
    shape = jax.ShapeDtypeStruct
    wide = (oq.shape[1] * oq.shape[2], oq.shape[3] * 4)
    return pl.pallas_call(
        finish_kernel,
        out_shape=[shape(a.shape, F32) for a in (ix, oi, oo, ob)] + [shape(wide, F32)],
        in_specs=[vmem_spec()] * 5,
        out_specs=[any_spec()] * 5,
        scratch_shapes=[pltpu.VMEM(wide, F32), dma(5)],
        name="finish",
    )(ix, oi, oo, ob, oq)


def on_device_fast(
    inputs, segments, w_qkv, b_query, b_value, w_out, b_attn, gain_one, shift_one,
    w_in, b_in, w_back, b_back, gain_two, shift_two, cotangent,
):
    nseq, span, width = inputs.shape
    tokens = nseq * span
    ff = w_in.shape[1]
    depth = w_in.shape[0]
    d, t, z, c, _, _ = place()
    per = width // 4
    vecs = (b_query, b_value, b_attn, gain_one, shift_one, b_back, gain_two, shift_two)
    ffd = b_in.shape[0]
    xs, ids, gi, go, gb, fv, bi, att, qkv, o32, lse, wt = front(
        inputs, segments, w_in.reshape(depth // 8, 8, ff), w_out.reshape(depth // 8, 8, width),
        w_back.reshape(ffd // 8, 8, width),
        jnp.stack(vecs), b_in.reshape(1, ffd), w_qkv.reshape(depth // 8, 8, 3 * width))
    output, d_one, d_att, grad_w_in, grad_w_out, grad_w_back, g_small = mid(
        inputs.reshape(tokens, width), att.reshape(nseq, width, span), go.reshape(width, width),
        gi.reshape(width, ff), gb.reshape(ff, width), fv, bi, cotangent.reshape(tokens, width))
    output = output.reshape(nseq, span, width)
    owner = (2, 2, 4, 2)
    input_grad, oi, oo, ob, os_, oq = back(
        d_att.reshape(8, per, span),
        grad_w_in.reshape(owner + (depth // 8, 8, ff)),
        grad_w_out.reshape(owner + (depth // 8, 8, width)),
        grad_w_back.reshape(owner + (ffd // 8, 8, width)),
        g_small, qkv, ids, o32, lse, wt, xs, d_one.reshape(nseq, span, width),
    )
    input_grad, oi, oo, ob, g_qkv = finish(input_grad, oi, oo, ob, oq)
    vec = lambda k: os_[k, :depth]
    return (
        output, input_grad, g_qkv, vec(8), vec(9), oo.reshape(depth, width), vec(0), vec(1), vec(2),
        oi.reshape(depth, ff), os_[6, :ffd], ob.reshape(ffd, width),
        vec(3), vec(4), vec(5),
    )


negative_fill = -1e30


def layer_norm(resid, gain, shift):
    center = resid - jnp.mean(resid, axis=-1, keepdims=True)
    spread = jnp.mean(center * center, axis=-1, keepdims=True)
    return center * lax.rsqrt(spread + layer_eps) * gain + shift


def gelu_exact(values):
    return jax.nn.gelu(values, approximate=False)


def attend_forward(entries):
    query_rows, key_rows, value_rows, query_ids, key_ids = entries
    scores = jnp.einsum(
        "qhd,khd->hqk", query_rows, key_rows, preferred_element_type=jnp.float32
    ) * HEAD_DIM ** (-0.5)
    allowed = (query_ids[:, None] == key_ids[None, :])[None]
    scores = jnp.where(allowed, scores, negative_fill)
    peak = jnp.max(scores, axis=-1, keepdims=True)
    raised = jnp.exp(scores - peak)
    total = jnp.sum(raised, axis=-1, keepdims=True)
    probs_low = (raised / total).astype(jnp.bfloat16)
    context = jnp.einsum("hqk,khd->qhd", probs_low, value_rows, preferred_element_type=jnp.float32)
    return (context, (peak + jnp.log(total))[..., 0])


def score_terms(query_rows, key_rows, value_rows, grad_context, log_total, query_ids, key_ids):
    scale = HEAD_DIM ** (-0.5)
    scores = (
        jnp.einsum("qhd,khd->hqk", query_rows, key_rows, preferred_element_type=jnp.float32) * scale
    )
    allowed = (query_ids[:, None] == key_ids[None, :])[None]
    probs = jnp.where(allowed, jnp.exp(scores - log_total[..., None]), 0.0)
    d_probs = jnp.einsum(
        "qhd,khd->hqk", grad_context, value_rows, preferred_element_type=jnp.float32
    )
    return (probs, d_probs)


def attend_backward(entries):
    query_rows, key_rows, value_rows, grad_context, log_total, query_ids, key_ids = entries
    scale = HEAD_DIM ** (-0.5)
    probs, d_probs = score_terms(
        query_rows, key_rows, value_rows, grad_context, log_total, query_ids, key_ids
    )
    inner = jnp.sum(probs * d_probs, axis=-1, keepdims=True)
    d_scores = (probs * (d_probs - inner)).astype(jnp.bfloat16)
    d_queries = (
        jnp.einsum("hqk,khd->qhd", d_scores, key_rows, preferred_element_type=jnp.float32) * scale
    )
    d_keys = (
        jnp.einsum("hqk,qhd->khd", d_scores, query_rows, preferred_element_type=jnp.float32) * scale
    )
    d_values = jnp.einsum(
        "hqk,qhd->khd", probs.astype(jnp.bfloat16), grad_context, preferred_element_type=jnp.float32
    )
    length = key_rows.shape[0]
    return (
        d_queries,
        d_keys.reshape(length, HEADS * HEAD_DIM),
        d_values.reshape(length, HEADS * HEAD_DIM),
    )


def on_device_general(
    inputs,
    segments,
    w_qkv,
    b_query,
    b_value,
    w_out,
    b_attn,
    gain_one,
    shift_one,
    w_in,
    b_in,
    w_back,
    b_back,
    gain_two,
    shift_two,
    cotangent,
):
    seq_count, group_len, model_width = inputs.shape
    tok_count = seq_count * group_len
    gathered = (
        lax.all_gather(w_qkv, ("dp", "ctx"), axis=0, tiled=True),
        lax.all_gather(b_query, ("dp", "ctx"), axis=0, tiled=True),
        lax.all_gather(b_value, ("dp", "ctx"), axis=0, tiled=True),
        lax.all_gather(w_out, ("dp", "ctx"), axis=0, tiled=True),
        lax.all_gather(b_attn, ("dp", "ctx"), axis=0, tiled=True),
        lax.all_gather(gain_one, ("dp", "ctx"), axis=0, tiled=True),
        lax.all_gather(shift_one, ("dp", "ctx"), axis=0, tiled=True),
        lax.all_gather(w_in, ("dp", "ctx"), axis=0, tiled=True),
        lax.all_gather(b_in, ("dp", "ctx"), axis=0, tiled=True),
        lax.all_gather(w_back, ("dp", "ctx"), axis=0, tiled=True),
        lax.all_gather(b_back, ("dp", "ctx"), axis=0, tiled=True),
        lax.all_gather(gain_two, ("dp", "ctx"), axis=0, tiled=True),
        lax.all_gather(shift_two, ("dp", "ctx"), axis=0, tiled=True),
    )
    (
        wide_qkv,
        full_b_query,
        full_b_value,
        wide_out,
        full_b_attn,
        full_gain_one,
        full_shift_one,
        wide_in,
        full_b_in,
        wide_back,
        full_b_back,
        full_gain_two,
        full_shift_two,
    ) = gathered
    tokens = inputs.reshape(tok_count, model_width)
    projected = jnp.dot(tokens, wide_qkv, preferred_element_type=jnp.float32)
    query_low = (projected[:, :model_width] + full_b_query.astype(jnp.float32)).astype(jnp.bfloat16)
    key_low = projected[:, model_width : 2 * model_width].astype(jnp.bfloat16)
    value_low = (projected[:, 2 * model_width :] + full_b_value.astype(jnp.float32)).astype(
        jnp.bfloat16
    )
    key_ids = lax.all_gather(segments, "ctx", axis=1, tiled=True)
    key_local = key_low.reshape(seq_count, group_len, model_width)
    value_local = value_low.reshape(seq_count, group_len, model_width)
    key_whole, value_whole = (
        lax.all_gather(key_local, "ctx", axis=1, tiled=True),
        lax.all_gather(value_local, "ctx", axis=1, tiled=True),
    )
    seq_len = key_whole.shape[1]
    query_heads = query_low.reshape(seq_count, group_len, HEADS, HEAD_DIM)
    context, log_total = lax.map(
        attend_forward,
        (
            query_heads,
            key_whole.reshape(seq_count, seq_len, HEADS, HEAD_DIM),
            value_whole.reshape(seq_count, seq_len, HEADS, HEAD_DIM),
            segments,
            key_ids,
        ),
    )
    attended = context.reshape(tok_count, model_width).astype(jnp.bfloat16)
    attn_out = jnp.dot(attended, wide_out, preferred_element_type=jnp.float32) + full_b_attn.astype(
        jnp.float32
    )
    resid_one = tokens.astype(jnp.float32) + attn_out
    normed, norm_one_back = jax.vjp(
        layer_norm, resid_one, full_gain_one.astype(jnp.float32), full_shift_one.astype(jnp.float32)
    )
    normed_low = normed.astype(jnp.bfloat16)
    pre_act = jnp.dot(normed_low, wide_in, preferred_element_type=jnp.float32) + full_b_in.astype(
        jnp.float32
    )
    activ_f, gelu_back = jax.vjp(gelu_exact, pre_act)
    activ = activ_f.astype(jnp.bfloat16)
    branch = jnp.dot(activ, wide_back, preferred_element_type=jnp.float32) + full_b_back.astype(
        jnp.float32
    )
    resid_two = normed + branch
    final_norm, norm_two_back = jax.vjp(
        layer_norm, resid_two, full_gain_two.astype(jnp.float32), full_shift_two.astype(jnp.float32)
    )
    output = final_norm.astype(jnp.bfloat16).reshape(seq_count, group_len, model_width)
    back_qkv, back_out, back_in, back_back = (
        lax.all_gather(w_qkv, ("dp", "ctx"), axis=0, tiled=True),
        lax.all_gather(w_out, ("dp", "ctx"), axis=0, tiled=True),
        lax.all_gather(w_in, ("dp", "ctx"), axis=0, tiled=True),
        lax.all_gather(w_back, ("dp", "ctx"), axis=0, tiled=True),
    )
    d_final = cotangent.reshape(tok_count, model_width).astype(jnp.float32)
    d_two, grad_gain_two, grad_shift_two = norm_two_back(d_final)
    d_branch = d_two.astype(jnp.bfloat16)
    grad_b_back = jnp.sum(d_branch.astype(jnp.float32), axis=0)
    grad_w_back = jnp.einsum("tf,td->fd", activ, d_branch, preferred_element_type=jnp.float32)
    d_activ = jnp.einsum("td,fd->tf", d_branch, back_back, preferred_element_type=jnp.float32)
    d_pre = gelu_back(d_activ)[0].astype(jnp.bfloat16)
    grad_b_in = jnp.sum(d_pre.astype(jnp.float32), axis=0)
    grad_w_in = jnp.einsum("td,tf->df", normed_low, d_pre, preferred_element_type=jnp.float32)
    d_normed = d_two + jnp.einsum("tf,df->td", d_pre, back_in, preferred_element_type=jnp.float32)
    d_one, grad_gain_one, grad_shift_one = norm_one_back(d_normed)
    d_attn = d_one.astype(jnp.bfloat16)
    grad_b_attn = jnp.sum(d_attn.astype(jnp.float32), axis=0)
    grad_w_out = jnp.einsum("ti,td->id", attended, d_attn, preferred_element_type=jnp.float32)
    d_attended = jnp.einsum(
        "td,id->ti", d_attn, back_out, preferred_element_type=jnp.float32
    ).astype(jnp.bfloat16)
    key_back, value_back = (
        lax.all_gather(key_local, "ctx", axis=1, tiled=True),
        lax.all_gather(value_local, "ctx", axis=1, tiled=True),
    )
    grad_heads = d_attended.reshape(seq_count, group_len, HEADS, HEAD_DIM)
    d_query_part, d_key_part, d_value_part = lax.map(
        attend_backward,
        (
            query_heads,
            key_back.reshape(seq_count, seq_len, HEADS, HEAD_DIM),
            value_back.reshape(seq_count, seq_len, HEADS, HEAD_DIM),
            grad_heads,
            log_total,
            segments,
            key_ids,
        ),
    )
    d_key_sum, d_value_sum = (
        lax.psum_scatter(
            d_key_part.astype(jnp.bfloat16), "ctx", scatter_dimension=1, tiled=True
        ).astype(jnp.float32),
        lax.psum_scatter(
            d_value_part.astype(jnp.bfloat16), "ctx", scatter_dimension=1, tiled=True
        ).astype(jnp.float32),
    )
    d_queries = d_query_part.reshape(tok_count, model_width).astype(jnp.bfloat16)
    d_keys = d_key_sum.reshape(tok_count, model_width).astype(jnp.bfloat16)
    d_values = d_value_sum.reshape(tok_count, model_width).astype(jnp.bfloat16)
    d_proj = jnp.concatenate([d_queries, d_keys, d_values], axis=1)
    grad_w_qkv = jnp.einsum("td,te->de", tokens, d_proj, preferred_element_type=jnp.float32)
    grad_b_query = jnp.sum(d_queries.astype(jnp.float32), axis=0)
    grad_b_value = jnp.sum(d_values.astype(jnp.float32), axis=0)
    input_grad = d_one + jnp.einsum(
        "te,de->td", d_proj, back_qkv, preferred_element_type=jnp.float32
    )
    summed = (
        lax.psum_scatter(grad_w_qkv, ("dp", "ctx"), scatter_dimension=0, tiled=True),
        lax.psum_scatter(grad_b_query, ("dp", "ctx"), scatter_dimension=0, tiled=True),
        lax.psum_scatter(grad_b_value, ("dp", "ctx"), scatter_dimension=0, tiled=True),
        lax.psum_scatter(grad_w_out, ("dp", "ctx"), scatter_dimension=0, tiled=True),
        lax.psum_scatter(grad_b_attn, ("dp", "ctx"), scatter_dimension=0, tiled=True),
        lax.psum_scatter(grad_gain_one, ("dp", "ctx"), scatter_dimension=0, tiled=True),
        lax.psum_scatter(grad_shift_one, ("dp", "ctx"), scatter_dimension=0, tiled=True),
        lax.psum_scatter(grad_w_in, ("dp", "ctx"), scatter_dimension=0, tiled=True),
        lax.psum_scatter(grad_b_in, ("dp", "ctx"), scatter_dimension=0, tiled=True),
        lax.psum_scatter(grad_w_back, ("dp", "ctx"), scatter_dimension=0, tiled=True),
        lax.psum_scatter(grad_b_back, ("dp", "ctx"), scatter_dimension=0, tiled=True),
        lax.psum_scatter(grad_gain_two, ("dp", "ctx"), scatter_dimension=0, tiled=True),
        lax.psum_scatter(grad_shift_two, ("dp", "ctx"), scatter_dimension=0, tiled=True),
    )
    return (
        output,
        input_grad.reshape(seq_count, group_len, model_width),
        summed[0],
        summed[1],
        summed[2],
        summed[3],
        summed[4],
        summed[5],
        summed[6],
        summed[7],
        summed[8],
        summed[9],
        summed[10],
        summed[11],
        summed[12],
    )


def solution(mesh):
    placed = (
        P("dp", "ctx", None),
        P("dp", "ctx"),
        P(("dp", "ctx"), None),
        P(("dp", "ctx")),
        P(("dp", "ctx")),
        P(("dp", "ctx"), None),
        P(("dp", "ctx")),
        P(("dp", "ctx")),
        P(("dp", "ctx")),
        P(("dp", "ctx"), None),
        P(("dp", "ctx")),
        P(("dp", "ctx"), None),
        P(("dp", "ctx")),
        P(("dp", "ctx")),
        P(("dp", "ctx")),
        P("dp", "ctx", None),
    )
    fits = mesh.shape["dp"] == 4 and mesh.shape["ctx"] == 8
    return jax.shard_map(
        on_device_fast if fits else on_device_general,
        mesh=mesh,
        in_specs=placed,
        out_specs=(
            P("dp", "ctx", None),
            P("dp", "ctx", None),
            P(("dp", "ctx"), None),
            P(("dp", "ctx")),
            P(("dp", "ctx")),
            P(("dp", "ctx"), None),
            P(("dp", "ctx")),
            P(("dp", "ctx")),
            P(("dp", "ctx")),
            P(("dp", "ctx"), None),
            P(("dp", "ctx")),
            P(("dp", "ctx"), None),
            P(("dp", "ctx")),
            P(("dp", "ctx")),
            P(("dp", "ctx")),
        ),
        check_vma=False,
    )
```

```python
import functools
import jax
import jax.numpy as jnp
from jax import lax
from jax.experimental import pallas as pl
from jax.experimental.pallas import tpu as pltpu
from jax.sharding import PartitionSpec as P

HEADS = 12
HEAD_DIM = 64
layer_eps = 1e-12
MESH_ID = pl.DeviceIdType.MESH
BF = jnp.bfloat16
F32 = jnp.float32
VMEM_LIMIT = 64 * 1024 * 1024 - 65536
SCORE_SCALE = 0.125 * 1.4426950408889634
EXCLUDE = -1e30


def place():
    d = lax.axis_index("dp")
    t = lax.axis_index("ctx")
    z = t // 2
    c = t % 2
    dx = d + 1 - 2 * (d % 2)
    dy = (d + 2) % 4
    return d, t, z, c, dx, dy


def remote(src, dst, ss, rs, dev):
    return pltpu.make_async_remote_copy(
        src_ref=src, dst_ref=dst, send_sem=ss, recv_sem=rs, device_id=dev, device_id_type=MESH_ID
    )


def greet(devices):
    bar = pltpu.get_barrier_semaphore()
    for dev in devices:
        pl.semaphore_signal(bar, inc=1, device_id=dev, device_id_type=MESH_ID)
    pl.semaphore_wait(bar, len(devices))


QB = 256
KB = 256
NH = 3


def marks_of(ids_row):
    kinds = lax.broadcasted_iota(jnp.int32, (16, ids_row.shape[1]), 0).astype(F32)
    return kinds == ids_row


N_ARR = 7
WIDE = (0, 1, 2)
EARLY = (3, 4, 5, 6)
FIRST_X = (0, 1, 3)
FIRST_Y = (2, 4, 5, 6)


def window(i):
    return (i // 4) * (i % 4), 8 - (1 - i // 4) * (3 - i % 4)


def front_kernel(x, seg, wi, wo, wb, vs, bv, wq,
                 xs, ids, gi, go, gb, fv, bi, att, qkv, o32, lse, wt,
                 idb, sm, gs, gq, ka, va, qa, sb,
                 loc, s_x, r_x, s_xf, s_xd, r_xd, s_z, r_z, s_up, s_dn, s_px, r_px, s_py, r_py, s_f, r_f,
                 s_c, r_c, s_e, r_e):
    d, t, z, c, dx, dy = place()
    h = z // 2
    zp = z + 1 - 2 * (z % 2)
    inner = (z + h) % 2 == 1
    dxy = (dx + 2) % 4
    z1, z2 = 2 - h, 3 * (1 - h)
    others = [zp, z1, z2]
    far = [z1, z2]
    me = lambda zz: (d, zz * 2 + c)
    core = (d, z * 2 + 1 - c)
    nx, ny = (dx, t), (dy, t)
    for hh in range(2):
        idb[hh] = jnp.broadcast_to(seg[hh:hh + 1].astype(F32), idb.shape[1:])
    sm[...] = jnp.zeros_like(sm)
    sm[0:8, 0:24] = vs[...].astype(F32)
    sm[8:9, 0:96] = bv[...].astype(F32)
    greet([(d, (t + k) % 8) for k in range(1, 8)] + [nx, ny])
    sends = []

    def go_(cp):
        cp.start()
        sends.append(cp)

    def got(ref, ss, rs, dev):
        remote(ref, ref, ss, rs, dev).wait_recv()

    per = wq.shape[2] // 6
    dst = [gi, go, gb, gs, gq.at[0], gq.at[1], gq.at[2]]

    def mine(a, zz):
        if a < 4:
            return (wi, wo, wb, sm)[a]
        return wq.at[:, :, pl.ds(pl.multiple_of((a - 4) * 2 * per + (zz % 2) * per, per), per)]

    half = x.shape[1] // 2

    def piece(k, hh, tt):
        if k == 2:
            return idb.at[hh], ids.at[tt]
        rows = pl.ds(k * half, half)
        return x.at[hh, rows], xs.at[tt, rows]

    for a in EARLY:
        for k in range(3):
            zz = others[k]
            go_(remote(mine(a, zz), dst[a].at[d, z, c], s_z.at[a - 3, k], r_z.at[a, z], me(zz)))

    def plane(arrs, zz, first):
        for a in arrs:
            src = mine(a, z) if first else dst[a].at[d, zz, c]
            go_(remote(src, dst[a].at[d, zz, c], s_px.at[a, zz], r_px.at[a, zz], nx))
            go_(remote(src, dst[a].at[d, zz, c], s_py.at[a, zz], r_py.at[a, zz], ny))

    plane(EARLY, z, True)
    for k in (2, 0, 1):
        src, to = piece(k, 1 - h, t)
        go_(remote(src, to, s_x.at[0, k], r_x.at[z, k], me(z1)))
        src, to = piece(k, h, t)
        go_(remote(src, to, s_x.at[1, k], r_x.at[z, k], me(zp)))

    def chain(zz, first, wait):
        for a in WIDE:
            src = mine(a, z) if first else dst[a].at[d, zz, c]
            up = remote(src, dst[a].at[d, zz, c], s_up.at[a, zz], r_z.at[a, zz], me((z + 1) % 4))
            dn = remote(src, dst[a].at[d, zz, c], s_dn.at[a, zz], r_z.at[a, zz], me((z + 3) % 4))

            @pl.when(jnp.logical_and(zz <= z, z < 3))
            def _(up=up):
                if wait:
                    up.wait_send()
                else:
                    up.start()

            @pl.when(jnp.logical_and(zz >= z, z > 0))
            def _(dn=dn):
                if wait:
                    dn.wait_send()
                else:
                    dn.start()

    chain(z, True, False)
    plane(WIDE, z, True)
    locals_ = [pltpu.make_async_copy(piece(k, h, t)[0], piece(k, h, t)[1], loc.at[N_ARR + k]) for k in range(3)]
    for a in (4, 5, 6, 3, 0, 1, 2):
        locals_.append(pltpu.make_async_copy(mine(a, z), dst[a].at[d, z, c], loc.at[a]))
    for cp in locals_:
        cp.start()

    def forward(arrs, zz):
        for a in arrs:
            if a in FIRST_Y:
                got(dst[a].at[dy, zz, c], s_py.at[a, zz], r_py.at[a, zz], ny)
                go_(remote(dst[a].at[dy, zz, c], dst[a].at[dy, zz, c], s_f.at[a, zz], r_f.at[a, zz], nx))
            else:
                got(dst[a].at[dx, zz, c], s_px.at[a, zz], r_px.at[a, zz], nx)
                go_(remote(dst[a].at[dx, zz, c], dst[a].at[dx, zz, c], s_f.at[a, zz], r_f.at[a, zz], ny))

    def across(arrs, zz):
        for a in arrs:
            if a in FIRST_Y:
                got(dst[a].at[dx, zz, c], s_px.at[a, zz], r_px.at[a, zz], nx)
                got(dst[a].at[dxy, zz, c], s_f.at[a, zz], r_f.at[a, zz], nx)
            else:
                got(dst[a].at[dy, zz, c], s_py.at[a, zz], r_py.at[a, zz], ny)
                got(dst[a].at[dxy, zz, c], s_f.at[a, zz], r_f.at[a, zz], ny)
            go_(remote(dst[a].at[:, zz, c], dst[a].at[:, zz, c], s_c.at[a, zz], r_c.at[a, zz], core))

    def crossed(arrs, zz):
        for a in arrs:
            ref = dst[a].at[:, zz, 1 - c]
            got(ref, s_c.at[a, zz], r_c.at[a, zz], core)

    def arrive(arrs, k):
        for a in arrs:
            got(dst[a].at[d, others[k], c], s_z.at[0, 0], r_z.at[a, others[k]], me(others[k]))

    for k in range(3):
        arrive(EARLY, k)
        plane(EARLY, others[k], False)
    for cp in locals_[:7]:
        cp.wait()
    for zz in [z] + others:
        forward(EARLY, zz)

    def relay(k, wait):
        for j in range(2):
            ref = piece(k, h, far[j] * 2 + c)[1]
            cp = remote(ref, ref, s_xf.at[j, k], r_x.at[far[j], k], me(zp))

            @pl.when(inner)
            def _(cp=cp):
                if wait:
                    cp.wait_send()
                else:
                    cp.wait_recv()
                    cp.start()

    def relayed(k):
        for j in range(2):
            ref = piece(k, h, far[j] * 2 + c)[1]

            @pl.when(jnp.logical_not(inner))
            def _(ref=ref, j=j):
                got(ref, s_x.at[0, k], r_x.at[far[j], k], me(zp))

    def to_core(zz):
        for k in range(3):
            ref = piece(k, h, zz * 2 + c)[1]
            go_(remote(ref, ref, s_xd.at[zz, k], r_xd.at[zz, k], core))

    def from_core(zz):
        for k in range(3):
            got(piece(k, h, zz * 2 + 1 - c)[1], s_xd.at[zz, k], r_xd.at[zz, k], core)

    to_core(z)
    for k in (2, 0):
        relay(k, False)
    for zz in [z] + others:
        across(EARLY, zz)
    relay(1, False)
    for k in range(3):
        got(piece(k, h, zp * 2 + c)[1], s_x.at[1, k], r_x.at[zp, k], me(zp))
    to_core(zp)
    for zz in [z] + others:
        crossed(EARLY, zz)
    width = wt.shape[3]
    for j in range(3):
        for q in range(2):
            w = gq[j, 2 * q:2 * q + 2].astype(F32).reshape(width // 2, per)
            w = w.T.astype(BF)
            for cc in range(2):
                wt[j, cc, :, q * (width // 2):(q + 1) * (width // 2)] = w[cc * (per // 2):(cc + 1) * (per // 2)]
    group = (z % 2) * 2 + c
    span = x.shape[1]

    def column(row):
        v = gs[group, :, :, row].reshape(8, 128).T
        return jnp.concatenate([v[:24, r:r + 1] for r in range(8)], axis=0)

    bias = [column(0), None, column(1)]
    for g in range(NH):
        va[g, 64:] = jnp.ones((16, va.shape[2]), BF)

    def project(zz):
        def one(j, _):
            tb = zz * 2 + j
            cols = pl.ds(pl.multiple_of(tb * span, span), span)
            xb = xs[tb]
            hit = marks_of(ids[tb, 0:1])
            ones = jnp.where(hit, 1.0, 0.0)
            away = jnp.where(hit, 0.0, EXCLUDE).astype(BF)
            for s in range(3):
                r = lax.dot_general(wt[s, c], xb, (((1,), (1,)), ((), ())), preferred_element_type=F32)
                if bias[s] is not None:
                    r = r + bias[s]
                low = r.astype(BF)
                qkv[s, :, cols] = low
                for g in range(NH):
                    part = low[g * 64:(g + 1) * 64]
                    if s == 0:
                        qa[g, :64, cols] = part
                        qa[g, 64:, cols] = away
                    elif s == 1:
                        ka[g, cols, :] = jnp.concatenate([part.astype(F32), ones], axis=0).T.astype(BF)
                    else:
                        va[g, :64, cols] = part
            return 0

        lax.fori_loop(0, 2, one, 0)

    forward(WIDE, z)
    for zz in (z, zp):
        from_core(zz)
        project(zz)
    for k in (2, 0, 1):
        relayed(k)
    for zz in far:
        to_core(zz)
    for zz in far:
        from_core(zz)
        project(zz)

    def attend(k):
        i = (t + k) % 8
        cols = pl.ds(pl.multiple_of(i * QB, QB), QB)
        lo, hi = window(i)

        def block(j, carry):
            at = pl.ds(pl.multiple_of(j * KB, KB), KB)
            out = []
            s = [jnp.dot(ka[g, at, :], qa[g, :, cols], preferred_element_type=F32) for g in range(NH)]
            for g in range(NH):
                m, acc = carry[g]
                m2 = jnp.maximum(m, jnp.max(s[g], axis=0, keepdims=True))
                p = jnp.exp2((s[g] - m2) * SCORE_SCALE).astype(BF)
                acc = acc * jnp.exp2((m - m2) * SCORE_SCALE) + jnp.dot(
                    va[g, :, at], p, preferred_element_type=F32)
                out.append((m2, acc))
            return tuple(out)

        first = tuple((jnp.full((1, QB), -3e38, F32), jnp.zeros((80, QB), F32)) for _ in range(NH))
        res = lax.fori_loop(lo, hi, block, first)
        for g in range(NH):
            m, acc = res[g]
            total = acc[64:65]
            o = acc[:64] / total
            o32[i, g * 64:(g + 1) * 64] = o
            if k:
                sb[i, g * 64:(g + 1) * 64] = o.astype(BF)
            else:
                att[t, g * 64:(g + 1) * 64] = o.astype(BF)
            lse[g, pl.ds(i, 1)] = m * SCORE_SCALE + jnp.log2(total)
        if k:
            go_(remote(sb.at[i], att.at[t], s_e.at[k - 1], r_e.at[k - 1], (d, i)))

    def onward(k):
        arrive(WIDE, k)
        chain(others[k], False, False)
        plane(WIDE, others[k], False)

    order = ORDER_K
    onward(0)
    attend(order[0])
    attend(order[1])
    for cp in locals_[7:]:
        cp.wait()
    across(WIDE, z)
    onward(1)
    attend(order[2])
    attend(order[3])
    forward(WIDE, zp)
    onward(2)
    attend(order[4])
    attend(order[5])
    forward(WIDE, z1)
    across(WIDE, zp)
    attend(order[6])
    attend(order[7])
    forward(WIDE, z2)
    across(WIDE, z1)
    across(WIDE, z2)
    for r in range(32):
        v = gs.at[r // 8, (r // 2) % 4, r % 2]
        fv[:, 24 * r:24 * r + 24] = v[0:8, 0:24]
        bi[:, 96 * r:96 * r + 96] = v[8:9, 0:96]
    for zz in [z] + others:
        crossed(WIDE, zz)
    for k in range(1, 8):
        src = (t + 8 - k) % 8
        got(att.at[src], s_e.at[k - 1], r_e.at[k - 1], (d, src))
    for cp in sends:
        cp.wait_send()
    chain(z, True, True)
    for zz in others:
        chain(zz, False, True)
    for k in range(3):
        relay(k, True)


ORDER_K = (4, 5, 3, 6, 2, 7, 1, 0)


def any_spec():
    return pl.BlockSpec(memory_space=pl.ANY)


def vmem_spec():
    return pl.BlockSpec(memory_space=pltpu.VMEM)


def dma(*shape):
    return pltpu.SemaphoreType.DMA(shape)


def front(x, seg, wi, wo, wb, vs, bv, wq):
    span, width = x.shape[1:]
    n = 8 * span
    per = width // 4
    grid_of = lambda a: jax.ShapeDtypeStruct((4, 4, 2) + a.shape, a.dtype)
    return pl.pallas_call(
        front_kernel,
        out_shape=[
            jax.ShapeDtypeStruct((8, span, width), x.dtype),
            jax.ShapeDtypeStruct((8, 8, span), F32),
            grid_of(wi), grid_of(wo), grid_of(wb),
            jax.ShapeDtypeStruct((8, width), F32), jax.ShapeDtypeStruct((1, wi.shape[2]), F32),
            jax.ShapeDtypeStruct((8, per, span), BF),
            jax.ShapeDtypeStruct((3, per, n), BF),
            jax.ShapeDtypeStruct((8, per, span), F32),
            jax.ShapeDtypeStruct((NH, 8, span), F32),
            jax.ShapeDtypeStruct((3, 2, per, width), BF),
        ],
        in_specs=[any_spec(), vmem_spec()] + [any_spec()] * 3 + [vmem_spec()] * 2 + [any_spec()],
        out_specs=[vmem_spec()] * 2 + [any_spec()] * 3 + [vmem_spec()] * 7,
        scratch_shapes=[
            pltpu.VMEM((2, 8, span), F32), pltpu.VMEM((16, 128), F32), pltpu.VMEM((4, 4, 2, 16, 128), F32),
            pltpu.VMEM((3, 4, 4, 2) + wq.shape[:2] + (2 * per,), BF),
            pltpu.VMEM((NH, n, 80), BF), pltpu.VMEM((NH, 80, n), BF), pltpu.VMEM((NH, 80, n), BF),
            pltpu.VMEM((8, per, span), BF),
            dma(N_ARR + 3), dma(2, 3), dma(4, 3), dma(2, 3), dma(4, 3), dma(4, 3), dma(4, 3), dma(N_ARR, 4),
            dma(3, 4), dma(3, 4),
            dma(N_ARR, 4), dma(N_ARR, 4), dma(N_ARR, 4), dma(N_ARR, 4), dma(N_ARR, 4), dma(N_ARR, 4),
            dma(N_ARR, 4), dma(N_ARR, 4), dma(7), dma(7),
        ],
        compiler_params=pltpu.CompilerParams(
            collective_id=1, has_side_effects=True, vmem_limit_bytes=VMEM_LIMIT),
        name="front",
    )(x, seg, wi, wo, wb, vs, bv, wq)


def back_kernel(dat, di, do_, db, ds_, qkv, ids, o32, lse, wt, xs, d_one,
                ox, oi, oo, ob, os_, oq, *rest):
    rd, own, r1, r2, r3, r4, r5 = [rest[4 * i:4 * i + 4] for i in range(7)]
    (da, ka, qa, vk, dkv, pr, xv, dxp, dw, lq, lv,
     xd, x3, x4, x5, q0, q1, q2, qr, v0, v1, v2, vr,
     loc, s_e, r_e, s_d, r_d, s_1, r_1, s_2, r_2, s_3, r_3, s_4, r_4, s_5, r_5,
     s_q1, r_q1, s_q2, r_q2, s_qe, r_qe) = rest[28:]
    d, t, z, c, dx, dy = place()
    x, y = d % 2, d // 2
    h = z // 2
    zp = z + 1 - 2 * (z % 2)
    inner = (z + h) % 2 == 1
    me = lambda zz: (d, zz * 2 + c)
    core = (d, z * 2 + 1 - c)
    nx, ny = (dx, t), (dy, t)
    line = [(t + k) % 8 for k in range(1, 8)]
    far = [2 * (1 - h), 2 * (1 - h) + 1]
    order = [far[0], far[1], zp, z]
    group = (z % 2) * 2 + c
    part = [di, do_, db, ds_]
    outs = [oi, oo, ob, os_.at[pl.ds(0, 8)]]
    by_x = [True, True, False, True]
    sends = []
    greet([(d, o) for o in line] + [nx, ny])

    def go_(cp):
        cp.start()
        sends.append(cp)

    def got(ref, ss, rs, dev):
        remote(ref, ref, ss, rs, dev).wait_recv()

    for k in NEAR[1:]:
        i = line[k - 1]
        go_(remote(dat.at[i], da.at[t], s_e.at[k - 1], r_e.at[k - 1], (d, i)))
    for n_, zz in enumerate(order):
        for a in range(4):
            for yy in range(2):
                go_(remote(part[a].at[yy, :, zz, 1 - c], rd[a].at[yy, :, zz], s_d.at[1 + 2 * a + yy, n_],
                           r_d.at[1 + 2 * a + yy, n_], core))
    local = []

    def here(src, to):
        cp = pltpu.make_async_copy(src, to, loc.at[len(local)])
        cp.start()
        local.append(cp)

    here(dat.at[t], da.at[t])
    for a in range(4):
        for yy in range(2):
            here(part[a].at[yy, :, :, c], own[a].at[yy])
    here(xs, xv)

    n = qkv.shape[2]
    span = da.shape[2]

    def fill(tb, _):
        cols = pl.ds(pl.multiple_of(tb * span, span), span)
        hit = marks_of(ids[tb, 0:1])
        ones = jnp.where(hit, 1.0, 0.0)
        away = jnp.where(hit, 0.0, EXCLUDE).astype(BF)
        for g in range(NH):
            rows = slice(g * 64, (g + 1) * 64)
            ka[g, cols, :] = jnp.concatenate([qkv[1, rows, cols].astype(F32), ones], axis=0).T.astype(BF)
            vk[g, cols, :] = qkv[2, rows, cols].astype(F32).T.astype(BF)
            qa[g, :64, cols] = qkv[0, rows, cols]
            qa[g, 64:, cols] = away
            dkv[g, cols, :] = jnp.zeros((span, 128), F32)
        return 0

    lax.fori_loop(0, 8, fill, 0)

    def attend(k):
        i = (t + 8 - k) % 8
        if k:
            got(da.at[i], s_e.at[k - 1], r_e.at[k - 1], (d, i))
        cols = pl.ds(pl.multiple_of(i * QB, QB), QB)
        lo, hi = window(i)
        fixed = []
        for g in range(NH):
            rows = slice(g * 64, (g + 1) * 64)
            do = da[i, rows].astype(F32)
            inside = jnp.sum(do * o32[i, rows], axis=0, keepdims=True)
            zero = jnp.zeros((64, QB), F32)
            ra = jnp.concatenate([do, zero], axis=0).T.astype(BF)
            rb = jnp.concatenate([zero, qkv[0, rows, cols].astype(F32)], axis=0).T.astype(BF)
            fixed.append((inside, lse[g, pl.ds(i, 1)], jnp.concatenate([ra, rb], axis=0)))

        def block(j, carry):
            at = pl.ds(pl.multiple_of(j * KB, KB), KB)
            out = []
            s = [jnp.dot(ka[g, at, :], qa[g, :, cols], preferred_element_type=F32) for g in range(NH)]
            dp = [jnp.dot(vk[g, at, :], da[i, g * 64:(g + 1) * 64], preferred_element_type=F32)
                  for g in range(NH)]
            for g in range(NH):
                inside, lse_i, rab = fixed[g]
                p = jnp.exp2(s[g] * SCORE_SCALE - lse_i)
                ds = (p * (dp[g] - inside)).astype(BF)
                dkv[g, at, :] += jnp.dot(
                    jnp.concatenate([p.astype(BF), ds], axis=1), rab, preferred_element_type=F32)
                out.append(carry[g] + jnp.dot(qkv[1, g * 64:(g + 1) * 64, at], ds, preferred_element_type=F32))
            return tuple(out)

        dq = lax.fori_loop(lo, hi, block, tuple(jnp.zeros((64, QB), F32) for _ in range(NH)))
        for g in range(NH):
            pr[0, g * 64:(g + 1) * 64, cols] = (dq[g] * 0.125).astype(BF)

    def add_rows(dst, src):
        def step(i, _):
            dst[i] = dst[i] + src[i]
            return 0

        lax.fori_loop(0, dst.shape[0], step, 0)

    def add_tok(dst, src):
        def step(i, _):
            at = pl.ds(pl.multiple_of(i * 32, 32), 32)
            dst[at, :] = dst[at, :] + src[at, :]
            return 0

        lax.fori_loop(0, dst.shape[0] // 32, step, 0)

    def first(n_):
        zz = order[n_]
        for a in range(4):
            for yy in range(2):
                got(rd[a].at[yy, :, zz], s_d.at[1 + 2 * a + yy, n_], r_d.at[1 + 2 * a + yy, n_], core)
                for xx in range(2):
                    add_rows(rd[a].at[yy, xx, zz], own[a].at[yy, xx, zz])
            if by_x[a]:
                go_(remote(rd[a].at[:, 1 - x, zz], r1[a].at[n_], s_1.at[a, n_], r_1.at[a, n_], nx))
            else:
                go_(remote(rd[a].at[1 - y, :, zz], r1[a].at[n_], s_1.at[a, n_], r_1.at[a, n_], ny))

    def second(n_):
        zz = order[n_]
        for a in range(4):
            got(r1[a].at[n_], s_1.at[a, n_], r_1.at[a, n_], nx if by_x[a] else ny)
            for w in range(2):
                add_rows(rd[a].at[w, x, zz] if by_x[a] else rd[a].at[y, w, zz], r1[a].at[n_, w])
            if by_x[a]:
                go_(remote(rd[a].at[1 - y, x, zz], r2[a].at[n_], s_2.at[a, n_], r_2.at[a, n_], ny))
            else:
                go_(remote(rd[a].at[y, 1 - x, zz], r2[a].at[n_], s_2.at[a, n_], r_2.at[a, n_], nx))

    def to_inner(a, n_):
        ref = xd.at[far[n_]] if a == 4 else rd[a].at[y, x, far[n_]]
        land = x3 if a == 4 else r3[a]
        return remote(ref, land.at[n_], s_3.at[a, n_], r_3.at[a, n_], me(zp))

    def to_far(a, n_):
        ref = xd.at[far[n_]] if a == 4 else rd[a].at[y, x, far[n_]]
        return remote(ref, x4 if a == 4 else r4[a], s_4.at[a, n_], r_4.at[a], me(far[n_]))

    def third(n_):
        zz = order[n_]
        for a in range(4):
            got(r2[a].at[n_], s_2.at[a, n_], r_2.at[a, n_], ny if by_x[a] else nx)
            add_rows(rd[a].at[y, x, zz], r2[a].at[n_])
            if n_ < 2:
                @pl.when(jnp.logical_not(inner))
                def _(a=a):
                    to_inner(a, n_).start()
            elif n_ == 2:
                go_(remote(rd[a].at[y, x, zz], r5[a], s_5.at[a], r_5.at[a], me(zz)))

    def fourth(n_, arrs):
        @pl.when(inner)
        def _():
            for a in arrs:
                to_inner(a, n_).wait_recv()
                if a == 4:
                    add_tok(xd.at[far[n_]], x3.at[n_])
                else:
                    add_rows(rd[a].at[y, x, far[n_]], r3[a].at[n_])
                to_far(a, n_).start()

    for cp in local:
        cp.wait()
    first(0)
    first(1)
    attend(NEAR[0])
    attend(NEAR[1])
    second(0)
    first(2)
    attend(NEAR[2])
    attend(NEAR[3])
    second(1)
    first(3)
    attend(NEAR[4])
    third(0)
    attend(NEAR[5])
    second(2)
    attend(NEAR[6])
    third(1)
    fourth(0, range(4))
    attend(NEAR[7])
    second(3)
    for g in range(NH):
        rows = slice(g * 64, (g + 1) * 64)
        flip = dkv[g].T
        pr[1, rows] = (flip[64:] * 0.125).astype(BF)
        pr[2, rows] = flip[:64].astype(BF)

    def token_grad(tb):
        cols = pl.ds(pl.multiple_of(tb * span, span), span)
        acc = None
        for s in range(3):
            term = jnp.dot(pr[s, :, cols].astype(F32).T.astype(BF), wt[s, c], preferred_element_type=F32)
            acc = term if acc is None else acc + term
        dxp[tb] = acc.astype(BF)

    def token_pair(j, _):
        token_grad(j * 2 + 1 - c)
        return 0

    per = pr.shape[1]
    width = wt.shape[3]

    def weight_grad(n_, q):
        xall = xv[:, :, pl.ds(pl.multiple_of(q * (width // 2), 128), width // 2)].reshape(n, width // 2)
        for s in range(3):
            dw[s * per:(s + 1) * per] = jnp.dot(pr[s], xall, preferred_element_type=F32)
        lq[q] = dw[...].T.reshape(lq.shape[1:]).astype(BF)
        go_(remote(lq.at[q, 1 - x], q1.at[q], s_q1.at[n_], r_q1.at[n_], nx))

    def summed(yy):
        for zc in range(8):
            at = (zc // 2, zc % 2)
            q0[(yy,) + at] = q1[(yy,) + at] + lq[(yy, x) + at]

    lax.fori_loop(0, 4, token_pair, 0)
    for n_, zz in enumerate(order):
        go_(remote(dxp.at[zz * 2 + 1 - c], xd.at[zz], s_d.at[0, n_], r_d.at[0, n_], core))
    third(2)
    fourth(1, range(4))
    weight_grad(0, 1 - y)
    def token_mine(j, _):
        token_grad(j * 2 + c)
        return 0

    lax.fori_loop(0, 4, token_mine, 0)
    for n_, zz in enumerate(order):
        got(xd.at[zz], s_d.at[0, n_], r_d.at[0, n_], core)
        add_tok(xd.at[zz], dxp.at[zz * 2 + c])
        if n_ < 2:
            @pl.when(jnp.logical_not(inner))
            def _(n_=n_):
                to_inner(4, n_).start()
        elif n_ == 2:
            go_(remote(xd.at[zz], x5, s_5.at[4], r_5.at[4], me(zz)))
    weight_grad(1, y)
    lv[...] = jnp.zeros_like(lv)
    for row, s in ((0, 0), (1, 2)):
        col = jnp.sum(pr[s].astype(F32), axis=1, keepdims=True)
        for r in range(8):
            piece = jnp.broadcast_to(col[24 * r:24 * r + 24], (24, 128)).T
            lv[group // 2, group % 2, r // 2, r % 2, row:row + 1, :24] = piece[0:1]
    go_(remote(lv.at[:, 1 - x], v1, s_q1.at[2], r_q1.at[2], nx))
    got(q1.at[1 - y], s_q1.at[0], r_q1.at[0], nx)
    summed(1 - y)
    go_(remote(q0.at[1 - y], q2, s_q2.at[0], r_q2.at[0], ny))
    got(v1, s_q1.at[2], r_q1.at[2], nx)
    for yy in range(2):
        for zc in range(8):
            at = (zc // 2, zc % 2)
            v0[(yy,) + at] = v1[(yy,) + at] + lv[(yy, x) + at]
    go_(remote(v0.at[1 - y], v2, s_q2.at[1], r_q2.at[1], ny))
    third(3)
    fourth(0, (4,))
    got(q1.at[y], s_q1.at[1], r_q1.at[1], nx)
    summed(y)
    got(q2, s_q2.at[0], r_q2.at[0], ny)
    got(v2, s_q2.at[1], r_q2.at[1], ny)
    for zc in range(8):
        at = (zc // 2, zc % 2)
        q0[(y,) + at] = q0[(y,) + at] + q2[at]
        v0[(y,) + at] = v0[(y,) + at] + v2[at]
    for k in range(1, 8):
        to = line[k - 1]
        go_(remote(q0.at[y, to // 2, to % 2], qr.at[t], s_qe.at[0, k - 1], r_qe.at[0, k - 1], (d, to)))
        go_(remote(v0.at[y, to // 2, to % 2], vr.at[t], s_qe.at[1, k - 1], r_qe.at[1, k - 1], (d, to)))
    qr[t] = q0[y, z, c]
    vr[t] = v0[y, z, c]
    fourth(1, (4,))
    src_in = 2 - h
    for a in range(4):
        got(r5[a], s_5.at[a], r_5.at[a], me(zp))
        got(r4[a], s_4.at[a, 0], r_4.at[a], me(src_in))
        acc = rd[a].at[y, x, z]
        for i in range(acc.shape[0]):
            outs[a][i] = acc[i].astype(F32) + r5[a][i].astype(F32) + r4[a][i].astype(F32)
    got(x5, s_5.at[4], r_5.at[4], me(zp))
    got(x4, s_4.at[4, 0], r_4.at[4], me(src_in))

    def tok(i, _):
        at = pl.ds(pl.multiple_of(i * 32, 32), 32)
        ox[h, at, :] = d_one[h, at, :] + (xd[z, at, :].astype(F32) + x5[at, :].astype(F32))
        ox[1 - h, at, :] = d_one[1 - h, at, :] + x4[at, :].astype(F32)
        return 0

    lax.fori_loop(0, span // 32, tok, 0)
    for k in range(1, 8):
        src = (t + 8 - k) % 8
        got(qr.at[src], s_qe.at[0, k - 1], r_qe.at[0, k - 1], (d, src))
        got(vr.at[src], s_qe.at[1, k - 1], r_qe.at[1, k - 1], (d, src))
    for g in range(4):
        oq[g] = qr[g].astype(F32) + qr[4 + g].astype(F32)
    total = vr[0]
    for k in range(1, 8):
        total = total + vr[k]
    os_[8:16] = total
    for cp in sends:
        cp.wait_send()
    for n_ in range(2):
        @pl.when(jnp.logical_not(inner))
        def _(n_=n_):
            for a in range(5):
                to_inner(a, n_).wait_send()

        @pl.when(inner)
        def _(n_=n_):
            for a in range(5):
                to_far(a, n_).wait_send()


NEAR = (0, 1, 7, 2, 6, 3, 5, 4)


def back(dat, di, do_, db, ds_, qkv, ids, o32, lse, wt, xs, d_one):
    arrs = [di, do_, db, ds_]
    tails = [a.shape[4:] for a in arrs]
    per, width = wt.shape[2:]
    n = qkv.shape[2]
    tok = xs.shape[1:]
    qt = di.shape[4:6] + (3 * per,)
    vt = (8, 128)
    scratch = []
    for lead in ((2, 2, 4), (2, 2, 4), (4, 2), (4,), (2,), (), ()):
        for a, tail in zip(arrs, tails):
            scratch.append(pltpu.VMEM(lead + tail, a.dtype))
    grid = (2, 2, 4, 2)
    scratch += [
        pltpu.VMEM(dat.shape, BF),
        pltpu.VMEM((NH, n, 80), BF), pltpu.VMEM((NH, 80, n), BF), pltpu.VMEM((NH, n, 64), BF),
        pltpu.VMEM((NH, n, 128), F32), pltpu.VMEM((3, per, n), BF),
        pltpu.VMEM(xs.shape, BF), pltpu.VMEM(xs.shape, BF), pltpu.VMEM((3 * per, width // 2), F32),
        pltpu.VMEM(grid + qt, BF), pltpu.VMEM(grid + vt, F32),
        pltpu.VMEM((4,) + tok, BF), pltpu.VMEM((2,) + tok, BF), pltpu.VMEM(tok, BF), pltpu.VMEM(tok, BF),
        pltpu.VMEM((2, 4, 2) + qt, BF), pltpu.VMEM((2, 4, 2) + qt, BF), pltpu.VMEM((4, 2) + qt, BF),
        pltpu.VMEM((8,) + qt, BF),
        pltpu.VMEM((2, 4, 2) + vt, F32), pltpu.VMEM((2, 4, 2) + vt, F32), pltpu.VMEM((4, 2) + vt, F32),
        pltpu.VMEM((8,) + vt, F32),
        dma(10), dma(7), dma(7), dma(9, 4), dma(9, 4), dma(4, 4), dma(4, 4), dma(4, 4), dma(4, 4),
        dma(5, 2), dma(5, 2), dma(5, 2), dma(5), dma(5), dma(5),
        dma(3), dma(3), dma(2), dma(2), dma(2, 7), dma(2, 7),
    ]
    return pl.pallas_call(
        back_kernel,
        out_shape=[jax.ShapeDtypeStruct((2,) + tok, F32)]
        + [jax.ShapeDtypeStruct(tail, F32) for tail in tails[:3] + [(16, 128)]]
        + [jax.ShapeDtypeStruct((4,) + qt, F32)],
        in_specs=[any_spec()] * 5 + [vmem_spec()] * 5 + [any_spec(), vmem_spec()],
        out_specs=[vmem_spec()] * 6,
        scratch_shapes=scratch,
        compiler_params=pltpu.CompilerParams(
            collective_id=4, has_side_effects=True, vmem_limit_bytes=VMEM_LIMIT),
        name="back",
    )(dat, di, do_, db, ds_, qkv, ids, o32, lse, wt, xs, d_one)


def erf_parts(u):
    phi_c = 0.5 * (1.0 + lax.erf(u * 0.7071067811865476))
    return phi_c, phi_c + u * jnp.exp(-0.5 * u * u) * 0.3989422804014327


def norm_forward(r):
    center = r - jnp.mean(r, axis=-1, keepdims=True)
    inv = lax.rsqrt(jnp.mean(center * center, axis=-1, keepdims=True) + layer_eps)
    return center * inv, inv


def norm_backward(n, inv, gain, dy):
    gd = gain * dy
    return (gd - jnp.mean(gd, axis=-1, keepdims=True) - n * jnp.mean(gd * n, axis=-1, keepdims=True)) * inv


def mid_kernel(x, att, wo, wi, wb, fv, bi, cot,
               out, d_one, dat, g_in, g_out, g_back, g_small,
               vo, vi, vb, att_t, acc, n1, inv1, low, low_t, slope, act, act_t, d_pre, d_two, d_br, d_attn,
               yi, yo, yb, yx, yd, ys, part, sums, sum_in, sem_w, sem_o):
    tokens, width = x.shape
    span = tokens // 2
    ff = vi.shape[1]
    loads = [pltpu.make_async_copy(a, b, sem_w.at[k]) for k, (a, b) in enumerate(((wo, vo), (wi, vi), (wb, vb)))]
    for cp in loads:
        cp.start()
    outs = []

    def put(src, to):
        cp = pltpu.make_async_copy(src, to, sem_o.at[len(outs)])
        cp.start()
        outs.append(cp)

    def loop(count, size, fn):
        def one(j, _):
            fn(pl.ds(pl.multiple_of(j * size, size), size))
            return 0

        lax.fori_loop(0, count, one, 0)

    halves = (slice(0, span), slice(span, tokens))
    rb = tokens // 4
    nt = (((1,), (1,)), ((), ()))
    part[...] = jnp.zeros_like(part)

    def count_in(k, v):
        part[k] += jnp.sum(v.reshape(v.shape[0] // 8, 8, width), axis=0)

    for s in range(2):
        att_t[halves[s]] = att[s].astype(F32).T.astype(BF)
    loads[0].wait()
    for s in range(2):
        acc[halves[s]] = jnp.dot(att_t[halves[s]], vo[...], preferred_element_type=F32)

    def norm_one(r):
        n, inv = norm_forward(x[r].astype(F32) + acc[r] + fv[2:3])
        n1[r] = n
        inv1[r] = inv
        low[r] = (n * fv[3:4] + fv[4:5]).astype(BF)

    loop(4, rb, norm_one)
    loads[1].wait()

    def widen(f):
        pre = [jnp.dot(low[r], vi[:, f], preferred_element_type=F32) + bi[:, f] for r in halves]
        for r, u in zip(halves, pre):
            phi_c, sl = erf_parts(u)
            slope[r, f] = sl
            a = u * phi_c
            act[r, f] = a.astype(BF)
            act_t[f, r] = a.T.astype(BF)

    loop(ff // 256, 256, widen)
    loads[2].wait()

    def narrow(f):
        for r in halves:
            acc[r, f] = jnp.dot(act[r], vb[:, f], preferred_element_type=F32)

    loop(width // 256, 256, narrow)

    def norm_two(r):
        normed = n1[r] * fv[3:4] + fv[4:5]
        n2, inv2 = norm_forward(normed + acc[r] + fv[5:6])
        yx[r] = (n2 * fv[6:7] + fv[7:8]).astype(BF)
        dy = cot[r].astype(F32)
        d2 = norm_backward(n2, inv2, fv[6:7], dy)
        d_two[r] = d2
        d2 = d2.astype(BF)
        d_br[r] = d2
        count_in(3, d2.astype(F32))
        count_in(4, dy * n2)
        count_in(5, dy)

    loop(4, rb, norm_two)
    put(yx, out)

    def back_widen(f):
        da = [lax.dot_general(d_br[r], vb[f, :], nt, preferred_element_type=F32) for r in halves]
        total = None
        for r, v in zip(halves, da):
            dp = (v * slope[r, f]).astype(BF)
            d_pre[r, f] = dp
            col = jnp.sum(dp.astype(F32), axis=0, keepdims=True)
            total = col if total is None else total + col
        sum_in[:, f] = total

    loop(ff // 256, 256, back_widen)

    def back_narrow(k):
        for r in halves:
            acc[r, k] = lax.dot_general(d_pre[r], vi[k, :], nt, preferred_element_type=F32)

    loop(width // 256, 256, back_narrow)

    def back_one(r):
        dn = d_two[r] + acc[r]
        n = n1[r]
        d1 = norm_backward(n, inv1[r], fv[3:4], dn)
        d_one[r] = d1
        d1 = d1.astype(BF)
        d_attn[r] = d1
        count_in(0, d1.astype(F32))
        count_in(1, dn * n)
        count_in(2, dn)

    loop(4, rb, back_one)
    for s in range(2):
        yd[s] = lax.dot_general(vo[...], d_attn[halves[s]], nt, preferred_element_type=F32).astype(BF)
    put(yd, dat)

    def grad_back(f):
        yb[f, :] = jnp.dot(act_t[f, :], d_br[...], preferred_element_type=F32).astype(BF)

    loop(ff // 256, 256, grad_back)
    put(yb, g_back)
    for k in range(3):
        low_t[k * 256:(k + 1) * 256] = low[:, k * 256:(k + 1) * 256].astype(F32).T.astype(BF)
    for k in range(3):
        rows = slice(k * 256, (k + 1) * 256)

        def grad_in(f, rows=rows):
            yi[rows, f] = jnp.dot(low_t[rows], d_pre[:, f], preferred_element_type=F32).astype(BF)

        loop(ff // 768, 768, grad_in)
        put(yi.at[rows], g_in.at[rows])

    def grad_out(k):
        yo[k] = (jnp.dot(att[0, k], d_attn[halves[0]], preferred_element_type=F32)
                 + jnp.dot(att[1, k], d_attn[halves[1]], preferred_element_type=F32)).astype(BF)

    loop(3, 256, grad_out)
    put(yo, g_out)
    ys[...] = jnp.zeros_like(ys)
    for k in range(6):
        sums[k:k + 1] = jnp.sum(part[k], axis=0, keepdims=True)
    for r in range(32):
        at = (r // 16, (r // 8) % 2, (r // 2) % 4, r % 2)
        ys[at + (slice(0, 6), slice(0, 24))] = sums[0:6, 24 * r:24 * r + 24]
        ys[at + (slice(6, 7), slice(0, 96))] = sum_in[:, 96 * r:96 * r + 96]
    put(ys, g_small)
    for cp in outs:
        cp.wait()


def mid(x, att, wo, wi, wb, fv, bi, cot):
    tokens, width = x.shape
    ff = wi.shape[1]
    tok = lambda dt: pltpu.VMEM((tokens, width), dt)
    wide = lambda dt: pltpu.VMEM((tokens, ff), dt)
    owner = (2, 2, 4, 2, 8, 128)
    shape = jax.ShapeDtypeStruct
    return pl.pallas_call(
        mid_kernel,
        out_shape=[
            shape((tokens, width), BF), shape((tokens, width), F32), shape(att.shape, BF), shape(wi.shape, BF),
            shape(wo.shape, BF), shape(wb.shape, BF), shape(owner, F32),
        ],
        in_specs=[vmem_spec()] * 2 + [any_spec()] * 3 + [vmem_spec()] * 3,
        out_specs=[any_spec(), vmem_spec()] + [any_spec()] * 5,
        scratch_shapes=[
            pltpu.VMEM(wo.shape, BF), pltpu.VMEM(wi.shape, BF), pltpu.VMEM(wb.shape, BF),
            tok(BF), tok(F32), tok(F32), pltpu.VMEM((tokens, 1), F32), tok(BF), pltpu.VMEM((width, tokens), BF),
            wide(F32), wide(BF), pltpu.VMEM((ff, tokens), BF), wide(BF), tok(F32), tok(BF), tok(BF),
            pltpu.VMEM(wi.shape, BF), pltpu.VMEM(wo.shape, BF), pltpu.VMEM(wb.shape, BF),
            tok(BF), pltpu.VMEM(att.shape, BF), pltpu.VMEM(owner, F32),
            pltpu.VMEM((6, 8, width), F32), pltpu.VMEM((8, width), F32), pltpu.VMEM((1, ff), F32),
            dma(3), dma(8),
        ],
        compiler_params=pltpu.CompilerParams(vmem_limit_bytes=VMEM_LIMIT),
        name="mid",
    )(x, att, wo, wi, wb, fv, bi, cot)


def finish_kernel(ix, oi, oo, ob, oq, px, pi, po, pb, pq, wide, sem):
    copies = [pltpu.make_async_copy(a, b, sem.at[k]) for k, (a, b) in enumerate(((ix, px), (oi, pi), (ob, pb), (oo, po)))]
    for cp in copies:
        cp.start()
    per = oq.shape[3] // 3
    for g in range(4):
        v = oq[g].reshape(wide.shape[0], 3 * per)
        for k in range(3):
            wide[:, (k * 4 + g) * per:(k * 4 + g + 1) * per] = v[:, k * per:(k + 1) * per]
    copies.append(pltpu.make_async_copy(wide, pq, sem.at[4]))
    copies[4].start()
    for cp in copies:
        cp.wait()


def finish(ix, oi, oo, ob, oq):
    shape = jax.ShapeDtypeStruct
    wide = (oq.shape[1] * oq.shape[2], oq.shape[3] * 4)
    return pl.pallas_call(
        finish_kernel,
        out_shape=[shape(a.shape, F32) for a in (ix, oi, oo, ob)] + [shape(wide, F32)],
        in_specs=[vmem_spec()] * 5,
        out_specs=[any_spec()] * 5,
        scratch_shapes=[pltpu.VMEM(wide, F32), dma(5)],
        name="finish",
    )(ix, oi, oo, ob, oq)


def on_device_fast(
    inputs, segments, w_qkv, b_query, b_value, w_out, b_attn, gain_one, shift_one,
    w_in, b_in, w_back, b_back, gain_two, shift_two, cotangent,
):
    nseq, span, width = inputs.shape
    tokens = nseq * span
    ff = w_in.shape[1]
    depth = w_in.shape[0]
    d, t, z, c, _, _ = place()
    per = width // 4
    vecs = (b_query, b_value, b_attn, gain_one, shift_one, b_back, gain_two, shift_two)
    ffd = b_in.shape[0]
    xs, ids, gi, go, gb, fv, bi, att, qkv, o32, lse, wt = front(
        inputs, segments, w_in.reshape(depth // 8, 8, ff), w_out.reshape(depth // 8, 8, width),
        w_back.reshape(ffd // 8, 8, width),
        jnp.stack(vecs), b_in.reshape(1, ffd), w_qkv.reshape(depth // 8, 8, 3 * width))
    output, d_one, d_att, grad_w_in, grad_w_out, grad_w_back, g_small = mid(
        inputs.reshape(tokens, width), att.reshape(nseq, width, span), go.reshape(width, width),
        gi.reshape(width, ff), gb.reshape(ff, width), fv, bi, cotangent.reshape(tokens, width))
    output = output.reshape(nseq, span, width)
    owner = (2, 2, 4, 2)
    input_grad, oi, oo, ob, os_, oq = back(
        d_att.reshape(8, per, span),
        grad_w_in.reshape(owner + (depth // 8, 8, ff)),
        grad_w_out.reshape(owner + (depth // 8, 8, width)),
        grad_w_back.reshape(owner + (ffd // 8, 8, width)),
        g_small, qkv, ids, o32, lse, wt, xs, d_one.reshape(nseq, span, width),
    )
    input_grad, oi, oo, ob, g_qkv = finish(input_grad, oi, oo, ob, oq)
    vec = lambda k: os_[k, :depth]
    return (
        output, input_grad, g_qkv, vec(8), vec(9), oo.reshape(depth, width), vec(0), vec(1), vec(2),
        oi.reshape(depth, ff), os_[6, :ffd], ob.reshape(ffd, width),
        vec(3), vec(4), vec(5),
    )


negative_fill = -1e30


def layer_norm(resid, gain, shift):
    center = resid - jnp.mean(resid, axis=-1, keepdims=True)
    spread = jnp.mean(center * center, axis=-1, keepdims=True)
    return center * lax.rsqrt(spread + layer_eps) * gain + shift


def gelu_exact(values):
    return jax.nn.gelu(values, approximate=False)


def attend_forward(entries):
    query_rows, key_rows, value_rows, query_ids, key_ids = entries
    scores = jnp.einsum(
        "qhd,khd->hqk", query_rows, key_rows, preferred_element_type=jnp.float32
    ) * HEAD_DIM ** (-0.5)
    allowed = (query_ids[:, None] == key_ids[None, :])[None]
    scores = jnp.where(allowed, scores, negative_fill)
    peak = jnp.max(scores, axis=-1, keepdims=True)
    raised = jnp.exp(scores - peak)
    total = jnp.sum(raised, axis=-1, keepdims=True)
    probs_low = (raised / total).astype(jnp.bfloat16)
    context = jnp.einsum("hqk,khd->qhd", probs_low, value_rows, preferred_element_type=jnp.float32)
    return (context, (peak + jnp.log(total))[..., 0])


def score_terms(query_rows, key_rows, value_rows, grad_context, log_total, query_ids, key_ids):
    scale = HEAD_DIM ** (-0.5)
    scores = (
        jnp.einsum("qhd,khd->hqk", query_rows, key_rows, preferred_element_type=jnp.float32) * scale
    )
    allowed = (query_ids[:, None] == key_ids[None, :])[None]
    probs = jnp.where(allowed, jnp.exp(scores - log_total[..., None]), 0.0)
    d_probs = jnp.einsum(
        "qhd,khd->hqk", grad_context, value_rows, preferred_element_type=jnp.float32
    )
    return (probs, d_probs)


def attend_backward(entries):
    query_rows, key_rows, value_rows, grad_context, log_total, query_ids, key_ids = entries
    scale = HEAD_DIM ** (-0.5)
    probs, d_probs = score_terms(
        query_rows, key_rows, value_rows, grad_context, log_total, query_ids, key_ids
    )
    inner = jnp.sum(probs * d_probs, axis=-1, keepdims=True)
    d_scores = (probs * (d_probs - inner)).astype(jnp.bfloat16)
    d_queries = (
        jnp.einsum("hqk,khd->qhd", d_scores, key_rows, preferred_element_type=jnp.float32) * scale
    )
    d_keys = (
        jnp.einsum("hqk,qhd->khd", d_scores, query_rows, preferred_element_type=jnp.float32) * scale
    )
    d_values = jnp.einsum(
        "hqk,qhd->khd", probs.astype(jnp.bfloat16), grad_context, preferred_element_type=jnp.float32
    )
    length = key_rows.shape[0]
    return (
        d_queries,
        d_keys.reshape(length, HEADS * HEAD_DIM),
        d_values.reshape(length, HEADS * HEAD_DIM),
    )


def on_device_general(
    inputs,
    segments,
    w_qkv,
    b_query,
    b_value,
    w_out,
    b_attn,
    gain_one,
    shift_one,
    w_in,
    b_in,
    w_back,
    b_back,
    gain_two,
    shift_two,
    cotangent,
):
    seq_count, group_len, model_width = inputs.shape
    tok_count = seq_count * group_len
    gathered = (
        lax.all_gather(w_qkv, ("dp", "ctx"), axis=0, tiled=True),
        lax.all_gather(b_query, ("dp", "ctx"), axis=0, tiled=True),
        lax.all_gather(b_value, ("dp", "ctx"), axis=0, tiled=True),
        lax.all_gather(w_out, ("dp", "ctx"), axis=0, tiled=True),
        lax.all_gather(b_attn, ("dp", "ctx"), axis=0, tiled=True),
        lax.all_gather(gain_one, ("dp", "ctx"), axis=0, tiled=True),
        lax.all_gather(shift_one, ("dp", "ctx"), axis=0, tiled=True),
        lax.all_gather(w_in, ("dp", "ctx"), axis=0, tiled=True),
        lax.all_gather(b_in, ("dp", "ctx"), axis=0, tiled=True),
        lax.all_gather(w_back, ("dp", "ctx"), axis=0, tiled=True),
        lax.all_gather(b_back, ("dp", "ctx"), axis=0, tiled=True),
        lax.all_gather(gain_two, ("dp", "ctx"), axis=0, tiled=True),
        lax.all_gather(shift_two, ("dp", "ctx"), axis=0, tiled=True),
    )
    (
        wide_qkv,
        full_b_query,
        full_b_value,
        wide_out,
        full_b_attn,
        full_gain_one,
        full_shift_one,
        wide_in,
        full_b_in,
        wide_back,
        full_b_back,
        full_gain_two,
        full_shift_two,
    ) = gathered
    tokens = inputs.reshape(tok_count, model_width)
    projected = jnp.dot(tokens, wide_qkv, preferred_element_type=jnp.float32)
    query_low = (projected[:, :model_width] + full_b_query.astype(jnp.float32)).astype(jnp.bfloat16)
    key_low = projected[:, model_width : 2 * model_width].astype(jnp.bfloat16)
    value_low = (projected[:, 2 * model_width :] + full_b_value.astype(jnp.float32)).astype(
        jnp.bfloat16
    )
    key_ids = lax.all_gather(segments, "ctx", axis=1, tiled=True)
    key_local = key_low.reshape(seq_count, group_len, model_width)
    value_local = value_low.reshape(seq_count, group_len, model_width)
    key_whole, value_whole = (
        lax.all_gather(key_local, "ctx", axis=1, tiled=True),
        lax.all_gather(value_local, "ctx", axis=1, tiled=True),
    )
    seq_len = key_whole.shape[1]
    query_heads = query_low.reshape(seq_count, group_len, HEADS, HEAD_DIM)
    context, log_total = lax.map(
        attend_forward,
        (
            query_heads,
            key_whole.reshape(seq_count, seq_len, HEADS, HEAD_DIM),
            value_whole.reshape(seq_count, seq_len, HEADS, HEAD_DIM),
            segments,
            key_ids,
        ),
    )
    attended = context.reshape(tok_count, model_width).astype(jnp.bfloat16)
    attn_out = jnp.dot(attended, wide_out, preferred_element_type=jnp.float32) + full_b_attn.astype(
        jnp.float32
    )
    resid_one = tokens.astype(jnp.float32) + attn_out
    normed, norm_one_back = jax.vjp(
        layer_norm, resid_one, full_gain_one.astype(jnp.float32), full_shift_one.astype(jnp.float32)
    )
    normed_low = normed.astype(jnp.bfloat16)
    pre_act = jnp.dot(normed_low, wide_in, preferred_element_type=jnp.float32) + full_b_in.astype(
        jnp.float32
    )
    activ_f, gelu_back = jax.vjp(gelu_exact, pre_act)
    activ = activ_f.astype(jnp.bfloat16)
    branch = jnp.dot(activ, wide_back, preferred_element_type=jnp.float32) + full_b_back.astype(
        jnp.float32
    )
    resid_two = normed + branch
    final_norm, norm_two_back = jax.vjp(
        layer_norm, resid_two, full_gain_two.astype(jnp.float32), full_shift_two.astype(jnp.float32)
    )
    output = final_norm.astype(jnp.bfloat16).reshape(seq_count, group_len, model_width)
    back_qkv, back_out, back_in, back_back = (
        lax.all_gather(w_qkv, ("dp", "ctx"), axis=0, tiled=True),
        lax.all_gather(w_out, ("dp", "ctx"), axis=0, tiled=True),
        lax.all_gather(w_in, ("dp", "ctx"), axis=0, tiled=True),
        lax.all_gather(w_back, ("dp", "ctx"), axis=0, tiled=True),
    )
    d_final = cotangent.reshape(tok_count, model_width).astype(jnp.float32)
    d_two, grad_gain_two, grad_shift_two = norm_two_back(d_final)
    d_branch = d_two.astype(jnp.bfloat16)
    grad_b_back = jnp.sum(d_branch.astype(jnp.float32), axis=0)
    grad_w_back = jnp.einsum("tf,td->fd", activ, d_branch, preferred_element_type=jnp.float32)
    d_activ = jnp.einsum("td,fd->tf", d_branch, back_back, preferred_element_type=jnp.float32)
    d_pre = gelu_back(d_activ)[0].astype(jnp.bfloat16)
    grad_b_in = jnp.sum(d_pre.astype(jnp.float32), axis=0)
    grad_w_in = jnp.einsum("td,tf->df", normed_low, d_pre, preferred_element_type=jnp.float32)
    d_normed = d_two + jnp.einsum("tf,df->td", d_pre, back_in, preferred_element_type=jnp.float32)
    d_one, grad_gain_one, grad_shift_one = norm_one_back(d_normed)
    d_attn = d_one.astype(jnp.bfloat16)
    grad_b_attn = jnp.sum(d_attn.astype(jnp.float32), axis=0)
    grad_w_out = jnp.einsum("ti,td->id", attended, d_attn, preferred_element_type=jnp.float32)
    d_attended = jnp.einsum(
        "td,id->ti", d_attn, back_out, preferred_element_type=jnp.float32
    ).astype(jnp.bfloat16)
    key_back, value_back = (
        lax.all_gather(key_local, "ctx", axis=1, tiled=True),
        lax.all_gather(value_local, "ctx", axis=1, tiled=True),
    )
    grad_heads = d_attended.reshape(seq_count, group_len, HEADS, HEAD_DIM)
    d_query_part, d_key_part, d_value_part = lax.map(
        attend_backward,
        (
            query_heads,
            key_back.reshape(seq_count, seq_len, HEADS, HEAD_DIM),
            value_back.reshape(seq_count, seq_len, HEADS, HEAD_DIM),
            grad_heads,
            log_total,
            segments,
            key_ids,
        ),
    )
    d_key_sum, d_value_sum = (
        lax.psum_scatter(
            d_key_part.astype(jnp.bfloat16), "ctx", scatter_dimension=1, tiled=True
        ).astype(jnp.float32),
        lax.psum_scatter(
            d_value_part.astype(jnp.bfloat16), "ctx", scatter_dimension=1, tiled=True
        ).astype(jnp.float32),
    )
    d_queries = d_query_part.reshape(tok_count, model_width).astype(jnp.bfloat16)
    d_keys = d_key_sum.reshape(tok_count, model_width).astype(jnp.bfloat16)
    d_values = d_value_sum.reshape(tok_count, model_width).astype(jnp.bfloat16)
    d_proj = jnp.concatenate([d_queries, d_keys, d_values], axis=1)
    grad_w_qkv = jnp.einsum("td,te->de", tokens, d_proj, preferred_element_type=jnp.float32)
    grad_b_query = jnp.sum(d_queries.astype(jnp.float32), axis=0)
    grad_b_value = jnp.sum(d_values.astype(jnp.float32), axis=0)
    input_grad = d_one + jnp.einsum(
        "te,de->td", d_proj, back_qkv, preferred_element_type=jnp.float32
    )
    summed = (
        lax.psum_scatter(grad_w_qkv, ("dp", "ctx"), scatter_dimension=0, tiled=True),
        lax.psum_scatter(grad_b_query, ("dp", "ctx"), scatter_dimension=0, tiled=True),
        lax.psum_scatter(grad_b_value, ("dp", "ctx"), scatter_dimension=0, tiled=True),
        lax.psum_scatter(grad_w_out, ("dp", "ctx"), scatter_dimension=0, tiled=True),
        lax.psum_scatter(grad_b_attn, ("dp", "ctx"), scatter_dimension=0, tiled=True),
        lax.psum_scatter(grad_gain_one, ("dp", "ctx"), scatter_dimension=0, tiled=True),
        lax.psum_scatter(grad_shift_one, ("dp", "ctx"), scatter_dimension=0, tiled=True),
        lax.psum_scatter(grad_w_in, ("dp", "ctx"), scatter_dimension=0, tiled=True),
        lax.psum_scatter(grad_b_in, ("dp", "ctx"), scatter_dimension=0, tiled=True),
        lax.psum_scatter(grad_w_back, ("dp", "ctx"), scatter_dimension=0, tiled=True),
        lax.psum_scatter(grad_b_back, ("dp", "ctx"), scatter_dimension=0, tiled=True),
        lax.psum_scatter(grad_gain_two, ("dp", "ctx"), scatter_dimension=0, tiled=True),
        lax.psum_scatter(grad_shift_two, ("dp", "ctx"), scatter_dimension=0, tiled=True),
    )
    return (
        output,
        input_grad.reshape(seq_count, group_len, model_width),
        summed[0],
        summed[1],
        summed[2],
        summed[3],
        summed[4],
        summed[5],
        summed[6],
        summed[7],
        summed[8],
        summed[9],
        summed[10],
        summed[11],
        summed[12],
    )


def solution(mesh):
    placed = (
        P("dp", "ctx", None),
        P("dp", "ctx"),
        P(("dp", "ctx"), None),
        P(("dp", "ctx")),
        P(("dp", "ctx")),
        P(("dp", "ctx"), None),
        P(("dp", "ctx")),
        P(("dp", "ctx")),
        P(("dp", "ctx")),
        P(("dp", "ctx"), None),
        P(("dp", "ctx")),
        P(("dp", "ctx"), None),
        P(("dp", "ctx")),
        P(("dp", "ctx")),
        P(("dp", "ctx")),
        P("dp", "ctx", None),
    )
    fits = mesh.shape["dp"] == 4 and mesh.shape["ctx"] == 8
    return jax.shard_map(
        on_device_fast if fits else on_device_general,
        mesh=mesh,
        in_specs=placed,
        out_specs=(
            P("dp", "ctx", None),
            P("dp", "ctx", None),
            P(("dp", "ctx"), None),
            P(("dp", "ctx")),
            P(("dp", "ctx")),
            P(("dp", "ctx"), None),
            P(("dp", "ctx")),
            P(("dp", "ctx")),
            P(("dp", "ctx")),
            P(("dp", "ctx"), None),
            P(("dp", "ctx")),
            P(("dp", "ctx"), None),
            P(("dp", "ctx")),
            P(("dp", "ctx")),
            P(("dp", "ctx")),
        ),
        check_vma=False,
    )
```
